32 devices in a mesh: fsdp: 4 (over y, x), ctx: 2 (over core), tp: 4 (over z).
Axes of the slice: x: 2, y: 2, z: 4, core: 2. Of those that a mesh axis runs over, the one named last changes fastest.
Arguments:
- tokens: bfloat16 [4, 2048, 1600], P('fsdp', ('ctx', 'tp')), may hold values from -6 to 6
- segments: int32 [4, 2048], P('fsdp'), may hold values from 0 to 7, never falling along the last dimension, each value on 1 to 1536 neighbouring positions
- cotangent: bfloat16 [4, 2048, 1600], P('fsdp', ('ctx', 'tp')), may hold values from -6 to 6
- meta_tokens: bfloat16 [1600, 128], P(('fsdp', 'ctx')), may hold values from -6 to 6
- gain_mix: bfloat16 [1600], P(('fsdp', 'ctx')), may hold values from 0.5 to 1.5
- query_weight: bfloat16 [1600, 1600], P(('fsdp', 'ctx')), may hold values from -0.15625 to 0.15625
- key_value_weight: bfloat16 [1600, 640], P(('fsdp', 'ctx')), may hold values from -0.15625 to 0.15625
- attn_output: bfloat16 [1600, 1600], P(('fsdp', 'ctx')), may hold values from -0.15625 to 0.15625
- gain_attn: bfloat16 [1600], P(('fsdp', 'ctx')), may hold values from 0.5 to 1.5
- mamba_input: bfloat16 [1600, 3, 3200], P(('fsdp', 'ctx'), None, 'tp'), may hold values from -0.15625 to 0.15625
- mamba_select: bfloat16 [1600, 32], P(('fsdp', 'ctx')), may hold values from -0.15625 to 0.15625
- step_bias: float32 [3200], P('tp'), may hold values from -1 to 1
- decay_log: float32 [3200], P('tp'), may hold values from -9.2 to -3
- state_skip: float32 [3200], P('tp'), may hold values from 0.5 to 1.5
- mamba_output: bfloat16 [1600, 3200], P(('fsdp', 'ctx'), 'tp'), may hold values from -0.109375 to 0.109375
- gain_mamba: bfloat16 [1600], P(('fsdp', 'ctx')), may hold values from 0.5 to 1.5
- gain_ffn: bfloat16 [1600], P(('fsdp', 'ctx')), may hold values from 0.5 to 1.5
- ffn_input: bfloat16 [1600, 2, 5504], P(('fsdp', 'ctx')), may hold values from -0.15625 to 0.15625
- ffn_output: bfloat16 [1600, 5504], P(('fsdp', 'ctx')), may hold values from -0.078125 to 0.078125
Outputs:
- layer_out: bfloat16 [4, 2048, 1600], P('fsdp', ('ctx', 'tp'))
- grad_tokens: bfloat16 [4, 2048, 1600], P('fsdp', ('ctx', 'tp'))
- grad_meta: float32 [1600, 128], P(('fsdp', 'ctx'), 'tp')
- grad_gain_mix: float32 [1600], P(('fsdp', 'ctx'))
- grad_query: float32 [1600, 1600], P(('fsdp', 'ctx'), 'tp')
- grad_keyval: float32 [1600, 640], P(('fsdp', 'ctx'), 'tp')
- grad_attn_output: float32 [1600, 1600], P(('fsdp', 'ctx'), 'tp')
- grad_gain_attn: float32 [1600], P(('fsdp', 'ctx'))
- grad_mamba_input: float32 [1600, 3, 3200], P(('fsdp', 'ctx'), None, 'tp')
- grad_mamba_select: float32 [1600, 32], P(('fsdp', 'ctx'), 'tp')
- grad_step_bias: float32 [3200], P('tp')
- grad_decay_log: float32 [3200], P('tp')
- grad_state_skip: float32 [3200], P('tp')
- grad_mamba_output: float32 [1600, 3200], P(('fsdp', 'ctx'), 'tp')
- grad_gain_mamba: float32 [1600], P(('fsdp', 'ctx'))
- grad_gain_ffn: float32 [1600], P(('fsdp', 'ctx'))
- grad_ffn_input: float32 [1600, 2, 5504], P(('fsdp', 'ctx'), None, 'tp')
- grad_ffn_output: float32 [1600, 5504], P(('fsdp', 'ctx'), 'tp')
The draws below stay inside these ranges and needn't reach their ends.
Inputs may be any that keep to these rules, and one draw needn't show every extreme that they name: `segments`: in every sequence the segment numbers start at 0, never fall, and each document holds at most 1536 tokens.
All inputs are finite; a program needn't handle non-finite values.
Results may differ from the reference program's by a relative error of at most 0.019.
Values may be sent and summed in bfloat16 or wider, within the bound.
A program may use at most 384 MiB of HBM per device.

```python
import math
import jax
import jax.numpy as jnp
import numpy as np
from jax import lax

MODEL_WIDTH = 1600
QUERY_HEAD_COUNT = 25
KEY_VALUE_HEADS = 5
HEAD_SIZE = 64
INNER = 3200
STATE = 16
FF = 5504
META = 128
WIN = 1024
STRETCH = 16
NSEG = 8
LEN_DEV = 1024
SEQ_LEN = 2048
SEQS = 4
N_CTX = 2


def block_levels(key, dims, cuts, smallest, top_value):
    level = 1.0
    for dim, parts in cuts:
        steps = jax.random.uniform(jax.random.fold_in(jax.random.fold_in(key, 6), dim), (parts,), jnp.float32, smallest / len(cuts), top_value / len(cuts))
        level = level * jnp.repeat(jnp.exp(steps), dims[dim] // parts).reshape((-1,) + (1,) * (len(dims) - 1 - dim))
    return level


def length_profile(count, total, limit, lean):
    weights = [(1 << 20) // math.isqrt(grade ** lean) + 1 for grade in range(2, count + 1)]
    rest, given = total - limit - (count - 1), [1] * (count - 1)
    while rest > 0:
        candidates = [i for i in range(count - 1) if given[i] < limit]
        pool, budget = sum([weights[i] for i in candidates]), rest
        for i in candidates:
            more = min(limit - given[i], max(1, budget * weights[i] // pool), rest)
            given[i] = given[i] + more
            rest = rest - more
    return np.array([limit] + given)


def ragged(own_key, number_of, total, most, skew):
    if number_of == 2:
        one = jax.random.randint(own_key, (), max(1, total - most), min(most, total - 1) + 1)
        return jnp.stack([one, total - one])
    tallies = jnp.asarray(length_profile(number_of, total, most, skew), jnp.int32)
    couples = (number_of - 1) // 2
    donor, taker = tallies[1:1 + 2 * couples:2], tallies[2:2 + 2 * couples:2]
    room = jnp.minimum(donor - 1, most - taker)
    moved = jax.random.randint(jax.random.fold_in(own_key, 1), (couples,), 0, 1 << 20) % (room + 1)
    tallies = tallies.at[1:1 + 2 * couples:2].set(donor - moved).at[2:2 + 2 * couples:2].set(taker + moved)
    return tallies[jax.random.permutation(jax.random.fold_in(own_key, 2), number_of)]


def gaussian(rng, shape, scale, reach, shards=(), kind=jnp.bfloat16):
    drawn = jax.random.normal(rng, shape, jnp.float32) * scale
    if len(shards) > 0:
        drawn = block_levels(rng, shape, shards, -0.22, 0.18) * drawn
    return jnp.clip(drawn, min=-reach, max=reach).astype(kind)


def setup_inputs(seed: int = 0) -> dict:
    streams_of = jax.random.split(jax.random.key(seed), 20)
    tokens = gaussian(streams_of[0], (SEQS, SEQ_LEN, MODEL_WIDTH), 1.0, 6.0, ((0, 4), (1, 8)))
    segments = jax.vmap(lambda own: jnp.searchsorted(jnp.cumsum(ragged(own, NSEG, SEQ_LEN, LEN_DEV * N_CTX * 3 // 4, 2)), jnp.arange(SEQ_LEN), side="right"))(jax.random.split(streams_of[1], SEQS)).reshape((SEQS, SEQ_LEN)).astype(jnp.int32)
    cotangent = gaussian(streams_of[2], (SEQS, SEQ_LEN, MODEL_WIDTH), 1.0, 6.0, ((0, 4), (1, 8)))
    meta_tokens = gaussian(streams_of[3], (MODEL_WIDTH, META), 1.0, 6.0, ((0, 8),))
    gain_mix = jnp.clip(1.0 + 0.1 * jax.random.normal(streams_of[4], (MODEL_WIDTH,), jnp.float32), 0.5, 1.5).astype(jnp.bfloat16)
    query_weight = gaussian(streams_of[5], (MODEL_WIDTH, QUERY_HEAD_COUNT * HEAD_SIZE), MODEL_WIDTH ** -0.5, 0.15625, ((0, 8),))
    key_value_weight = gaussian(streams_of[6], (MODEL_WIDTH, 2 * KEY_VALUE_HEADS * HEAD_SIZE), MODEL_WIDTH ** -0.5, 0.15625, ((0, 8),))
    attn_output = gaussian(streams_of[7], (MODEL_WIDTH, QUERY_HEAD_COUNT * HEAD_SIZE), (QUERY_HEAD_COUNT * HEAD_SIZE) ** -0.5, 0.15625, ((0, 8),))
    gain_attn = jnp.clip(1.0 + 0.1 * jax.random.normal(streams_of[8], (MODEL_WIDTH,), jnp.float32), 0.5, 1.5).astype(jnp.bfloat16)
    mamba_input = gaussian(streams_of[9], (MODEL_WIDTH, 3, INNER), MODEL_WIDTH ** -0.5, 0.15625, ((0, 8), (2, 4)))
    mamba_select = gaussian(streams_of[10], (MODEL_WIDTH, 2 * STATE), MODEL_WIDTH ** -0.5, 0.15625, ((0, 8),))
    step_bias = jnp.clip(jax.random.uniform(streams_of[11], (INNER,), jnp.float32, -1.0, 1.0) * block_levels(streams_of[11], (INNER,), ((0, 4),), -0.4, 0.0), -1.0, 1.0)
    decay_log = jnp.clip(-9.2 + 6.2 * jax.random.uniform(streams_of[12], (INNER,), jnp.float32) ** block_levels(streams_of[12], (INNER,), ((0, 4),), -0.2, 0.2), -9.2, -3.0)
    state_skip = jnp.clip(0.5 + 1.0 * jax.random.uniform(streams_of[13], (INNER,), jnp.float32) ** block_levels(streams_of[13], (INNER,), ((0, 4),), -0.2, 0.2), 0.5, 1.5)
    mamba_output = gaussian(streams_of[14], (MODEL_WIDTH, INNER), INNER ** -0.5, 0.109375, ((0, 8), (1, 4)))
    gain_mamba = jnp.clip(1.0 + 0.1 * jax.random.normal(streams_of[15], (MODEL_WIDTH,), jnp.float32), 0.5, 1.5).astype(jnp.bfloat16)
    gain_ffn = jnp.clip(1.0 + 0.1 * jax.random.normal(streams_of[16], (MODEL_WIDTH,), jnp.float32), 0.5, 1.5).astype(jnp.bfloat16)
    ffn_input = gaussian(streams_of[17], (MODEL_WIDTH, 2, FF), MODEL_WIDTH ** -0.5, 0.15625, ((0, 8),))
    ffn_output = gaussian(streams_of[18], (MODEL_WIDTH, FF), FF ** -0.5, 0.078125, ((0, 8),))
    return dict(tokens=tokens, segments=segments, cotangent=cotangent, meta_tokens=meta_tokens, gain_mix=gain_mix, query_weight=query_weight, key_value_weight=key_value_weight, attn_output=attn_output, gain_attn=gain_attn, mamba_input=mamba_input, mamba_select=mamba_select, step_bias=step_bias, decay_log=decay_log, state_skip=state_skip, mamba_output=mamba_output, gain_mamba=gain_mamba, gain_ffn=gain_ffn, ffn_input=ffn_input, ffn_output=ffn_output)


epsilon = 1e-05
highest = lax.Precision.HIGHEST
masked_score = -1e+30

@jax.custom_vjp
def low(v):
    return lax.optimization_barrier(v.astype(jnp.bfloat16)).astype(jnp.float32)

@jax.custom_vjp
def low_back(v):
    return v

def low_keep(v):
    return (low(v), None)

def low_pass(kept, grad):
    return (grad,)

def back_keep(v):
    return (v, None)

def back_low(kept, grad):
    return (low(grad),)
low.defvjp(low_keep, low_pass)
low_back.defvjp(back_keep, back_low)

def low_both(values):
    return low_back(low(values))

def rms_norm(values, gain):
    return values * lax.rsqrt(lax.optimization_barrier(jnp.mean(values * values, axis=-1, keepdims=True)) + epsilon) * gain

def state_blocks(inputs, step_raw, in_map, out_map, step_bias, decay_log, segment, segment_before):
    sequence_batch, sequence_length, channels = inputs.shape
    width = in_map.shape[-1]
    step_size = jax.nn.softplus(step_raw + step_bias)
    log_decay = -step_size * jnp.exp(decay_log)
    driven = step_size * inputs
    blocks = sequence_length // STRETCH

    def split(values):
        return jnp.swapaxes(values.reshape((sequence_batch, blocks, STRETCH) + values.shape[2:]), 0, 1)
    order = jnp.arange(STRETCH, dtype=jnp.int32)
    lower = order[:, None] >= order[None, :]

    def advance(carry, piece):
        state, factor, previous = carry
        piece_decay, piece_driven, piece_in, piece_out, piece_segment = piece
        cumulative = jnp.cumsum(piece_decay, axis=1)
        same = (piece_segment[:, :, None] == piece_segment[:, None, :]) & lower[None]
        spread = cumulative[:, :, None, :] - cumulative[:, None, :, :]
        weights = jnp.where(same[..., None], jnp.exp(jnp.minimum(spread, 0.0)), 0.0)
        intersection = jnp.einsum('atn,asn->ats', piece_out, piece_in, precision=highest)
        result = jnp.einsum('atsc,ats,asc->atc', weights, intersection, piece_driven, precision=highest)
        alive = (piece_segment == previous[:, None]).astype(jnp.float32)
        carried = alive[:, :, None] * jnp.exp(cumulative)
        result = result + carried * jnp.einsum('atn,acn->atc', piece_out, state, precision=highest)
        row_factor = carried * factor[:, None, :]
        tail = (piece_segment == piece_segment[:, -1:]).astype(jnp.float32)[:, :, None] * jnp.exp(cumulative[:, -1:, :] - cumulative)
        state = carried[:, -1, :, None] * state + jnp.einsum('asc,asn->acn', tail * piece_driven, piece_in, precision=highest)
        factor = carried[:, -1, :] * factor
        return ((state, factor, piece_segment[:, -1]), (result, row_factor))
    start = (jnp.zeros((sequence_batch, channels, width), jnp.float32), jnp.ones((sequence_batch, channels), jnp.float32), segment_before)
    final, (result, row_factor) = lax.scan(jax.checkpoint(advance), start, (split(log_decay), split(driven), split(in_map), split(out_map), split(segment)))

    def join(values):
        return jnp.swapaxes(values, 0, 1).reshape((sequence_batch, sequence_length) + values.shape[3:])
    return (join(result), join(row_factor), final[0], final[1])

def layer(params, resid, segment):
    meta_tokens, gain_mix, query_weight, key_value_weight, attn_output, gain_attn, mamba_input, mamba_select, step_bias, decay_log, state_skip, mamba_output, gain_mamba, gain_ffn, ffn_input, ffn_output = params
    sequence_length = resid.shape[0]
    key_value_width = KEY_VALUE_HEADS * HEAD_SIZE
    head_group = QUERY_HEAD_COUNT // KEY_VALUE_HEADS
    normed = low(rms_norm(resid, gain_mix))
    meta_normed = low(rms_norm(meta_tokens.T, gain_mix))
    query_rows = low_both(jnp.dot(normed, query_weight, precision=highest))
    keyvals = low_both(jnp.dot(normed, key_value_weight, precision=highest))
    meta_keyvals = low(jnp.dot(meta_normed, key_value_weight, precision=highest))
    every_key_value = jnp.concatenate([meta_keyvals, keyvals], axis=0)
    key_head_rows = every_key_value[:, :key_value_width].reshape(-1, KEY_VALUE_HEADS, HEAD_SIZE)
    value_head_rows = every_key_value[:, key_value_width:].reshape(-1, KEY_VALUE_HEADS, HEAD_SIZE)
    query_head_rows = query_rows.reshape(sequence_length, KEY_VALUE_HEADS, head_group, HEAD_SIZE)
    block = min(512, sequence_length)
    positions = jnp.arange(sequence_length, dtype=jnp.int32)

    def attend_block(index):
        start = index * block
        rows = lax.dynamic_slice_in_dim(query_head_rows, start, block, 0)
        query_pos = start + jnp.arange(block, dtype=jnp.int32)
        query_seg = lax.dynamic_slice_in_dim(segment, start, block, 0)
        near = (positions[None, :] <= query_pos[:, None]) & (query_pos[:, None] - positions[None, :] < WIN) & (query_seg[:, None] == segment[None, :])
        keep = jnp.concatenate([jnp.ones((block, META), jnp.bool_), near], axis=1)
        scores = low_back(jnp.einsum('rhgd,khd->hgrk', rows, key_head_rows, precision=highest) * HEAD_SIZE ** (-0.5))
        scores = jnp.where(keep[None, None], scores, masked_score)
        top = lax.optimization_barrier(jnp.max(scores, axis=-1, keepdims=True))
        expd = jnp.exp(scores - top)
        probs = low(expd / lax.optimization_barrier(jnp.sum(expd, axis=-1, keepdims=True)))
        return jnp.einsum('hgrk,khd->rhgd', probs, value_head_rows, precision=highest)
    attended = lax.map(jax.checkpoint(attend_block), jnp.arange(sequence_length // block, dtype=jnp.int32))
    attended = low_both(attended.reshape(sequence_length, QUERY_HEAD_COUNT * HEAD_SIZE))
    attn_out = low_back(jnp.dot(attended, attn_output.T, precision=highest))
    mixed = jnp.einsum('ld,dkc->lkc', normed, mamba_input, precision=highest)
    inputs = low_back(mixed[:, 0])
    gates = low_back(mixed[:, 1])
    step_raw = low_back(mixed[:, 2])
    selects = low_both(jnp.dot(normed, mamba_select, precision=highest))
    inner, row_factor, state_end, factor_end = state_blocks(inputs[None], step_raw[None], selects[None, :, :STATE], selects[None, :, STATE:], step_bias, decay_log, segment[None], jnp.full((1,), -1, jnp.int32))
    gated = low((inner[0] + state_skip * inputs) * jax.nn.silu(gates))
    mamba_out = low_back(jnp.dot(gated, mamba_output.T, precision=highest))
    mid = resid + 0.5 * (rms_norm(attn_out, gain_attn) + rms_norm(mamba_out, gain_mamba))
    ffn_normed = low(rms_norm(mid, gain_ffn))
    gate_up = low_back(jnp.einsum('ld,dkf->lkf', ffn_normed, ffn_input, precision=highest))
    hidden = low(jax.nn.silu(gate_up[:, 0]) * gate_up[:, 1])
    return mid + jnp.dot(hidden, ffn_output.T, precision=highest)

def reference(tokens, segments, cotangent, meta_tokens, gain_mix, query_weight, key_value_weight, attn_output, gain_attn, mamba_input, mamba_select, step_bias, decay_log, state_skip, mamba_output, gain_mamba, gain_ffn, ffn_input, ffn_output):
    params = tuple((value.astype(jnp.float32) for value in (meta_tokens, gain_mix, query_weight, key_value_weight, attn_output, gain_attn, mamba_input, mamba_select, step_bias, decay_log, state_skip, mamba_output, gain_mamba, gain_ffn, ffn_input, ffn_output)))

    def one_sequence(totals, item):
        resid, segment, grad_out = item
        result, pull = jax.vjp(lambda weights, start: layer(weights, start, segment), params, resid.astype(jnp.float32))
        weight_grads, input_grad = pull(grad_out.astype(jnp.float32))
        totals = jax.tree.map(lambda left, right: left + right, totals, weight_grads)
        return (totals, (result.astype(jnp.bfloat16), input_grad.astype(jnp.bfloat16)))
    totals, (layer_out, grad_tokens) = lax.scan(one_sequence, jax.tree.map(jnp.zeros_like, params), (tokens, segments, cotangent))
    return (layer_out, grad_tokens, totals[0], totals[1], totals[2], totals[3], totals[4], totals[5], totals[6], totals[7], totals[8], totals[9], totals[10], totals[11], totals[12], totals[13], totals[14], totals[15])
```

```python
import functools

import jax
import jax.numpy as jnp
from jax import lax
from jax.experimental import pallas as pl
from jax.experimental.pallas import tpu as pltpu
from jax.sharding import PartitionSpec as P

HEAD_SIZE = 64
STATE = 16
WIN = 1024
SUB = 4
TILE = 128

bf16 = jnp.bfloat16
f32 = jnp.float32
epsilon = 1e-05
masked_score = -1e30


def mm(a, b):
    return lax.dot_general(a, b, (((1,), (0,)), ((), ())), preferred_element_type=f32)


def mm_nt(a, b):
    return lax.dot_general(a, b, (((1,), (1,)), ((), ())), preferred_element_type=f32)


def iota(shape, dim):
    return lax.broadcasted_iota(jnp.int32, shape, dim)


def split_mm(a, b):
    high = b.astype(bf16)
    return mm(a, high) + mm(a, (b - high.astype(f32)).astype(bf16))


def ones_where(cond):
    return jnp.where(cond, 1.0, 0.0)


def softplus(v):
    return jnp.maximum(v, 0.0) + jnp.log1p(jnp.exp(-jnp.abs(v)))


def logistic(v):
    return 1.0 / (1.0 + jnp.exp(-v))


def group_mask(rows, columns, row_unit, column_unit):
    return iota((rows, columns), 0) // row_unit == iota((rows, columns), 1) // column_unit


def sums_matrix():
    rows = 2 * TILE + TILE // SUB
    row = iota((rows, TILE), 0)
    column = iota((rows, TILE), 1)
    token = row % TILE
    same = token // SUB == column // SUB
    upto = (row < TILE) & same & (column <= token)
    after = (row >= TILE) & (row < 2 * TILE) & same & (column > token)
    whole = (row >= 2 * TILE) & (row - 2 * TILE == column // SUB)
    return ones_where(upto | after | whole).astype(bf16)


def part(mixed, k):
    channels = mixed.shape[1] // 3
    return mixed[:, k * channels : (k + 1) * channels]


def decays(step_raw, bias_ref, rate_ref, alive_last_ref):
    raw = step_raw + bias_ref[...]
    step = softplus(raw)
    log_decay = -step * rate_ref[...]
    sums = split_mm(sums_matrix(), log_decay)
    upto = jnp.exp(sums[:TILE])
    after = sums[TILE : 2 * TILE]
    block = jnp.exp(sums[2 * TILE :]) * alive_last_ref[...]
    return raw, step, log_decay, upto, after, block


def in_blocks(select_t_ref, aux_t_ref):
    width = TILE // SUB * STATE
    tiled = jnp.concatenate([select_t_ref[:STATE, :].astype(f32) * aux_t_ref[1:2, :]] * (TILE // SUB), axis=0)
    return jnp.where(group_mask(width, TILE, STATE, SUB), tiled, 0.0).astype(bf16)


def out_blocks_t(select_t_ref, aux_t_ref):
    width = TILE // SUB * STATE
    tiled = jnp.concatenate([select_t_ref[STATE:, :].astype(f32) * aux_t_ref[0:1, :]] * (TILE // SUB), axis=0)
    return jnp.where(group_mask(width, TILE, STATE, SUB), tiled, 0.0).astype(bf16)


def spread(part, factor):
    width = TILE // SUB * STATE
    places = ones_where(iota((STATE, width), 0) == iota((STATE, width), 1) % STATE).astype(bf16)
    wide = mm(part, places) * factor
    return jnp.where(group_mask(TILE, width, SUB, STATE), wide, 0.0).astype(bf16)


def fold(wide, factor):
    width = TILE // SUB * STATE
    places = ones_where(iota((width, STATE), 0) % STATE == iota((width, STATE), 1)).astype(bf16)
    kept = jnp.where(group_mask(TILE, width, SUB, STATE), wide * factor, 0.0)
    return split_left(kept, places)


def split_left(a, b):
    high = a.astype(bf16)
    return mm(high, b) + mm((a - high.astype(f32)).astype(bf16), b)


def pairs(aux_ref, aux_t_ref, lower):
    row, column = iota((TILE, TILE), 0), iota((TILE, TILE), 1)
    order = column <= row if lower else column >= row
    return (row // SUB == column // SUB) & order & (aux_ref[:, 2:3] == aux_t_ref[2:3, :])


def run_states(state, local_ref, block_ref, keep=None):
    def one(k, state):
        if keep is not None:
            keep[pl.ds(pl.multiple_of(k * STATE, STATE), STATE), :] = state.astype(bf16)
        return block_ref[pl.ds(k, 1), :] * state + local_ref[pl.ds(pl.multiple_of(k * STATE, STATE), STATE), :]

    return lax.fori_loop(0, TILE // SUB, one, state, unroll=8)


def end_state_kernel(mixed, select_t, aux, aux_t, alive_last, bias, rate, end, state, local, block):
    @pl.when(pl.program_id(0) == 0)
    def _():
        state[...] = jnp.zeros_like(state)

    raw, step, log_decay, upto, after, total = decays(part(mixed, 2), bias, rate, alive_last)
    driven = (jnp.exp(after) * step * part(mixed, 0)).astype(bf16)
    local[...] = mm(in_blocks(select_t, aux_t), driven)
    block[...] = total
    state[...] = run_states(state[...], local, block)
    end[...] = state[...]


def forward_kernel(mixed, select, select_t, aux, aux_t, alive_last, bias, rate, skip, start, gated, states, end, state, local, block):
    @pl.when(pl.program_id(0) == 0)
    def _():
        state[...] = start[...]

    raw, step, log_decay, upto, after, total = decays(part(mixed, 2), bias, rate, alive_last)
    x = part(mixed, 0)
    driven = (jnp.exp(after) * step * x).astype(bf16)
    local[...] = mm(in_blocks(select_t, aux_t), driven)
    block[...] = total
    state[...] = run_states(state[...], local, block, states)
    end[...] = state[...]
    out_part = select[:, STATE:]
    cross = jnp.where(pairs(aux, aux_t, True), mm(out_part, select_t[:STATE, :]), 0.0).astype(bf16)
    y = upto * mm(spread(out_part, aux[:, 0:1]), states[...]) + jnp.exp(-after) * mm(cross, driven) + skip[...] * x
    gates = part(mixed, 1)
    gated[...] = (y * gates * logistic(gates)).astype(bf16)


def back_run(carry, local_ref, block_ref, keep, states=None, bound=None):
    count = TILE // SUB

    def one(i, carry):
        k = count - 1 - i
        rows = pl.ds(pl.multiple_of(k * STATE, STATE), STATE)
        if keep is not None:
            keep[rows, :] = carry[0].astype(bf16)
            bound[pl.ds(k, 1), :] = carry[1]
        new = block_ref[pl.ds(k, 1), :] * carry[0] + local_ref[rows, :]
        if keep is None:
            return (new, carry[1])
        return (new, jnp.sum(new * states[rows, :].astype(f32), axis=0, keepdims=True))

    return lax.fori_loop(0, count, one, carry, unroll=8)


def end_adjoint_kernel(gated_grad, mixed, select_t, aux, aux_t, alive_last, bias, rate, end, state, local, block):
    @pl.when(pl.program_id(0) == 0)
    def _():
        state[...] = jnp.zeros_like(state)

    raw, step, log_decay, upto, after, total = decays(part(mixed, 2), bias, rate, alive_last)
    gates = part(mixed, 1)
    dy = gated_grad[...] * gates * logistic(gates)
    local[...] = mm(out_blocks_t(select_t, aux_t), (upto * dy).astype(bf16))
    block[...] = total
    state[...] = back_run((state[...], jnp.zeros((1, state.shape[1]), f32)), local, block, None)[0]
    end[...] = state[...]


def backward_kernel(gated_grad, mixed, select, select_t, states, aux, aux_t, alive_last, bias, rate, skip, start, final,
                    mix_grad, select_grad, sums, state, local, block, adjoint, bound, edge):
    @pl.when(pl.program_id(0) == 0)
    def _():
        state[...] = start[...]
        edge[...] = jnp.sum(start[...] * final[...], axis=0, keepdims=True)
        sums[...] = jnp.zeros_like(sums)

    raw, step, log_decay, upto, after, total = decays(part(mixed, 2), bias, rate, alive_last)
    channels = state.shape[1]
    x = part(mixed, 0)
    decay_after = jnp.exp(after)
    grow = jnp.exp(-after)
    driven = (decay_after * step * x).astype(bf16)
    in_part, out_part = select[:, :STATE], select[:, STATE:]
    in_part_t, out_part_t = select_t[:STATE, :], select_t[STATE:, :]
    lower, upper = pairs(aux, aux_t, True), pairs(aux, aux_t, False)
    cross = jnp.where(lower, mm(out_part, in_part_t), 0.0).astype(bf16)
    cross_t = jnp.where(upper, mm(in_part, out_part_t), 0.0).astype(bf16)
    y = upto * mm(spread(out_part, aux[:, 0:1]), states[...]) + grow * mm(cross, driven)
    gates = part(mixed, 1)
    sigma = logistic(gates)
    grad = gated_grad[...]
    dy = grad * gates * sigma
    mix_grad[:, channels : 2 * channels] = (grad * (y + skip[...] * x) * (sigma * (1.0 + gates * (1.0 - sigma)))).astype(bf16)
    dy_low = (upto * dy).astype(bf16)
    dy_grown = (grow * dy).astype(bf16)
    local[...] = mm(out_blocks_t(select_t, aux_t), dy_low)
    block[...] = total
    new_state, new_edge = back_run((state[...], edge[...]), local, block, adjoint, states, bound)
    state[...] = new_state
    edge[...] = new_edge
    du = decay_after * (mm(spread(in_part, aux[:, 1:2]), adjoint[...]) + mm(cross_t, dy_grown))
    out_grad = fold(mm_nt(dy_low, states[...]), aux[:, 0:1])
    in_grad = fold(mm_nt(driven, adjoint[...]), aux[:, 1:2])
    cross_grad = jnp.where(lower, mm_nt(dy_grown, driven), 0.0)
    cross_grad_t = jnp.where(upper, mm_nt(driven, dy_grown), 0.0)
    out_grad = out_grad + split_left(cross_grad, in_part)
    in_grad = in_grad + split_left(cross_grad_t, out_part)
    select_grad[...] = jnp.concatenate([in_grad, out_grad], axis=1)
    flow = dy * y - step * x * du
    places = ones_where(group_mask(TILE, TILE // SUB, SUB, 1)) * aux[:, 1:2]
    decay_grad = aux[:, 3:4] * (
        split_mm(ones_where(upper).astype(bf16), flow) + split_mm(places.astype(bf16), bound[...])
    )
    step_grad = (x * du - rate[...] * decay_grad) * logistic(raw)
    mix_grad[:, :channels] = (skip[...] * dy + step * du).astype(bf16)
    mix_grad[:, 2 * channels :] = step_grad.astype(bf16)
    sums[0:1, :] += jnp.sum(step_grad, axis=0, keepdims=True)
    sums[1:2, :] += jnp.sum(decay_grad * log_decay, axis=0, keepdims=True)
    sums[2:3, :] += jnp.sum(dy * x, axis=0, keepdims=True)


def scan_specs(tiles, channels, back):
    at = (lambda i: tiles - 1 - i) if back else (lambda i: i)

    mixed = pl.BlockSpec((TILE, 3 * channels), lambda i: (at(i), 0))
    rows = pl.BlockSpec((TILE, channels), lambda i: (at(i), 0))
    select = pl.BlockSpec((TILE, 2 * STATE), lambda i: (at(i), 0))
    select_t = pl.BlockSpec((2 * STATE, TILE), lambda i: (0, at(i)))
    states = pl.BlockSpec((TILE // SUB * STATE, channels), lambda i: (at(i), 0))
    aux = pl.BlockSpec((TILE, 8), lambda i: (at(i), 0))
    aux_t = pl.BlockSpec((8, TILE), lambda i: (0, at(i)))
    last = pl.BlockSpec((TILE // SUB, 1), lambda i: (at(i), 0))
    row = pl.BlockSpec((1, channels), lambda i: (0, 0))
    state = pl.BlockSpec((STATE, channels), lambda i: (0, 0))
    return mixed, rows, select, select_t, states, aux, aux_t, last, row, state


def scan_scratch(channels):
    return [
        pltpu.VMEM((STATE, channels), f32),
        pltpu.VMEM((TILE // SUB * STATE, channels), f32),
        pltpu.VMEM((TILE // SUB, channels), f32),
    ]


PARAMS = pltpu.CompilerParams(vmem_limit_bytes=48 << 20, dimension_semantics=("arbitrary",))


def scan_aux(segment, before):
    count = segment.shape[0]
    blocks = segment.reshape(count // SUB, SUB)
    ends = jnp.concatenate([before[None], blocks[:-1, -1]])
    alive = (blocks == ends[:, None]).reshape(-1).astype(f32)
    tail = (blocks == blocks[:, -1:]).reshape(-1).astype(f32)
    joined = (segment == jnp.concatenate([before[None], segment[:-1]])).astype(f32)
    zero = jnp.zeros_like(alive)
    aux_t = jnp.stack([alive, tail, segment.astype(f32), joined, zero, zero, zero, zero])
    last = (blocks[:, -1] == ends).astype(f32)[:, None]
    return aux_t.T, aux_t, last


def end_state(mixed, select_t, aux, bias, rate):
    tokens, channels = mixed.shape[0], mixed.shape[1] // 3
    tiles = tokens // TILE
    mixed_s, rows, select_s, select_t_s, states_s, aux_s, aux_t_s, last_s, row, state = scan_specs(tiles, channels, False)
    return pl.pallas_call(
        end_state_kernel, grid=(tiles,),
        in_specs=[mixed_s, select_t_s, aux_s, aux_t_s, last_s, row, row],
        out_specs=state, out_shape=jax.ShapeDtypeStruct((STATE, channels), f32),
        scratch_shapes=scan_scratch(channels), compiler_params=PARAMS,
    )(mixed, select_t, *aux, bias, rate)


def forward_scan(mixed, select, select_t, aux, bias, rate, skip, start):
    tokens, channels = mixed.shape[0], mixed.shape[1] // 3
    tiles = tokens // TILE
    mixed_s, rows, select_s, select_t_s, states_s, aux_s, aux_t_s, last_s, row, state = scan_specs(tiles, channels, False)
    return pl.pallas_call(
        forward_kernel, grid=(tiles,),
        in_specs=[mixed_s, select_s, select_t_s, aux_s, aux_t_s, last_s, row, row, row, state],
        out_specs=[rows, states_s, state],
        out_shape=[jax.ShapeDtypeStruct((tokens, channels), bf16), jax.ShapeDtypeStruct((tokens // SUB * STATE, channels), bf16), jax.ShapeDtypeStruct((STATE, channels), f32)],
        scratch_shapes=scan_scratch(channels), compiler_params=PARAMS,
    )(mixed, select, select_t, *aux, bias, rate, skip, start)


def end_adjoint(gated_grad, mixed, select_t, aux, bias, rate):
    tokens, channels = mixed.shape[0], mixed.shape[1] // 3
    tiles = tokens // TILE
    mixed_s, rows, select_s, select_t_s, states_s, aux_s, aux_t_s, last_s, row, state = scan_specs(tiles, channels, True)
    return pl.pallas_call(
        end_adjoint_kernel, grid=(tiles,),
        in_specs=[rows, mixed_s, select_t_s, aux_s, aux_t_s, last_s, row, row],
        out_specs=state, out_shape=jax.ShapeDtypeStruct((STATE, channels), f32),
        scratch_shapes=scan_scratch(channels), compiler_params=PARAMS,
    )(gated_grad, mixed, select_t, *aux, bias, rate)


def backward_scan(gated_grad, mixed, select, select_t, states, aux, bias, rate, skip, start, final):
    tokens, channels = mixed.shape[0], mixed.shape[1] // 3
    tiles = tokens // TILE
    mixed_s, rows, select_s, select_t_s, states_s, aux_s, aux_t_s, last_s, row, state = scan_specs(tiles, channels, True)
    return pl.pallas_call(
        backward_kernel, grid=(tiles,),
        in_specs=[rows, mixed_s, select_s, select_t_s, states_s, aux_s, aux_t_s, last_s, row, row, row, state, state],
        out_specs=[mixed_s, select_s, pl.BlockSpec((8, channels), lambda i: (0, 0))],
        out_shape=[jax.ShapeDtypeStruct((tokens, 3 * channels), bf16), jax.ShapeDtypeStruct((tokens, 2 * STATE), f32), jax.ShapeDtypeStruct((8, channels), f32)],
        scratch_shapes=scan_scratch(channels) + [
            pltpu.VMEM((TILE // SUB * STATE, channels), bf16),
            pltpu.VMEM((TILE // SUB, channels), f32),
            pltpu.VMEM((1, channels), f32),
        ],
        compiler_params=PARAMS,
    )(gated_grad, mixed, select, select_t, states, *aux, bias, rate, skip, start, final)


PARAMS_A = pltpu.CompilerParams(vmem_limit_bytes=56 << 20, dimension_semantics=("arbitrary",))


def attend_kernel(group, query_t, key_t, value_t, bias, out_t, log_total):
    keys = key_t[...].T
    values_t = value_t[...]
    for g in range(group):
        at = slice(g * HEAD_SIZE, (g + 1) * HEAD_SIZE)
        scores = mm(keys, query_t[at, :] * 0.125) + bias[...]
        top = jnp.max(scores, axis=0, keepdims=True)
        probs = jnp.exp(scores - top)
        total = jnp.sum(probs, axis=0, keepdims=True)
        out_t[at, :] = (mm(values_t, probs.astype(bf16)) / total).astype(bf16)
        log_total[g : g + 1, :] = top + jnp.log(total)


def attend_back_kernel(group, query_t, key_t, value_t, bias, out_t, log_total, grad_t, query_grad_t, key_grad_t, value_grad_t):
    keys_t = key_t[...]
    keys = keys_t.T
    values = value_t[...].T
    key_sum = jnp.zeros(key_grad_t.shape, f32)
    value_sum = jnp.zeros(value_grad_t.shape, f32)
    for g in range(group):
        at = slice(g * HEAD_SIZE, (g + 1) * HEAD_SIZE)
        query = query_t[at, :] * 0.125
        grad = grad_t[at, :]
        probs = jnp.exp(mm(keys, query) + bias[...] - log_total[g : g + 1, :])
        centre = jnp.sum(grad.astype(f32) * out_t[at, :].astype(f32), axis=0, keepdims=True)
        score_grad = (probs * (mm(values, grad) - centre)).astype(bf16)
        query_grad_t[at, :] = (mm(keys_t, score_grad) * 0.125).astype(bf16)
        key_sum = key_sum + mm_nt(query, score_grad)
        value_sum = value_sum + mm_nt(grad, probs.astype(bf16))
    key_grad_t[...] = key_sum
    value_grad_t[...] = value_sum


def attend(query_t, keyval_t, bias, key_value_heads):
    width, rows = query_t.shape
    keys = keyval_t.shape[1]
    group = width // HEAD_SIZE // key_value_heads
    kv = key_value_heads
    return pl.pallas_call(
        functools.partial(attend_kernel, group), grid=(kv,),
        in_specs=[
            pl.BlockSpec((group * HEAD_SIZE, rows), lambda h: (h, 0)),
            pl.BlockSpec((HEAD_SIZE, keys), lambda h: (h, 0)),
            pl.BlockSpec((HEAD_SIZE, keys), lambda h: (h + kv, 0)),
            pl.BlockSpec((keys, rows), lambda h: (0, 0)),
        ],
        out_specs=[
            pl.BlockSpec((group * HEAD_SIZE, rows), lambda h: (h, 0)),
            pl.BlockSpec((None, 8, rows), lambda h: (h, 0, 0)),
        ],
        out_shape=[jax.ShapeDtypeStruct((width, rows), bf16), jax.ShapeDtypeStruct((kv, 8, rows), f32)],
        compiler_params=PARAMS_A,
    )(query_t, keyval_t, keyval_t, bias)


def attend_back(query_t, keyval_t, bias, out_t, log_total, grad_t, key_value_heads):
    width, rows = query_t.shape
    keys = keyval_t.shape[1]
    group = width // HEAD_SIZE // key_value_heads
    kv = key_value_heads
    wide = pl.BlockSpec((group * HEAD_SIZE, rows), lambda h: (h, 0))
    head = pl.BlockSpec((HEAD_SIZE, keys), lambda h: (h, 0))
    return pl.pallas_call(
        functools.partial(attend_back_kernel, group), grid=(kv,),
        in_specs=[
            wide, head,
            pl.BlockSpec((HEAD_SIZE, keys), lambda h: (h + kv, 0)),
            pl.BlockSpec((keys, rows), lambda h: (0, 0)),
            wide,
            pl.BlockSpec((None, 8, rows), lambda h: (h, 0, 0)),
            wide,
        ],
        out_specs=[wide, head, head],
        out_shape=[jax.ShapeDtypeStruct((width, rows), bf16), jax.ShapeDtypeStruct((kv * HEAD_SIZE, keys), f32), jax.ShapeDtypeStruct((kv * HEAD_SIZE, keys), f32)],
        compiler_params=PARAMS_A,
    )(query_t, keyval_t, keyval_t, bias, out_t, log_total, grad_t)


def rms_norm(values, gain):
    return values * lax.rsqrt(jnp.mean(values * values, axis=-1, keepdims=True) + epsilon) * gain


def rms_back(values, gain, grad):
    scale = lax.rsqrt(jnp.mean(values * values, axis=-1, keepdims=True) + epsilon)
    normal = values * scale
    weighted = grad * gain
    back = scale * (weighted - normal * jnp.mean(weighted * normal, axis=-1, keepdims=True))
    return back, grad * normal


def dot(left, right, left_dim, right_dim):
    return lax.dot_general(
        left, right, (((left_dim,), (right_dim,)), ((), ())), preferred_element_type=f32
    )


def gather_rows(pieces):
    return lax.all_gather(jnp.concatenate(pieces, axis=1), ("fsdp", "ctx"), axis=0, tiled=True)


def scatter_rows(pieces):
    whole = jnp.concatenate([piece.astype(bf16) for piece in pieces], axis=1)
    return lax.psum_scatter(whole, ("fsdp", "ctx"), scatter_dimension=0, tiled=True)


def cut(values, widths):
    pieces = []
    offset = 0
    for count in widths:
        pieces.append(values[:, offset : offset + count])
        offset = offset + count
    return pieces


def per_device(
    tokens,
    segments,
    cotangent,
    meta_tokens,
    gain_mix,
    query_weight,
    key_value_weight,
    attn_output,
    gain_attn,
    mamba_input,
    mamba_select,
    step_bias,
    decay_log,
    state_skip,
    mamba_output,
    gain_mamba,
    gain_ffn,
    ffn_input,
    ffn_output,
):
    tokens, segments, cotangent = tokens[0], segments[0], cotangent[0]
    rows, width = tokens.shape
    shard = meta_tokens.shape[0]
    tp = lax.axis_size("tp")
    tp_index = lax.axis_index("tp")
    ctx_index = lax.axis_index("ctx")
    span = rows * tp
    query_width = query_weight.shape[1]
    keyval_width = key_value_weight.shape[1]
    heads = keyval_width // (2 * HEAD_SIZE)
    channels = mamba_input.shape[2]
    ff = ffn_input.shape[2] // tp
    meta_count = meta_tokens.shape[1]
    window = WIN + rows

    gains = jnp.stack([gain_mix, gain_attn, gain_mamba, gain_ffn], axis=1)
    flat_input = mamba_input.reshape(shard, 3 * channels)
    first = gather_rows([key_value_weight, meta_tokens, query_weight, flat_input, mamba_select, gains])
    second = gather_rows([mamba_output, attn_output])
    ffn_up_shard = lax.dynamic_slice_in_dim(ffn_input, tp_index * ff, ff, 2).reshape(shard, 2 * ff)
    ffn_down_shard = lax.dynamic_slice_in_dim(ffn_output, tp_index * ff, ff, 1)
    third = gather_rows([ffn_up_shard, ffn_down_shard])
    tokens_group = lax.all_gather(tokens, "tp", axis=0, tiled=True)
    cotangent_group = lax.all_gather(cotangent, "tp", axis=0, tiled=True)

    keyval_map, meta_full, query_map, state_map, select_map, gain_columns = cut(
        first, [keyval_width, meta_count, query_width, 3 * channels, 2 * STATE, 4]
    )
    state_out_map, attn_map = cut(second, [channels, query_width])
    up_map, down_map = cut(third, [2 * ff, ff])
    gain_rows = gain_columns.astype(f32).T
    mix_gain, attn_gain, mamba_gain, ffn_gain = [gain_rows[k : k + 1] for k in range(4)]

    residual = tokens.astype(f32)
    residual_group = tokens_group.astype(f32)
    normed = rms_norm(residual, mix_gain).astype(bf16)
    normed_group = rms_norm(residual_group, mix_gain).astype(bf16)
    meta_rows = meta_full.astype(f32).T
    meta_normed = rms_norm(meta_rows, mix_gain).astype(bf16)

    query_t = dot(query_map, normed, 0, 1).astype(bf16)
    keyval_group_t = dot(keyval_map, normed_group, 0, 1).astype(bf16)
    meta_keyval_t = dot(keyval_map, meta_normed, 0, 1).astype(bf16)
    selects = dot(normed_group, select_map, 1, 0).astype(bf16)
    selects_t = selects.T
    earlier_t = lax.ppermute(keyval_group_t, "ctx", [(0, 1)])
    mixed = dot(normed_group, state_map, 1, 0)

    key_start = span + tp_index * rows - WIN
    keyval_t = jnp.concatenate(
        [
            meta_keyval_t,
            lax.dynamic_slice_in_dim(
                jnp.concatenate([earlier_t, keyval_group_t], axis=1), key_start, window, 1
            ),
        ],
        axis=1,
    )
    query_pos = ctx_index * span + tp_index * rows + jnp.arange(rows, dtype=jnp.int32)
    key_pos = (ctx_index - 1) * span + key_start + jnp.arange(window, dtype=jnp.int32)
    seg_current = lax.dynamic_slice_in_dim(segments, ctx_index * span, span, 0)
    seg_earlier = lax.dynamic_slice_in_dim(segments, jnp.maximum(ctx_index - 1, 0) * span, span, 0)
    seg_query = lax.dynamic_slice_in_dim(seg_current, tp_index * rows, rows, 0)
    seg_keys = lax.dynamic_slice_in_dim(
        jnp.concatenate([seg_earlier, seg_current]), key_start, window, 0
    )
    keep = (
        (key_pos[:, None] <= query_pos[None, :])
        & (query_pos[None, :] - key_pos[:, None] < WIN)
        & (key_pos[:, None] >= 0)
        & (seg_keys[:, None] == seg_query[None, :])
    )
    bias = jnp.concatenate(
        [jnp.zeros((meta_count, rows), f32), jnp.where(keep, 0.0, masked_score)], axis=0
    )
    attended_t, log_total = attend(query_t, keyval_t, bias, heads)
    attended_columns = lax.all_to_all(
        attended_t.reshape(tp, query_width // tp, rows), "tp", 0, 0
    )

    seg_before = jnp.where(
        ctx_index > 0,
        lax.dynamic_index_in_dim(segments, jnp.maximum(ctx_index * span - 1, 0), 0, False),
        -1,
    )
    aux = scan_aux(seg_current, seg_before)
    bias_row = step_bias[None]
    rate_row = jnp.exp(decay_log)[None]
    skip_row = state_skip[None]
    state_end = end_state(mixed, selects_t, aux, bias_row, rate_row)
    state_start = lax.ppermute(state_end, "ctx", [(0, 1)])
    gated, states, state_final = forward_scan(
        mixed, selects, selects_t, aux, bias_row, rate_row, skip_row, state_start
    )
    mamba_part = dot(gated, state_out_map, 1, 1).astype(bf16)
    mamba_out = lax.psum_scatter(mamba_part, "tp", scatter_dimension=0, tiled=True).astype(f32)
    attn_out = dot(attended_t, attn_map, 0, 1)
    mid = residual + 0.5 * (rms_norm(attn_out, attn_gain) + rms_norm(mamba_out, mamba_gain))
    ffn_normed = rms_norm(mid, ffn_gain).astype(bf16)
    ffn_normed_group = lax.all_gather(ffn_normed, "tp", axis=0, tiled=True)

    gate_up = dot(ffn_normed_group, up_map, 1, 0)
    gate, up = gate_up[:, :ff], gate_up[:, ff:]
    sigma = jax.nn.sigmoid(gate)
    hidden = (gate * sigma * up).astype(bf16)
    hidden_grad = dot(cotangent_group, down_map, 1, 0)
    gate_up_grad = jnp.concatenate(
        [
            (hidden_grad * up * (sigma * (1.0 + gate * (1.0 - sigma)))).astype(bf16),
            (hidden_grad * gate * sigma).astype(bf16),
        ],
        axis=1,
    )
    ffn_grad_part = dot(gate_up_grad, up_map, 1, 1).astype(bf16)
    ffn_normed_grad = lax.psum_scatter(
        ffn_grad_part, "tp", scatter_dimension=0, tiled=True
    ).astype(f32)
    out_part = dot(hidden, down_map, 1, 1).astype(bf16)
    layer_out = (
        mid + lax.psum_scatter(out_part, "tp", scatter_dimension=0, tiled=True).astype(f32)
    ).astype(bf16)

    mid_extra, ffn_gain_terms = rms_back(mid, ffn_gain, ffn_normed_grad)
    mid_grad = cotangent.astype(f32) + mid_extra
    attn_grad, attn_gain_terms = rms_back(attn_out, attn_gain, 0.5 * mid_grad)
    mamba_grad, mamba_gain_terms = rms_back(mamba_out, mamba_gain, 0.5 * mid_grad)
    attn_grad = attn_grad.astype(bf16)
    mamba_grad = mamba_grad.astype(bf16)
    mamba_grad_group = lax.all_gather(mamba_grad, "tp", axis=0, tiled=True)
    attn_grad_group = lax.all_gather(attn_grad, "tp", axis=0, tiled=True)

    attended_grad_t = dot(attn_map, attn_grad, 0, 1).astype(bf16)
    query_grad_t, key_grad_t, value_grad_t = attend_back(
        query_t, keyval_t, bias, attended_t, log_total, attended_grad_t, heads
    )
    gated_grad = dot(mamba_grad_group, state_out_map, 1, 0)
    adjoint_end = end_adjoint(gated_grad, mixed, selects_t, aux, bias_row, rate_row)
    adjoint_start = lax.ppermute(adjoint_end, "ctx", [(1, 0)])
    mix_grad, select_grad, scan_sums = backward_scan(
        gated_grad,
        mixed,
        selects,
        selects_t,
        states,
        aux,
        bias_row,
        rate_row,
        skip_row,
        adjoint_start,
        state_final,
    )

    keyval_grad_t = jnp.concatenate([key_grad_t, value_grad_t], axis=0).astype(bf16)
    placed = lax.dynamic_update_slice_in_dim(
        jnp.zeros((keyval_width, 2 * span), bf16), keyval_grad_t[:, meta_count:], key_start, 1
    )
    earlier_back = lax.ppermute(placed[:, :span], "ctx", [(1, 0)])
    current = placed[:, span:].astype(f32) + earlier_back.astype(f32)
    with_meta = jnp.concatenate([keyval_grad_t[:, :meta_count], current.astype(bf16)], axis=1)
    select_rows = jnp.concatenate(
        [jnp.zeros((2 * STATE, meta_count), bf16), select_grad.T.astype(bf16)], axis=1
    )
    columns = jnp.concatenate(
        [
            with_meta.reshape(tp, keyval_width // tp, meta_count + span),
            select_rows.reshape(tp, 2 * STATE // tp, meta_count + span),
        ],
        axis=1,
    )
    columns = lax.psum_scatter(columns, "tp", scatter_dimension=0, tiled=True)[0]
    keyval_columns_t = columns[: keyval_width // tp]
    select_columns_t = columns[keyval_width // tp :, meta_count:]
    query_columns = lax.all_to_all(
        query_grad_t.reshape(tp, query_width // tp, rows), "tp", 0, 0
    )

    keyval_part = lax.dynamic_slice_in_dim(
        keyval_map, tp_index * (keyval_width // tp), keyval_width // tp, 1
    )
    query_term = dot(query_grad_t, query_map, 0, 1)
    normed_grad_part = (
        dot(mix_grad, state_map, 1, 1)
        + dot(select_grad.astype(bf16), select_map, 1, 1)
        + dot(keyval_columns_t[:, meta_count:], keyval_part, 0, 1)
    )
    meta_grad_part = dot(keyval_columns_t[:, :meta_count], keyval_part, 0, 1)
    _, group_terms = rms_back(residual_group, mix_gain, normed_grad_part)
    _, meta_terms = rms_back(meta_rows, mix_gain, meta_grad_part)
    _, query_terms = rms_back(residual, mix_gain, query_term)
    mix_gain_sum = jnp.sum(group_terms, 0) + jnp.sum(meta_terms, 0) + jnp.sum(query_terms, 0)
    gain_sums = jnp.stack(
        [
            mix_gain_sum,
            jnp.sum(attn_gain_terms, 0),
            jnp.sum(mamba_gain_terms, 0),
            jnp.sum(ffn_gain_terms, 0),
        ]
    ).astype(bf16)
    gain_block = jnp.concatenate([gain_sums, jnp.zeros((4, width), bf16)])
    extended = jnp.concatenate(
        [
            normed_grad_part.astype(bf16).reshape(tp, rows, width),
            meta_grad_part.astype(bf16).reshape(tp, meta_count // tp, width),
            jnp.broadcast_to(gain_block[None], (tp, 8, width)),
        ],
        axis=1,
    )
    extended = lax.psum_scatter(extended, "tp", scatter_dimension=0, tiled=True)[0].astype(f32)
    normed_grad = extended[:rows] + query_term
    residual_extra, _ = rms_back(residual, mix_gain, normed_grad)
    grad_tokens = (mid_grad + residual_extra).astype(bf16)
    own_meta_rows = lax.dynamic_slice_in_dim(
        meta_rows, tp_index * (meta_count // tp), meta_count // tp, 0
    )
    own_meta_grad, _ = rms_back(own_meta_rows, mix_gain, extended[rows : rows + meta_count // tp])
    gain_totals = extended[rows + meta_count // tp :][:4]

    ffn_columns = scatter_rows(
        [dot(ffn_normed_group, gate_up_grad, 0, 0), dot(cotangent_group, hidden, 0, 0)]
    ).astype(f32)
    attended_wide = jnp.swapaxes(attended_columns, 1, 2).reshape(span, query_width // tp)
    query_wide = jnp.swapaxes(query_columns, 1, 2).reshape(span, query_width // tp)
    out_columns = scatter_rows(
        [dot(mamba_grad_group, gated, 0, 0), dot(attn_grad_group, attended_wide, 0, 0)]
    ).astype(f32)
    vector_columns = -(-3 * channels // shard)
    vectors = jnp.pad(scan_sums[:3].reshape(-1), (0, vector_columns * shard - 3 * channels))
    vectors = jnp.tile(vectors.reshape(shard, vector_columns), (width // shard, 1))
    last_columns = scatter_rows(
        [
            dot(normed_group, mix_grad, 0, 0),
            dot(normed_group, query_wide, 0, 0),
            dot(normed_group, keyval_columns_t[:, meta_count:], 0, 1)
            + dot(meta_normed, keyval_columns_t[:, :meta_count], 0, 1),
            dot(normed_group, select_columns_t, 0, 1),
            own_meta_grad.T,
            gain_totals.T,
            vectors,
        ]
    ).astype(f32)
    grad_ffn_input, grad_ffn_output = cut(ffn_columns, [2 * ff, ff])
    grad_mamba_output, grad_attn_output = cut(out_columns, [channels, query_width // tp])
    grad_mamba_input, grad_query, grad_keyval, grad_select, grad_meta, grad_gains, grad_vectors = cut(
        last_columns,
        [
            3 * channels,
            query_width // tp,
            keyval_width // tp,
            2 * STATE // tp,
            meta_count // tp,
            4,
            vector_columns,
        ],
    )
    grad_vectors = grad_vectors.reshape(-1)[: 3 * channels].reshape(3, channels)
    return (
        layer_out[None],
        grad_tokens[None],
        grad_meta,
        grad_gains[:, 0],
        grad_query,
        grad_keyval,
        grad_attn_output,
        grad_gains[:, 1],
        grad_mamba_input.reshape(shard, 3, channels),
        grad_select,
        grad_vectors[0],
        grad_vectors[1],
        grad_vectors[2],
        grad_mamba_output,
        grad_gains[:, 2],
        grad_gains[:, 3],
        grad_ffn_input.reshape(shard, 2, ff),
        grad_ffn_output,
    )


def solution(mesh):
    rows = ("fsdp", "ctx")
    in_specs = (
        P("fsdp", ("ctx", "tp"), None),
        P("fsdp", None),
        P("fsdp", ("ctx", "tp"), None),
        P(rows, None),
        P(rows),
        P(rows, None),
        P(rows, None),
        P(rows, None),
        P(rows),
        P(rows, None, "tp"),
        P(rows, None),
        P("tp"),
        P("tp"),
        P("tp"),
        P(rows, "tp"),
        P(rows),
        P(rows),
        P(rows, None, None),
        P(rows, None),
    )
    out_specs = (
        P("fsdp", ("ctx", "tp"), None),
        P("fsdp", ("ctx", "tp"), None),
        P(rows, "tp"),
        P(rows),
        P(rows, "tp"),
        P(rows, "tp"),
        P(rows, "tp"),
        P(rows),
        P(rows, None, "tp"),
        P(rows, "tp"),
        P("tp"),
        P("tp"),
        P("tp"),
        P(rows, "tp"),
        P(rows),
        P(rows),
        P(rows, None, "tp"),
        P(rows, "tp"),
    )
    return jax.shard_map(
        per_device, mesh=mesh, in_specs=in_specs, out_specs=out_specs, check_vma=False
    )
```

```python
import functools

import jax
import jax.numpy as jnp
from jax import lax
from jax.experimental import pallas as pl
from jax.experimental.pallas import tpu as pltpu
from jax.sharding import PartitionSpec as P

HEAD_SIZE = 64
STATE = 16
WIN = 1024
SUB = 4
TILE = 128

bf16 = jnp.bfloat16
f32 = jnp.float32
epsilon = 1e-05
masked_score = -1e30


def mm(a, b):
    return lax.dot_general(a, b, (((1,), (0,)), ((), ())), preferred_element_type=f32)


def mm_nt(a, b):
    return lax.dot_general(a, b, (((1,), (1,)), ((), ())), preferred_element_type=f32)


def iota(shape, dim):
    return lax.broadcasted_iota(jnp.int32, shape, dim)


def split_mm(a, b):
    high = b.astype(bf16)
    return mm(a, high) + mm(a, (b - high.astype(f32)).astype(bf16))


def ones_where(cond):
    return jnp.where(cond, 1.0, 0.0)


def softplus(v):
    return jnp.maximum(v, 0.0) + jnp.log1p(jnp.exp(-jnp.abs(v)))


def logistic(v):
    return 1.0 / (1.0 + jnp.exp(-v))


def group_mask(rows, columns, row_unit, column_unit):
    return iota((rows, columns), 0) // row_unit == iota((rows, columns), 1) // column_unit


def sums_matrix():
    rows = 2 * TILE + TILE // SUB
    row = iota((rows, TILE), 0)
    column = iota((rows, TILE), 1)
    token = row % TILE
    same = token // SUB == column // SUB
    upto = (row < TILE) & same & (column <= token)
    after = (row >= TILE) & (row < 2 * TILE) & same & (column > token)
    whole = (row >= 2 * TILE) & (row - 2 * TILE == column // SUB)
    return ones_where(upto | after | whole).astype(bf16)


def part(mixed, k):
    channels = mixed.shape[1] // 3
    return mixed[:, k * channels : (k + 1) * channels]


def decays(step_raw, bias_ref, rate_ref, alive_last_ref):
    raw = step_raw + bias_ref[...]
    step = softplus(raw)
    log_decay = -step * rate_ref[...]
    sums = split_mm(sums_matrix(), log_decay)
    upto = jnp.exp(sums[:TILE])
    after = sums[TILE : 2 * TILE]
    block = jnp.exp(sums[2 * TILE :]) * alive_last_ref[...]
    return raw, step, log_decay, upto, after, block


def in_blocks(select_t_ref, aux_t_ref):
    width = TILE // SUB * STATE
    tiled = jnp.concatenate([select_t_ref[:STATE, :].astype(f32) * aux_t_ref[1:2, :]] * (TILE // SUB), axis=0)
    return jnp.where(group_mask(width, TILE, STATE, SUB), tiled, 0.0).astype(bf16)


def out_blocks_t(select_t_ref, aux_t_ref):
    width = TILE // SUB * STATE
    tiled = jnp.concatenate([select_t_ref[STATE:, :].astype(f32) * aux_t_ref[0:1, :]] * (TILE // SUB), axis=0)
    return jnp.where(group_mask(width, TILE, STATE, SUB), tiled, 0.0).astype(bf16)


def spread(part, factor):
    width = TILE // SUB * STATE
    places = ones_where(iota((STATE, width), 0) == iota((STATE, width), 1) % STATE).astype(bf16)
    wide = mm(part, places) * factor
    return jnp.where(group_mask(TILE, width, SUB, STATE), wide, 0.0).astype(bf16)


def fold(wide, factor):
    width = TILE // SUB * STATE
    places = ones_where(iota((width, STATE), 0) % STATE == iota((width, STATE), 1)).astype(bf16)
    kept = jnp.where(group_mask(TILE, width, SUB, STATE), wide * factor, 0.0)
    return split_left(kept, places)


def split_left(a, b):
    high = a.astype(bf16)
    return mm(high, b) + mm((a - high.astype(f32)).astype(bf16), b)


def pairs(aux_ref, aux_t_ref, lower):
    row, column = iota((TILE, TILE), 0), iota((TILE, TILE), 1)
    order = column <= row if lower else column >= row
    return (row // SUB == column // SUB) & order & (aux_ref[:, 2:3] == aux_t_ref[2:3, :])


def run_states(state, local_ref, block_ref, keep=None):
    def one(k, state):
        if keep is not None:
            keep[pl.ds(pl.multiple_of(k * STATE, STATE), STATE), :] = state.astype(bf16)
        return block_ref[pl.ds(k, 1), :] * state + local_ref[pl.ds(pl.multiple_of(k * STATE, STATE), STATE), :]

    return lax.fori_loop(0, TILE // SUB, one, state, unroll=8)


def end_state_kernel(mixed, select_t, aux, aux_t, alive_last, bias, rate, end, state, local, block):
    @pl.when(pl.program_id(0) == 0)
    def _():
        state[...] = jnp.zeros_like(state)

    raw, step, log_decay, upto, after, total = decays(part(mixed, 2), bias, rate, alive_last)
    driven = (jnp.exp(after) * step * part(mixed, 0)).astype(bf16)
    local[...] = mm(in_blocks(select_t, aux_t), driven)
    block[...] = total
    state[...] = run_states(state[...], local, block)
    end[...] = state[...]


def forward_kernel(mixed, select, select_t, aux, aux_t, alive_last, bias, rate, skip, start, gated, states, end, state, local, block):
    @pl.when(pl.program_id(0) == 0)
    def _():
        state[...] = start[...]

    raw, step, log_decay, upto, after, total = decays(part(mixed, 2), bias, rate, alive_last)
    x = part(mixed, 0)
    driven = (jnp.exp(after) * step * x).astype(bf16)
    local[...] = mm(in_blocks(select_t, aux_t), driven)
    block[...] = total
    state[...] = run_states(state[...], local, block, states)
    end[...] = state[...]
    out_part = select[:, STATE:]
    cross = jnp.where(pairs(aux, aux_t, True), mm(out_part, select_t[:STATE, :]), 0.0).astype(bf16)
    y = upto * mm(spread(out_part, aux[:, 0:1]), states[...]) + jnp.exp(-after) * mm(cross, driven) + skip[...] * x
    gates = part(mixed, 1)
    gated[...] = (y * gates * logistic(gates)).astype(bf16)


def back_run(carry, local_ref, block_ref, keep, states=None, bound=None):
    count = TILE // SUB

    def one(i, carry):
        k = count - 1 - i
        rows = pl.ds(pl.multiple_of(k * STATE, STATE), STATE)
        if keep is not None:
            keep[rows, :] = carry[0].astype(bf16)
            bound[pl.ds(k, 1), :] = carry[1]
        new = block_ref[pl.ds(k, 1), :] * carry[0] + local_ref[rows, :]
        if keep is None:
            return (new, carry[1])
        return (new, jnp.sum(new * states[rows, :].astype(f32), axis=0, keepdims=True))

    return lax.fori_loop(0, count, one, carry, unroll=8)


def end_adjoint_kernel(gated_grad, mixed, select_t, aux, aux_t, alive_last, bias, rate, end, state, local, block):
    @pl.when(pl.program_id(0) == 0)
    def _():
        state[...] = jnp.zeros_like(state)

    raw, step, log_decay, upto, after, total = decays(part(mixed, 2), bias, rate, alive_last)
    gates = part(mixed, 1)
    dy = gated_grad[...] * gates * logistic(gates)
    local[...] = mm(out_blocks_t(select_t, aux_t), (upto * dy).astype(bf16))
    block[...] = total
    state[...] = back_run((state[...], jnp.zeros((1, state.shape[1]), f32)), local, block, None)[0]
    end[...] = state[...]


def backward_kernel(gated_grad, mixed, select, select_t, states, aux, aux_t, alive_last, bias, rate, skip, start, final,
                    mix_grad, select_grad, sums, state, local, block, adjoint, bound, edge):
    @pl.when(pl.program_id(0) == 0)
    def _():
        state[...] = start[...]
        edge[...] = jnp.sum(start[...] * final[...], axis=0, keepdims=True)
        sums[...] = jnp.zeros_like(sums)

    raw, step, log_decay, upto, after, total = decays(part(mixed, 2), bias, rate, alive_last)
    channels = state.shape[1]
    x = part(mixed, 0)
    decay_after = jnp.exp(after)
    grow = jnp.exp(-after)
    driven = (decay_after * step * x).astype(bf16)
    in_part, out_part = select[:, :STATE], select[:, STATE:]
    in_part_t, out_part_t = select_t[:STATE, :], select_t[STATE:, :]
    lower, upper = pairs(aux, aux_t, True), pairs(aux, aux_t, False)
    cross = jnp.where(lower, mm(out_part, in_part_t), 0.0).astype(bf16)
    cross_t = jnp.where(upper, mm(in_part, out_part_t), 0.0).astype(bf16)
    y = upto * mm(spread(out_part, aux[:, 0:1]), states[...]) + grow * mm(cross, driven)
    gates = part(mixed, 1)
    sigma = logistic(gates)
    grad = gated_grad[...]
    dy = grad * gates * sigma
    mix_grad[:, channels : 2 * channels] = (grad * (y + skip[...] * x) * (sigma * (1.0 + gates * (1.0 - sigma)))).astype(bf16)
    dy_low = (upto * dy).astype(bf16)
    dy_grown = (grow * dy).astype(bf16)
    local[...] = mm(out_blocks_t(select_t, aux_t), dy_low)
    block[...] = total
    new_state, new_edge = back_run((state[...], edge[...]), local, block, adjoint, states, bound)
    state[...] = new_state
    edge[...] = new_edge
    du = decay_after * (mm(spread(in_part, aux[:, 1:2]), adjoint[...]) + mm(cross_t, dy_grown))
    out_grad = fold(mm_nt(dy_low, states[...]), aux[:, 0:1])
    in_grad = fold(mm_nt(driven, adjoint[...]), aux[:, 1:2])
    cross_grad = jnp.where(lower, mm_nt(dy_grown, driven), 0.0)
    cross_grad_t = jnp.where(upper, mm_nt(driven, dy_grown), 0.0)
    out_grad = out_grad + split_left(cross_grad, in_part)
    in_grad = in_grad + split_left(cross_grad_t, out_part)
    select_grad[...] = jnp.concatenate([in_grad, out_grad], axis=1)
    flow = dy * y - step * x * du
    places = ones_where(group_mask(TILE, TILE // SUB, SUB, 1)) * aux[:, 1:2]
    decay_grad = aux[:, 3:4] * (
        split_mm(ones_where(upper).astype(bf16), flow) + split_mm(places.astype(bf16), bound[...])
    )
    step_grad = (x * du - rate[...] * decay_grad) * logistic(raw)
    mix_grad[:, :channels] = (skip[...] * dy + step * du).astype(bf16)
    mix_grad[:, 2 * channels :] = step_grad.astype(bf16)
    sums[0:1, :] += jnp.sum(step_grad, axis=0, keepdims=True)
    sums[1:2, :] += jnp.sum(decay_grad * log_decay, axis=0, keepdims=True)
    sums[2:3, :] += jnp.sum(dy * x, axis=0, keepdims=True)


def scan_specs(tokens, channels, back):
    tiles = tokens // TILE

    def at(i):
        return tiles - 1 - i if back else i

    mixed = pl.BlockSpec((TILE, 3 * channels), lambda i: (at(i), 0))
    rows = pl.BlockSpec((TILE, channels), lambda i: (at(i), 0))
    select = pl.BlockSpec((TILE, 2 * STATE), lambda i: (at(i), 0))
    select_t = pl.BlockSpec((2 * STATE, TILE), lambda i: (0, at(i)))
    states = pl.BlockSpec((TILE // SUB * STATE, channels), lambda i: (at(i), 0))
    aux = pl.BlockSpec((TILE, 8), lambda i: (at(i), 0))
    aux_t = pl.BlockSpec((8, TILE), lambda i: (0, at(i)))
    last = pl.BlockSpec((TILE // SUB, 1), lambda i: (at(i), 0))
    row = pl.BlockSpec((1, channels), lambda i: (0, 0))
    state = pl.BlockSpec((STATE, channels), lambda i: (0, 0))
    return tiles, mixed, rows, select, select_t, states, aux, aux_t, last, row, state


def scan_call(kernel, name, tiles, in_specs, out_specs, out_shape, scratch, flops):
    return pl.pallas_call(
        kernel,
        name=name,
        grid=(tiles,),
        in_specs=in_specs,
        out_specs=out_specs,
        scratch_shapes=scratch,
        out_shape=out_shape,
        compiler_params=PARAMS,
        cost_estimate=pl.CostEstimate(flops=flops, bytes_accessed=1 << 24, transcendentals=0),
    )


def scan_scratch(channels):
    return [
        pltpu.VMEM((STATE, channels), f32),
        pltpu.VMEM((TILE // SUB * STATE, channels), f32),
        pltpu.VMEM((TILE // SUB, channels), f32),
    ]


PARAMS = pltpu.CompilerParams(vmem_limit_bytes=48 << 20, dimension_semantics=("arbitrary",))


def scan_aux(segment, before):
    count = segment.shape[0]
    blocks = segment.reshape(count // SUB, SUB)
    ends = jnp.concatenate([before[None], blocks[:-1, -1]])
    alive = (blocks == ends[:, None]).reshape(-1).astype(f32)
    tail = (blocks == blocks[:, -1:]).reshape(-1).astype(f32)
    joined = (segment == jnp.concatenate([before[None], segment[:-1]])).astype(f32)
    zero = jnp.zeros_like(alive)
    aux_t = jnp.stack([alive, tail, segment.astype(f32), joined, zero, zero, zero, zero])
    last = (blocks[:, -1] == ends).astype(f32)[:, None]
    return aux_t.T, aux_t, last


def end_state(mixed, select_t, aux, bias, rate):
    tokens, channels = mixed.shape[0], mixed.shape[1] // 3
    tiles, mixed_s, rows, select_s, select_t_s, states_s, aux_s, aux_t_s, last_s, row, state = scan_specs(
        tokens, channels, False
    )
    return scan_call(
        end_state_kernel,
        "end_state",
        tiles,
        [mixed_s, select_t_s, aux_s, aux_t_s, last_s, row, row],
        state,
        jax.ShapeDtypeStruct((STATE, channels), f32),
        scan_scratch(channels),
        10**10,
    )(mixed, select_t, *aux, bias, rate)


def forward_scan(mixed, select, select_t, aux, bias, rate, skip, start):
    tokens, channels = mixed.shape[0], mixed.shape[1] // 3
    tiles, mixed_s, rows, select_s, select_t_s, states_s, aux_s, aux_t_s, last_s, row, state = scan_specs(
        tokens, channels, False
    )
    return scan_call(
        forward_kernel,
        "forward_scan",
        tiles,
        [mixed_s, select_s, select_t_s, aux_s, aux_t_s, last_s, row, row, row, state],
        [rows, states_s, state],
        [
            jax.ShapeDtypeStruct((tokens, channels), bf16),
            jax.ShapeDtypeStruct((tokens // SUB * STATE, channels), bf16),
            jax.ShapeDtypeStruct((STATE, channels), f32),
        ],
        scan_scratch(channels),
        16 * 10**9,
    )(mixed, select, select_t, *aux, bias, rate, skip, start)


def end_adjoint(gated_grad, mixed, select_t, aux, bias, rate):
    tokens, channels = mixed.shape[0], mixed.shape[1] // 3
    tiles, mixed_s, rows, select_s, select_t_s, states_s, aux_s, aux_t_s, last_s, row, state = scan_specs(
        tokens, channels, True
    )
    return scan_call(
        end_adjoint_kernel,
        "end_adjoint",
        tiles,
        [rows, mixed_s, select_t_s, aux_s, aux_t_s, last_s, row, row],
        state,
        jax.ShapeDtypeStruct((STATE, channels), f32),
        scan_scratch(channels),
        10**10,
    )(gated_grad, mixed, select_t, *aux, bias, rate)


def backward_scan(gated_grad, mixed, select, select_t, states, aux, bias, rate, skip, start, final):
    tokens, channels = mixed.shape[0], mixed.shape[1] // 3
    tiles, mixed_s, rows, select_s, select_t_s, states_s, aux_s, aux_t_s, last_s, row, state = scan_specs(
        tokens, channels, True
    )
    return scan_call(
        backward_kernel,
        "backward_scan",
        tiles,
        [rows, mixed_s, select_s, select_t_s, states_s, aux_s, aux_t_s, last_s, row, row, row, state, state],
        [mixed_s, select_s, pl.BlockSpec((8, channels), lambda i: (0, 0))],
        [
            jax.ShapeDtypeStruct((tokens, 3 * channels), bf16),
            jax.ShapeDtypeStruct((tokens, 2 * STATE), f32),
            jax.ShapeDtypeStruct((8, channels), f32),
        ],
        scan_scratch(channels)
        + [
            pltpu.VMEM((TILE // SUB * STATE, channels), bf16),
            pltpu.VMEM((TILE // SUB, channels), f32),
            pltpu.VMEM((1, channels), f32),
        ],
        36 * 10**9,
    )(gated_grad, mixed, select, select_t, states, *aux, bias, rate, skip, start, final)


MESH = pl.DeviceIdType.MESH
COMM = {"has_side_effects": True}


def neighbour_barrier(count):
    place = lax.axis_index("tp")
    ready = pltpu.get_barrier_semaphore()
    sides = ((place < count - 1, place + 1), (place > 0, place - 1))
    for there, other in sides:

        @pl.when(there)
        def _():
            pl.semaphore_signal(ready, inc=1, device_id={"tp": other}, device_id_type=MESH)

    peers = jnp.where(place < count - 1, 1, 0) + jnp.where(place > 0, 1, 0)
    pl.semaphore_wait(ready, peers)


def line_steps(count, source, target, copies, send_sems, recv_sems):
    place = lax.axis_index("tp")
    width = source.shape[1]

    def at(owner):
        return target.at[:, pl.ds(pl.multiple_of(owner * width, width), width)]

    def local():
        return pltpu.make_async_copy(source, at(place), copies)

    def remote(side, step):
        owner = place - step if side == 0 else place + step
        return pltpu.make_async_remote_copy(
            src_ref=source if step == 0 else at(owner),
            dst_ref=at(owner),
            send_sem=send_sems.at[side, step],
            recv_sem=recv_sems.at[side, step],
            device_id={"tp": place + 1 if side == 0 else place - 1},
            device_id_type=MESH,
        )

    def has(side, step):
        return place - step >= 0 if side == 0 else place + step < count

    def neighbour(side):
        return place < count - 1 if side == 0 else place > 0

    def send(step):
        for side in (0, 1):

            @pl.when(neighbour(side) & has(side, step))
            def _():
                remote(side, step).start()

    def receive(step):
        for side in (0, 1):

            @pl.when(has(side, step + 1))
            def _():
                remote(side, step).wait_recv()

    def start():
        neighbour_barrier(count)
        local().start()
        send(0)

    def step(k):
        receive(k - 1)
        if k < count - 1:
            send(k)

    def finish():
        for k in range(count - 1):
            for side in (0, 1):

                @pl.when(neighbour(side) & has(side, k))
                def _():
                    remote(side, k).wait_send()

        local().wait()

    return start, step, finish


def line_scratch(count):
    return [
        pltpu.SemaphoreType.DMA,
        pltpu.SemaphoreType.DMA((2, count - 1)),
        pltpu.SemaphoreType.DMA((2, count - 1)),
    ]


def line_gather_kernel(count, source, target, copies, send_sems, recv_sems):
    start, step, finish = line_steps(count, source, target, copies, send_sems, recv_sems)
    start()
    for k in range(1, count):
        step(k)
    finish()


def line_gather(source, count, collective):
    return pl.pallas_call(
        functools.partial(line_gather_kernel, count),
        name="line_gather",
        in_specs=[pl.BlockSpec(memory_space=pl.ANY)],
        out_specs=pl.BlockSpec(memory_space=pl.ANY),
        out_shape=jax.ShapeDtypeStruct((source.shape[0], source.shape[1] * count), source.dtype),
        scratch_shapes=line_scratch(count),
        compiler_params=pltpu.CompilerParams(collective_id=collective, has_side_effects=True),
    )(source)


def line_sum_steps(count, source, own, sent, got, total, loads, send_sems, recv_sems):
    place = lax.axis_index("tp")
    width = total.shape[1]

    def whose(side, step):
        return place + (count - step) if side == 0 else place - (count - step)

    def sends(side, step):
        owner = whose(side, step)
        return owner < count if side == 0 else owner >= 0

    def receives(side, step):
        return (place >= 1) & (place <= step) if side == 0 else (place <= count - 2) & (place >= count - 1 - step)

    def load(side, step):
        owner = whose(side, step)
        return pltpu.make_async_copy(
            source.at[:, pl.ds(pl.multiple_of(owner * width, width), width)],
            sent.at[side, step - 1],
            loads.at[side, step - 1],
        )

    def mine():
        return pltpu.make_async_copy(
            source.at[:, pl.ds(pl.multiple_of(place * width, width), width)], own, loads.at[2, 0]
        )

    def remote(side, step):
        return pltpu.make_async_remote_copy(
            src_ref=sent.at[side, step - 1],
            dst_ref=got.at[side, step - 1],
            send_sem=send_sems.at[side, step - 1],
            recv_sem=recv_sems.at[side, step - 1],
            device_id={"tp": place + 1 if side == 0 else place - 1},
            device_id_type=MESH,
        )

    def start():
        neighbour_barrier(count)
        mine().start()
        for step in range(1, count):
            for side in (0, 1):

                @pl.when(sends(side, step))
                def _():
                    load(side, step).start()

        step_out(1)

    def step_out(step):
        for side in (0, 1):

            @pl.when(sends(side, step))
            def _():
                load(side, step).wait()

            if step > 1:

                @pl.when(sends(side, step) & receives(side, step - 1))
                def _():
                    sent[side, step - 1] = (
                        sent[side, step - 1].astype(f32) + got[side, step - 2].astype(f32)
                    ).astype(bf16)

            @pl.when(sends(side, step))
            def _():
                remote(side, step).start()

    def step(k):
        for side in (0, 1):

            @pl.when(receives(side, k))
            def _():
                remote(side, k).wait_recv()

        if k < count - 1:
            step_out(k + 1)

    def finish():
        mine().wait()
        total[...] = own[...].astype(f32)
        for side in (0, 1):

            @pl.when(receives(side, count - 1))
            def _():
                total[...] = total[...] + got[side, count - 2].astype(f32)

            for k in range(1, count):

                @pl.when(sends(side, k))
                def _():
                    remote(side, k).wait_send()

    return start, step, finish


def line_sum_scratch(count, height, width):
    return [
        pltpu.VMEM((height, width), bf16),
        pltpu.VMEM((2, count - 1, height, width), bf16),
        pltpu.VMEM((2, count - 1, height, width), bf16),
        pltpu.SemaphoreType.DMA((3, count - 1)),
        pltpu.SemaphoreType.DMA((2, count - 1)),
        pltpu.SemaphoreType.DMA((2, count - 1)),
    ]


def line_sum_kernel(count, source, total, own, sent, got, loads, send_sems, recv_sems):
    start, step, finish = line_sum_steps(
        count, source, own, sent, got, total, loads, send_sems, recv_sems
    )
    start()
    for k in range(1, count):
        step(k)
    finish()


def line_sum(source, count, collective):
    height, width = source.shape[0], source.shape[1] // count
    return pl.pallas_call(
        functools.partial(line_sum_kernel, count),
        name="line_sum",
        in_specs=[pl.BlockSpec(memory_space=pl.ANY)],
        out_specs=pl.BlockSpec(memory_space=pltpu.VMEM),
        out_shape=jax.ShapeDtypeStruct((height, width), f32),
        scratch_shapes=line_sum_scratch(count, height, width),
        compiler_params=pltpu.CompilerParams(
            vmem_limit_bytes=24 << 20, collective_id=collective, has_side_effects=True
        ),
    )(source)


def attend_kernel(
    group,
    count,
    query_t,
    key_t,
    value_t,
    bias,
    source,
    out_t,
    log_total,
    total_out,
    own,
    sent,
    got,
    loads,
    send_sems,
    recv_sems,
):
    head, heads = pl.program_id(0), pl.num_programs(0)
    start, step, finish = line_sum_steps(
        count, source, own, sent, got, total_out, loads, send_sems, recv_sems
    )

    @pl.when(head == 0)
    def _():
        start()

    @pl.when(head == heads - 2)
    def _():
        step(1)

    keys = key_t[...].T
    values_t = value_t[...]
    for g in range(group):
        at = slice(g * HEAD_SIZE, (g + 1) * HEAD_SIZE)
        scores = mm(keys, query_t[at, :] * 0.125) + bias[...]
        top = jnp.max(scores, axis=0, keepdims=True)
        probs = jnp.exp(scores - top)
        total = jnp.sum(probs, axis=0, keepdims=True)
        out_t[at, :] = (mm(values_t, probs.astype(bf16)) / total).astype(bf16)
        log_total[g : g + 1, :] = top + jnp.log(total)

    @pl.when(head == heads - 1)
    def _():
        for k in range(2, count):
            step(k)
        finish()


def attend_back_kernel(
    group,
    count,
    query_t,
    key_t,
    value_t,
    bias,
    out_t,
    log_total,
    grad_t,
    source,
    query_grad_t,
    key_grad_t,
    value_grad_t,
    target,
    copies,
    send_sems,
    recv_sems,
):
    head, heads = pl.program_id(0), pl.num_programs(0)
    start, step, finish = line_steps(count, source, target, copies, send_sems, recv_sems)

    @pl.when(head == 0)
    def _():
        start()

    @pl.when(head == heads - 2)
    def _():
        step(1)

    keys_t = key_t[...]
    keys = keys_t.T
    values = value_t[...].T
    key_sum = jnp.zeros(key_grad_t.shape, f32)
    value_sum = jnp.zeros(value_grad_t.shape, f32)
    for g in range(group):
        at = slice(g * HEAD_SIZE, (g + 1) * HEAD_SIZE)
        query = query_t[at, :] * 0.125
        grad = grad_t[at, :]
        probs = jnp.exp(mm(keys, query) + bias[...] - log_total[g : g + 1, :])
        centre = jnp.sum(grad.astype(f32) * out_t[at, :].astype(f32), axis=0, keepdims=True)
        score_grad = (probs * (mm(values, grad) - centre)).astype(bf16)
        query_grad_t[at, :] = (mm(keys_t, score_grad) * 0.125).astype(bf16)
        key_sum = key_sum + mm_nt(query, score_grad)
        value_sum = value_sum + mm_nt(grad, probs.astype(bf16))
    key_grad_t[...] = key_sum
    value_grad_t[...] = value_sum

    @pl.when(head == heads - 1)
    def _():
        for k in range(2, count):
            step(k)
        finish()


def attend(query_t, keyval_t, bias, source, key_value_heads, count, collective):
    width, rows = query_t.shape
    keys = keyval_t.shape[1]
    group = width // HEAD_SIZE // key_value_heads
    kv = key_value_heads
    height, each = source.shape[0], source.shape[1] // count
    return pl.pallas_call(
        functools.partial(attend_kernel, group, count),
        name="attend",
        grid=(kv,),
        in_specs=[
            pl.BlockSpec((group * HEAD_SIZE, rows), lambda h: (h, 0)),
            pl.BlockSpec((HEAD_SIZE, keys), lambda h: (h, 0)),
            pl.BlockSpec((HEAD_SIZE, keys), lambda h: (h + kv, 0)),
            pl.BlockSpec((keys, rows), lambda h: (0, 0)),
            pl.BlockSpec(memory_space=pl.ANY),
        ],
        out_specs=[
            pl.BlockSpec((group * HEAD_SIZE, rows), lambda h: (h, 0)),
            pl.BlockSpec((None, 8, rows), lambda h: (h, 0, 0)),
            pl.BlockSpec((height, each), lambda h: (0, 0)),
        ],
        out_shape=[
            jax.ShapeDtypeStruct((width, rows), bf16),
            jax.ShapeDtypeStruct((kv, 8, rows), f32),
            jax.ShapeDtypeStruct((height, each), f32),
        ],
        scratch_shapes=line_sum_scratch(count, height, each),
        compiler_params=pltpu.CompilerParams(
            vmem_limit_bytes=56 << 20,
            dimension_semantics=("arbitrary",),
            collective_id=collective,
            has_side_effects=True,
        ),
    )(query_t, keyval_t, keyval_t, bias, source)


def attend_back(query_t, keyval_t, bias, out_t, log_total, grad_t, source, key_value_heads, count, collective):
    width, rows = query_t.shape
    keys = keyval_t.shape[1]
    group = width // HEAD_SIZE // key_value_heads
    kv = key_value_heads
    wide = pl.BlockSpec((group * HEAD_SIZE, rows), lambda h: (h, 0))
    head = pl.BlockSpec((HEAD_SIZE, keys), lambda h: (h, 0))
    anywhere = pl.BlockSpec(memory_space=pl.ANY)
    return pl.pallas_call(
        functools.partial(attend_back_kernel, group, count),
        name="attend_back",
        grid=(kv,),
        in_specs=[
            wide,
            head,
            pl.BlockSpec((HEAD_SIZE, keys), lambda h: (h + kv, 0)),
            pl.BlockSpec((keys, rows), lambda h: (0, 0)),
            wide,
            pl.BlockSpec((None, 8, rows), lambda h: (h, 0, 0)),
            wide,
            anywhere,
        ],
        out_specs=[wide, head, head, anywhere],
        out_shape=[
            jax.ShapeDtypeStruct((width, rows), bf16),
            jax.ShapeDtypeStruct((kv * HEAD_SIZE, keys), f32),
            jax.ShapeDtypeStruct((kv * HEAD_SIZE, keys), f32),
            jax.ShapeDtypeStruct((source.shape[0], source.shape[1] * count), source.dtype),
        ],
        scratch_shapes=line_scratch(count),
        compiler_params=pltpu.CompilerParams(
            vmem_limit_bytes=56 << 20,
            dimension_semantics=("arbitrary",),
            collective_id=collective,
            has_side_effects=True,
        ),
    )(query_t, keyval_t, keyval_t, bias, out_t, log_total, grad_t, source)


def rms_norm(values, gain):
    return values * lax.rsqrt(jnp.mean(values * values, axis=0, keepdims=True) + epsilon) * gain


def rms_back(values, gain, grad):
    scale = lax.rsqrt(jnp.mean(values * values, axis=0, keepdims=True) + epsilon)
    normal = values * scale
    weighted = grad * gain
    back = scale * (weighted - normal * jnp.mean(weighted * normal, axis=0, keepdims=True))
    return back, grad * normal


def dot(left, right, left_dim, right_dim):
    return lax.dot_general(
        left, right, (((left_dim,), (right_dim,)), ((), ())), preferred_element_type=f32
    )


def gather_rows(whole):
    return lax.all_gather(whole, ("fsdp", "ctx"), axis=0, tiled=True)


def scatter_rows(whole):
    return lax.psum_scatter(whole, ("fsdp", "ctx"), scatter_dimension=0, tiled=True)


def send(values, by):
    count = lax.axis_size("tp")
    return lax.ppermute(values, "tp", [(i, (i + by) % count) for i in range(count)])


def permute_gather(own):
    count = lax.axis_size("tp")
    return [own] + [send(own, k) for k in range(1, count)]


def in_order(pieces):
    count, place = lax.axis_size("tp"), lax.axis_index("tp")
    return jnp.concatenate(
        [lax.select_n(lax.rem(place - p + count, count), *pieces) for p in range(count)], axis=1
    )


def permute_sums(values, axis):
    count, place = lax.axis_size("tp"), lax.axis_index("tp")
    each = values.shape[axis] // count
    shares = [
        lax.dynamic_slice_in_dim(values, lax.rem(place + k, count) * each, each, axis)
        for k in range(count)
    ]
    total = shares[0].astype(f32)
    for k in (2, 1, 3):
        total = total + send(shares[k], k).astype(f32)
    return total


def permute_exchange(values):
    count, place = lax.axis_size("tp"), lax.axis_index("tp")
    shares = values.reshape(count, values.shape[0] // count, values.shape[1])
    pieces = [
        lax.dynamic_index_in_dim(shares, lax.rem(place + k, count), 0, False) for k in range(count)
    ]
    return [pieces[0]] + [send(pieces[k], k) for k in range(1, count)]


def cut(values, widths):
    pieces = []
    offset = 0
    for count in widths:
        pieces.append(values[:, offset : offset + count])
        offset = offset + count
    return pieces


def per_device(
    tokens,
    segments,
    cotangent,
    meta_tokens,
    gain_mix,
    query_weight,
    key_value_weight,
    attn_output,
    gain_attn,
    mamba_input,
    mamba_select,
    step_bias,
    decay_log,
    state_skip,
    mamba_output,
    gain_mamba,
    gain_ffn,
    ffn_input,
    ffn_output,
):
    tokens_t, segments, cotangent_t = tokens[0].T, segments[0], cotangent[0].T
    width, rows = tokens_t.shape
    shard = meta_tokens.shape[0]
    tp = lax.axis_size("tp")
    tp_index = lax.axis_index("tp")
    ctx_index = lax.axis_index("ctx")
    span = rows * tp
    query_width = query_weight.shape[1]
    keyval_width = key_value_weight.shape[1]
    heads = keyval_width // (2 * HEAD_SIZE)
    channels = mamba_input.shape[2]
    ff = ffn_input.shape[2] // tp
    ff_wide = -(-ff // 128) * 128
    meta_count = meta_tokens.shape[1]
    window = WIN + rows

    gains = jnp.stack([gain_mix, gain_attn, gain_mamba, gain_ffn], axis=1)
    flat_input = mamba_input.reshape(shard, 3 * channels)
    small = jnp.concatenate(
        [mamba_select, gains, jnp.zeros((shard, 128 - 2 * STATE - 4), bf16)], axis=1
    )
    first = jnp.concatenate([small, flat_input], axis=1)
    first, second_parts = lax.optimization_barrier(
        (first, (key_value_weight, meta_tokens, query_weight))
    )
    second = jnp.concatenate(second_parts, axis=1)
    first, second, tokens_t = lax.optimization_barrier((first, second, tokens_t))
    first = gather_rows(first)
    second = gather_rows(second)
    tokens_group_t = line_gather(tokens_t, tp, 0)
    late_cotangent_t, tokens_group_t = lax.optimization_barrier((cotangent_t, tokens_group_t))
    cotangent_pieces = permute_gather(late_cotangent_t)

    select_map, gain_columns, _, state_map = cut(
        first, [2 * STATE, 4, 128 - 2 * STATE - 4, 3 * channels]
    )
    keyval_map, meta_full, query_map = cut(second, [keyval_width, meta_count, query_width])
    state_out_map = gather_rows(mamba_output)
    attn_map = gather_rows(attn_output)
    gain_columns = gain_columns.astype(f32)
    mix_gain, attn_gain, mamba_gain, ffn_gain = [gain_columns[:, k : k + 1] for k in range(4)]

    residual = tokens_t.astype(f32)
    residual_group = tokens_group_t.astype(f32)
    normed_t = rms_norm(residual, mix_gain).astype(bf16)
    normed_group_t = rms_norm(residual_group, mix_gain).astype(bf16)
    meta_rows = meta_full.astype(f32)
    meta_normed_t = rms_norm(meta_rows, mix_gain).astype(bf16)

    mixed = dot(normed_group_t, state_map, 0, 0)
    selects_t = dot(select_map, normed_group_t, 0, 0).astype(bf16)
    selects = selects_t.T
    seg_current = lax.dynamic_slice_in_dim(segments, ctx_index * span, span, 0)
    seg_earlier = lax.dynamic_slice_in_dim(segments, jnp.maximum(ctx_index - 1, 0) * span, span, 0)
    seg_before = jnp.where(
        ctx_index > 0,
        lax.dynamic_index_in_dim(segments, jnp.maximum(ctx_index * span - 1, 0), 0, False),
        -1,
    )
    aux = scan_aux(seg_current, seg_before)
    bias_row = step_bias[None]
    rate_row = jnp.exp(decay_log)[None]
    skip_row = state_skip[None]
    selects_t, late_up, late_down = lax.optimization_barrier((selects_t, ffn_input, ffn_output))
    ffn_shards = [
        lax.dynamic_slice_in_dim(whole, tp_index * ff, ff, 1)
        for whole in (late_up[:, 0], late_up[:, 1], late_down)
    ]
    state_end = end_state(mixed, selects_t, aux, bias_row, rate_row)
    state_start = lax.ppermute(state_end, "ctx", [(0, 1)])

    query_t = dot(query_map, normed_t, 0, 0).astype(bf16)
    keyval_group_t = dot(keyval_map, normed_group_t, 0, 0).astype(bf16)
    meta_keyval_t = dot(keyval_map, meta_normed_t, 0, 0).astype(bf16)
    earlier_t = lax.ppermute(keyval_group_t, "ctx", [(0, 1)])

    gated, states, state_final = forward_scan(
        mixed, selects, selects_t, aux, bias_row, rate_row, skip_row, state_start
    )
    mamba_part_t = dot(state_out_map, gated, 1, 1).astype(bf16)
    third = jnp.concatenate(
        [jnp.pad(piece, ((0, 0), (0, ff_wide - ff))) for piece in ffn_shards], axis=1
    )
    mamba_part_t, third, *cotangent_pieces = lax.optimization_barrier(
        (mamba_part_t, third, *cotangent_pieces)
    )
    third = gather_rows(third)
    up_map, down_map = cut(third, [2 * ff_wide, ff_wide])

    key_start = span + tp_index * rows - WIN
    keyval_t = jnp.concatenate(
        [
            meta_keyval_t,
            lax.dynamic_slice_in_dim(
                jnp.concatenate([earlier_t, keyval_group_t], axis=1), key_start, window, 1
            ),
        ],
        axis=1,
    )
    query_pos = ctx_index * span + tp_index * rows + jnp.arange(rows, dtype=jnp.int32)
    key_pos = (ctx_index - 1) * span + key_start + jnp.arange(window, dtype=jnp.int32)
    seg_query = lax.dynamic_slice_in_dim(seg_current, tp_index * rows, rows, 0)
    seg_keys = lax.dynamic_slice_in_dim(
        jnp.concatenate([seg_earlier, seg_current]), key_start, window, 0
    )
    keep = (
        (key_pos[:, None] <= query_pos[None, :])
        & (query_pos[None, :] - key_pos[:, None] < WIN)
        & (key_pos[:, None] >= 0)
        & (seg_keys[:, None] == seg_query[None, :])
    )
    bias = jnp.concatenate(
        [jnp.zeros((meta_count, rows), f32), jnp.where(keep, 0.0, masked_score)], axis=0
    )
    cotangent_group_t = in_order(cotangent_pieces)
    attended_t, log_total, mamba_out = attend(
        query_t, keyval_t, bias, mamba_part_t, heads, tp, 3
    )
    attn_out = dot(attn_map, attended_t, 1, 0)

    mid = residual + 0.5 * (rms_norm(attn_out, attn_gain) + rms_norm(mamba_out, mamba_gain))
    ffn_normed_t = rms_norm(mid, ffn_gain).astype(bf16)
    ffn_normed_group_t = line_gather(ffn_normed_t, tp, 1)

    gate_up = dot(up_map, ffn_normed_group_t, 0, 0)
    gate, up = gate_up[:ff_wide], gate_up[ff_wide:]
    sigma = jax.nn.sigmoid(gate)
    hidden_t = (gate * sigma * up).astype(bf16)
    hidden_grad = dot(down_map, cotangent_group_t, 0, 0)
    gate_up_grad_t = jnp.concatenate(
        [
            (hidden_grad * up * (sigma * (1.0 + gate * (1.0 - sigma)))).astype(bf16),
            (hidden_grad * gate * sigma).astype(bf16),
        ],
        axis=0,
    )
    late_attended_t, gate_up_grad_t = lax.optimization_barrier((attended_t, gate_up_grad_t))
    attended_columns_t = jnp.concatenate(permute_exchange(late_attended_t), axis=1)
    ffn_grad_part_t = dot(up_map, gate_up_grad_t, 1, 0).astype(bf16)
    ffn_grad_part_t, attended_columns_t = lax.optimization_barrier(
        (ffn_grad_part_t, attended_columns_t)
    )
    ffn_normed_grad_t = lax.psum_scatter(ffn_grad_part_t, "tp", scatter_dimension=1, tiled=True)
    up_wide = dot(ffn_normed_group_t, gate_up_grad_t, 1, 1).astype(bf16)
    down_wide = dot(cotangent_group_t, hidden_t, 1, 1).astype(bf16)
    ffn_wide = jnp.concatenate([up_wide, down_wide], axis=1)
    out_part_t = dot(down_map, hidden_t, 1, 0).astype(bf16)
    ffn_normed_grad_t, ffn_wide, out_part_t = lax.optimization_barrier(
        (ffn_normed_grad_t, ffn_wide, out_part_t)
    )
    ffn_columns = scatter_rows(ffn_wide)

    ffn_normed_grad = ffn_normed_grad_t.astype(f32)
    mid_extra, ffn_gain_terms = rms_back(mid, ffn_gain, ffn_normed_grad)
    mid_grad = cotangent_t.astype(f32) + mid_extra
    attn_grad, attn_gain_terms = rms_back(attn_out, attn_gain, 0.5 * mid_grad)
    mamba_grad, mamba_gain_terms = rms_back(mamba_out, mamba_gain, 0.5 * mid_grad)
    attn_grad_t = attn_grad.astype(bf16)
    mamba_grad_t = mamba_grad.astype(bf16)
    attended_grad_t = dot(attn_map, attn_grad_t, 0, 0).astype(bf16)
    query_grad_t, key_grad_t, value_grad_t, mamba_grad_group_t = attend_back(
        query_t,
        keyval_t,
        bias,
        attended_t,
        log_total,
        attended_grad_t,
        mamba_grad_t,
        heads,
        tp,
        2,
    )
    keyval_grad_t = jnp.concatenate([key_grad_t, value_grad_t], axis=0).astype(bf16)
    placed = lax.dynamic_update_slice_in_dim(
        jnp.zeros((keyval_width, 2 * span), bf16), keyval_grad_t[:, meta_count:], key_start, 1
    )
    earlier_back = lax.ppermute(placed[:, :span], "ctx", [(1, 0)])
    current = placed[:, span:].astype(f32) + earlier_back.astype(f32)
    with_meta = jnp.concatenate([keyval_grad_t[:, :meta_count], current.astype(bf16)], axis=1)
    keyval_columns_t = permute_sums(with_meta, 0).astype(bf16)
    out_wide = dot(mamba_grad_group_t, gated, 1, 0).astype(bf16)
    out_columns = scatter_rows(out_wide)
    query_pieces = permute_exchange(query_grad_t)
    late_attn_grad_t, query_grad_t = lax.optimization_barrier((attn_grad_t, query_grad_t))
    attn_grad_pieces = permute_gather(late_attn_grad_t)

    gated_grad = dot(mamba_grad_group_t, state_out_map, 0, 0)
    adjoint_end = end_adjoint(gated_grad, mixed, selects_t, aux, bias_row, rate_row)
    adjoint_start = lax.ppermute(adjoint_end, "ctx", [(1, 0)])
    adjoint_start, ffn_columns = lax.optimization_barrier((adjoint_start, ffn_columns))
    mix_grad, select_grad, scan_sums = backward_scan(
        gated_grad,
        mixed,
        selects,
        selects_t,
        states,
        aux,
        bias_row,
        rate_row,
        skip_row,
        adjoint_start,
        state_final,
    )
    state_wide = dot(normed_group_t, mix_grad, 1, 0).astype(bf16)
    state_wide, out_columns = lax.optimization_barrier((state_wide, out_columns))
    state_columns = scatter_rows(state_wide)
    (
        state_wide,
        mix_grad,
        keyval_columns_t,
        out_part_t,
        query_pieces,
        attn_grad_pieces,
    ) = lax.optimization_barrier(
        (state_wide, mix_grad, keyval_columns_t, out_part_t, query_pieces, attn_grad_pieces)
    )
    query_columns_t = in_order(query_pieces)
    attn_grad_group_t = jnp.concatenate(attn_grad_pieces, axis=1)
    select_grad_t = select_grad.T.astype(bf16)
    keyval_part = lax.dynamic_slice_in_dim(
        keyval_map, tp_index * (keyval_width // tp), keyval_width // tp, 1
    )
    query_term = dot(query_map, query_grad_t, 1, 0)
    normed_grad_part = (
        dot(state_map, mix_grad, 1, 1)
        + dot(select_map, select_grad_t, 1, 0)
        + dot(keyval_part, keyval_columns_t[:, meta_count:], 1, 0)
    )
    meta_grad_part = dot(keyval_part, keyval_columns_t[:, :meta_count], 1, 0)
    _, group_terms = rms_back(residual_group, mix_gain, normed_grad_part)
    meta_back, meta_terms = rms_back(meta_rows, mix_gain, meta_grad_part)
    _, query_terms = rms_back(residual, mix_gain, query_term)
    gain_sums = jnp.stack(
        [
            jnp.sum(group_terms, 1) + jnp.sum(meta_terms, 1) + jnp.sum(query_terms, 1),
            jnp.sum(attn_gain_terms, 1),
            jnp.sum(mamba_gain_terms, 1),
            jnp.sum(ffn_gain_terms, 1),
        ],
        axis=1,
    )
    vector_columns = -(-3 * channels // shard)
    vectors = jnp.pad(scan_sums[:3].reshape(-1), (0, vector_columns * shard - 3 * channels))
    vectors = jnp.tile(vectors.reshape(shard, vector_columns), (width // shard, 1))
    each = query_width // tp
    each_wide = -(-each // 128) * 128
    room = ((0, each_wide - each), (0, 0))
    small = [
        meta_back,
        dot(normed_group_t, keyval_columns_t[:, meta_count:], 1, 1)
        + dot(meta_normed_t, keyval_columns_t[:, :meta_count], 1, 1),
        dot(normed_group_t, select_grad_t, 1, 1),
        gain_sums,
        vectors,
    ]
    last_wide = jnp.concatenate(
        [
            dot(attn_grad_group_t, jnp.pad(attended_columns_t, room), 1, 1).astype(bf16),
            dot(normed_group_t, jnp.pad(query_columns_t, room), 1, 1).astype(bf16),
            jnp.concatenate([piece.astype(bf16) for piece in small], axis=1),
        ],
        axis=1,
    )
    last_wide, normed_grad_low = lax.optimization_barrier(
        (last_wide, normed_grad_part.astype(bf16))
    )
    last_wide, state_columns = lax.optimization_barrier((last_wide, state_columns))
    last_columns = scatter_rows(last_wide)
    normed_grad = line_sum(normed_grad_low, tp, 4) + query_term
    late_out_part_t, normed_grad = lax.optimization_barrier((out_part_t, normed_grad))
    layer_out_t = (mid + line_sum(late_out_part_t, tp, 5)).astype(bf16)
    residual_extra, _ = rms_back(residual, mix_gain, normed_grad)
    grad_tokens_t = (mid_grad + residual_extra).astype(bf16)
    grad_gate, grad_up, grad_ffn_output = [
        piece[:, :ff].astype(f32) for piece in cut(ffn_columns, [ff_wide] * 3)
    ]
    grad_ffn_input = jnp.stack([grad_gate, grad_up], axis=1)
    grad_mamba_input = state_columns.astype(f32)
    grad_mamba_output = out_columns.astype(f32)
    (
        grad_attn_output,
        _,
        grad_query,
        _,
        meta_shares,
        grad_keyval,
        select_shares,
        gain_shares,
        grad_vectors,
    ) = cut(
        last_columns,
        [
            each,
            each_wide - each,
            each,
            each_wide - each,
            meta_count,
            keyval_width // tp,
            2 * STATE,
            4,
            vector_columns,
        ],
    )
    grad_attn_output, grad_query, grad_keyval, grad_vectors = [
        v.astype(f32) for v in (grad_attn_output, grad_query, grad_keyval, grad_vectors)
    ]
    meta_each, select_each = meta_count // tp, 2 * STATE // tp

    def to_device(values):
        return jnp.swapaxes(values.reshape(shard, tp, values.shape[1] // tp), 0, 1)

    shares = jnp.concatenate(
        [
            to_device(meta_shares),
            to_device(select_shares),
            jnp.broadcast_to(gain_shares[None], (tp, shard, 4)),
        ],
        axis=2,
    )
    grad_meta, grad_select, grad_gains = cut(
        permute_sums(shares, 0)[0], [meta_each, select_each, 4]
    )
    grad_vectors = grad_vectors.reshape(-1)[: 3 * channels].reshape(3, channels)
    return (
        layer_out_t.T[None],
        grad_tokens_t.T[None],
        grad_meta,
        grad_gains[:, 0],
        grad_query,
        grad_keyval,
        grad_attn_output,
        grad_gains[:, 1],
        grad_mamba_input.reshape(shard, 3, channels),
        grad_select,
        grad_vectors[0],
        grad_vectors[1],
        grad_vectors[2],
        grad_mamba_output,
        grad_gains[:, 2],
        grad_gains[:, 3],
        grad_ffn_input,
        grad_ffn_output,
    )


def solution(mesh):
    rows = ("fsdp", "ctx")
    in_specs = (
        P("fsdp", ("ctx", "tp"), None),
        P("fsdp", None),
        P("fsdp", ("ctx", "tp"), None),
        P(rows, None),
        P(rows),
        P(rows, None),
        P(rows, None),
        P(rows, None),
        P(rows),
        P(rows, None, "tp"),
        P(rows, None),
        P("tp"),
        P("tp"),
        P("tp"),
        P(rows, "tp"),
        P(rows),
        P(rows),
        P(rows, None, None),
        P(rows, None),
    )
    out_specs = (
        P("fsdp", ("ctx", "tp"), None),
        P("fsdp", ("ctx", "tp"), None),
        P(rows, "tp"),
        P(rows),
        P(rows, "tp"),
        P(rows, "tp"),
        P(rows, "tp"),
        P(rows),
        P(rows, None, "tp"),
        P(rows, "tp"),
        P("tp"),
        P("tp"),
        P("tp"),
        P(rows, "tp"),
        P(rows),
        P(rows),
        P(rows, None, "tp"),
        P(rows, "tp"),
    )
    return jax.shard_map(
        per_device, mesh=mesh, in_specs=in_specs, out_specs=out_specs, check_vma=False
    )
```

```python
import functools

import jax
import jax.numpy as jnp
from jax import lax
from jax.experimental import pallas as pl
from jax.experimental.layout import Layout, with_layout_constraint
from jax.experimental.pallas import tpu as pltpu
from jax.sharding import PartitionSpec as P

HEAD_SIZE = 64
STATE = 16
WIN = 1024
SUB = 4
TILE = 128

bf16 = jnp.bfloat16
f32 = jnp.float32
epsilon = 1e-05
masked_score = -1e30


def mm(a, b):
    return lax.dot_general(a, b, (((1,), (0,)), ((), ())), preferred_element_type=f32)


def mm_nt(a, b):
    return lax.dot_general(a, b, (((1,), (1,)), ((), ())), preferred_element_type=f32)


def iota(shape, dim):
    return lax.broadcasted_iota(jnp.int32, shape, dim)


def split_mm(a, b):
    high = b.astype(bf16)
    return mm(a, high) + mm(a, (b - high.astype(f32)).astype(bf16))


def ones_where(cond):
    return jnp.where(cond, 1.0, 0.0)


def softplus(v):
    return jnp.maximum(v, 0.0) + jnp.log1p(jnp.exp(-jnp.abs(v)))


def logistic(v):
    return 1.0 / (1.0 + jnp.exp(-v))


def group_mask(rows, columns, row_unit, column_unit):
    return iota((rows, columns), 0) // row_unit == iota((rows, columns), 1) // column_unit


def sums_matrix():
    rows = 2 * TILE + TILE // SUB
    row = iota((rows, TILE), 0)
    column = iota((rows, TILE), 1)
    token = row % TILE
    same = token // SUB == column // SUB
    upto = (row < TILE) & same & (column <= token)
    after = (row >= TILE) & (row < 2 * TILE) & same & (column > token)
    whole = (row >= 2 * TILE) & (row - 2 * TILE == column // SUB)
    return ones_where(upto | after | whole).astype(bf16)


def part(mixed, k):
    channels = mixed.shape[1] // 3
    return mixed[:, k * channels : (k + 1) * channels]


def decays(step_raw, bias_ref, rate_ref, alive_last_ref):
    raw = step_raw + bias_ref[...]
    step = softplus(raw)
    log_decay = -step * rate_ref[...]
    sums = split_mm(sums_matrix(), log_decay)
    upto = jnp.exp(sums[:TILE])
    after = sums[TILE : 2 * TILE]
    block = jnp.exp(sums[2 * TILE :]) * alive_last_ref[...]
    return raw, step, log_decay, upto, after, block


def in_blocks(select_t_ref, aux_t_ref):
    width = TILE // SUB * STATE
    tiled = jnp.concatenate([select_t_ref[:STATE, :].astype(f32) * aux_t_ref[1:2, :]] * (TILE // SUB), axis=0)
    return jnp.where(group_mask(width, TILE, STATE, SUB), tiled, 0.0).astype(bf16)


def out_blocks_t(select_t_ref, aux_t_ref):
    width = TILE // SUB * STATE
    tiled = jnp.concatenate([select_t_ref[STATE:, :].astype(f32) * aux_t_ref[0:1, :]] * (TILE // SUB), axis=0)
    return jnp.where(group_mask(width, TILE, STATE, SUB), tiled, 0.0).astype(bf16)


def spread(part, factor):
    width = TILE // SUB * STATE
    places = ones_where(iota((STATE, width), 0) == iota((STATE, width), 1) % STATE).astype(bf16)
    wide = mm(part, places) * factor
    return jnp.where(group_mask(TILE, width, SUB, STATE), wide, 0.0).astype(bf16)


def fold(wide, factor):
    width = TILE // SUB * STATE
    places = ones_where(iota((width, STATE), 0) % STATE == iota((width, STATE), 1)).astype(bf16)
    kept = jnp.where(group_mask(TILE, width, SUB, STATE), wide * factor, 0.0)
    return split_left(kept, places)


def split_left(a, b):
    high = a.astype(bf16)
    return mm(high, b) + mm((a - high.astype(f32)).astype(bf16), b)


def pairs(aux_ref, aux_t_ref, lower):
    row, column = iota((TILE, TILE), 0), iota((TILE, TILE), 1)
    order = column <= row if lower else column >= row
    return (row // SUB == column // SUB) & order & (aux_ref[:, 2:3] == aux_t_ref[2:3, :])


def run_states(state, local_ref, block_ref, keep=None):
    def one(k, state):
        if keep is not None:
            keep[pl.ds(pl.multiple_of(k * STATE, STATE), STATE), :] = state.astype(bf16)
        return block_ref[pl.ds(k, 1), :] * state + local_ref[pl.ds(pl.multiple_of(k * STATE, STATE), STATE), :]

    return lax.fori_loop(0, TILE // SUB, one, state, unroll=8)


def end_state_kernel(mixed, select_t, aux, aux_t, alive_last, bias, rate, end, state, local, block):
    @pl.when(pl.program_id(0) == 0)
    def _():
        state[...] = jnp.zeros_like(state)

    raw, step, log_decay, upto, after, total = decays(part(mixed, 2), bias, rate, alive_last)
    driven = (jnp.exp(after) * step * part(mixed, 0)).astype(bf16)
    local[...] = mm(in_blocks(select_t, aux_t), driven)
    block[...] = total
    state[...] = run_states(state[...], local, block)
    end[...] = state[...]


def forward_kernel(mixed, select, select_t, aux, aux_t, alive_last, bias, rate, skip, start, gated, states, end, state, local, block):
    @pl.when(pl.program_id(0) == 0)
    def _():
        state[...] = start[...]

    raw, step, log_decay, upto, after, total = decays(part(mixed, 2), bias, rate, alive_last)
    x = part(mixed, 0)
    driven = (jnp.exp(after) * step * x).astype(bf16)
    local[...] = mm(in_blocks(select_t, aux_t), driven)
    block[...] = total
    state[...] = run_states(state[...], local, block, states)
    end[...] = state[...]
    out_part = select[:, STATE:]
    cross = jnp.where(pairs(aux, aux_t, True), mm(out_part, select_t[:STATE, :]), 0.0).astype(bf16)
    y = upto * mm(spread(out_part, aux[:, 0:1]), states[...]) + jnp.exp(-after) * mm(cross, driven) + skip[...] * x
    gates = part(mixed, 1)
    gated[...] = (y * gates * logistic(gates)).astype(bf16)


def back_run(carry, local_ref, block_ref, keep, states=None, bound=None):
    count = TILE // SUB

    def one(i, carry):
        k = count - 1 - i
        rows = pl.ds(pl.multiple_of(k * STATE, STATE), STATE)
        if keep is not None:
            keep[rows, :] = carry[0].astype(bf16)
            bound[pl.ds(k, 1), :] = carry[1]
        new = block_ref[pl.ds(k, 1), :] * carry[0] + local_ref[rows, :]
        if keep is None:
            return (new, carry[1])
        return (new, jnp.sum(new * states[rows, :].astype(f32), axis=0, keepdims=True))

    return lax.fori_loop(0, count, one, carry, unroll=8)


def end_adjoint_kernel(gated_grad, mixed, select_t, aux, aux_t, alive_last, bias, rate, end, state, local, block):
    @pl.when(pl.program_id(0) == 0)
    def _():
        state[...] = jnp.zeros_like(state)

    raw, step, log_decay, upto, after, total = decays(part(mixed, 2), bias, rate, alive_last)
    gates = part(mixed, 1)
    dy = gated_grad[...] * gates * logistic(gates)
    local[...] = mm(out_blocks_t(select_t, aux_t), (upto * dy).astype(bf16))
    block[...] = total
    state[...] = back_run((state[...], jnp.zeros((1, state.shape[1]), f32)), local, block, None)[0]
    end[...] = state[...]


def backward_kernel(
    count,
    gated_grad,
    mixed,
    select,
    select_t,
    states,
    aux,
    aux_t,
    alive_last,
    bias,
    rate,
    skip,
    start,
    final,
    source,
    mix_grad,
    select_grad,
    sums,
    total_out,
    state,
    local,
    block,
    adjoint,
    bound,
    edge,
    own,
    sent,
    got,
    loads,
    send_sems,
    recv_sems,
):
    tile, tiles = pl.program_id(0), pl.num_programs(0)
    begin, step_line, finish = line_sum_steps(
        count, source, own, sent, got, total_out, loads, send_sems, recv_sems
    )

    @pl.when(tile == 0)
    def _():
        begin()
        state[...] = start[...]
        edge[...] = jnp.sum(start[...] * final[...], axis=0, keepdims=True)
        sums[...] = jnp.zeros_like(sums)

    @pl.when(tile == tiles // 2)
    def _():
        step_line(1)

    raw, step, log_decay, upto, after, total = decays(part(mixed, 2), bias, rate, alive_last)
    channels = state.shape[1]
    x = part(mixed, 0)
    decay_after = jnp.exp(after)
    grow = jnp.exp(-after)
    driven = (decay_after * step * x).astype(bf16)
    in_part, out_part = select[:, :STATE], select[:, STATE:]
    in_part_t, out_part_t = select_t[:STATE, :], select_t[STATE:, :]
    lower, upper = pairs(aux, aux_t, True), pairs(aux, aux_t, False)
    cross = jnp.where(lower, mm(out_part, in_part_t), 0.0).astype(bf16)
    cross_t = jnp.where(upper, mm(in_part, out_part_t), 0.0).astype(bf16)
    y = upto * mm(spread(out_part, aux[:, 0:1]), states[...]) + grow * mm(cross, driven)
    gates = part(mixed, 1)
    sigma = logistic(gates)
    grad = gated_grad[...]
    dy = grad * gates * sigma
    mix_grad[:, channels : 2 * channels] = (grad * (y + skip[...] * x) * (sigma * (1.0 + gates * (1.0 - sigma)))).astype(bf16)
    dy_low = (upto * dy).astype(bf16)
    dy_grown = (grow * dy).astype(bf16)
    local[...] = mm(out_blocks_t(select_t, aux_t), dy_low)
    block[...] = total
    new_state, new_edge = back_run((state[...], edge[...]), local, block, adjoint, states, bound)
    state[...] = new_state
    edge[...] = new_edge
    du = decay_after * (mm(spread(in_part, aux[:, 1:2]), adjoint[...]) + mm(cross_t, dy_grown))
    out_grad = fold(mm_nt(dy_low, states[...]), aux[:, 0:1])
    in_grad = fold(mm_nt(driven, adjoint[...]), aux[:, 1:2])
    cross_grad = jnp.where(lower, mm_nt(dy_grown, driven), 0.0)
    cross_grad_t = jnp.where(upper, mm_nt(driven, dy_grown), 0.0)
    out_grad = out_grad + split_left(cross_grad, in_part)
    in_grad = in_grad + split_left(cross_grad_t, out_part)
    select_grad[...] = jnp.concatenate([in_grad, out_grad], axis=1)
    flow = dy * y - step * x * du
    places = ones_where(group_mask(TILE, TILE // SUB, SUB, 1)) * aux[:, 1:2]
    decay_grad = aux[:, 3:4] * (
        split_mm(ones_where(upper).astype(bf16), flow) + split_mm(places.astype(bf16), bound[...])
    )
    step_grad = (x * du - rate[...] * decay_grad) * logistic(raw)
    mix_grad[:, :channels] = (skip[...] * dy + step * du).astype(bf16)
    mix_grad[:, 2 * channels :] = step_grad.astype(bf16)
    sums[0:1, :] += jnp.sum(step_grad, axis=0, keepdims=True)
    sums[1:2, :] += jnp.sum(decay_grad * log_decay, axis=0, keepdims=True)
    sums[2:3, :] += jnp.sum(dy * x, axis=0, keepdims=True)

    @pl.when(tile == tiles - 1)
    def _():
        for k in range(2, count):
            step_line(k)
        finish()


def scan_specs(tokens, channels, back):
    tiles = tokens // TILE

    def at(i):
        return tiles - 1 - i if back else i

    mixed = pl.BlockSpec((TILE, 3 * channels), lambda i: (at(i), 0))
    rows = pl.BlockSpec((TILE, channels), lambda i: (at(i), 0))
    select = pl.BlockSpec((TILE, 2 * STATE), lambda i: (at(i), 0))
    select_t = pl.BlockSpec((2 * STATE, TILE), lambda i: (0, at(i)))
    states = pl.BlockSpec((TILE // SUB * STATE, channels), lambda i: (at(i), 0))
    aux = pl.BlockSpec((TILE, 8), lambda i: (at(i), 0))
    aux_t = pl.BlockSpec((8, TILE), lambda i: (0, at(i)))
    last = pl.BlockSpec((TILE // SUB, 1), lambda i: (at(i), 0))
    row = pl.BlockSpec((1, channels), lambda i: (0, 0))
    state = pl.BlockSpec((STATE, channels), lambda i: (0, 0))
    return tiles, mixed, rows, select, select_t, states, aux, aux_t, last, row, state


def scan_scratch(channels):
    return [
        pltpu.VMEM((STATE, channels), f32),
        pltpu.VMEM((TILE // SUB * STATE, channels), f32),
        pltpu.VMEM((TILE // SUB, channels), f32),
    ]


def scan_call(kernel, name, tiles, in_specs, out_specs, out_shape, scratch, flops, collective=None):
    return pl.pallas_call(
        kernel,
        name=name,
        grid=(tiles,),
        in_specs=in_specs,
        out_specs=out_specs,
        scratch_shapes=scratch,
        out_shape=out_shape,
        compiler_params=pltpu.CompilerParams(
            vmem_limit_bytes=48 << 20,
            dimension_semantics=("arbitrary",),
            collective_id=collective,
            has_side_effects=collective is not None,
        ),
        cost_estimate=pl.CostEstimate(flops=flops, bytes_accessed=1 << 24, transcendentals=0),
    )


def scan_aux(segment, before):
    count = segment.shape[0]
    blocks = segment.reshape(count // SUB, SUB)
    ends = jnp.concatenate([before[None], blocks[:-1, -1]])
    alive = (blocks == ends[:, None]).reshape(-1).astype(f32)
    tail = (blocks == blocks[:, -1:]).reshape(-1).astype(f32)
    joined = (segment == jnp.concatenate([before[None], segment[:-1]])).astype(f32)
    zero = jnp.zeros_like(alive)
    aux_t = jnp.stack([alive, tail, segment.astype(f32), joined, zero, zero, zero, zero])
    last = (blocks[:, -1] == ends).astype(f32)[:, None]
    return aux_t.T, aux_t, last


def end_state(mixed, select_t, aux, bias, rate):
    tokens, channels = mixed.shape[0], mixed.shape[1] // 3
    tiles, mixed_s, rows, select_s, select_t_s, states_s, aux_s, aux_t_s, last_s, row, state = scan_specs(
        tokens, channels, False
    )
    return scan_call(
        end_state_kernel,
        "end_state",
        tiles,
        [mixed_s, select_t_s, aux_s, aux_t_s, last_s, row, row],
        state,
        jax.ShapeDtypeStruct((STATE, channels), f32),
        scan_scratch(channels),
        10**10,
    )(mixed, select_t, *aux, bias, rate)


def forward_scan(mixed, select, select_t, aux, bias, rate, skip, start):
    tokens, channels = mixed.shape[0], mixed.shape[1] // 3
    tiles, mixed_s, rows, select_s, select_t_s, states_s, aux_s, aux_t_s, last_s, row, state = scan_specs(
        tokens, channels, False
    )
    return scan_call(
        forward_kernel,
        "forward_scan",
        tiles,
        [mixed_s, select_s, select_t_s, aux_s, aux_t_s, last_s, row, row, row, state],
        [rows, states_s, state],
        [
            jax.ShapeDtypeStruct((tokens, channels), bf16),
            jax.ShapeDtypeStruct((tokens // SUB * STATE, channels), bf16),
            jax.ShapeDtypeStruct((STATE, channels), f32),
        ],
        scan_scratch(channels),
        16 * 10**9,
    )(mixed, select, select_t, *aux, bias, rate, skip, start)


def end_adjoint(gated_grad, mixed, select_t, aux, bias, rate):
    tokens, channels = mixed.shape[0], mixed.shape[1] // 3
    tiles, mixed_s, rows, select_s, select_t_s, states_s, aux_s, aux_t_s, last_s, row, state = scan_specs(
        tokens, channels, True
    )
    return scan_call(
        end_adjoint_kernel,
        "end_adjoint",
        tiles,
        [rows, mixed_s, select_t_s, aux_s, aux_t_s, last_s, row, row],
        state,
        jax.ShapeDtypeStruct((STATE, channels), f32),
        scan_scratch(channels),
        10**10,
    )(gated_grad, mixed, select_t, *aux, bias, rate)


def backward_scan(
    gated_grad, mixed, select, select_t, states, aux, bias, rate, skip, start, final, source, count, collective
):
    height, each = source.shape[0], source.shape[1] // count
    tokens, channels = mixed.shape[0], mixed.shape[1] // 3
    tiles, mixed_s, rows, select_s, select_t_s, states_s, aux_s, aux_t_s, last_s, row, state = scan_specs(
        tokens, channels, True
    )
    return scan_call(
        functools.partial(backward_kernel, count),
        "backward_scan",
        tiles,
        [rows, mixed_s, select_s, select_t_s, states_s, aux_s, aux_t_s, last_s, row, row, row, state, state]
        + [pl.BlockSpec(memory_space=pl.ANY)],
        [
            mixed_s,
            select_s,
            pl.BlockSpec((8, channels), lambda i: (0, 0)),
            pl.BlockSpec((height, each), lambda i: (0, 0)),
        ],
        [
            jax.ShapeDtypeStruct((tokens, 3 * channels), bf16),
            jax.ShapeDtypeStruct((tokens, 2 * STATE), f32),
            jax.ShapeDtypeStruct((8, channels), f32),
            jax.ShapeDtypeStruct((height, each), f32),
        ],
        scan_scratch(channels)
        + [
            pltpu.VMEM((TILE // SUB * STATE, channels), bf16),
            pltpu.VMEM((TILE // SUB, channels), f32),
            pltpu.VMEM((1, channels), f32),
        ]
        + line_sum_scratch(count, height, each),
        36 * 10**9,
        collective,
    )(gated_grad, mixed, select, select_t, states, *aux, bias, rate, skip, start, final, source)


MESH = pl.DeviceIdType.MESH
COMM = {"has_side_effects": True}


def neighbour_barrier(count):
    place = lax.axis_index("tp")
    ready = pltpu.get_barrier_semaphore()
    sides = ((place < count - 1, place + 1), (place > 0, place - 1))
    for there, other in sides:

        @pl.when(there)
        def _():
            pl.semaphore_signal(ready, inc=1, device_id={"tp": other}, device_id_type=MESH)

    peers = jnp.where(place < count - 1, 1, 0) + jnp.where(place > 0, 1, 0)
    pl.semaphore_wait(ready, peers)


def line_steps(count, source, target, copies, send_sems, recv_sems):
    place = lax.axis_index("tp")
    width = source.shape[1]

    def at(owner):
        return target.at[:, pl.ds(pl.multiple_of(owner * width, width), width)]

    def local():
        return pltpu.make_async_copy(source, at(place), copies)

    def remote(side, step):
        owner = place - step if side == 0 else place + step
        return pltpu.make_async_remote_copy(
            src_ref=source if step == 0 else at(owner),
            dst_ref=at(owner),
            send_sem=send_sems.at[side, step],
            recv_sem=recv_sems.at[side, step],
            device_id={"tp": place + 1 if side == 0 else place - 1},
            device_id_type=MESH,
        )

    def has(side, step):
        return place - step >= 0 if side == 0 else place + step < count

    def neighbour(side):
        return place < count - 1 if side == 0 else place > 0

    def send(step):
        for side in (0, 1):

            @pl.when(neighbour(side) & has(side, step))
            def _():
                remote(side, step).start()

    def receive(step):
        for side in (0, 1):

            @pl.when(has(side, step + 1))
            def _():
                remote(side, step).wait_recv()

    def start():
        neighbour_barrier(count)
        local().start()
        send(0)

    def step(k):
        receive(k - 1)
        if k < count - 1:
            send(k)

    def finish():
        for k in range(count - 1):
            for side in (0, 1):

                @pl.when(neighbour(side) & has(side, k))
                def _():
                    remote(side, k).wait_send()

        local().wait()

    return start, step, finish


def line_scratch(count):
    return [
        pltpu.SemaphoreType.DMA,
        pltpu.SemaphoreType.DMA((2, count - 1)),
        pltpu.SemaphoreType.DMA((2, count - 1)),
    ]


def line_gather_kernel(count, source, target, copies, send_sems, recv_sems):
    start, step, finish = line_steps(count, source, target, copies, send_sems, recv_sems)
    start()
    for k in range(1, count):
        step(k)
    finish()


def line_gather(source, count, collective):
    return pl.pallas_call(
        functools.partial(line_gather_kernel, count),
        name="line_gather",
        in_specs=[pl.BlockSpec(memory_space=pl.ANY)],
        out_specs=pl.BlockSpec(memory_space=pl.ANY),
        out_shape=jax.ShapeDtypeStruct((source.shape[0], source.shape[1] * count), source.dtype),
        scratch_shapes=line_scratch(count),
        compiler_params=pltpu.CompilerParams(collective_id=collective, has_side_effects=True),
    )(source)


def line_sum_steps(count, source, own, sent, got, total, loads, send_sems, recv_sems):
    place = lax.axis_index("tp")
    width = total.shape[1]

    def whose(side, step):
        return place + (count - step) if side == 0 else place - (count - step)

    def sends(side, step):
        owner = whose(side, step)
        return owner < count if side == 0 else owner >= 0

    def receives(side, step):
        return (place >= 1) & (place <= step) if side == 0 else (place <= count - 2) & (place >= count - 1 - step)

    def load(side, step):
        owner = whose(side, step)
        return pltpu.make_async_copy(
            source.at[:, pl.ds(pl.multiple_of(owner * width, width), width)],
            sent.at[side, step - 1],
            loads.at[side, step - 1],
        )

    def mine():
        return pltpu.make_async_copy(
            source.at[:, pl.ds(pl.multiple_of(place * width, width), width)], own, loads.at[2, 0]
        )

    def remote(side, step):
        return pltpu.make_async_remote_copy(
            src_ref=sent.at[side, step - 1],
            dst_ref=got.at[side, step - 1],
            send_sem=send_sems.at[side, step - 1],
            recv_sem=recv_sems.at[side, step - 1],
            device_id={"tp": place + 1 if side == 0 else place - 1},
            device_id_type=MESH,
        )

    def start():
        neighbour_barrier(count)
        mine().start()
        for step in range(1, count):
            for side in (0, 1):

                @pl.when(sends(side, step))
                def _():
                    load(side, step).start()

        step_out(1)

    def step_out(step):
        for side in (0, 1):

            @pl.when(sends(side, step))
            def _():
                load(side, step).wait()

            if step > 1:

                @pl.when(sends(side, step) & receives(side, step - 1))
                def _():
                    sent[side, step - 1] = (
                        sent[side, step - 1].astype(f32) + got[side, step - 2].astype(f32)
                    ).astype(bf16)

            @pl.when(sends(side, step))
            def _():
                remote(side, step).start()

    def step(k):
        for side in (0, 1):

            @pl.when(receives(side, k))
            def _():
                remote(side, k).wait_recv()

        if k < count - 1:
            step_out(k + 1)

    def finish():
        mine().wait()
        total[...] = own[...].astype(f32)
        for side in (0, 1):

            @pl.when(receives(side, count - 1))
            def _():
                total[...] = total[...] + got[side, count - 2].astype(f32)

            for k in range(1, count):

                @pl.when(sends(side, k))
                def _():
                    remote(side, k).wait_send()

    return start, step, finish


def line_sum_scratch(count, height, width):
    return [
        pltpu.VMEM((height, width), bf16),
        pltpu.VMEM((2, count - 1, height, width), bf16),
        pltpu.VMEM((2, count - 1, height, width), bf16),
        pltpu.SemaphoreType.DMA((3, count - 1)),
        pltpu.SemaphoreType.DMA((2, count - 1)),
        pltpu.SemaphoreType.DMA((2, count - 1)),
    ]


def line_sum_kernel(count, source, total, own, sent, got, loads, send_sems, recv_sems):
    start, step, finish = line_sum_steps(
        count, source, own, sent, got, total, loads, send_sems, recv_sems
    )
    start()
    for k in range(1, count):
        step(k)
    finish()


def line_sum(source, count, collective):
    height, width = source.shape[0], source.shape[1] // count
    return pl.pallas_call(
        functools.partial(line_sum_kernel, count),
        name="line_sum",
        in_specs=[pl.BlockSpec(memory_space=pl.ANY)],
        out_specs=pl.BlockSpec(memory_space=pltpu.VMEM),
        out_shape=jax.ShapeDtypeStruct((height, width), f32),
        scratch_shapes=line_sum_scratch(count, height, width),
        compiler_params=pltpu.CompilerParams(
            vmem_limit_bytes=24 << 20, collective_id=collective, has_side_effects=True
        ),
    )(source)


def attend_kernel(
    group,
    count,
    query_t,
    key_t,
    value_t,
    bias,
    source,
    out_t,
    log_total,
    total_out,
    own,
    sent,
    got,
    loads,
    send_sems,
    recv_sems,
):
    head, heads = pl.program_id(0), pl.num_programs(0)
    start, step, finish = line_sum_steps(
        count, source, own, sent, got, total_out, loads, send_sems, recv_sems
    )

    @pl.when(head == 0)
    def _():
        start()

    @pl.when(head == heads - 2)
    def _():
        step(1)

    keys = key_t[...].T
    values_t = value_t[...]
    for g in range(group):
        at = slice(g * HEAD_SIZE, (g + 1) * HEAD_SIZE)
        scores = mm(keys, query_t[at, :] * 0.125) + bias[...]
        top = jnp.max(scores, axis=0, keepdims=True)
        probs = jnp.exp(scores - top)
        total = jnp.sum(probs, axis=0, keepdims=True)
        out_t[at, :] = (mm(values_t, probs.astype(bf16)) / total).astype(bf16)
        log_total[g : g + 1, :] = top + jnp.log(total)

    @pl.when(head == heads - 1)
    def _():
        for k in range(2, count):
            step(k)
        finish()


def attend_back_kernel(
    group,
    count,
    query_t,
    key_t,
    value_t,
    bias,
    out_t,
    log_total,
    grad_t,
    source,
    query_grad_t,
    keyval_grad_t,
    target,
    copies,
    send_sems,
    recv_sems,
):
    head, heads = pl.program_id(0), pl.num_programs(0)
    start, step, finish = line_steps(count, source, target, copies, send_sems, recv_sems)

    @pl.when(head == 0)
    def _():
        start()

    @pl.when(head == heads - 2)
    def _():
        step(1)

    keys_t = key_t[...]
    keys = keys_t.T
    values = value_t[...].T
    key_sum = jnp.zeros(keys_t.shape, f32)
    value_sum = jnp.zeros(keys_t.shape, f32)
    for g in range(group):
        at = slice(g * HEAD_SIZE, (g + 1) * HEAD_SIZE)
        query = query_t[at, :] * 0.125
        grad = grad_t[at, :]
        probs = jnp.exp(mm(keys, query) + bias[...] - log_total[g : g + 1, :])
        centre = jnp.sum(grad.astype(f32) * out_t[at, :].astype(f32), axis=0, keepdims=True)
        score_grad = (probs * (mm(values, grad) - centre)).astype(bf16)
        query_grad_t[at, :] = (mm(keys_t, score_grad) * 0.125).astype(bf16)
        key_sum = key_sum + mm_nt(query, score_grad)
        value_sum = value_sum + mm_nt(grad, probs.astype(bf16))
    keyval_grad_t[0] = key_sum.astype(bf16)
    keyval_grad_t[1] = value_sum.astype(bf16)

    @pl.when(head == heads - 1)
    def _():
        for k in range(2, count):
            step(k)
        finish()


def attend(query_t, keyval_t, bias, source, key_value_heads, count, collective):
    width, rows = query_t.shape
    keys = keyval_t.shape[1]
    group = width // HEAD_SIZE // key_value_heads
    kv = key_value_heads
    height, each = source.shape[0], source.shape[1] // count
    return pl.pallas_call(
        functools.partial(attend_kernel, group, count),
        name="attend",
        grid=(kv,),
        in_specs=[
            pl.BlockSpec((group * HEAD_SIZE, rows), lambda h: (h, 0)),
            pl.BlockSpec((HEAD_SIZE, keys), lambda h: (h, 0)),
            pl.BlockSpec((HEAD_SIZE, keys), lambda h: (h + kv, 0)),
            pl.BlockSpec((keys, rows), lambda h: (0, 0)),
            pl.BlockSpec(memory_space=pl.ANY),
        ],
        out_specs=[
            pl.BlockSpec((group * HEAD_SIZE, rows), lambda h: (h, 0)),
            pl.BlockSpec((None, 8, rows), lambda h: (h, 0, 0)),
            pl.BlockSpec((height, each), lambda h: (0, 0)),
        ],
        out_shape=[
            jax.ShapeDtypeStruct((width, rows), bf16),
            jax.ShapeDtypeStruct((kv, 8, rows), f32),
            jax.ShapeDtypeStruct((height, each), f32),
        ],
        scratch_shapes=line_sum_scratch(count, height, each),
        compiler_params=pltpu.CompilerParams(
            vmem_limit_bytes=56 << 20,
            dimension_semantics=("arbitrary",),
            collective_id=collective,
            has_side_effects=True,
        ),
    )(query_t, keyval_t, keyval_t, bias, source)


def attend_back(query_t, keyval_t, bias, out_t, log_total, grad_t, source, key_value_heads, count, collective):
    width, rows = query_t.shape
    keys = keyval_t.shape[1]
    group = width // HEAD_SIZE // key_value_heads
    kv = key_value_heads
    wide = pl.BlockSpec((group * HEAD_SIZE, rows), lambda h: (h, 0))
    head = pl.BlockSpec((HEAD_SIZE, keys), lambda h: (h, 0))
    anywhere = pl.BlockSpec(memory_space=pl.ANY)
    return pl.pallas_call(
        functools.partial(attend_back_kernel, group, count),
        name="attend_back",
        grid=(kv,),
        in_specs=[
            wide,
            head,
            pl.BlockSpec((HEAD_SIZE, keys), lambda h: (h + kv, 0)),
            pl.BlockSpec((keys, rows), lambda h: (0, 0)),
            wide,
            pl.BlockSpec((None, 8, rows), lambda h: (h, 0, 0)),
            wide,
            anywhere,
        ],
        out_specs=[wide, pl.BlockSpec((2, HEAD_SIZE, keys), lambda h: (0, h, 0)), anywhere],
        out_shape=[
            jax.ShapeDtypeStruct((width, rows), bf16),
            jax.ShapeDtypeStruct((2, kv * HEAD_SIZE, keys), bf16),
            jax.ShapeDtypeStruct((source.shape[0], source.shape[1] * count), source.dtype),
        ],
        scratch_shapes=line_scratch(count),
        compiler_params=pltpu.CompilerParams(
            vmem_limit_bytes=56 << 20,
            dimension_semantics=("arbitrary",),
            collective_id=collective,
            has_side_effects=True,
        ),
    )(query_t, keyval_t, keyval_t, bias, out_t, log_total, grad_t, source)


def rms_norm(values, gain):
    return values * lax.rsqrt(jnp.mean(values * values, axis=0, keepdims=True) + epsilon) * gain


def rms_back(values, gain, grad):
    scale = lax.rsqrt(jnp.mean(values * values, axis=0, keepdims=True) + epsilon)
    normal = values * scale
    weighted = grad * gain
    back = scale * (weighted - normal * jnp.mean(weighted * normal, axis=0, keepdims=True))
    return back, grad * normal


def dot(left, right, left_dim, right_dim):
    return lax.dot_general(
        left, right, (((left_dim,), (right_dim,)), ((), ())), preferred_element_type=f32
    )


def gather_rows(whole):
    return lax.all_gather(whole, ("fsdp", "ctx"), axis=0, tiled=True)


def by_rows(values):
    return with_layout_constraint(values, Layout((0, 1)))


def scatter_rows(whole):
    return by_rows(
        lax.psum_scatter(by_rows(whole), ("fsdp", "ctx"), scatter_dimension=0, tiled=True)
    )


def send(values, by):
    count = lax.axis_size("tp")
    return lax.ppermute(values, "tp", [(i, (i + by) % count) for i in range(count)])


def permute_gather(own):
    count = lax.axis_size("tp")
    return [own] + [send(own, k) for k in range(1, count)]


def in_order(pieces):
    count, place = lax.axis_size("tp"), lax.axis_index("tp")
    return jnp.concatenate(
        [lax.select_n(lax.rem(place - p + count, count), *pieces) for p in range(count)], axis=1
    )


def permute_sums(values, axis):
    count, place = lax.axis_size("tp"), lax.axis_index("tp")
    each = values.shape[axis] // count
    shares = [
        lax.dynamic_slice_in_dim(values, lax.rem(place + k, count) * each, each, axis)
        for k in range(count)
    ]
    total = shares[0].astype(f32)
    for k in (2, 1, 3):
        total = total + send(shares[k], k).astype(f32)
    return total


def permute_exchange(values):
    count, place = lax.axis_size("tp"), lax.axis_index("tp")
    shares = values.reshape(count, values.shape[0] // count, values.shape[1])
    pieces = [
        lax.dynamic_index_in_dim(shares, lax.rem(place + k, count), 0, False) for k in range(count)
    ]
    return [pieces[0]] + [send(pieces[k], k) for k in range(1, count)]


def cut(values, widths):
    pieces = []
    offset = 0
    for count in widths:
        pieces.append(values[:, offset : offset + count])
        offset = offset + count
    return pieces


def per_device(
    tokens,
    segments,
    cotangent,
    meta_tokens,
    gain_mix,
    query_weight,
    key_value_weight,
    attn_output,
    gain_attn,
    mamba_input,
    mamba_select,
    step_bias,
    decay_log,
    state_skip,
    mamba_output,
    gain_mamba,
    gain_ffn,
    ffn_input,
    ffn_output,
):
    tokens_t, segments, cotangent_t = tokens[0].T, segments[0], cotangent[0].T
    width, rows = tokens_t.shape
    shard = meta_tokens.shape[0]
    tp = lax.axis_size("tp")
    tp_index = lax.axis_index("tp")
    ctx_index = lax.axis_index("ctx")
    span = rows * tp
    query_width = query_weight.shape[1]
    keyval_width = key_value_weight.shape[1]
    heads = keyval_width // (2 * HEAD_SIZE)
    channels = mamba_input.shape[2]
    ff = ffn_input.shape[2] // tp
    ff_wide = -(-ff // 128) * 128
    meta_count = meta_tokens.shape[1]
    window = WIN + rows

    gains = jnp.stack([gain_mix, gain_attn, gain_mamba, gain_ffn], axis=1)
    flat_input = mamba_input.reshape(shard, 3 * channels)
    small = jnp.concatenate(
        [mamba_select, gains, jnp.zeros((shard, 128 - 2 * STATE - 4), bf16)], axis=1
    )
    first = jnp.concatenate([small, flat_input], axis=1)
    first, second_parts = lax.optimization_barrier(
        (first, (key_value_weight, meta_tokens, query_weight))
    )
    second = jnp.concatenate(second_parts, axis=1)
    first, second, tokens_t = lax.optimization_barrier((first, second, tokens_t))
    first = gather_rows(first)
    second = gather_rows(second)
    tokens_group_t = line_gather(tokens_t, tp, 0)
    late_cotangent_t, tokens_group_t = lax.optimization_barrier((cotangent_t, tokens_group_t))
    cotangent_pieces = permute_gather(late_cotangent_t)

    select_map, gain_columns, _, state_map = cut(
        first, [2 * STATE, 4, 128 - 2 * STATE - 4, 3 * channels]
    )
    keyval_map, meta_full, query_map = cut(second, [keyval_width, meta_count, query_width])
    state_out_map = gather_rows(mamba_output)
    attn_map = gather_rows(attn_output)
    gain_columns = gain_columns.astype(f32)
    mix_gain, attn_gain, mamba_gain, ffn_gain = [gain_columns[:, k : k + 1] for k in range(4)]

    residual = tokens_t.astype(f32)
    residual_group = tokens_group_t.astype(f32)
    normed_t = rms_norm(residual, mix_gain).astype(bf16)
    normed_group_t = rms_norm(residual_group, mix_gain).astype(bf16)
    meta_rows = meta_full.astype(f32)
    meta_normed_t = rms_norm(meta_rows, mix_gain).astype(bf16)

    mixed = dot(normed_group_t, state_map, 0, 0)
    selects_t = dot(select_map, normed_group_t, 0, 0).astype(bf16)
    selects = selects_t.T
    seg_current = lax.dynamic_slice_in_dim(segments, ctx_index * span, span, 0)
    seg_earlier = lax.dynamic_slice_in_dim(segments, jnp.maximum(ctx_index - 1, 0) * span, span, 0)
    seg_before = jnp.where(
        ctx_index > 0,
        lax.dynamic_index_in_dim(segments, jnp.maximum(ctx_index * span - 1, 0), 0, False),
        -1,
    )
    aux = scan_aux(seg_current, seg_before)
    bias_row = step_bias[None]
    rate_row = jnp.exp(decay_log)[None]
    skip_row = state_skip[None]
    selects_t, late_up, late_down = lax.optimization_barrier((selects_t, ffn_input, ffn_output))
    ffn_shards = [
        lax.dynamic_slice_in_dim(whole, tp_index * ff, ff, 1)
        for whole in (late_up[:, 0], late_up[:, 1], late_down)
    ]
    state_end = end_state(mixed, selects_t, aux, bias_row, rate_row)
    state_start = lax.ppermute(state_end, "ctx", [(0, 1)])

    query_t = dot(query_map, normed_t, 0, 0).astype(bf16)
    keyval_group_t = dot(keyval_map, normed_group_t, 0, 0).astype(bf16)
    meta_keyval_t = dot(keyval_map, meta_normed_t, 0, 0).astype(bf16)
    earlier_t = lax.ppermute(keyval_group_t, "ctx", [(0, 1)])

    gated, states, state_final = forward_scan(
        mixed, selects, selects_t, aux, bias_row, rate_row, skip_row, state_start
    )
    mamba_part_t = dot(state_out_map, gated, 1, 1).astype(bf16)
    third = jnp.concatenate(
        [jnp.pad(piece, ((0, 0), (0, ff_wide - ff))) for piece in ffn_shards], axis=1
    )
    mamba_part_t, third, *cotangent_pieces = lax.optimization_barrier(
        (mamba_part_t, third, *cotangent_pieces)
    )
    third = gather_rows(third)
    up_map, down_map = cut(third, [2 * ff_wide, ff_wide])

    key_start = span + tp_index * rows - WIN
    keyval_t = jnp.concatenate(
        [
            meta_keyval_t,
            lax.dynamic_slice_in_dim(
                jnp.concatenate([earlier_t, keyval_group_t], axis=1), key_start, window, 1
            ),
        ],
        axis=1,
    )
    query_pos = ctx_index * span + tp_index * rows + jnp.arange(rows, dtype=jnp.int32)
    key_pos = (ctx_index - 1) * span + key_start + jnp.arange(window, dtype=jnp.int32)
    seg_query = lax.dynamic_slice_in_dim(seg_current, tp_index * rows, rows, 0)
    seg_keys = lax.dynamic_slice_in_dim(
        jnp.concatenate([seg_earlier, seg_current]), key_start, window, 0
    )
    keep = (
        (key_pos[:, None] <= query_pos[None, :])
        & (query_pos[None, :] - key_pos[:, None] < WIN)
        & (key_pos[:, None] >= 0)
        & (seg_keys[:, None] == seg_query[None, :])
    )
    bias = jnp.concatenate(
        [jnp.zeros((meta_count, rows), f32), jnp.where(keep, 0.0, masked_score)], axis=0
    )
    cotangent_group_t = in_order(cotangent_pieces)
    attended_t, log_total, mamba_out = attend(
        query_t, keyval_t, bias, mamba_part_t, heads, tp, 3
    )
    attn_out = dot(attn_map, attended_t, 1, 0)

    mid = residual + 0.5 * (rms_norm(attn_out, attn_gain) + rms_norm(mamba_out, mamba_gain))
    ffn_normed_t = rms_norm(mid, ffn_gain).astype(bf16)
    ffn_normed_group_t = line_gather(ffn_normed_t, tp, 1)

    gate_up = dot(up_map, ffn_normed_group_t, 0, 0)
    gate, up = gate_up[:ff_wide], gate_up[ff_wide:]
    sigma = jax.nn.sigmoid(gate)
    hidden_t = (gate * sigma * up).astype(bf16)
    hidden_grad = dot(down_map, cotangent_group_t, 0, 0)
    gate_up_grad_t = jnp.concatenate(
        [
            (hidden_grad * up * (sigma * (1.0 + gate * (1.0 - sigma)))).astype(bf16),
            (hidden_grad * gate * sigma).astype(bf16),
        ],
        axis=0,
    )
    ffn_grad_part_t = dot(up_map, gate_up_grad_t, 1, 0).astype(bf16)
    ffn_normed_grad_t = lax.psum_scatter(ffn_grad_part_t, "tp", scatter_dimension=1, tiled=True)
    up_wide = dot(ffn_normed_group_t, gate_up_grad_t, 1, 1).astype(bf16)
    down_wide = dot(cotangent_group_t, hidden_t, 1, 1).astype(bf16)
    ffn_wide = jnp.concatenate([up_wide, down_wide], axis=1)
    out_part_t = dot(down_map, hidden_t, 1, 0).astype(bf16)
    ffn_normed_grad_t, ffn_wide, out_part_t = lax.optimization_barrier(
        (ffn_normed_grad_t, ffn_wide, out_part_t)
    )
    ffn_columns = scatter_rows(ffn_wide)

    ffn_normed_grad = ffn_normed_grad_t.astype(f32)
    mid_extra, ffn_gain_terms = rms_back(mid, ffn_gain, ffn_normed_grad)
    mid_grad = cotangent_t.astype(f32) + mid_extra
    attn_grad, attn_gain_terms = rms_back(attn_out, attn_gain, 0.5 * mid_grad)
    mamba_grad, mamba_gain_terms = rms_back(mamba_out, mamba_gain, 0.5 * mid_grad)
    attn_grad_t = attn_grad.astype(bf16)
    mamba_grad_t = mamba_grad.astype(bf16)
    attended_grad_t = dot(attn_map, attn_grad_t, 0, 0).astype(bf16)
    query_grad_t, keyval_grad_t, mamba_grad_group_t = attend_back(
        query_t,
        keyval_t,
        bias,
        attended_t,
        log_total,
        attended_grad_t,
        mamba_grad_t,
        heads,
        tp,
        2,
    )
    query_pieces = permute_exchange(query_grad_t)
    keyval_grad_t = keyval_grad_t.reshape(keyval_width, meta_count + window)
    placed = lax.dynamic_update_slice_in_dim(
        jnp.zeros((keyval_width, 2 * span), bf16), keyval_grad_t[:, meta_count:], key_start, 1
    )
    earlier_back = lax.ppermute(placed[:, :span], "ctx", [(1, 0)])
    current = placed[:, span:].astype(f32) + earlier_back.astype(f32)
    keyval_part_t = current.astype(bf16)
    keyval_meta_t = keyval_grad_t[:, :meta_count]
    gated_grad = dot(mamba_grad_group_t, state_out_map, 0, 0)
    adjoint_end = end_adjoint(gated_grad, mixed, selects_t, aux, bias_row, rate_row)
    adjoint_end, late_attended_t, late_gated = lax.optimization_barrier(
        (adjoint_end, attended_t, gated)
    )
    adjoint_start = lax.ppermute(adjoint_end, "ctx", [(1, 0)])
    late_attended_t, late_gated, query_pieces = lax.optimization_barrier(
        (late_attended_t, late_gated, query_pieces)
    )
    meta_back, meta_terms = rms_back(meta_rows, mix_gain, dot(keyval_map, keyval_meta_t, 1, 0))
    query_columns_t = in_order(query_pieces)
    each = query_width // tp

    def room(count):
        return ((0, -count % 128), (0, 0))

    query_wide = dot(normed_group_t, jnp.pad(query_columns_t, room(each)), 1, 1)
    keyval_wide = dot(normed_group_t, keyval_part_t, 1, 1) + dot(
        meta_normed_t, keyval_meta_t, 1, 1
    )
    early_pieces = [
        dot(attn_grad_t, jnp.pad(late_attended_t, room(query_width)), 1, 1),
        query_wide,
        meta_back,
        keyval_wide,
        dot(mamba_grad_group_t, late_gated, 1, 0),
    ]
    early_wide = by_rows(
        jnp.concatenate([by_rows(piece.astype(bf16)) for piece in early_pieces], axis=1)
    )
    early_columns = scatter_rows(early_wide)
    adjoint_start, early_wide, ffn_columns = lax.optimization_barrier(
        (adjoint_start, early_wide, ffn_columns)
    )
    mix_grad, select_grad, scan_sums, out_total = backward_scan(
        gated_grad,
        mixed,
        selects,
        selects_t,
        states,
        aux,
        bias_row,
        rate_row,
        skip_row,
        adjoint_start,
        state_final,
        out_part_t,
        tp,
        5,
    )
    layer_out_t = (mid + out_total).astype(bf16)
    select_grad_t = select_grad.T.astype(bf16)
    query_term = dot(query_map, query_grad_t, 1, 0)
    normed_grad_part = (
        dot(state_map, mix_grad, 1, 1)
        + dot(select_map, select_grad_t, 1, 0)
        + dot(keyval_map, keyval_part_t, 1, 0)
    )
    _, group_terms = rms_back(residual_group, mix_gain, normed_grad_part)
    _, query_terms = rms_back(residual, mix_gain, query_term)
    normed_grad_low, mix_grad = lax.optimization_barrier(
        (normed_grad_part.astype(bf16), mix_grad)
    )
    state_wide = dot(normed_group_t, mix_grad, 1, 0)
    vector_columns = -(-3 * channels // shard)
    vectors = jnp.pad(scan_sums[:3].reshape(-1), (0, vector_columns * shard - 3 * channels))
    vectors = jnp.tile(vectors.reshape(shard, vector_columns), (width // shard, 1))
    tail = [
        dot(normed_group_t, select_grad_t, 1, 1),
        (jnp.sum(group_terms, 1) + jnp.sum(meta_terms, 1) + jnp.sum(query_terms, 1))[:, None],
        jnp.sum(attn_gain_terms, 1, keepdims=True),
        jnp.sum(mamba_gain_terms, 1, keepdims=True),
        jnp.sum(ffn_gain_terms, 1, keepdims=True),
        vectors,
    ]
    tail = jnp.concatenate([piece.astype(bf16) for piece in tail], axis=1)
    tail = jnp.pad(tail, ((0, 0), (0, -tail.shape[1] % 128)))
    last_wide = by_rows(
        jnp.concatenate([by_rows(tail), by_rows(state_wide.astype(bf16))], axis=1)
    )
    last_wide, early_columns = lax.optimization_barrier((last_wide, early_columns))
    last_columns = scatter_rows(last_wide)
    normed_grad_low, last_wide = lax.optimization_barrier((normed_grad_low, last_wide))
    normed_grad = line_sum(normed_grad_low, tp, 4) + query_term
    early_columns, ffn_columns, normed_grad = lax.optimization_barrier(
        (early_columns, ffn_columns, normed_grad)
    )
    residual_extra, _ = rms_back(residual, mix_gain, normed_grad)
    grad_tokens_t = (mid_grad + residual_extra).astype(bf16)
    grad_gate, grad_up, grad_ffn_output = [
        piece[:, :ff].astype(f32) for piece in cut(ffn_columns, [ff_wide] * 3)
    ]
    grad_ffn_input = jnp.stack([grad_gate, grad_up], axis=1)
    attn_shares, _, grad_query, _, meta_shares, keyval_shares, grad_mamba_output = cut(
        early_columns,
        [
            query_width,
            -query_width % 128,
            each,
            -each % 128,
            meta_count,
            keyval_width,
            channels,
        ],
    )

    def to_device(values):
        return jnp.swapaxes(values.reshape(shard, tp, values.shape[1] // tp), 0, 1)

    shares = jnp.concatenate(
        [to_device(attn_shares), to_device(keyval_shares), to_device(meta_shares)], axis=2
    )
    grad_attn_output, grad_keyval, grad_meta = cut(
        permute_sums(shares, 0)[0], [each, keyval_width // tp, meta_count // tp]
    )
    last_columns, grad_attn_output, grad_keyval, grad_meta, grad_tokens_t = lax.optimization_barrier(
        (last_columns, grad_attn_output, grad_keyval, grad_meta, grad_tokens_t)
    )
    select_shares, gain_shares, grad_vectors, _, grad_mamba_input = cut(
        last_columns,
        [
            2 * STATE,
            4,
            vector_columns,
            -(2 * STATE + 4 + vector_columns) % 128,
            3 * channels,
        ],
    )
    grad_mamba_output, grad_mamba_input, grad_query, grad_vectors = [
        v.astype(f32) for v in (grad_mamba_output, grad_mamba_input, grad_query, grad_vectors)
    ]
    shares = jnp.concatenate(
        [to_device(select_shares), jnp.broadcast_to(gain_shares[None], (tp, shard, 4))], axis=2
    )
    grad_select, grad_gains = cut(permute_sums(shares, 0)[0], [2 * STATE // tp, 4])
    grad_vectors = grad_vectors.reshape(-1)[: 3 * channels].reshape(3, channels)
    return (
        layer_out_t.T[None],
        grad_tokens_t.T[None],
        grad_meta,
        grad_gains[:, 0],
        grad_query,
        grad_keyval,
        grad_attn_output,
        grad_gains[:, 1],
        grad_mamba_input.reshape(shard, 3, channels),
        grad_select,
        grad_vectors[0],
        grad_vectors[1],
        grad_vectors[2],
        grad_mamba_output,
        grad_gains[:, 2],
        grad_gains[:, 3],
        grad_ffn_input,
        grad_ffn_output,
    )


def solution(mesh):
    rows = ("fsdp", "ctx")
    in_specs = (
        P("fsdp", ("ctx", "tp"), None),
        P("fsdp", None),
        P("fsdp", ("ctx", "tp"), None),
        P(rows, None),
        P(rows),
        P(rows, None),
        P(rows, None),
        P(rows, None),
        P(rows),
        P(rows, None, "tp"),
        P(rows, None),
        P("tp"),
        P("tp"),
        P("tp"),
        P(rows, "tp"),
        P(rows),
        P(rows),
        P(rows, None, None),
        P(rows, None),
    )
    out_specs = (
        P("fsdp", ("ctx", "tp"), None),
        P("fsdp", ("ctx", "tp"), None),
        P(rows, "tp"),
        P(rows),
        P(rows, "tp"),
        P(rows, "tp"),
        P(rows, "tp"),
        P(rows),
        P(rows, None, "tp"),
        P(rows, "tp"),
        P("tp"),
        P("tp"),
        P("tp"),
        P(rows, "tp"),
        P(rows),
        P(rows),
        P(rows, None, "tp"),
        P(rows, "tp"),
    )
    return jax.shard_map(
        per_device, mesh=mesh, in_specs=in_specs, out_specs=out_specs, check_vma=False
    )
```

```python
import functools

import jax
import jax.numpy as jnp
from jax import lax
from jax.experimental import pallas as pl
from jax.experimental.layout import Layout, with_layout_constraint
from jax.experimental.pallas import tpu as pltpu
from jax.sharding import PartitionSpec as P

HEAD_SIZE = 64
STATE = 16
WIN = 1024
SUB = 4
TILE = 128
HEAD = 128

bf16 = jnp.bfloat16
f32 = jnp.float32
epsilon = 1e-05
masked_score = -1e30


def mm(a, b):
    return lax.dot_general(a, b, (((1,), (0,)), ((), ())), preferred_element_type=f32)


def mm_nt(a, b):
    return lax.dot_general(a, b, (((1,), (1,)), ((), ())), preferred_element_type=f32)


def iota(shape, dim):
    return lax.broadcasted_iota(jnp.int32, shape, dim)


def split_mm(a, b):
    high = b.astype(bf16)
    return mm(a, high) + mm(a, (b - high.astype(f32)).astype(bf16))


def ones_where(cond):
    return jnp.where(cond, 1.0, 0.0)


def softplus(v):
    return jnp.maximum(v, 0.0) + jnp.log1p(jnp.exp(-jnp.abs(v)))


def group_mask(rows, columns, row_unit, column_unit):
    return iota((rows, columns), 0) // row_unit == iota((rows, columns), 1) // column_unit


def scan_tables():
    rows = 2 * TILE + TILE // SUB
    width = TILE // SUB * STATE
    row = iota((rows, TILE), 0)
    column = iota((rows, TILE), 1)
    token = row % TILE
    same = token // SUB == column // SUB
    upto = (row < TILE) & same & (column <= token)
    after = (row >= TILE) & (row < 2 * TILE) & same & (column > token)
    whole = (row >= 2 * TILE) & (row - 2 * TILE == column // SUB)
    places = iota((STATE, width), 0) == iota((STATE, width), 1) % STATE
    tables = (upto | after | whole, group_mask(width, TILE, STATE, SUB), places)
    sums, mask, places = [ones_where(table).astype(bf16) for table in tables]
    return sums, mask, mask.T, places, places.T


def part(mixed, k):
    channels = (mixed.shape[1] - HEAD) // 3
    return mixed[:, HEAD + k * channels : HEAD + (k + 1) * channels]


def both_ways(mixed):
    head = mixed[:, :HEAD]
    return head.astype(bf16), head.T.astype(bf16)


def decays(step_raw, bias_ref, rate_ref, alive_last_ref, sums_ref):
    raw = step_raw + bias_ref[...]
    step = softplus(raw)
    log_decay = -step * rate_ref[...]
    sums = split_mm(sums_ref[...], log_decay)
    upto = jnp.exp(sums[:TILE])
    after = sums[TILE : 2 * TILE]
    block = jnp.exp(sums[2 * TILE :]) * alive_last_ref[...]
    return raw, step, log_decay, upto, after, block


def in_blocks(values_t, factor_t, mask):
    kept = values_t * factor_t.astype(bf16)
    return jnp.concatenate([kept] * (TILE // SUB), axis=0) * mask[...]


def spread(values, factor, mask_t, places):
    return mm(values * factor.astype(bf16), places[...]).astype(bf16) * mask_t[...]


def fold(wide, factor, mask_t, places_t):
    return mm(wide.astype(bf16) * mask_t[...], places_t[...]) * factor


def pairs(aux_ref, aux_t_ref, lower):
    row, column = iota((TILE, TILE), 0), iota((TILE, TILE), 1)
    order = column <= row if lower else column >= row
    return (row // SUB == column // SUB) & order & (aux_ref[:, 2:3] == aux_t_ref[2:3, :])


def run_states(state, local_ref, block_ref, keep=None):
    def one(k, state):
        if keep is not None:
            keep[pl.ds(pl.multiple_of(k * STATE, STATE), STATE), :] = state.astype(bf16)
        return block_ref[pl.ds(k, 1), :] * state + local_ref[pl.ds(pl.multiple_of(k * STATE, STATE), STATE), :]

    return lax.fori_loop(0, TILE // SUB, one, state, unroll=8)


def end_state_kernel(
    mixed, aux, aux_t, alive_last, bias, rate, sums_table, mask, mask_t, places, places_t, end, state, local, block
):
    @pl.when(pl.program_id(0) == 0)
    def _():
        state[...] = jnp.zeros_like(state)

    _, maps_t = both_ways(mixed)
    raw, step, log_decay, upto, after, total = decays(
        part(mixed, 2), bias, rate, alive_last, sums_table
    )
    driven = (jnp.exp(after) * step * part(mixed, 0)).astype(bf16)
    local[...] = mm(in_blocks(maps_t[:STATE], aux_t[1:2, :], mask), driven)
    block[...] = total
    state[...] = run_states(state[...], local, block)
    end[...] = state[...]


def forward_kernel(
    mixed,
    aux,
    aux_t,
    alive_last,
    bias,
    rate,
    sums_table,
    mask,
    mask_t,
    places,
    places_t,
    skip,
    start,
    gated,
    states,
    end,
    state,
    local,
    block,
):
    @pl.when(pl.program_id(0) == 0)
    def _():
        state[...] = start[...]

    maps, maps_t = both_ways(mixed)
    raw, step, log_decay, upto, after, total = decays(
        part(mixed, 2), bias, rate, alive_last, sums_table
    )
    x = part(mixed, 0)
    driven = (jnp.exp(after) * step * x).astype(bf16)
    local[...] = mm(in_blocks(maps_t[:STATE], aux_t[1:2, :], mask), driven)
    block[...] = total
    state[...] = run_states(state[...], local, block, states)
    end[...] = state[...]
    out_part = maps[:, STATE : 2 * STATE]
    cross = jnp.where(pairs(aux, aux_t, True), mm(out_part, maps_t[:STATE]), 0.0).astype(bf16)
    y = (
        upto * mm(spread(out_part, aux[:, 0:1], mask_t, places), states[...])
        + jnp.exp(-after) * mm(cross, driven)
        + skip[...] * x
    )
    gates = part(mixed, 1)
    gated[...] = (y * gates * lax.logistic(gates)).astype(bf16)


def back_run(carry, local_ref, block_ref, keep, states=None, bound=None):
    count = TILE // SUB

    def one(i, carry):
        k = count - 1 - i
        rows = pl.ds(pl.multiple_of(k * STATE, STATE), STATE)
        if keep is not None:
            keep[rows, :] = carry[0].astype(bf16)
            bound[pl.ds(k, 1), :] = carry[1]
        new = block_ref[pl.ds(k, 1), :] * carry[0] + local_ref[rows, :]
        if keep is None:
            return (new, carry[1])
        return (new, jnp.sum(new * states[rows, :].astype(f32), axis=0, keepdims=True))

    return lax.fori_loop(0, count, one, carry, unroll=8)


def end_adjoint_kernel(
    count,
    gated_grad,
    mixed,
    aux,
    aux_t,
    alive_last,
    bias,
    rate,
    sums_table,
    mask,
    mask_t,
    places,
    places_t,
    source,
    end,
    total_out,
    state,
    local,
    block,
    own,
    sent,
    got,
    loads,
    send_sems,
    recv_sems,
):
    tile, tiles = pl.program_id(0), pl.num_programs(0)
    begin, step_line, finish = line_sum_steps(
        count, source, own, sent, got, total_out, loads, send_sems, recv_sems
    )

    @pl.when(tile == 0)
    def _():
        begin()
        state[...] = jnp.zeros_like(state)

    for k in range(1, count - 1):

        @pl.when(tile == tiles * k // (count - 1))
        def _():
            step_line(k)

    _, maps_t = both_ways(mixed)
    raw, step, log_decay, upto, after, total = decays(
        part(mixed, 2), bias, rate, alive_last, sums_table
    )
    gates = part(mixed, 1)
    dy = gated_grad[...] * gates * lax.logistic(gates)
    local[...] = mm(in_blocks(maps_t[STATE : 2 * STATE], aux_t[0:1, :], mask), (upto * dy).astype(bf16))
    block[...] = total
    state[...] = back_run((state[...], jnp.zeros((1, state.shape[1]), f32)), local, block, None)[0]
    end[...] = state[...]

    @pl.when(tile == tiles - 1)
    def _():
        step_line(count - 1)
        finish()


def backward_kernel(
    count,
    gated_grad,
    mixed,
    states,
    aux,
    aux_t,
    alive_last,
    bias,
    rate,
    sums_table,
    mask,
    mask_t,
    places,
    places_t,
    skip,
    start,
    final,
    source,
    mix_grad,
    sums,
    total_out,
    state,
    local,
    block,
    adjoint,
    bound,
    edge,
    own,
    sent,
    got,
    loads,
    send_sems,
    recv_sems,
):
    tile, tiles = pl.program_id(0), pl.num_programs(0)
    begin, step_line, finish = line_sum_steps(
        count, source, own, sent, got, total_out, loads, send_sems, recv_sems
    )

    @pl.when(tile == 0)
    def _():
        begin()
        state[...] = start[...]
        edge[...] = jnp.sum(start[...] * final[...], axis=0, keepdims=True)
        sums[...] = jnp.zeros_like(sums)

    for k in range(1, count - 1):

        @pl.when(tile == tiles * k // (count - 1))
        def _():
            step_line(k)

    maps, maps_t = both_ways(mixed)
    raw, step, log_decay, upto, after, total = decays(
        part(mixed, 2), bias, rate, alive_last, sums_table
    )
    channels = state.shape[1]
    x = part(mixed, 0)
    decay_after = jnp.exp(after)
    grow = jnp.exp(-after)
    driven = (decay_after * step * x).astype(bf16)
    in_part, out_part = maps[:, :STATE], maps[:, STATE : 2 * STATE]
    in_part_t, out_part_t = maps_t[:STATE], maps_t[STATE : 2 * STATE]
    lower, upper = pairs(aux, aux_t, True), pairs(aux, aux_t, False)
    cross = jnp.where(lower, mm(out_part, in_part_t), 0.0).astype(bf16)
    cross_t = jnp.where(upper, mm(in_part, out_part_t), 0.0).astype(bf16)
    y = upto * mm(spread(out_part, aux[:, 0:1], mask_t, places), states[...]) + grow * mm(cross, driven)
    gates = part(mixed, 1)
    sigma = lax.logistic(gates)
    grad = gated_grad[...]
    dy = grad * gates * sigma
    mix_grad[:, HEAD + channels : HEAD + 2 * channels] = (
        grad * (y + skip[...] * x) * (sigma * (1.0 + gates * (1.0 - sigma)))
    ).astype(bf16)
    dy_low = (upto * dy).astype(bf16)
    dy_grown = (grow * dy).astype(bf16)
    local[...] = mm(in_blocks(out_part_t, aux_t[0:1, :], mask), dy_low)
    block[...] = total
    new_state, new_edge = back_run((state[...], edge[...]), local, block, adjoint, states, bound)
    state[...] = new_state
    edge[...] = new_edge
    du = decay_after * (
        mm(spread(in_part, aux[:, 1:2], mask_t, places), adjoint[...]) + mm(cross_t, dy_grown)
    )
    out_grad = fold(mm_nt(dy_low, states[...]), aux[:, 0:1], mask_t, places_t)
    in_grad = fold(mm_nt(driven, adjoint[...]), aux[:, 1:2], mask_t, places_t)
    cross_grad = jnp.where(lower, mm_nt(dy_grown, driven), 0.0).astype(bf16)
    cross_grad_t = jnp.where(upper, mm_nt(driven, dy_grown), 0.0).astype(bf16)
    out_grad = out_grad + mm(cross_grad, in_part)
    in_grad = in_grad + mm(cross_grad_t, out_part)
    mix_grad[:, :HEAD] = jnp.concatenate(
        [in_grad, out_grad, jnp.zeros((TILE, HEAD - 2 * STATE), f32)], axis=1
    ).astype(bf16)
    flow = dy * y - step * x * du
    to_tokens = ones_where(group_mask(TILE, TILE // SUB, SUB, 1)) * aux[:, 1:2]
    decay_grad = aux[:, 3:4] * (
        mm(ones_where(upper).astype(bf16), flow.astype(bf16))
        + split_mm(to_tokens.astype(bf16), bound[...])
    )
    step_grad = (x * du - rate[...] * decay_grad) * lax.logistic(raw)
    mix_grad[:, HEAD : HEAD + channels] = (skip[...] * dy + step * du).astype(bf16)
    mix_grad[:, HEAD + 2 * channels :] = step_grad.astype(bf16)
    sums[0:1, :] += jnp.sum(step_grad, axis=0, keepdims=True)
    sums[1:2, :] += jnp.sum(decay_grad * log_decay, axis=0, keepdims=True)
    sums[2:3, :] += jnp.sum(dy * x, axis=0, keepdims=True)

    @pl.when(tile == tiles - 1)
    def _():
        step_line(count - 1)
        finish()


def scan_specs(tokens, channels, back):
    tiles = tokens // TILE
    at = (lambda i: tiles - 1 - i) if back else (lambda i: i)

    def fixed(*shape):
        return pl.BlockSpec(shape, lambda i: (0,) * len(shape))

    width = TILE // SUB * STATE
    mixed = pl.BlockSpec((TILE, HEAD + 3 * channels), lambda i: (at(i), 0))
    rows = pl.BlockSpec((TILE, channels), lambda i: (at(i), 0))
    states = pl.BlockSpec((width, channels), lambda i: (at(i), 0))
    side = [
        pl.BlockSpec((TILE, 8), lambda i: (at(i), 0)),
        pl.BlockSpec((8, TILE), lambda i: (0, at(i))),
        pl.BlockSpec((TILE // SUB, 1), lambda i: (at(i), 0)),
        fixed(1, channels),
        fixed(1, channels),
        fixed(2 * TILE + TILE // SUB, TILE),
        fixed(width, TILE),
        fixed(TILE, width),
        fixed(STATE, width),
        fixed(width, STATE),
    ]
    return tiles, mixed, rows, states, side, fixed(1, channels), fixed(STATE, channels)


def scan_scratch(channels):
    return [
        pltpu.VMEM((STATE, channels), f32),
        pltpu.VMEM((TILE // SUB * STATE, channels), f32),
        pltpu.VMEM((TILE // SUB, channels), f32),
    ]


def scan_call(kernel, name, tiles, in_specs, out_specs, out_shape, scratch, flops, collective=None):
    return pl.pallas_call(
        kernel,
        name=name,
        grid=(tiles,),
        in_specs=in_specs,
        out_specs=out_specs,
        scratch_shapes=scratch,
        out_shape=out_shape,
        compiler_params=pltpu.CompilerParams(
            vmem_limit_bytes=48 << 20,
            dimension_semantics=("arbitrary",),
            collective_id=collective,
            has_side_effects=collective is not None,
        ),
        cost_estimate=pl.CostEstimate(flops=flops, bytes_accessed=1 << 24, transcendentals=0),
    )


def scan_aux(segment, before):
    count = segment.shape[0]
    blocks = segment.reshape(count // SUB, SUB)
    ends = jnp.concatenate([before[None], blocks[:-1, -1]])
    alive = (blocks == ends[:, None]).reshape(-1).astype(f32)
    tail = (blocks == blocks[:, -1:]).reshape(-1).astype(f32)
    joined = (segment == jnp.concatenate([before[None], segment[:-1]])).astype(f32)
    zero = jnp.zeros_like(alive)
    aux_t = jnp.stack([alive, tail, segment.astype(f32), joined, zero, zero, zero, zero])
    last = (blocks[:, -1] == ends).astype(f32)[:, None]
    return aux_t.T, aux_t, last


def end_state(mixed, side):
    tokens, channels = mixed.shape[0], (mixed.shape[1] - HEAD) // 3
    tiles, mixed_s, rows, states, side_s, row, state = scan_specs(tokens, channels, False)
    return scan_call(
        end_state_kernel,
        "end_state",
        tiles,
        [mixed_s, *side_s],
        state,
        jax.ShapeDtypeStruct((STATE, channels), f32),
        scan_scratch(channels),
        10**10,
    )(mixed, *side)


def forward_scan(mixed, side, skip, start):
    tokens, channels = mixed.shape[0], (mixed.shape[1] - HEAD) // 3
    tiles, mixed_s, rows, states, side_s, row, state = scan_specs(tokens, channels, False)
    return scan_call(
        forward_kernel,
        "forward_scan",
        tiles,
        [mixed_s, *side_s, row, state],
        [rows, states, state],
        [
            jax.ShapeDtypeStruct((tokens, channels), bf16),
            jax.ShapeDtypeStruct((tokens // SUB * STATE, channels), bf16),
            jax.ShapeDtypeStruct((STATE, channels), f32),
        ],
        scan_scratch(channels),
        16 * 10**9,
    )(mixed, *side, skip, start)


def end_adjoint(gated_grad, mixed, side, source, count, collective):
    height, each = source.shape[0], source.shape[1] // count
    tokens, channels = mixed.shape[0], (mixed.shape[1] - HEAD) // 3
    tiles, mixed_s, rows, states, side_s, row, state = scan_specs(tokens, channels, True)
    return scan_call(
        functools.partial(end_adjoint_kernel, count),
        "end_adjoint",
        tiles,
        [rows, mixed_s, *side_s, pl.BlockSpec(memory_space=pl.ANY)],
        [state, pl.BlockSpec((height, each), lambda i: (0, 0))],
        [
            jax.ShapeDtypeStruct((STATE, channels), f32),
            jax.ShapeDtypeStruct((height, each), f32),
        ],
        scan_scratch(channels) + line_sum_scratch(count, height, each),
        10**10,
        collective,
    )(gated_grad, mixed, *side, source)


def backward_scan(gated_grad, mixed, states, side, skip, start, final, source, count, collective):
    height, each = source.shape[0], source.shape[1] // count
    tokens, channels = mixed.shape[0], (mixed.shape[1] - HEAD) // 3
    tiles, mixed_s, rows, states_s, side_s, row, state = scan_specs(tokens, channels, True)
    return scan_call(
        functools.partial(backward_kernel, count),
        "backward_scan",
        tiles,
        [
            rows,
            mixed_s,
            states_s,
            *side_s,
            row,
            state,
            state,
            pl.BlockSpec(memory_space=pl.ANY),
        ],
        [
            mixed_s,
            pl.BlockSpec((8, channels), lambda i: (0, 0)),
            pl.BlockSpec((height, each), lambda i: (0, 0)),
        ],
        [
            jax.ShapeDtypeStruct(mixed.shape, bf16),
            jax.ShapeDtypeStruct((8, channels), f32),
            jax.ShapeDtypeStruct((height, each), f32),
        ],
        scan_scratch(channels)
        + [
            pltpu.VMEM((TILE // SUB * STATE, channels), bf16),
            pltpu.VMEM((TILE // SUB, channels), f32),
            pltpu.VMEM((1, channels), f32),
        ]
        + line_sum_scratch(count, height, each),
        36 * 10**9,
        collective,
    )(gated_grad, mixed, states, *side, skip, start, final, source)


MESH = pl.DeviceIdType.MESH
COMM = {"has_side_effects": True}


def neighbour_barrier(count):
    place = lax.axis_index("tp")
    ready = pltpu.get_barrier_semaphore()
    sides = ((place < count - 1, place + 1), (place > 0, place - 1))
    for there, other in sides:

        @pl.when(there)
        def _():
            pl.semaphore_signal(ready, inc=1, device_id={"tp": other}, device_id_type=MESH)

    peers = jnp.where(place < count - 1, 1, 0) + jnp.where(place > 0, 1, 0)
    pl.semaphore_wait(ready, peers)


def line_steps(count, source, target, copies, send_sems, recv_sems):
    place = lax.axis_index("tp")
    width = source.shape[1]

    def at(owner):
        return target.at[:, pl.ds(pl.multiple_of(owner * width, width), width)]

    def local():
        return pltpu.make_async_copy(source, at(place), copies)

    def remote(side, step):
        owner = place - step if side == 0 else place + step
        return pltpu.make_async_remote_copy(
            src_ref=source if step == 0 else at(owner),
            dst_ref=at(owner),
            send_sem=send_sems.at[side, step],
            recv_sem=recv_sems.at[side, step],
            device_id={"tp": place + 1 if side == 0 else place - 1},
            device_id_type=MESH,
        )

    def has(side, step):
        return place - step >= 0 if side == 0 else place + step < count

    def neighbour(side):
        return place < count - 1 if side == 0 else place > 0

    def send(step):
        for side in (0, 1):

            @pl.when(neighbour(side) & has(side, step))
            def _():
                remote(side, step).start()

    def receive(step):
        for side in (0, 1):

            @pl.when(has(side, step + 1))
            def _():
                remote(side, step).wait_recv()

    def start():
        neighbour_barrier(count)
        local().start()
        send(0)

    def step(k):
        receive(k - 1)
        if k < count - 1:
            send(k)

    def finish():
        for k in range(count - 1):
            for side in (0, 1):

                @pl.when(neighbour(side) & has(side, k))
                def _():
                    remote(side, k).wait_send()

        local().wait()

    return start, step, finish


def line_scratch(count):
    return [
        pltpu.SemaphoreType.DMA,
        pltpu.SemaphoreType.DMA((2, count - 1)),
        pltpu.SemaphoreType.DMA((2, count - 1)),
    ]


def line_gather_kernel(count, source, target, copies, send_sems, recv_sems):
    start, step, finish = line_steps(count, source, target, copies, send_sems, recv_sems)
    start()
    for k in range(1, count):
        step(k)
    finish()


def line_gather(source, count, collective):
    return pl.pallas_call(
        functools.partial(line_gather_kernel, count),
        name="line_gather",
        in_specs=[pl.BlockSpec(memory_space=pl.ANY)],
        out_specs=pl.BlockSpec(memory_space=pl.ANY),
        out_shape=jax.ShapeDtypeStruct((source.shape[0], source.shape[1] * count), source.dtype),
        scratch_shapes=line_scratch(count),
        compiler_params=pltpu.CompilerParams(collective_id=collective, has_side_effects=True),
    )(source)


def line_sum_steps(count, source, own, sent, got, total, loads, send_sems, recv_sems):
    place = lax.axis_index("tp")
    width = total.shape[1]

    def whose(side, step):
        return place + (count - step) if side == 0 else place - (count - step)

    def sends(side, step):
        owner = whose(side, step)
        return owner < count if side == 0 else owner >= 0

    def receives(side, step):
        return (place >= 1) & (place <= step) if side == 0 else (place <= count - 2) & (place >= count - 1 - step)

    def load(side, step):
        owner = whose(side, step)
        return pltpu.make_async_copy(
            source.at[:, pl.ds(pl.multiple_of(owner * width, width), width)],
            sent.at[side, step - 1],
            loads.at[side, step - 1],
        )

    def mine():
        return pltpu.make_async_copy(
            source.at[:, pl.ds(pl.multiple_of(place * width, width), width)], own, loads.at[2, 0]
        )

    def remote(side, step):
        return pltpu.make_async_remote_copy(
            src_ref=sent.at[side, step - 1],
            dst_ref=got.at[side, step - 1],
            send_sem=send_sems.at[side, step - 1],
            recv_sem=recv_sems.at[side, step - 1],
            device_id={"tp": place + 1 if side == 0 else place - 1},
            device_id_type=MESH,
        )

    def start():
        neighbour_barrier(count)
        mine().start()
        for step in range(1, count):
            for side in (0, 1):

                @pl.when(sends(side, step))
                def _():
                    load(side, step).start()

        step_out(1)

    def step_out(step):
        for side in (0, 1):

            @pl.when(sends(side, step))
            def _():
                load(side, step).wait()

            if step > 1:

                @pl.when(sends(side, step) & receives(side, step - 1))
                def _():
                    sent[side, step - 1] = (
                        sent[side, step - 1].astype(f32) + got[side, step - 2].astype(f32)
                    ).astype(bf16)

            @pl.when(sends(side, step))
            def _():
                remote(side, step).start()

    def step(k):
        for side in (0, 1):

            @pl.when(receives(side, k))
            def _():
                remote(side, k).wait_recv()

        if k < count - 1:
            step_out(k + 1)

    def finish():
        mine().wait()
        total[...] = own[...].astype(f32)
        for side in (0, 1):

            @pl.when(receives(side, count - 1))
            def _():
                total[...] = total[...] + got[side, count - 2].astype(f32)

            for k in range(1, count):

                @pl.when(sends(side, k))
                def _():
                    remote(side, k).wait_send()

    return start, step, finish


def line_sum_scratch(count, height, width):
    return [
        pltpu.VMEM((height, width), bf16),
        pltpu.VMEM((2, count - 1, height, width), bf16),
        pltpu.VMEM((2, count - 1, height, width), bf16),
        pltpu.SemaphoreType.DMA((3, count - 1)),
        pltpu.SemaphoreType.DMA((2, count - 1)),
        pltpu.SemaphoreType.DMA((2, count - 1)),
    ]


def line_sum_kernel(count, source, total, own, sent, got, loads, send_sems, recv_sems):
    start, step, finish = line_sum_steps(
        count, source, own, sent, got, total, loads, send_sems, recv_sems
    )
    start()
    for k in range(1, count):
        step(k)
    finish()


def line_sum(source, count, collective):
    height, width = source.shape[0], source.shape[1] // count
    return pl.pallas_call(
        functools.partial(line_sum_kernel, count),
        name="line_sum",
        in_specs=[pl.BlockSpec(memory_space=pl.ANY)],
        out_specs=pl.BlockSpec(memory_space=pltpu.VMEM),
        out_shape=jax.ShapeDtypeStruct((height, width), f32),
        scratch_shapes=line_sum_scratch(count, height, width),
        compiler_params=pltpu.CompilerParams(
            vmem_limit_bytes=24 << 20, collective_id=collective, has_side_effects=True
        ),
    )(source)


def attend_kernel(
    group,
    count,
    query_t,
    key_t,
    value_t,
    bias,
    source,
    out_t,
    log_total,
    total_out,
    own,
    sent,
    got,
    loads,
    send_sems,
    recv_sems,
):
    head, heads = pl.program_id(0), pl.num_programs(0)
    start, step, finish = line_sum_steps(
        count, source, own, sent, got, total_out, loads, send_sems, recv_sems
    )

    @pl.when(head == 0)
    def _():
        start()

    @pl.when(head == heads - 2)
    def _():
        step(1)

    keys = key_t[...].T
    values_t = value_t[...]
    for g in range(group):
        at = slice(g * HEAD_SIZE, (g + 1) * HEAD_SIZE)
        scores = mm(keys, query_t[at, :] * 0.125) + bias[...]
        top = jnp.max(scores, axis=0, keepdims=True)
        probs = jnp.exp(scores - top)
        total = jnp.sum(probs, axis=0, keepdims=True)
        out_t[at, :] = (mm(values_t, probs.astype(bf16)) / total).astype(bf16)
        log_total[g : g + 1, :] = top + jnp.log(total)

    @pl.when(head == heads - 1)
    def _():
        for k in range(2, count):
            step(k)
        finish()


def attend_back_kernel(
    group,
    count,
    query_t,
    key_t,
    value_t,
    bias,
    out_t,
    log_total,
    grad_t,
    source,
    query_grad_t,
    keyval_grad_t,
    target,
    copies,
    send_sems,
    recv_sems,
):
    head, heads = pl.program_id(0), pl.num_programs(0)
    start, step, finish = line_steps(count, source, target, copies, send_sems, recv_sems)

    @pl.when(head == 0)
    def _():
        start()

    @pl.when(head == heads - 2)
    def _():
        step(1)

    keys_t = key_t[...]
    keys = keys_t.T
    values = value_t[...].T
    key_sum = jnp.zeros(keys_t.shape, f32)
    value_sum = jnp.zeros(keys_t.shape, f32)
    for g in range(group):
        at = slice(g * HEAD_SIZE, (g + 1) * HEAD_SIZE)
        query = query_t[at, :] * 0.125
        grad = grad_t[at, :]
        probs = jnp.exp(mm(keys, query) + bias[...] - log_total[g : g + 1, :])
        centre = jnp.sum(grad.astype(f32) * out_t[at, :].astype(f32), axis=0, keepdims=True)
        score_grad = (probs * (mm(values, grad) - centre)).astype(bf16)
        query_grad_t[at, :] = (mm(keys_t, score_grad) * 0.125).astype(bf16)
        key_sum = key_sum + mm_nt(query, score_grad)
        value_sum = value_sum + mm_nt(grad, probs.astype(bf16))
    keyval_grad_t[0] = key_sum.astype(bf16)
    keyval_grad_t[1] = value_sum.astype(bf16)

    @pl.when(head == heads - 1)
    def _():
        for k in range(2, count):
            step(k)
        finish()


def attend(query_t, keyval_t, bias, source, key_value_heads, count, collective):
    width, rows = query_t.shape
    keys = keyval_t.shape[1]
    group = width // HEAD_SIZE // key_value_heads
    kv = key_value_heads
    height, each = source.shape[0], source.shape[1] // count
    return pl.pallas_call(
        functools.partial(attend_kernel, group, count),
        name="attend",
        grid=(kv,),
        in_specs=[
            pl.BlockSpec((group * HEAD_SIZE, rows), lambda h: (h, 0)),
            pl.BlockSpec((HEAD_SIZE, keys), lambda h: (h, 0)),
            pl.BlockSpec((HEAD_SIZE, keys), lambda h: (h + kv, 0)),
            pl.BlockSpec((keys, rows), lambda h: (0, 0)),
            pl.BlockSpec(memory_space=pl.ANY),
        ],
        out_specs=[
            pl.BlockSpec((group * HEAD_SIZE, rows), lambda h: (h, 0)),
            pl.BlockSpec((None, 8, rows), lambda h: (h, 0, 0)),
            pl.BlockSpec((height, each), lambda h: (0, 0)),
        ],
        out_shape=[
            jax.ShapeDtypeStruct((width, rows), bf16),
            jax.ShapeDtypeStruct((kv, 8, rows), f32),
            jax.ShapeDtypeStruct((height, each), f32),
        ],
        scratch_shapes=line_sum_scratch(count, height, each),
        compiler_params=pltpu.CompilerParams(
            vmem_limit_bytes=56 << 20,
            dimension_semantics=("arbitrary",),
            collective_id=collective,
            has_side_effects=True,
        ),
    )(query_t, keyval_t, keyval_t, bias, source)


def attend_back(query_t, keyval_t, bias, out_t, log_total, grad_t, source, key_value_heads, count, collective):
    width, rows = query_t.shape
    keys = keyval_t.shape[1]
    group = width // HEAD_SIZE // key_value_heads
    kv = key_value_heads
    wide = pl.BlockSpec((group * HEAD_SIZE, rows), lambda h: (h, 0))
    head = pl.BlockSpec((HEAD_SIZE, keys), lambda h: (h, 0))
    anywhere = pl.BlockSpec(memory_space=pl.ANY)
    return pl.pallas_call(
        functools.partial(attend_back_kernel, group, count),
        name="attend_back",
        grid=(kv,),
        in_specs=[
            wide,
            head,
            pl.BlockSpec((HEAD_SIZE, keys), lambda h: (h + kv, 0)),
            pl.BlockSpec((keys, rows), lambda h: (0, 0)),
            wide,
            pl.BlockSpec((None, 8, rows), lambda h: (h, 0, 0)),
            wide,
            anywhere,
        ],
        out_specs=[wide, pl.BlockSpec((2, HEAD_SIZE, keys), lambda h: (0, h, 0)), anywhere],
        out_shape=[
            jax.ShapeDtypeStruct((width, rows), bf16),
            jax.ShapeDtypeStruct((2, kv * HEAD_SIZE, keys), bf16),
            jax.ShapeDtypeStruct((source.shape[0], source.shape[1] * count), source.dtype),
        ],
        scratch_shapes=line_scratch(count),
        compiler_params=pltpu.CompilerParams(
            vmem_limit_bytes=56 << 20,
            dimension_semantics=("arbitrary",),
            collective_id=collective,
            has_side_effects=True,
        ),
    )(query_t, keyval_t, keyval_t, bias, out_t, log_total, grad_t, source)


def rms_norm(values, gain):
    return values * lax.rsqrt(jnp.mean(values * values, axis=0, keepdims=True) + epsilon) * gain


def rms_back(values, gain, grad):
    scale = lax.rsqrt(jnp.mean(values * values, axis=0, keepdims=True) + epsilon)
    normal = values * scale
    weighted = grad * gain
    back = scale * (weighted - normal * jnp.mean(weighted * normal, axis=0, keepdims=True))
    return back, grad * normal


def dot(left, right, left_dim, right_dim):
    return lax.dot_general(
        left, right, (((left_dim,), (right_dim,)), ((), ())), preferred_element_type=f32
    )


def gather_rows(whole):
    return lax.all_gather(whole, ("fsdp", "ctx"), axis=0, tiled=True)


def by_rows(values):
    return with_layout_constraint(values, Layout((0, 1)))


def scatter_rows(whole):
    return by_rows(
        lax.psum_scatter(by_rows(whole), ("fsdp", "ctx"), scatter_dimension=0, tiled=True)
    )


def send(values, by):
    count = lax.axis_size("tp")
    return lax.ppermute(values, "tp", [(i, (i + by) % count) for i in range(count)])


def permute_gather(own):
    count = lax.axis_size("tp")
    return [own] + [send(own, k) for k in range(1, count)]


def in_order(pieces):
    count, place = lax.axis_size("tp"), lax.axis_index("tp")
    return jnp.concatenate(
        [lax.select_n(lax.rem(place - p + count, count), *pieces) for p in range(count)], axis=1
    )


def permute_sums(values, axis):
    count, place = lax.axis_size("tp"), lax.axis_index("tp")
    each = values.shape[axis] // count
    shares = [
        lax.dynamic_slice_in_dim(values, lax.rem(place + k, count) * each, each, axis)
        for k in range(count)
    ]
    total = shares[0].astype(f32)
    for k in (2, 1, 3):
        total = total + send(shares[k], k).astype(f32)
    return total


def permute_exchange(values):
    count, place = lax.axis_size("tp"), lax.axis_index("tp")
    shares = values.reshape(count, values.shape[0] // count, values.shape[1])
    pieces = [
        lax.dynamic_index_in_dim(shares, lax.rem(place + k, count), 0, False) for k in range(count)
    ]
    return [pieces[0]] + [send(pieces[k], k) for k in range(1, count)]


def cut(values, widths):
    pieces = []
    offset = 0
    for count in widths:
        pieces.append(values[:, offset : offset + count])
        offset = offset + count
    return pieces


def per_device(
    tokens,
    segments,
    cotangent,
    meta_tokens,
    gain_mix,
    query_weight,
    key_value_weight,
    attn_output,
    gain_attn,
    mamba_input,
    mamba_select,
    step_bias,
    decay_log,
    state_skip,
    mamba_output,
    gain_mamba,
    gain_ffn,
    ffn_input,
    ffn_output,
):
    tokens_t, segments, cotangent_t = tokens[0].T, segments[0], cotangent[0].T
    width, rows = tokens_t.shape
    shard = meta_tokens.shape[0]
    tp = lax.axis_size("tp")
    tp_index = lax.axis_index("tp")
    ctx_index = lax.axis_index("ctx")
    span = rows * tp
    query_width = query_weight.shape[1]
    keyval_width = key_value_weight.shape[1]
    heads = keyval_width // (2 * HEAD_SIZE)
    channels = mamba_input.shape[2]
    ff = ffn_input.shape[2] // tp
    ff_wide = -(-ff // 128) * 128
    meta_count = meta_tokens.shape[1]
    window = WIN + rows

    place_of = jnp.arange(HEAD, dtype=jnp.int32)[None]
    head = jnp.pad(mamba_select, ((0, 0), (0, HEAD - 2 * STATE)))
    for k, gain in enumerate((gain_mix, gain_attn, gain_mamba, gain_ffn)):
        head = jnp.where(place_of == 2 * STATE + k, gain[:, None], head)
    first = jnp.concatenate([head] + [mamba_input[:, k] for k in range(3)], axis=1)
    first, second_parts = lax.optimization_barrier(
        (first, (key_value_weight, meta_tokens, query_weight, mamba_output))
    )
    second = jnp.concatenate(second_parts, axis=1)
    first, second, tokens_t = lax.optimization_barrier((first, second, tokens_t))
    first = gather_rows(first)
    second = gather_rows(second)
    tokens_group_t = line_gather(tokens_t, tp, 0)
    late_cotangent_t, tokens_group_t = lax.optimization_barrier((cotangent_t, tokens_group_t))
    cotangent_pieces = permute_gather(late_cotangent_t)

    gain_columns = first[:, 2 * STATE : 2 * STATE + 4]
    keyval_map, meta_full, query_map, state_out_map = cut(
        second, [keyval_width, meta_count, query_width, channels]
    )
    attn_map = gather_rows(attn_output)
    gain_columns = gain_columns.astype(f32)
    mix_gain, attn_gain, mamba_gain, ffn_gain = [gain_columns[:, k : k + 1] for k in range(4)]

    residual = tokens_t.astype(f32)
    residual_group = tokens_group_t.astype(f32)
    normed_t = rms_norm(residual, mix_gain).astype(bf16)
    normed_group_t = rms_norm(residual_group, mix_gain).astype(bf16)
    meta_rows = meta_full.astype(f32)
    meta_normed_t = rms_norm(meta_rows, mix_gain).astype(bf16)

    mixed = dot(normed_group_t, first, 0, 0)
    seg_current = lax.dynamic_slice_in_dim(segments, ctx_index * span, span, 0)
    seg_earlier = lax.dynamic_slice_in_dim(segments, jnp.maximum(ctx_index - 1, 0) * span, span, 0)
    seg_before = jnp.where(
        ctx_index > 0,
        lax.dynamic_index_in_dim(segments, jnp.maximum(ctx_index * span - 1, 0), 0, False),
        -1,
    )
    side = (
        *scan_aux(seg_current, seg_before),
        step_bias[None],
        jnp.exp(decay_log)[None],
        *scan_tables(),
    )
    skip_row = state_skip[None]
    state_end = end_state(mixed, side)
    state_end, late_up, late_down = lax.optimization_barrier((state_end, ffn_input, ffn_output))
    ffn_shards = [
        lax.dynamic_slice_in_dim(whole, tp_index * ff, ff, 1)
        for whole in (late_up[:, 0], late_up[:, 1], late_down)
    ]
    state_start = lax.ppermute(state_end, "ctx", [(0, 1)])

    query_t = dot(query_map, normed_t, 0, 0).astype(bf16)
    keyval_group_t = dot(keyval_map, normed_group_t, 0, 0).astype(bf16)
    meta_keyval_t = dot(keyval_map, meta_normed_t, 0, 0).astype(bf16)
    earlier_t = lax.ppermute(keyval_group_t, "ctx", [(0, 1)])

    gated, states, state_final = forward_scan(mixed, side, skip_row, state_start)
    mamba_part_t = dot(state_out_map, gated, 1, 1).astype(bf16)
    third = jnp.concatenate(
        [jnp.pad(piece, ((0, 0), (0, ff_wide - ff))) for piece in ffn_shards], axis=1
    )
    mamba_part_t, third, *cotangent_pieces = lax.optimization_barrier(
        (mamba_part_t, third, *cotangent_pieces)
    )
    third = gather_rows(third)
    up_map, down_map = cut(third, [2 * ff_wide, ff_wide])

    key_start = span + tp_index * rows - WIN
    keyval_t = jnp.concatenate(
        [
            meta_keyval_t,
            lax.dynamic_slice_in_dim(
                jnp.concatenate([earlier_t, keyval_group_t], axis=1), key_start, window, 1
            ),
        ],
        axis=1,
    )
    query_pos = ctx_index * span + tp_index * rows + jnp.arange(rows, dtype=jnp.int32)
    key_pos = (ctx_index - 1) * span + key_start + jnp.arange(window, dtype=jnp.int32)
    seg_query = lax.dynamic_slice_in_dim(seg_current, tp_index * rows, rows, 0)
    seg_keys = lax.dynamic_slice_in_dim(
        jnp.concatenate([seg_earlier, seg_current]), key_start, window, 0
    )
    keep = (
        (key_pos[:, None] <= query_pos[None, :])
        & (query_pos[None, :] - key_pos[:, None] < WIN)
        & (key_pos[:, None] >= 0)
        & (seg_keys[:, None] == seg_query[None, :])
    )
    bias = jnp.concatenate(
        [jnp.zeros((meta_count, rows), f32), jnp.where(keep, 0.0, masked_score)], axis=0
    )
    cotangent_group_t = in_order(cotangent_pieces)
    attended_t, log_total, mamba_out = attend(
        query_t, keyval_t, bias, mamba_part_t, heads, tp, 3
    )
    attn_out = dot(attn_map, attended_t, 1, 0)

    mid = residual + 0.5 * (rms_norm(attn_out, attn_gain) + rms_norm(mamba_out, mamba_gain))
    ffn_normed_t = rms_norm(mid, ffn_gain).astype(bf16)
    ffn_normed_group_t = line_gather(ffn_normed_t, tp, 1)

    gate_up = dot(up_map, ffn_normed_group_t, 0, 0)
    gate, up = gate_up[:ff_wide], gate_up[ff_wide:]
    sigma = jax.nn.sigmoid(gate)
    hidden_t = (gate * sigma * up).astype(bf16)
    hidden_grad = dot(down_map, cotangent_group_t, 0, 0)
    gate_up_grad_t = jnp.concatenate(
        [
            (hidden_grad * up * (sigma * (1.0 + gate * (1.0 - sigma)))).astype(bf16),
            (hidden_grad * gate * sigma).astype(bf16),
        ],
        axis=0,
    )
    ffn_grad_part_t = dot(up_map, gate_up_grad_t, 1, 0).astype(bf16)
    ffn_normed_grad_t = lax.psum_scatter(ffn_grad_part_t, "tp", scatter_dimension=1, tiled=True)
    up_wide = dot(ffn_normed_group_t, gate_up_grad_t, 1, 1).astype(bf16)
    down_wide = dot(cotangent_group_t, hidden_t, 1, 1).astype(bf16)
    ffn_wide = jnp.concatenate([up_wide, down_wide], axis=1)
    fourth = width // 4 // 16 * 16
    out_parts = [
        dot(down_map[:fourth], hidden_t, 1, 0).astype(bf16),
        dot(down_map[fourth:], hidden_t, 1, 0).astype(bf16),
    ]
    ffn_normed_grad_t, ffn_wide, out_parts = lax.optimization_barrier(
        (ffn_normed_grad_t, ffn_wide, out_parts)
    )
    ffn_columns = scatter_rows(ffn_wide)

    ffn_normed_grad = ffn_normed_grad_t.astype(f32)
    mid_extra, ffn_gain_terms = rms_back(mid, ffn_gain, ffn_normed_grad)
    mid_grad = cotangent_t.astype(f32) + mid_extra
    attn_grad, attn_gain_terms = rms_back(attn_out, attn_gain, 0.5 * mid_grad)
    mamba_grad, mamba_gain_terms = rms_back(mamba_out, mamba_gain, 0.5 * mid_grad)
    attn_grad_t = attn_grad.astype(bf16)
    mamba_grad_t = mamba_grad.astype(bf16)
    attended_grad_t = dot(attn_map, attn_grad_t, 0, 0).astype(bf16)
    query_grad_t, keyval_grad_t, mamba_grad_group_t = attend_back(
        query_t,
        keyval_t,
        bias,
        attended_t,
        log_total,
        attended_grad_t,
        mamba_grad_t,
        heads,
        tp,
        2,
    )
    query_pieces = permute_exchange(query_grad_t)
    keyval_grad_t = keyval_grad_t.reshape(keyval_width, meta_count + window)
    placed = lax.dynamic_update_slice_in_dim(
        jnp.zeros((keyval_width, 2 * span), bf16), keyval_grad_t[:, meta_count:], key_start, 1
    )
    earlier_back = lax.ppermute(placed[:, :span], "ctx", [(1, 0)])
    current = placed[:, span:].astype(f32) + earlier_back.astype(f32)
    keyval_part_t = current.astype(bf16)
    keyval_meta_t = keyval_grad_t[:, :meta_count]
    gated_grad = dot(mamba_grad_group_t, state_out_map, 0, 0)
    adjoint_end, out_head = end_adjoint(gated_grad, mixed, side, out_parts[0], tp, 6)
    adjoint_end, late_attended_t, late_gated, query_pieces = lax.optimization_barrier(
        (adjoint_end, attended_t, gated, query_pieces)
    )
    adjoint_start = lax.ppermute(adjoint_end, "ctx", [(1, 0)])
    meta_back, meta_terms = rms_back(meta_rows, mix_gain, dot(keyval_map, keyval_meta_t, 1, 0))
    query_columns_t = in_order(query_pieces)
    each = query_width // tp

    def room(count):
        return ((0, -count % 128), (0, 0))

    query_wide = dot(normed_group_t, jnp.pad(query_columns_t, room(each)), 1, 1)
    keyval_wide = dot(normed_group_t, keyval_part_t, 1, 1) + dot(
        meta_normed_t, keyval_meta_t, 1, 1
    )
    early_pieces = [
        dot(attn_grad_t, jnp.pad(late_attended_t, room(query_width)), 1, 1),
        query_wide,
        meta_back,
        keyval_wide,
        dot(mamba_grad_group_t, late_gated, 1, 0),
    ]
    early_wide = by_rows(
        jnp.concatenate([by_rows(piece.astype(bf16)) for piece in early_pieces], axis=1)
    )
    early_columns = scatter_rows(early_wide)
    adjoint_start, early_wide, ffn_columns = lax.optimization_barrier(
        (adjoint_start, early_wide, ffn_columns)
    )
    mix_grad, scan_sums, out_rest = backward_scan(
        gated_grad,
        mixed,
        states,
        side,
        skip_row,
        adjoint_start,
        state_final,
        out_parts[1],
        tp,
        5,
    )
    layer_out_t = (mid + jnp.concatenate([out_head, out_rest], axis=0)).astype(bf16)
    query_term = dot(query_map, query_grad_t, 1, 0)
    normed_grad_part = dot(first, mix_grad, 1, 1) + dot(keyval_map, keyval_part_t, 1, 0)
    _, group_terms = rms_back(residual_group, mix_gain, normed_grad_part)
    _, query_terms = rms_back(residual, mix_gain, query_term)
    normed_grad_low, mix_grad = lax.optimization_barrier(
        (normed_grad_part.astype(bf16), mix_grad)
    )
    vector_columns = -(-3 * channels // shard)
    vectors = jnp.pad(scan_sums[:3].reshape(-1), (0, vector_columns * shard - 3 * channels))
    vectors = jnp.tile(vectors.reshape(shard, vector_columns), (width // shard, 1))
    tail = [
        (jnp.sum(group_terms, 1) + jnp.sum(meta_terms, 1) + jnp.sum(query_terms, 1))[:, None],
        jnp.sum(attn_gain_terms, 1, keepdims=True),
        jnp.sum(mamba_gain_terms, 1, keepdims=True),
        jnp.sum(ffn_gain_terms, 1, keepdims=True),
        vectors,
    ]
    tail = jnp.concatenate(tail, axis=1)
    tail = jnp.pad(tail, ((0, 0), (2 * STATE, first.shape[1] - 2 * STATE - tail.shape[1])))
    last_wide = by_rows((dot(normed_group_t, mix_grad, 1, 0) + tail).astype(bf16))
    last_wide, early_columns = lax.optimization_barrier((last_wide, early_columns))
    last_columns = scatter_rows(last_wide)
    normed_grad_low, last_wide = lax.optimization_barrier((normed_grad_low, last_wide))
    normed_grad = line_sum(normed_grad_low, tp, 4) + query_term
    early_columns, ffn_columns, normed_grad = lax.optimization_barrier(
        (early_columns, ffn_columns, normed_grad)
    )
    residual_extra, _ = rms_back(residual, mix_gain, normed_grad)
    grad_tokens_t = (mid_grad + residual_extra).astype(bf16)
    grad_gate, grad_up, grad_ffn_output = [
        piece[:, :ff].astype(f32) for piece in cut(ffn_columns, [ff_wide] * 3)
    ]
    grad_ffn_input = jnp.stack([grad_gate, grad_up], axis=1)
    attn_shares, _, grad_query, _, meta_shares, keyval_shares, grad_mamba_output = cut(
        early_columns,
        [
            query_width,
            -query_width % 128,
            each,
            -each % 128,
            meta_count,
            keyval_width,
            channels,
        ],
    )

    def to_device(values):
        return jnp.swapaxes(values.reshape(shard, tp, values.shape[1] // tp), 0, 1)

    shares = jnp.concatenate(
        [to_device(attn_shares), to_device(keyval_shares), to_device(meta_shares)], axis=2
    )
    grad_attn_output, grad_keyval, grad_meta = cut(
        permute_sums(shares, 0)[0], [each, keyval_width // tp, meta_count // tp]
    )
    select_shares, gain_shares, grad_vectors = cut(last_columns, [2 * STATE, 4, vector_columns])
    shares = jnp.concatenate(
        [to_device(select_shares), jnp.broadcast_to(gain_shares[None], (tp, shard, 4))], axis=2
    )
    grad_select, grad_gains = cut(permute_sums(shares, 0)[0], [2 * STATE // tp, 4])
    grad_mamba_input = jnp.stack(
        [
            last_columns[:, HEAD + k * channels : HEAD + (k + 1) * channels].astype(f32)
            for k in range(3)
        ],
        axis=1,
    )
    grad_mamba_output, grad_query, grad_vectors = [
        v.astype(f32) for v in (grad_mamba_output, grad_query, grad_vectors)
    ]
    grad_vectors = grad_vectors.reshape(-1)[: 3 * channels].reshape(3, channels)
    return (
        layer_out_t.T[None],
        grad_tokens_t.T[None],
        grad_meta,
        grad_gains[:, 0],
        grad_query,
        grad_keyval,
        grad_attn_output,
        grad_gains[:, 1],
        grad_mamba_input,
        grad_select,
        grad_vectors[0],
        grad_vectors[1],
        grad_vectors[2],
        grad_mamba_output,
        grad_gains[:, 2],
        grad_gains[:, 3],
        grad_ffn_input,
        grad_ffn_output,
    )


def solution(mesh):
    rows = ("fsdp", "ctx")
    in_specs = (
        P("fsdp", ("ctx", "tp"), None),
        P("fsdp", None),
        P("fsdp", ("ctx", "tp"), None),
        P(rows, None),
        P(rows),
        P(rows, None),
        P(rows, None),
        P(rows, None),
        P(rows),
        P(rows, None, "tp"),
        P(rows, None),
        P("tp"),
        P("tp"),
        P("tp"),
        P(rows, "tp"),
        P(rows),
        P(rows),
        P(rows, None, None),
        P(rows, None),
    )
    out_specs = (
        P("fsdp", ("ctx", "tp"), None),
        P("fsdp", ("ctx", "tp"), None),
        P(rows, "tp"),
        P(rows),
        P(rows, "tp"),
        P(rows, "tp"),
        P(rows, "tp"),
        P(rows),
        P(rows, None, "tp"),
        P(rows, "tp"),
        P("tp"),
        P("tp"),
        P("tp"),
        P(rows, "tp"),
        P(rows),
        P(rows),
        P(rows, None, "tp"),
        P(rows, "tp"),
    )
    return jax.shard_map(
        per_device, mesh=mesh, in_specs=in_specs, out_specs=out_specs, check_vma=False
    )
```

```python
import functools

import jax
import jax.numpy as jnp
from jax import lax
from jax.experimental import pallas as pl
from jax.experimental.layout import Layout, with_layout_constraint
from jax.experimental.pallas import tpu as pltpu
from jax.sharding import PartitionSpec as P

HEAD_SIZE = 64
STATE = 16
WIN = 1024
SUB = 4
TILE = 128
HEAD = 128

bf16 = jnp.bfloat16
f32 = jnp.float32
epsilon = 1e-05
masked_score = -1e30


def mm(a, b):
    return lax.dot_general(a, b, (((1,), (0,)), ((), ())), preferred_element_type=f32)


def mm_nt(a, b):
    return lax.dot_general(a, b, (((1,), (1,)), ((), ())), preferred_element_type=f32)


def iota(shape, dim):
    return lax.broadcasted_iota(jnp.int32, shape, dim)


def split_mm(a, b):
    high = b.astype(bf16)
    return mm(a, high) + mm(a, (b - high.astype(f32)).astype(bf16))


def ones_where(cond):
    return jnp.where(cond, 1.0, 0.0)


def softplus(v):
    return jnp.maximum(v, 0.0) + jnp.log1p(jnp.exp(-jnp.abs(v)))


def group_mask(rows, columns, row_unit, column_unit):
    return iota((rows, columns), 0) // row_unit == iota((rows, columns), 1) // column_unit


def scan_tables():
    rows = 2 * TILE + TILE // SUB
    width = TILE // SUB * STATE
    row = iota((rows, TILE), 0)
    column = iota((rows, TILE), 1)
    token = row % TILE
    same = token // SUB == column // SUB
    upto = (row < TILE) & same & (column <= token)
    after = (row >= TILE) & (row < 2 * TILE) & same & (column > token)
    whole = (row >= 2 * TILE) & (row - 2 * TILE == column // SUB)
    places = iota((STATE, width), 0) == iota((STATE, width), 1) % STATE
    tables = (upto | after | whole, group_mask(width, TILE, STATE, SUB), places)
    sums, mask, places = [ones_where(table).astype(bf16) for table in tables]
    return sums, mask, mask.T, places, places.T


def part(mixed, k):
    channels = (mixed.shape[1] - HEAD) // 3
    return mixed[:, HEAD + k * channels : HEAD + (k + 1) * channels]


def both_ways(mixed):
    head = mixed[:, :HEAD]
    return head.astype(bf16), head.T.astype(bf16)


def decays(step_raw, bias_ref, rate_ref, alive_last_ref, sums_ref):
    raw = step_raw + bias_ref[...]
    step = softplus(raw)
    log_decay = -step * rate_ref[...]
    sums = split_mm(sums_ref[...], log_decay)
    upto = jnp.exp(sums[:TILE])
    after = sums[TILE : 2 * TILE]
    block = jnp.exp(sums[2 * TILE :]) * alive_last_ref[...]
    return raw, step, log_decay, upto, after, block


def in_blocks(values_t, factor_t, mask):
    kept = values_t * factor_t.astype(bf16)
    return jnp.concatenate([kept] * (TILE // SUB), axis=0) * mask[...]


def spread(values, factor, mask_t, places):
    return mm(values * factor.astype(bf16), places[...]).astype(bf16) * mask_t[...]


def fold(wide, factor, mask_t, places_t):
    return mm(wide.astype(bf16) * mask_t[...], places_t[...]) * factor


def pairs(aux_ref, aux_t_ref, lower):
    row, column = iota((TILE, TILE), 0), iota((TILE, TILE), 1)
    order = column <= row if lower else column >= row
    return (row // SUB == column // SUB) & order & (aux_ref[:, 2:3] == aux_t_ref[2:3, :])


def run_states(state, local_ref, block_ref, keep=None):
    def one(k, state):
        if keep is not None:
            keep[pl.ds(pl.multiple_of(k * STATE, STATE), STATE), :] = state.astype(bf16)
        return block_ref[pl.ds(k, 1), :] * state + local_ref[pl.ds(pl.multiple_of(k * STATE, STATE), STATE), :]

    return lax.fori_loop(0, TILE // SUB, one, state, unroll=True)


def end_state_kernel(
    mixed, aux, aux_t, alive_last, bias, rate, sums_table, mask, mask_t, places, places_t, end, state, local, block
):
    @pl.when(pl.program_id(0) == 0)
    def _():
        state[...] = jnp.zeros_like(state)

    _, maps_t = both_ways(mixed)
    raw, step, log_decay, upto, after, total = decays(
        part(mixed, 2), bias, rate, alive_last, sums_table
    )
    driven = (jnp.exp(after) * step * part(mixed, 0)).astype(bf16)
    local[...] = mm(in_blocks(maps_t[:STATE], aux_t[1:2, :], mask), driven)
    block[...] = total
    state[...] = run_states(state[...], local, block)
    end[...] = state[...]


def forward_kernel(
    mixed,
    aux,
    aux_t,
    alive_last,
    bias,
    rate,
    sums_table,
    mask,
    mask_t,
    places,
    places_t,
    skip,
    start,
    gated,
    states,
    end,
    state,
    local,
    block,
):
    @pl.when(pl.program_id(0) == 0)
    def _():
        state[...] = start[...]

    maps, maps_t = both_ways(mixed)
    raw, step, log_decay, upto, after, total = decays(
        part(mixed, 2), bias, rate, alive_last, sums_table
    )
    x = part(mixed, 0)
    driven = (jnp.exp(after) * step * x).astype(bf16)
    local[...] = mm(in_blocks(maps_t[:STATE], aux_t[1:2, :], mask), driven)
    block[...] = total
    state[...] = run_states(state[...], local, block, states)
    end[...] = state[...]
    out_part = maps[:, STATE : 2 * STATE]
    cross = jnp.where(pairs(aux, aux_t, True), mm(out_part, maps_t[:STATE]), 0.0).astype(bf16)
    y = (
        upto * mm(spread(out_part, aux[:, 0:1], mask_t, places), states[...])
        + jnp.exp(-after) * mm(cross, driven)
        + skip[...] * x
    )
    gates = part(mixed, 1)
    gated[...] = (y * gates * lax.logistic(gates)).astype(bf16)


def back_run(carry, local_ref, block_ref, keep, states=None, bound=None):
    count = TILE // SUB

    def one(i, carry):
        k = count - 1 - i
        rows = pl.ds(pl.multiple_of(k * STATE, STATE), STATE)
        if keep is not None:
            keep[rows, :] = carry[0].astype(bf16)
            bound[pl.ds(k, 1), :] = carry[1]
        new = block_ref[pl.ds(k, 1), :] * carry[0] + local_ref[rows, :]
        if keep is None:
            return (new, carry[1])
        return (new, jnp.sum(new * states[rows, :].astype(f32), axis=0, keepdims=True))

    return lax.fori_loop(0, count, one, carry, unroll=True)


def end_adjoint_kernel(
    count,
    gated_grad,
    mixed,
    aux,
    aux_t,
    alive_last,
    bias,
    rate,
    sums_table,
    mask,
    mask_t,
    places,
    places_t,
    source,
    end,
    total_out,
    state,
    local,
    block,
    own,
    sent,
    got,
    loads,
    send_sems,
    recv_sems,
):
    tile, tiles = pl.program_id(0), pl.num_programs(0)
    begin, step_line, finish = line_sum_steps(
        count, source, own, sent, got, total_out, loads, send_sems, recv_sems
    )

    @pl.when(tile == 0)
    def _():
        begin()
        state[...] = jnp.zeros_like(state)

    for k in range(1, count - 1):

        @pl.when(tile == tiles * k // (count - 1))
        def _():
            step_line(k)

    _, maps_t = both_ways(mixed)
    raw, step, log_decay, upto, after, total = decays(
        part(mixed, 2), bias, rate, alive_last, sums_table
    )
    gates = part(mixed, 1)
    dy = gated_grad[...] * gates * lax.logistic(gates)
    local[...] = mm(in_blocks(maps_t[STATE : 2 * STATE], aux_t[0:1, :], mask), (upto * dy).astype(bf16))
    block[...] = total
    state[...] = back_run((state[...], jnp.zeros((1, state.shape[1]), f32)), local, block, None)[0]
    end[...] = state[...]

    @pl.when(tile == tiles - 1)
    def _():
        step_line(count - 1)
        finish()


def backward_kernel(
    count,
    gated_grad,
    mixed,
    states,
    aux,
    aux_t,
    alive_last,
    bias,
    rate,
    sums_table,
    mask,
    mask_t,
    places,
    places_t,
    skip,
    start,
    final,
    source,
    mix_grad,
    sums,
    total_out,
    state,
    local,
    block,
    adjoint,
    bound,
    edge,
    own,
    sent,
    got,
    loads,
    send_sems,
    recv_sems,
):
    tile, tiles = pl.program_id(0), pl.num_programs(0)
    begin, step_line, finish = line_sum_steps(
        count, source, own, sent, got, total_out, loads, send_sems, recv_sems
    )

    @pl.when(tile == 0)
    def _():
        begin()
        state[...] = start[...]
        edge[...] = jnp.sum(start[...] * final[...], axis=0, keepdims=True)
        sums[...] = jnp.zeros_like(sums)

    for k in range(1, count - 1):

        @pl.when(tile == tiles * k // (count - 1))
        def _():
            step_line(k)

    maps, maps_t = both_ways(mixed)
    raw, step, log_decay, upto, after, total = decays(
        part(mixed, 2), bias, rate, alive_last, sums_table
    )
    channels = state.shape[1]
    x = part(mixed, 0)
    decay_after = jnp.exp(after)
    grow = jnp.exp(-after)
    driven = (decay_after * step * x).astype(bf16)
    in_part, out_part = maps[:, :STATE], maps[:, STATE : 2 * STATE]
    in_part_t, out_part_t = maps_t[:STATE], maps_t[STATE : 2 * STATE]
    lower, upper = pairs(aux, aux_t, True), pairs(aux, aux_t, False)
    cross = jnp.where(lower, mm(out_part, in_part_t), 0.0).astype(bf16)
    cross_t = jnp.where(upper, mm(in_part, out_part_t), 0.0).astype(bf16)
    y = upto * mm(spread(out_part, aux[:, 0:1], mask_t, places), states[...]) + grow * mm(cross, driven)
    gates = part(mixed, 1)
    sigma = lax.logistic(gates)
    grad = gated_grad[...]
    dy = grad * gates * sigma
    mix_grad[:, HEAD + channels : HEAD + 2 * channels] = (
        grad * (y + skip[...] * x) * (sigma * (1.0 + gates * (1.0 - sigma)))
    ).astype(bf16)
    dy_low = (upto * dy).astype(bf16)
    dy_grown = (grow * dy).astype(bf16)
    local[...] = mm(in_blocks(out_part_t, aux_t[0:1, :], mask), dy_low)
    block[...] = total
    new_state, new_edge = back_run((state[...], edge[...]), local, block, adjoint, states, bound)
    state[...] = new_state
    edge[...] = new_edge
    du = decay_after * (
        mm(spread(in_part, aux[:, 1:2], mask_t, places), adjoint[...]) + mm(cross_t, dy_grown)
    )
    out_grad = fold(mm_nt(dy_low, states[...]), aux[:, 0:1], mask_t, places_t)
    in_grad = fold(mm_nt(driven, adjoint[...]), aux[:, 1:2], mask_t, places_t)
    cross_grad = jnp.where(lower, mm_nt(dy_grown, driven), 0.0).astype(bf16)
    cross_grad_t = jnp.where(upper, mm_nt(driven, dy_grown), 0.0).astype(bf16)
    out_grad = out_grad + mm(cross_grad, in_part)
    in_grad = in_grad + mm(cross_grad_t, out_part)
    mix_grad[:, :HEAD] = jnp.concatenate(
        [in_grad, out_grad, jnp.zeros((TILE, HEAD - 2 * STATE), f32)], axis=1
    ).astype(bf16)
    flow = dy * y - step * x * du
    to_tokens = ones_where(group_mask(TILE, TILE // SUB, SUB, 1)) * aux[:, 1:2]
    decay_grad = aux[:, 3:4] * (
        mm(ones_where(upper).astype(bf16), flow.astype(bf16))
        + split_mm(to_tokens.astype(bf16), bound[...])
    )
    step_grad = (x * du - rate[...] * decay_grad) * lax.logistic(raw)
    mix_grad[:, HEAD : HEAD + channels] = (skip[...] * dy + step * du).astype(bf16)
    mix_grad[:, HEAD + 2 * channels :] = step_grad.astype(bf16)
    sums[0:1, :] += jnp.sum(step_grad, axis=0, keepdims=True)
    sums[1:2, :] += jnp.sum(decay_grad * log_decay, axis=0, keepdims=True)
    sums[2:3, :] += jnp.sum(dy * x, axis=0, keepdims=True)

    @pl.when(tile == tiles - 1)
    def _():
        step_line(count - 1)
        finish()


def scan_specs(tokens, channels, back):
    tiles = tokens // TILE
    at = (lambda i: tiles - 1 - i) if back else (lambda i: i)

    def fixed(*shape):
        return pl.BlockSpec(shape, lambda i: (0,) * len(shape))

    width = TILE // SUB * STATE
    mixed = pl.BlockSpec((TILE, HEAD + 3 * channels), lambda i: (at(i), 0))
    rows = pl.BlockSpec((TILE, channels), lambda i: (at(i), 0))
    states = pl.BlockSpec((width, channels), lambda i: (at(i), 0))
    side = [
        pl.BlockSpec((TILE, 8), lambda i: (at(i), 0)),
        pl.BlockSpec((8, TILE), lambda i: (0, at(i))),
        pl.BlockSpec((TILE // SUB, 1), lambda i: (at(i), 0)),
        fixed(1, channels),
        fixed(1, channels),
        fixed(2 * TILE + TILE // SUB, TILE),
        fixed(width, TILE),
        fixed(TILE, width),
        fixed(STATE, width),
        fixed(width, STATE),
    ]
    return tiles, mixed, rows, states, side, fixed(1, channels), fixed(STATE, channels)


def scan_scratch(channels):
    return [
        pltpu.VMEM((STATE, channels), f32),
        pltpu.VMEM((TILE // SUB * STATE, channels), f32),
        pltpu.VMEM((TILE // SUB, channels), f32),
    ]


def scan_call(kernel, name, tiles, in_specs, out_specs, out_shape, scratch, flops, collective=None, room=16):
    return pl.pallas_call(
        kernel,
        name=name,
        grid=(tiles,),
        in_specs=in_specs,
        out_specs=out_specs,
        scratch_shapes=scratch,
        out_shape=out_shape,
        compiler_params=pltpu.CompilerParams(
            vmem_limit_bytes=room << 20,
            dimension_semantics=("arbitrary",),
            collective_id=collective,
            has_side_effects=collective is not None,
        ),
        cost_estimate=pl.CostEstimate(flops=flops, bytes_accessed=flops // 100, transcendentals=0),
    )


def scan_aux(segment, before):
    count = segment.shape[0]
    blocks = segment.reshape(count // SUB, SUB)
    ends = jnp.concatenate([before[None], blocks[:-1, -1]])
    alive = (blocks == ends[:, None]).reshape(-1).astype(f32)
    tail = (blocks == blocks[:, -1:]).reshape(-1).astype(f32)
    joined = (segment == jnp.concatenate([before[None], segment[:-1]])).astype(f32)
    zero = jnp.zeros_like(alive)
    aux_t = jnp.stack([alive, tail, segment.astype(f32), joined, zero, zero, zero, zero])
    last = (blocks[:, -1] == ends).astype(f32)[:, None]
    return aux_t.T, aux_t, last


def end_state(mixed, side):
    tokens, channels = mixed.shape[0], (mixed.shape[1] - HEAD) // 3
    tiles, mixed_s, rows, states, side_s, row, state = scan_specs(tokens, channels, False)
    return scan_call(
        end_state_kernel,
        "end_state",
        tiles,
        [mixed_s, *side_s],
        state,
        jax.ShapeDtypeStruct((STATE, channels), f32),
        scan_scratch(channels),
        10**7,
    )(mixed, *side)


def forward_scan(mixed, side, skip, start):
    tokens, channels = mixed.shape[0], (mixed.shape[1] - HEAD) // 3
    tiles, mixed_s, rows, states, side_s, row, state = scan_specs(tokens, channels, False)
    return scan_call(
        forward_kernel,
        "forward_scan",
        tiles,
        [mixed_s, *side_s, row, state],
        [rows, states, state],
        [
            jax.ShapeDtypeStruct((tokens, channels), bf16),
            jax.ShapeDtypeStruct((tokens // SUB * STATE, channels), bf16),
            jax.ShapeDtypeStruct((STATE, channels), f32),
        ],
        scan_scratch(channels),
        10**7,
    )(mixed, *side, skip, start)


def end_adjoint(gated_grad, mixed, side, source, count, collective):
    height, each = source.shape[0], source.shape[1] // count
    tokens, channels = mixed.shape[0], (mixed.shape[1] - HEAD) // 3
    tiles, mixed_s, rows, states, side_s, row, state = scan_specs(tokens, channels, True)
    return scan_call(
        functools.partial(end_adjoint_kernel, count),
        "end_adjoint",
        tiles,
        [rows, mixed_s, *side_s, pl.BlockSpec(memory_space=pl.ANY)],
        [state, pl.BlockSpec((height, each), lambda i: (0, 0))],
        [
            jax.ShapeDtypeStruct((STATE, channels), f32),
            jax.ShapeDtypeStruct((height, each), f32),
        ],
        scan_scratch(channels) + line_sum_scratch(count, height, each),
        10**10,
        collective,
        24,
    )(gated_grad, mixed, *side, source)


def backward_scan(gated_grad, mixed, states, side, skip, start, final, source, count, collective):
    height, each = source.shape[0], source.shape[1] // count
    tokens, channels = mixed.shape[0], (mixed.shape[1] - HEAD) // 3
    tiles, mixed_s, rows, states_s, side_s, row, state = scan_specs(tokens, channels, True)
    return scan_call(
        functools.partial(backward_kernel, count),
        "backward_scan",
        tiles,
        [
            rows,
            mixed_s,
            states_s,
            *side_s,
            row,
            state,
            state,
            pl.BlockSpec(memory_space=pl.ANY),
        ],
        [
            mixed_s,
            pl.BlockSpec((8, channels), lambda i: (0, 0)),
            pl.BlockSpec((height, each), lambda i: (0, 0)),
        ],
        [
            jax.ShapeDtypeStruct(mixed.shape, bf16),
            jax.ShapeDtypeStruct((8, channels), f32),
            jax.ShapeDtypeStruct((height, each), f32),
        ],
        scan_scratch(channels)
        + [
            pltpu.VMEM((TILE // SUB * STATE, channels), bf16),
            pltpu.VMEM((TILE // SUB, channels), f32),
            pltpu.VMEM((1, channels), f32),
        ]
        + line_sum_scratch(count, height, each),
        36 * 10**9,
        collective,
        48,
    )(gated_grad, mixed, states, *side, skip, start, final, source)


MESH = pl.DeviceIdType.MESH
COMM = {"has_side_effects": True}


def neighbour_barrier(count):
    place = lax.axis_index("tp")
    ready = pltpu.get_barrier_semaphore()
    sides = ((place < count - 1, place + 1), (place > 0, place - 1))
    for there, other in sides:

        @pl.when(there)
        def _():
            pl.semaphore_signal(ready, inc=1, device_id={"tp": other}, device_id_type=MESH)

    peers = jnp.where(place < count - 1, 1, 0) + jnp.where(place > 0, 1, 0)
    pl.semaphore_wait(ready, peers)


def line_steps(count, source, target, copies, send_sems, recv_sems):
    place = lax.axis_index("tp")
    width = source.shape[1]

    def at(owner):
        return target.at[:, pl.ds(pl.multiple_of(owner * width, width), width)]

    def local():
        return pltpu.make_async_copy(source, at(place), copies)

    def remote(side, step):
        owner = place - step if side == 0 else place + step
        return pltpu.make_async_remote_copy(
            src_ref=source if step == 0 else at(owner),
            dst_ref=at(owner),
            send_sem=send_sems.at[side, step],
            recv_sem=recv_sems.at[side, step],
            device_id={"tp": place + 1 if side == 0 else place - 1},
            device_id_type=MESH,
        )

    def has(side, step):
        return place - step >= 0 if side == 0 else place + step < count

    def neighbour(side):
        return place < count - 1 if side == 0 else place > 0

    def send(side, step):
        @pl.when(neighbour(side) & has(side, step))
        def _():
            remote(side, step).start()

    def receive(side, step):
        @pl.when(has(side, step + 1))
        def _():
            remote(side, step).wait_recv()

    def start():
        neighbour_barrier(count)
        local().start()
        for side in (0, 1):
            send(side, 0)

    def step(k):
        for side in (0, 1):
            receive(side, k - 1)
        for side in (0, 1):
            if k < count - 1:
                send(side, k)

    step.send, step.receive = send, receive

    def finish():
        for k in range(count - 1):
            for side in (0, 1):

                @pl.when(neighbour(side) & has(side, k))
                def _():
                    remote(side, k).wait_send()

        local().wait()

    return start, step, finish


def line_scratch(count):
    return [
        pltpu.SemaphoreType.DMA,
        pltpu.SemaphoreType.DMA((2, count - 1)),
        pltpu.SemaphoreType.DMA((2, count - 1)),
    ]


def line_gather_kernel(count, source, target, copies, send_sems, recv_sems):
    start, step, finish = line_steps(count, source, target, copies, send_sems, recv_sems)
    start()
    for k in range(1, count):
        step(k)
    finish()


def line_gather(source, count, collective):
    return pl.pallas_call(
        functools.partial(line_gather_kernel, count),
        name="line_gather",
        in_specs=[pl.BlockSpec(memory_space=pl.ANY)],
        out_specs=pl.BlockSpec(memory_space=pl.ANY),
        out_shape=jax.ShapeDtypeStruct((source.shape[0], source.shape[1] * count), source.dtype),
        scratch_shapes=line_scratch(count),
        compiler_params=pltpu.CompilerParams(collective_id=collective, has_side_effects=True),
    )(source)


def line_sum_steps(count, source, own, sent, got, total, loads, send_sems, recv_sems):
    place = lax.axis_index("tp")
    width = total.shape[1]

    def whose(side, step):
        return place + (count - step) if side == 0 else place - (count - step)

    def sends(side, step):
        owner = whose(side, step)
        return owner < count if side == 0 else owner >= 0

    def receives(side, step):
        return (place >= 1) & (place <= step) if side == 0 else (place <= count - 2) & (place >= count - 1 - step)

    def load(side, step):
        owner = whose(side, step)
        return pltpu.make_async_copy(
            source.at[:, pl.ds(pl.multiple_of(owner * width, width), width)],
            sent.at[side, step - 1],
            loads.at[side, step - 1],
        )

    def mine():
        return pltpu.make_async_copy(
            source.at[:, pl.ds(pl.multiple_of(place * width, width), width)], own, loads.at[2, 0]
        )

    def remote(side, step):
        return pltpu.make_async_remote_copy(
            src_ref=sent.at[side, step - 1],
            dst_ref=got.at[side, step - 1],
            send_sem=send_sems.at[side, step - 1],
            recv_sem=recv_sems.at[side, step - 1],
            device_id={"tp": place + 1 if side == 0 else place - 1},
            device_id_type=MESH,
        )

    def start():
        neighbour_barrier(count)
        mine().start()
        for step in range(1, count):
            for side in (0, 1):

                @pl.when(sends(side, step))
                def _():
                    load(side, step).start()

        step_out(1)

    def step_out(step):
        for side in (0, 1):

            @pl.when(sends(side, step))
            def _():
                load(side, step).wait()

            if step > 1:

                @pl.when(sends(side, step) & receives(side, step - 1))
                def _():
                    sent[side, step - 1] = (
                        sent[side, step - 1].astype(f32) + got[side, step - 2].astype(f32)
                    ).astype(bf16)

            @pl.when(sends(side, step))
            def _():
                remote(side, step).start()

    def step(k):
        for side in (0, 1):

            @pl.when(receives(side, k))
            def _():
                remote(side, k).wait_recv()

        if k < count - 1:
            step_out(k + 1)

    def finish():
        mine().wait()
        total[...] = own[...].astype(f32)
        for side in (0, 1):

            @pl.when(receives(side, count - 1))
            def _():
                total[...] = total[...] + got[side, count - 2].astype(f32)

            for k in range(1, count):

                @pl.when(sends(side, k))
                def _():
                    remote(side, k).wait_send()

    return start, step, finish


def line_sum_scratch(count, height, width):
    return [
        pltpu.VMEM((height, width), bf16),
        pltpu.VMEM((2, count - 1, height, width), bf16),
        pltpu.VMEM((2, count - 1, height, width), bf16),
        pltpu.SemaphoreType.DMA((3, count - 1)),
        pltpu.SemaphoreType.DMA((2, count - 1)),
        pltpu.SemaphoreType.DMA((2, count - 1)),
    ]


def line_sum_kernel(count, source, total, own, sent, got, loads, send_sems, recv_sems):
    start, step, finish = line_sum_steps(
        count, source, own, sent, got, total, loads, send_sems, recv_sems
    )
    start()
    for k in range(1, count):
        step(k)
    finish()


def line_sum(source, count, collective):
    height, width = source.shape[0], source.shape[1] // count
    return pl.pallas_call(
        functools.partial(line_sum_kernel, count),
        name="line_sum",
        in_specs=[pl.BlockSpec(memory_space=pl.ANY)],
        out_specs=pl.BlockSpec(memory_space=pltpu.VMEM),
        out_shape=jax.ShapeDtypeStruct((height, width), f32),
        scratch_shapes=line_sum_scratch(count, height, width),
        compiler_params=pltpu.CompilerParams(
            vmem_limit_bytes=24 << 20, collective_id=collective, has_side_effects=True
        ),
        cost_estimate=pl.CostEstimate(flops=5 * 10**10, bytes_accessed=1 << 24, transcendentals=0),
    )(source)


def feed_kernel(
    count,
    blocks,
    source,
    other,
    weights,
    group,
    gate_up_grad,
    hidden,
    part_sum,
    maps,
    tokens,
    grads,
    grad_rows,
    hidden_rows,
    partial,
    copies,
    loads,
    stores,
    send_sems,
    recv_sems,
):
    place = lax.axis_index("tp")
    start, step, finish = line_steps(count, source, group, copies, send_sems, recv_sems)
    receive, send = step.receive, step.send
    ff = hidden.shape[1]
    width = source.shape[1]
    near = jnp.minimum(place, count - 1 - place)

    def owner_of(q):
        spread_out = jnp.where(q % 2 == 1, place - (q + 1) // 2, place + q // 2)
        rest = jnp.where(place < count - 1 - place, q, count - 1 - q)
        return jnp.where(q <= 2 * near, spread_out, rest)

    def load(what, where, k):
        return pltpu.make_async_copy(what, where, loads.at[k])

    def columns(array, owner):
        return array.at[:, pl.ds(pl.multiple_of(owner * width, width), width)]

    def store(q):
        owner, slot = owner_of(q), q % 2
        at = pl.ds(pl.multiple_of(owner * width, width), width)
        return [
            pltpu.make_async_copy(grad_rows.at[slot], gate_up_grad.at[at, :], stores.at[slot, 0]),
            pltpu.make_async_copy(hidden_rows.at[slot], hidden.at[at, :], stores.at[slot, 1]),
            pltpu.make_async_copy(partial.at[slot], columns(part_sum, owner), stores.at[slot, 2]),
        ]

    start()
    load(other, grads, 2).start()
    load(weights.at[:, : 3 * ff], maps, 0).start()

    def one(q, carry):
        owner, slot = owner_of(q), q % 2
        for far in range(1, count):
            for side in (0, 1):
                here = place - far if side == 0 else place + far

                @pl.when((q > 0) & (owner == here))
                def _():
                    receive(side, far - 1)
                    if far < count - 1:
                        send(side, far)

        @pl.when(q == 0)
        def _():
            load(source, tokens, 1).start()
            load(source, tokens, 1).wait()

        @pl.when(q > 0)
        def _():
            load(columns(group, owner), tokens, 1).start()
            load(columns(group, owner), tokens, 1).wait()

        @pl.when(q == 0)
        def _():
            load(other, grads, 2).wait()
            load(weights.at[:, : 3 * ff], maps, 0).wait()

        @pl.when(q > 1)
        def _():
            for copy in store(q - 2):
                copy.wait()

        rows = tokens[...].T
        outs = columns(grads, owner)[...].T
        for begin, wide in blocks:
            gate = mm(rows, maps[:, begin : begin + wide])
            up = mm(rows, maps[:, ff + begin : ff + begin + wide])
            grad = mm(outs, maps[:, 2 * ff + begin : 2 * ff + begin + wide])
            sigma = lax.logistic(gate)
            active = gate * sigma
            hidden_rows[slot, :, begin : begin + wide] = (active * up).astype(bf16)
            grad_rows[slot, :, begin : begin + wide] = (
                grad * up * (sigma * (1.0 + gate * (1.0 - sigma)))
            ).astype(bf16)
            grad_rows[slot, :, ff + begin : ff + begin + wide] = (grad * active).astype(bf16)
        partial[slot] = mm_nt(maps[:, : 2 * ff], grad_rows[slot]).astype(bf16)
        for copy in store(q):
            copy.start()
        return carry

    lax.fori_loop(0, count, one, 0)
    for q in (count - 2, count - 1):
        for copy in store(q):
            copy.wait()
    finish()


def feed_forward(source, other, weights, ff, count, collective):
    depth, width = source.shape
    blocks = []
    begin = 0
    while begin < ff:
        blocks.append((begin, min(256, ff - begin)))
        begin = begin + 256
    anywhere = pl.BlockSpec(memory_space=pl.ANY)
    return pl.pallas_call(
        functools.partial(feed_kernel, count, tuple(blocks)),
        name="feed_forward",
        in_specs=[anywhere] * 3,
        out_specs=[anywhere] * 4,
        out_shape=[
            jax.ShapeDtypeStruct((depth, width * count), bf16),
            jax.ShapeDtypeStruct((width * count, 2 * ff), bf16),
            jax.ShapeDtypeStruct((width * count, ff), bf16),
            jax.ShapeDtypeStruct((depth, width * count), bf16),
        ],
        scratch_shapes=[
            pltpu.VMEM((depth, 3 * ff), bf16),
            pltpu.VMEM((depth, width), bf16),
            pltpu.VMEM((depth, width * count), bf16),
            pltpu.VMEM((2, width, 2 * ff), bf16),
            pltpu.VMEM((2, width, ff), bf16),
            pltpu.VMEM((2, depth, width), bf16),
            pltpu.SemaphoreType.DMA,
            pltpu.SemaphoreType.DMA((3,)),
            pltpu.SemaphoreType.DMA((2, 3)),
            pltpu.SemaphoreType.DMA((2, count - 1)),
            pltpu.SemaphoreType.DMA((2, count - 1)),
        ],
        compiler_params=pltpu.CompilerParams(
            vmem_limit_bytes=56 << 20, collective_id=collective, has_side_effects=True
        ),
    )(source, other, weights)


def attend_kernel(
    group,
    count,
    query_t,
    key_t,
    value_t,
    bias,
    source,
    out_t,
    log_total,
    total_out,
    own,
    sent,
    got,
    loads,
    send_sems,
    recv_sems,
):
    head, heads = pl.program_id(0), pl.num_programs(0)
    start, step, finish = line_sum_steps(
        count, source, own, sent, got, total_out, loads, send_sems, recv_sems
    )

    @pl.when(head == 0)
    def _():
        start()

    @pl.when(head == heads - 2)
    def _():
        step(1)

    keys = key_t[...].T
    values_t = value_t[...]
    for g in range(group):
        at = slice(g * HEAD_SIZE, (g + 1) * HEAD_SIZE)
        scores = mm(keys, query_t[at, :] * 0.125) + bias[...]
        top = jnp.max(scores, axis=0, keepdims=True)
        probs = jnp.exp(scores - top)
        total = jnp.sum(probs, axis=0, keepdims=True)
        out_t[at, :] = (mm(values_t, probs.astype(bf16)) / total).astype(bf16)
        log_total[g : g + 1, :] = top + jnp.log(total)

    @pl.when(head == heads - 1)
    def _():
        for k in range(2, count):
            step(k)
        finish()


def attend_back_kernel(
    group,
    count,
    query_t,
    key_t,
    value_t,
    bias,
    out_t,
    log_total,
    grad_t,
    source,
    query_grad_t,
    keyval_grad_t,
    target,
    copies,
    send_sems,
    recv_sems,
):
    head, heads = pl.program_id(0), pl.num_programs(0)
    start, step, finish = line_steps(count, source, target, copies, send_sems, recv_sems)

    @pl.when(head == 0)
    def _():
        start()

    @pl.when(head == heads - 2)
    def _():
        step(1)

    keys_t = key_t[...]
    keys = keys_t.T
    values = value_t[...].T
    key_sum = jnp.zeros(keys_t.shape, f32)
    value_sum = jnp.zeros(keys_t.shape, f32)
    for g in range(group):
        at = slice(g * HEAD_SIZE, (g + 1) * HEAD_SIZE)
        query = query_t[at, :] * 0.125
        grad = grad_t[at, :]
        probs = jnp.exp(mm(keys, query) + bias[...] - log_total[g : g + 1, :])
        centre = jnp.sum(grad.astype(f32) * out_t[at, :].astype(f32), axis=0, keepdims=True)
        score_grad = (probs * (mm(values, grad) - centre)).astype(bf16)
        query_grad_t[at, :] = (mm(keys_t, score_grad) * 0.125).astype(bf16)
        key_sum = key_sum + mm_nt(query, score_grad)
        value_sum = value_sum + mm_nt(grad, probs.astype(bf16))
    keyval_grad_t[0] = key_sum.astype(bf16)
    keyval_grad_t[1] = value_sum.astype(bf16)

    @pl.when(head == heads - 1)
    def _():
        for k in range(2, count):
            step(k)
        finish()


def attend(query_t, keyval_t, bias, source, key_value_heads, count, collective):
    width, rows = query_t.shape
    keys = keyval_t.shape[1]
    group = width // HEAD_SIZE // key_value_heads
    kv = key_value_heads
    height, each = source.shape[0], source.shape[1] // count
    return pl.pallas_call(
        functools.partial(attend_kernel, group, count),
        name="attend",
        grid=(kv,),
        in_specs=[
            pl.BlockSpec((group * HEAD_SIZE, rows), lambda h: (h, 0)),
            pl.BlockSpec((HEAD_SIZE, keys), lambda h: (h, 0)),
            pl.BlockSpec((HEAD_SIZE, keys), lambda h: (h + kv, 0)),
            pl.BlockSpec((keys, rows), lambda h: (0, 0)),
            pl.BlockSpec(memory_space=pl.ANY),
        ],
        out_specs=[
            pl.BlockSpec((group * HEAD_SIZE, rows), lambda h: (h, 0)),
            pl.BlockSpec((None, 8, rows), lambda h: (h, 0, 0)),
            pl.BlockSpec((height, each), lambda h: (0, 0)),
        ],
        out_shape=[
            jax.ShapeDtypeStruct((width, rows), bf16),
            jax.ShapeDtypeStruct((kv, 8, rows), f32),
            jax.ShapeDtypeStruct((height, each), f32),
        ],
        scratch_shapes=line_sum_scratch(count, height, each),
        compiler_params=pltpu.CompilerParams(
            vmem_limit_bytes=56 << 20,
            dimension_semantics=("arbitrary",),
            collective_id=collective,
            has_side_effects=True,
        ),
    )(query_t, keyval_t, keyval_t, bias, source)


def attend_back(query_t, keyval_t, bias, out_t, log_total, grad_t, source, key_value_heads, count, collective):
    width, rows = query_t.shape
    keys = keyval_t.shape[1]
    group = width // HEAD_SIZE // key_value_heads
    kv = key_value_heads
    wide = pl.BlockSpec((group * HEAD_SIZE, rows), lambda h: (h, 0))
    head = pl.BlockSpec((HEAD_SIZE, keys), lambda h: (h, 0))
    anywhere = pl.BlockSpec(memory_space=pl.ANY)
    return pl.pallas_call(
        functools.partial(attend_back_kernel, group, count),
        name="attend_back",
        grid=(kv,),
        in_specs=[
            wide,
            head,
            pl.BlockSpec((HEAD_SIZE, keys), lambda h: (h + kv, 0)),
            pl.BlockSpec((keys, rows), lambda h: (0, 0)),
            wide,
            pl.BlockSpec((None, 8, rows), lambda h: (h, 0, 0)),
            wide,
            anywhere,
        ],
        out_specs=[wide, pl.BlockSpec((2, HEAD_SIZE, keys), lambda h: (0, h, 0)), anywhere],
        out_shape=[
            jax.ShapeDtypeStruct((width, rows), bf16),
            jax.ShapeDtypeStruct((2, kv * HEAD_SIZE, keys), bf16),
            jax.ShapeDtypeStruct((source.shape[0], source.shape[1] * count), source.dtype),
        ],
        scratch_shapes=line_scratch(count),
        compiler_params=pltpu.CompilerParams(
            vmem_limit_bytes=56 << 20,
            dimension_semantics=("arbitrary",),
            collective_id=collective,
            has_side_effects=True,
        ),
    )(query_t, keyval_t, keyval_t, bias, out_t, log_total, grad_t, source)


def rms_norm(values, gain):
    return values * lax.rsqrt(jnp.mean(values * values, axis=0, keepdims=True) + epsilon) * gain


def rms_back(values, gain, grad):
    scale = lax.rsqrt(jnp.mean(values * values, axis=0, keepdims=True) + epsilon)
    normal = values * scale
    weighted = grad * gain
    back = scale * (weighted - normal * jnp.mean(weighted * normal, axis=0, keepdims=True))
    return back, grad * normal


def dot(left, right, left_dim, right_dim):
    return lax.dot_general(
        left, right, (((left_dim,), (right_dim,)), ((), ())), preferred_element_type=f32
    )


def gather_rows(whole):
    return lax.all_gather(whole, ("fsdp", "ctx"), axis=0, tiled=True)


def by_rows(values):
    return with_layout_constraint(values, Layout((0, 1)))


def scatter_rows(whole):
    return by_rows(
        lax.psum_scatter(by_rows(whole), ("fsdp", "ctx"), scatter_dimension=0, tiled=True)
    )


def send(values, by):
    count = lax.axis_size("tp")
    return lax.ppermute(values, "tp", [(i, (i + by) % count) for i in range(count)])


def permute_gather(own):
    count = lax.axis_size("tp")
    return [own] + [send(own, k) for k in range(1, count)]


def in_order(pieces):
    count, place = lax.axis_size("tp"), lax.axis_index("tp")
    return jnp.concatenate(
        [lax.select_n(lax.rem(place - p + count, count), *pieces) for p in range(count)], axis=1
    )


def permute_sums(values, axis):
    count, place = lax.axis_size("tp"), lax.axis_index("tp")
    each = values.shape[axis] // count
    shares = [
        lax.dynamic_slice_in_dim(values, lax.rem(place + k, count) * each, each, axis)
        for k in range(count)
    ]
    total = shares[0].astype(f32)
    for k in (2, 1, 3):
        total = total + send(shares[k], k).astype(f32)
    return total


def permute_exchange(values):
    count, place = lax.axis_size("tp"), lax.axis_index("tp")
    shares = values.reshape(count, values.shape[0] // count, values.shape[1])
    pieces = [
        lax.dynamic_index_in_dim(shares, lax.rem(place + k, count), 0, False) for k in range(count)
    ]
    return [pieces[0]] + [send(pieces[k], k) for k in range(1, count)]


def cut(values, widths):
    pieces = []
    offset = 0
    for count in widths:
        pieces.append(values[:, offset : offset + count])
        offset = offset + count
    return pieces


def per_device(
    tokens,
    segments,
    cotangent,
    meta_tokens,
    gain_mix,
    query_weight,
    key_value_weight,
    attn_output,
    gain_attn,
    mamba_input,
    mamba_select,
    step_bias,
    decay_log,
    state_skip,
    mamba_output,
    gain_mamba,
    gain_ffn,
    ffn_input,
    ffn_output,
):
    tokens_t, segments, cotangent_t = tokens[0].T, segments[0], cotangent[0].T
    width, rows = tokens_t.shape
    shard = meta_tokens.shape[0]
    tp = lax.axis_size("tp")
    tp_index = lax.axis_index("tp")
    ctx_index = lax.axis_index("ctx")
    span = rows * tp
    query_width = query_weight.shape[1]
    keyval_width = key_value_weight.shape[1]
    heads = keyval_width // (2 * HEAD_SIZE)
    channels = mamba_input.shape[2]
    ff = ffn_input.shape[2] // tp
    ff_wide = -(-ff // 128) * 128
    meta_count = meta_tokens.shape[1]
    window = WIN + rows

    place_of = jnp.arange(HEAD, dtype=jnp.int32)[None]
    head = jnp.pad(mamba_select, ((0, 0), (0, HEAD - 2 * STATE)))
    for k, gain in enumerate((gain_mix, gain_attn, gain_mamba, gain_ffn)):
        head = jnp.where(place_of == 2 * STATE + k, gain[:, None], head)
    first = jnp.concatenate([head] + [mamba_input[:, k] for k in range(3)], axis=1)
    first, second_parts = lax.optimization_barrier(
        (first, (key_value_weight, meta_tokens, query_weight, mamba_output))
    )
    second = jnp.concatenate(second_parts, axis=1)
    first, second, tokens_t = lax.optimization_barrier((first, second, tokens_t))
    first = gather_rows(first)
    second = gather_rows(second)
    tokens_group_t = line_gather(tokens_t, tp, 0)
    late_cotangent_t, tokens_group_t = lax.optimization_barrier((cotangent_t, tokens_group_t))
    cotangent_pieces = permute_gather(late_cotangent_t)

    gain_columns = first[:, 2 * STATE : 2 * STATE + 4]
    keyval_map, meta_full, query_map, state_out_map = cut(
        second, [keyval_width, meta_count, query_width, channels]
    )
    attn_map = gather_rows(attn_output)
    gain_columns = gain_columns.astype(f32)
    mix_gain, attn_gain, mamba_gain, ffn_gain = [gain_columns[:, k : k + 1] for k in range(4)]

    residual = tokens_t.astype(f32)
    residual_group = tokens_group_t.astype(f32)
    normed_t = rms_norm(residual, mix_gain).astype(bf16)
    normed_group_t = rms_norm(residual_group, mix_gain).astype(bf16)
    meta_rows = meta_full.astype(f32)
    meta_normed_t = rms_norm(meta_rows, mix_gain).astype(bf16)

    mixed = dot(normed_group_t, first, 0, 0)
    seg_current = lax.dynamic_slice_in_dim(segments, ctx_index * span, span, 0)
    seg_earlier = lax.dynamic_slice_in_dim(segments, jnp.maximum(ctx_index - 1, 0) * span, span, 0)
    seg_before = jnp.where(
        ctx_index > 0,
        lax.dynamic_index_in_dim(segments, jnp.maximum(ctx_index * span - 1, 0), 0, False),
        -1,
    )
    side = (
        *scan_aux(seg_current, seg_before),
        step_bias[None],
        jnp.exp(decay_log)[None],
        *scan_tables(),
    )
    skip_row = state_skip[None]
    state_end = end_state(mixed, side)
    state_end, late_up, late_down = lax.optimization_barrier((state_end, ffn_input, ffn_output))
    ffn_shards = [
        lax.dynamic_slice_in_dim(whole, tp_index * ff, ff, 1)
        for whole in (late_up[:, 0], late_up[:, 1], late_down)
    ]
    state_start = lax.ppermute(state_end, "ctx", [(0, 1)])

    query_t = dot(query_map, normed_t, 0, 0).astype(bf16)
    keyval_group_t = dot(keyval_map, normed_group_t, 0, 0).astype(bf16)
    meta_keyval_t = dot(keyval_map, meta_normed_t, 0, 0).astype(bf16)
    earlier_t = lax.ppermute(keyval_group_t, "ctx", [(0, 1)])

    gated, states, state_final = forward_scan(mixed, side, skip_row, state_start)
    third = jnp.concatenate(
        [jnp.pad(piece, ((0, 0), (0, ff_wide - ff))) for piece in ffn_shards] + [attn_output],
        axis=1,
    )
    third, gated, *cotangent_pieces = lax.optimization_barrier((third, gated, *cotangent_pieces))
    third = gather_rows(third)
    mamba_part_t = dot(state_out_map, gated, 1, 1).astype(bf16)
    up_map, down_map, attn_map = cut(third, [2 * ff_wide, ff_wide, query_width])

    key_start = span + tp_index * rows - WIN
    keyval_t = jnp.concatenate(
        [
            meta_keyval_t,
            lax.dynamic_slice_in_dim(
                jnp.concatenate([earlier_t, keyval_group_t], axis=1), key_start, window, 1
            ),
        ],
        axis=1,
    )
    query_pos = ctx_index * span + tp_index * rows + jnp.arange(rows, dtype=jnp.int32)
    key_pos = (ctx_index - 1) * span + key_start + jnp.arange(window, dtype=jnp.int32)
    seg_query = lax.dynamic_slice_in_dim(seg_current, tp_index * rows, rows, 0)
    seg_keys = lax.dynamic_slice_in_dim(
        jnp.concatenate([seg_earlier, seg_current]), key_start, window, 0
    )
    keep = (
        (key_pos[:, None] <= query_pos[None, :])
        & (query_pos[None, :] - key_pos[:, None] < WIN)
        & (key_pos[:, None] >= 0)
        & (seg_keys[:, None] == seg_query[None, :])
    )
    bias = jnp.concatenate(
        [jnp.zeros((meta_count, rows), f32), jnp.where(keep, 0.0, masked_score)], axis=0
    )
    cotangent_group_t = in_order(cotangent_pieces)
    attended_t, log_total, mamba_out = attend(
        query_t, keyval_t, bias, mamba_part_t, heads, tp, 3
    )
    attn_out = dot(attn_map, attended_t, 1, 0)

    mid = residual + 0.5 * (rms_norm(attn_out, attn_gain) + rms_norm(mamba_out, mamba_gain))
    ffn_normed_t = rms_norm(mid, ffn_gain).astype(bf16)
    ffn_normed_group_t, gate_up_grad, hidden, ffn_grad_part_t = feed_forward(
        ffn_normed_t, cotangent_group_t, third, ff_wide, tp, 1
    )
    ffn_normed_grad_t = lax.psum_scatter(ffn_grad_part_t, "tp", scatter_dimension=1, tiled=True)
    up_wide = dot(ffn_normed_group_t, gate_up_grad, 1, 0).astype(bf16)
    down_wide = dot(cotangent_group_t, hidden, 1, 0).astype(bf16)
    ffn_wide = jnp.concatenate([up_wide, down_wide], axis=1)
    fourth = width // 4 // 16 * 16
    out_parts = [
        dot(down_map[:fourth], hidden, 1, 1).astype(bf16),
        dot(down_map[fourth:], hidden, 1, 1).astype(bf16),
    ]
    ffn_normed_grad_t, ffn_wide, out_parts = lax.optimization_barrier(
        (ffn_normed_grad_t, ffn_wide, out_parts)
    )
    ffn_columns = scatter_rows(ffn_wide)

    ffn_normed_grad = ffn_normed_grad_t.astype(f32)
    mid_extra, ffn_gain_terms = rms_back(mid, ffn_gain, ffn_normed_grad)
    mid_grad = cotangent_t.astype(f32) + mid_extra
    attn_grad, attn_gain_terms = rms_back(attn_out, attn_gain, 0.5 * mid_grad)
    mamba_grad, mamba_gain_terms = rms_back(mamba_out, mamba_gain, 0.5 * mid_grad)
    attn_grad_t = attn_grad.astype(bf16)
    mamba_grad_t = mamba_grad.astype(bf16)
    attended_grad_t = dot(attn_map, attn_grad_t, 0, 0).astype(bf16)
    query_grad_t, keyval_grad_t, mamba_grad_group_t = attend_back(
        query_t,
        keyval_t,
        bias,
        attended_t,
        log_total,
        attended_grad_t,
        mamba_grad_t,
        heads,
        tp,
        2,
    )
    query_pieces = permute_exchange(query_grad_t)
    keyval_grad_t = keyval_grad_t.reshape(keyval_width, meta_count + window)
    placed = lax.dynamic_update_slice_in_dim(
        jnp.zeros((keyval_width, 2 * span), bf16), keyval_grad_t[:, meta_count:], key_start, 1
    )
    earlier_back = lax.ppermute(placed[:, :span], "ctx", [(1, 0)])
    current = placed[:, span:].astype(f32) + earlier_back.astype(f32)
    keyval_part_t = current.astype(bf16)
    keyval_meta_t = keyval_grad_t[:, :meta_count]
    gated_grad = dot(mamba_grad_group_t, state_out_map, 0, 0)
    adjoint_end, out_head = end_adjoint(gated_grad, mixed, side, out_parts[0], tp, 6)
    adjoint_end, late_attended_t, late_gated, query_pieces = lax.optimization_barrier(
        (adjoint_end, attended_t, gated, query_pieces)
    )
    adjoint_start = lax.ppermute(adjoint_end, "ctx", [(1, 0)])
    meta_back, meta_terms = rms_back(meta_rows, mix_gain, dot(keyval_map, keyval_meta_t, 1, 0))
    query_columns_t = in_order(query_pieces)
    each = query_width // tp

    def room(count):
        return ((0, -count % 128), (0, 0))

    query_wide = dot(normed_group_t, jnp.pad(query_columns_t, room(each)), 1, 1)
    keyval_wide = dot(normed_group_t, keyval_part_t, 1, 1) + dot(
        meta_normed_t, keyval_meta_t, 1, 1
    )
    early_pieces = [
        dot(attn_grad_t, jnp.pad(late_attended_t, room(query_width)), 1, 1),
        query_wide,
        meta_back,
        keyval_wide,
        dot(mamba_grad_group_t, late_gated, 1, 0),
    ]
    early_wide = by_rows(
        jnp.concatenate([by_rows(piece.astype(bf16)) for piece in early_pieces], axis=1)
    )
    early_columns = scatter_rows(early_wide)
    adjoint_start, early_wide, ffn_columns = lax.optimization_barrier(
        (adjoint_start, early_wide, ffn_columns)
    )
    mix_grad, scan_sums, out_rest = backward_scan(
        gated_grad,
        mixed,
        states,
        side,
        skip_row,
        adjoint_start,
        state_final,
        out_parts[1],
        tp,
        5,
    )
    layer_out_t = (mid + jnp.concatenate([out_head, out_rest], axis=0)).astype(bf16)
    query_term = dot(query_map, query_grad_t, 1, 0)
    normed_grad_part = dot(first, mix_grad, 1, 1) + dot(keyval_map, keyval_part_t, 1, 0)
    _, group_terms = rms_back(residual_group, mix_gain, normed_grad_part)
    _, query_terms = rms_back(residual, mix_gain, query_term)
    normed_grad_low, mix_grad = lax.optimization_barrier(
        (normed_grad_part.astype(bf16), mix_grad)
    )
    vector_columns = -(-3 * channels // shard)
    vectors = jnp.pad(scan_sums[:3].reshape(-1), (0, vector_columns * shard - 3 * channels))
    vectors = jnp.tile(vectors.reshape(shard, vector_columns), (width // shard, 1))
    tail = [
        (jnp.sum(group_terms, 1) + jnp.sum(meta_terms, 1) + jnp.sum(query_terms, 1))[:, None],
        jnp.sum(attn_gain_terms, 1, keepdims=True),
        jnp.sum(mamba_gain_terms, 1, keepdims=True),
        jnp.sum(ffn_gain_terms, 1, keepdims=True),
        vectors,
    ]
    tail = jnp.concatenate(tail, axis=1)
    tail = jnp.pad(tail, ((0, 0), (2 * STATE, first.shape[1] - 2 * STATE - tail.shape[1])))
    last_wide = by_rows((dot(normed_group_t, mix_grad, 1, 0) + tail).astype(bf16))
    last_wide, early_columns = lax.optimization_barrier((last_wide, early_columns))
    last_columns = scatter_rows(last_wide)
    attn_shares, _, grad_query, _, meta_shares, keyval_shares, grad_mamba_output = cut(
        early_columns,
        [
            query_width,
            -query_width % 128,
            each,
            -each % 128,
            meta_count,
            keyval_width,
            channels,
        ],
    )

    def to_device(values):
        return jnp.swapaxes(values.reshape(shard, tp, values.shape[1] // tp), 0, 1)

    shares = jnp.concatenate(
        [to_device(attn_shares), to_device(keyval_shares), to_device(meta_shares)], axis=2
    )
    normed_grad_low, last_wide, shares = lax.optimization_barrier(
        (normed_grad_low, last_wide, shares)
    )
    grad_attn_output, grad_keyval, grad_meta = cut(
        permute_sums(shares, 0)[0], [each, keyval_width // tp, meta_count // tp]
    )
    normed_grad = line_sum(normed_grad_low, tp, 4) + query_term
    ffn_columns, normed_grad = lax.optimization_barrier((ffn_columns, normed_grad))
    residual_extra, _ = rms_back(residual, mix_gain, normed_grad)
    grad_tokens_t = (mid_grad + residual_extra).astype(bf16)
    grad_gate, grad_up, grad_ffn_output = [
        piece[:, :ff].astype(f32) for piece in cut(ffn_columns, [ff_wide] * 3)
    ]
    grad_ffn_input = jnp.stack([grad_gate, grad_up], axis=1)
    select_shares, gain_shares, grad_vectors = cut(last_columns, [2 * STATE, 4, vector_columns])
    shares = jnp.concatenate(
        [to_device(select_shares), jnp.broadcast_to(gain_shares[None], (tp, shard, 4))], axis=2
    )
    grad_select, grad_gains = cut(permute_sums(shares, 0)[0], [2 * STATE // tp, 4])
    grad_mamba_input = jnp.stack(
        [
            last_columns[:, HEAD + k * channels : HEAD + (k + 1) * channels].astype(f32)
            for k in range(3)
        ],
        axis=1,
    )
    grad_mamba_output, grad_query, grad_vectors = [
        v.astype(f32) for v in (grad_mamba_output, grad_query, grad_vectors)
    ]
    grad_vectors = grad_vectors.reshape(-1)[: 3 * channels].reshape(3, channels)
    return (
        layer_out_t.T[None],
        grad_tokens_t.T[None],
        grad_meta,
        grad_gains[:, 0],
        grad_query,
        grad_keyval,
        grad_attn_output,
        grad_gains[:, 1],
        grad_mamba_input,
        grad_select,
        grad_vectors[0],
        grad_vectors[1],
        grad_vectors[2],
        grad_mamba_output,
        grad_gains[:, 2],
        grad_gains[:, 3],
        grad_ffn_input,
        grad_ffn_output,
    )


def solution(mesh):
    rows = ("fsdp", "ctx")
    in_specs = (
        P("fsdp", ("ctx", "tp"), None),
        P("fsdp", None),
        P("fsdp", ("ctx", "tp"), None),
        P(rows, None),
        P(rows),
        P(rows, None),
        P(rows, None),
        P(rows, None),
        P(rows),
        P(rows, None, "tp"),
        P(rows, None),
        P("tp"),
        P("tp"),
        P("tp"),
        P(rows, "tp"),
        P(rows),
        P(rows),
        P(rows, None, None),
        P(rows, None),
    )
    out_specs = (
        P("fsdp", ("ctx", "tp"), None),
        P("fsdp", ("ctx", "tp"), None),
        P(rows, "tp"),
        P(rows),
        P(rows, "tp"),
        P(rows, "tp"),
        P(rows, "tp"),
        P(rows),
        P(rows, None, "tp"),
        P(rows, "tp"),
        P("tp"),
        P("tp"),
        P("tp"),
        P(rows, "tp"),
        P(rows),
        P(rows),
        P(rows, None, "tp"),
        P(rows, "tp"),
    )
    return jax.shard_map(
        per_device, mesh=mesh, in_specs=in_specs, out_specs=out_specs, check_vma=False
    )
```

```python
import functools

import jax
import jax.numpy as jnp
from jax import lax
from jax.experimental import pallas as pl
from jax.experimental.layout import Layout, with_layout_constraint
from jax.experimental.pallas import tpu as pltpu
from jax.sharding import PartitionSpec as P

HEAD_SIZE = 64
STATE = 16
WIN = 1024
SUB = 4
TILE = 128
HEAD = 128

bf16 = jnp.bfloat16
f32 = jnp.float32
epsilon = 1e-05
masked_score = -1e30


def mm(a, b):
    return lax.dot_general(a, b, (((1,), (0,)), ((), ())), preferred_element_type=f32)


def mm_nt(a, b):
    return lax.dot_general(a, b, (((1,), (1,)), ((), ())), preferred_element_type=f32)


def iota(shape, dim):
    return lax.broadcasted_iota(jnp.int32, shape, dim)


def split_mm(a, b):
    high = b.astype(bf16)
    return mm(a, high) + mm(a, (b - high.astype(f32)).astype(bf16))


def ones_where(cond):
    return jnp.where(cond, 1.0, 0.0)


def softplus(v):
    return jnp.maximum(v, 0.0) + jnp.log1p(jnp.exp(-jnp.abs(v)))


def group_mask(rows, columns, row_unit, column_unit):
    return iota((rows, columns), 0) // row_unit == iota((rows, columns), 1) // column_unit


def scan_tables():
    rows = 2 * TILE + TILE // SUB
    width = TILE // SUB * STATE
    row = iota((rows, TILE), 0)
    column = iota((rows, TILE), 1)
    token = row % TILE
    same = token // SUB == column // SUB
    upto = (row < TILE) & same & (column <= token)
    after = (row >= TILE) & (row < 2 * TILE) & same & (column > token)
    whole = (row >= 2 * TILE) & (row - 2 * TILE == column // SUB)
    places = iota((STATE, width), 0) == iota((STATE, width), 1) % STATE
    tables = (upto | after | whole, group_mask(width, TILE, STATE, SUB), places)
    sums, mask, places = [ones_where(table).astype(bf16) for table in tables]
    return sums, mask, mask.T, places, places.T


def part(mixed, k):
    channels = (mixed.shape[1] - HEAD) // 3
    return mixed[:, HEAD + k * channels : HEAD + (k + 1) * channels]


def both_ways(mixed):
    head = mixed[:, :HEAD]
    return head.astype(bf16), head.T.astype(bf16)


def decays(step_raw, bias_ref, rate_ref, alive_last_ref, sums_ref):
    raw = step_raw + bias_ref[...]
    step = softplus(raw)
    log_decay = -step * rate_ref[...]
    sums = split_mm(sums_ref[...], log_decay)
    upto = jnp.exp(sums[:TILE])
    after = sums[TILE : 2 * TILE]
    block = jnp.exp(sums[2 * TILE :]) * alive_last_ref[...]
    return raw, step, log_decay, upto, after, block


def in_blocks(values_t, factor_t, mask):
    kept = values_t * factor_t.astype(bf16)
    return jnp.concatenate([kept] * (TILE // SUB), axis=0) * mask[...]


def spread(values, factor, mask_t, places):
    return mm(values * factor.astype(bf16), places[...]).astype(bf16) * mask_t[...]


def fold(wide, factor, mask_t, places_t):
    return mm(wide.astype(bf16) * mask_t[...], places_t[...]) * factor


def pairs(aux_ref, aux_t_ref, lower):
    row, column = iota((TILE, TILE), 0), iota((TILE, TILE), 1)
    order = column <= row if lower else column >= row
    return (row // SUB == column // SUB) & order & (aux_ref[:, 2:3] == aux_t_ref[2:3, :])


def run_states(state, local_ref, block_ref, keep=None):
    def one(k, state):
        if keep is not None:
            keep[pl.ds(pl.multiple_of(k * STATE, STATE), STATE), :] = state.astype(bf16)
        return block_ref[pl.ds(k, 1), :] * state + local_ref[pl.ds(pl.multiple_of(k * STATE, STATE), STATE), :]

    return lax.fori_loop(0, TILE // SUB, one, state, unroll=True)


def end_state_kernel(
    mixed, aux, aux_t, alive_last, bias, rate, sums_table, mask, mask_t, places, places_t, end, state, local, block
):
    @pl.when(pl.program_id(0) == 0)
    def _():
        state[...] = jnp.zeros_like(state)

    _, maps_t = both_ways(mixed)
    raw, step, log_decay, upto, after, total = decays(
        part(mixed, 2), bias, rate, alive_last, sums_table
    )
    driven = (jnp.exp(after) * step * part(mixed, 0)).astype(bf16)
    local[...] = mm(in_blocks(maps_t[:STATE], aux_t[1:2, :], mask), driven)
    block[...] = total
    state[...] = run_states(state[...], local, block)
    end[...] = state[...]


def forward_kernel(
    mixed,
    aux,
    aux_t,
    alive_last,
    bias,
    rate,
    sums_table,
    mask,
    mask_t,
    places,
    places_t,
    skip,
    start,
    gated,
    states,
    end,
    state,
    local,
    block,
):
    @pl.when(pl.program_id(0) == 0)
    def _():
        state[...] = start[...]

    maps, maps_t = both_ways(mixed)
    raw, step, log_decay, upto, after, total = decays(
        part(mixed, 2), bias, rate, alive_last, sums_table
    )
    x = part(mixed, 0)
    driven = (jnp.exp(after) * step * x).astype(bf16)
    local[...] = mm(in_blocks(maps_t[:STATE], aux_t[1:2, :], mask), driven)
    block[...] = total
    state[...] = run_states(state[...], local, block, states)
    end[...] = state[...]
    out_part = maps[:, STATE : 2 * STATE]
    cross = jnp.where(pairs(aux, aux_t, True), mm(out_part, maps_t[:STATE]), 0.0).astype(bf16)
    y = (
        upto * mm(spread(out_part, aux[:, 0:1], mask_t, places), states[...])
        + jnp.exp(-after) * mm(cross, driven)
        + skip[...] * x
    )
    gates = part(mixed, 1)
    gated[...] = (y * gates * lax.logistic(gates)).astype(bf16)


def back_run(carry, local_ref, block_ref, keep, states=None, bound=None):
    count = TILE // SUB

    def one(i, carry):
        k = count - 1 - i
        rows = pl.ds(pl.multiple_of(k * STATE, STATE), STATE)
        if keep is not None:
            keep[rows, :] = carry[0].astype(bf16)
            bound[pl.ds(k, 1), :] = carry[1]
        new = block_ref[pl.ds(k, 1), :] * carry[0] + local_ref[rows, :]
        if keep is None:
            return (new, carry[1])
        return (new, jnp.sum(new * states[rows, :].astype(f32), axis=0, keepdims=True))

    return lax.fori_loop(0, count, one, carry, unroll=True)


def end_adjoint_kernel(
    count,
    gated_grad,
    mixed,
    aux,
    aux_t,
    alive_last,
    bias,
    rate,
    sums_table,
    mask,
    mask_t,
    places,
    places_t,
    source,
    end,
    total_out,
    state,
    local,
    block,
    own,
    sent,
    got,
    loads,
    send_sems,
    recv_sems,
):
    tile, tiles = pl.program_id(0), pl.num_programs(0)
    begin, step_line, finish = line_sum_steps(
        count, source.at[: total_out.shape[0]], own, sent, got, total_out, loads, send_sems, recv_sems
    )

    @pl.when(tile == 0)
    def _():
        begin()
        state[...] = jnp.zeros_like(state)

    for k in range(1, count - 1):

        @pl.when(tile == tiles * k // (count - 1))
        def _():
            step_line(k)

    _, maps_t = both_ways(mixed)
    raw, step, log_decay, upto, after, total = decays(
        part(mixed, 2), bias, rate, alive_last, sums_table
    )
    gates = part(mixed, 1)
    dy = gated_grad[...] * gates * lax.logistic(gates)
    local[...] = mm(in_blocks(maps_t[STATE : 2 * STATE], aux_t[0:1, :], mask), (upto * dy).astype(bf16))
    block[...] = total
    state[...] = back_run((state[...], jnp.zeros((1, state.shape[1]), f32)), local, block, None)[0]
    end[...] = state[...]

    @pl.when(tile == tiles - 1)
    def _():
        step_line(count - 1)
        finish()


def backward_kernel(
    count,
    gated_grad,
    mixed,
    states,
    aux,
    aux_t,
    alive_last,
    bias,
    rate,
    sums_table,
    mask,
    mask_t,
    places,
    places_t,
    skip,
    start,
    final,
    source,
    mix_grad,
    sums,
    total_out,
    state,
    local,
    block,
    adjoint,
    bound,
    edge,
    own,
    sent,
    got,
    loads,
    send_sems,
    recv_sems,
):
    tile, tiles = pl.program_id(0), pl.num_programs(0)
    begin, step_line, finish = line_sum_steps(
        count, source.at[source.shape[0] - total_out.shape[0] :], own, sent, got, total_out, loads, send_sems, recv_sems
    )

    @pl.when(tile == 0)
    def _():
        begin()
        state[...] = start[...]
        edge[...] = jnp.sum(start[...] * final[...], axis=0, keepdims=True)
        sums[...] = jnp.zeros_like(sums)

    for k in range(1, count - 1):

        @pl.when(tile == tiles * k // (count - 1))
        def _():
            step_line(k)

    maps, maps_t = both_ways(mixed)
    raw, step, log_decay, upto, after, total = decays(
        part(mixed, 2), bias, rate, alive_last, sums_table
    )
    channels = state.shape[1]
    x = part(mixed, 0)
    decay_after = jnp.exp(after)
    grow = jnp.exp(-after)
    driven = (decay_after * step * x).astype(bf16)
    in_part, out_part = maps[:, :STATE], maps[:, STATE : 2 * STATE]
    in_part_t, out_part_t = maps_t[:STATE], maps_t[STATE : 2 * STATE]
    lower, upper = pairs(aux, aux_t, True), pairs(aux, aux_t, False)
    cross = jnp.where(lower, mm(out_part, in_part_t), 0.0).astype(bf16)
    cross_t = jnp.where(upper, mm(in_part, out_part_t), 0.0).astype(bf16)
    y = upto * mm(spread(out_part, aux[:, 0:1], mask_t, places), states[...]) + grow * mm(cross, driven)
    gates = part(mixed, 1)
    sigma = lax.logistic(gates)
    grad = gated_grad[...]
    dy = grad * gates * sigma
    mix_grad[:, HEAD + channels : HEAD + 2 * channels] = (
        grad * (y + skip[...] * x) * (sigma * (1.0 + gates * (1.0 - sigma)))
    ).astype(bf16)
    dy_low = (upto * dy).astype(bf16)
    dy_grown = (grow * dy).astype(bf16)
    local[...] = mm(in_blocks(out_part_t, aux_t[0:1, :], mask), dy_low)
    block[...] = total
    new_state, new_edge = back_run((state[...], edge[...]), local, block, adjoint, states, bound)
    state[...] = new_state
    edge[...] = new_edge
    du = decay_after * (
        mm(spread(in_part, aux[:, 1:2], mask_t, places), adjoint[...]) + mm(cross_t, dy_grown)
    )
    out_grad = fold(mm_nt(dy_low, states[...]), aux[:, 0:1], mask_t, places_t)
    in_grad = fold(mm_nt(driven, adjoint[...]), aux[:, 1:2], mask_t, places_t)
    cross_grad = jnp.where(lower, mm_nt(dy_grown, driven), 0.0).astype(bf16)
    cross_grad_t = jnp.where(upper, mm_nt(driven, dy_grown), 0.0).astype(bf16)
    out_grad = out_grad + mm(cross_grad, in_part)
    in_grad = in_grad + mm(cross_grad_t, out_part)
    mix_grad[:, :HEAD] = jnp.concatenate(
        [in_grad, out_grad, jnp.zeros((TILE, HEAD - 2 * STATE), f32)], axis=1
    ).astype(bf16)
    flow = dy * y - step * x * du
    to_tokens = ones_where(group_mask(TILE, TILE // SUB, SUB, 1)) * aux[:, 1:2]
    decay_grad = aux[:, 3:4] * (
        mm(ones_where(upper).astype(bf16), flow.astype(bf16))
        + split_mm(to_tokens.astype(bf16), bound[...])
    )
    step_grad = (x * du - rate[...] * decay_grad) * lax.logistic(raw)
    mix_grad[:, HEAD : HEAD + channels] = (skip[...] * dy + step * du).astype(bf16)
    mix_grad[:, HEAD + 2 * channels :] = step_grad.astype(bf16)
    sums[0:1, :] += jnp.sum(step_grad, axis=0, keepdims=True)
    sums[1:2, :] += jnp.sum(decay_grad * log_decay, axis=0, keepdims=True)
    sums[2:3, :] += jnp.sum(dy * x, axis=0, keepdims=True)

    @pl.when(tile == tiles - 1)
    def _():
        step_line(count - 1)
        finish()


def scan_specs(tokens, channels, back):
    tiles = tokens // TILE
    at = (lambda i: tiles - 1 - i) if back else (lambda i: i)

    def fixed(*shape):
        return pl.BlockSpec(shape, lambda i: (0,) * len(shape))

    width = TILE // SUB * STATE
    mixed = pl.BlockSpec((TILE, HEAD + 3 * channels), lambda i: (at(i), 0))
    rows = pl.BlockSpec((TILE, channels), lambda i: (at(i), 0))
    states = pl.BlockSpec((width, channels), lambda i: (at(i), 0))
    side = [
        pl.BlockSpec((TILE, 8), lambda i: (at(i), 0)),
        pl.BlockSpec((8, TILE), lambda i: (0, at(i))),
        pl.BlockSpec((TILE // SUB, 1), lambda i: (at(i), 0)),
        fixed(1, channels),
        fixed(1, channels),
        fixed(2 * TILE + TILE // SUB, TILE),
        fixed(width, TILE),
        fixed(TILE, width),
        fixed(STATE, width),
        fixed(width, STATE),
    ]
    return tiles, mixed, rows, states, side, fixed(1, channels), fixed(STATE, channels)


def scan_scratch(channels):
    return [
        pltpu.VMEM((STATE, channels), f32),
        pltpu.VMEM((TILE // SUB * STATE, channels), f32),
        pltpu.VMEM((TILE // SUB, channels), f32),
    ]


def scan_call(kernel, name, tiles, in_specs, out_specs, out_shape, scratch, flops, collective=None, room=16):
    return pl.pallas_call(
        kernel,
        name=name,
        grid=(tiles,),
        in_specs=in_specs,
        out_specs=out_specs,
        scratch_shapes=scratch,
        out_shape=out_shape,
        compiler_params=pltpu.CompilerParams(
            vmem_limit_bytes=room << 20,
            dimension_semantics=("arbitrary",),
            collective_id=collective,
            has_side_effects=collective is not None,
        ),
        cost_estimate=pl.CostEstimate(flops=flops, bytes_accessed=flops // 100, transcendentals=0),
    )


def scan_aux(segment, before):
    count = segment.shape[0]
    blocks = segment.reshape(count // SUB, SUB)
    ends = jnp.concatenate([before[None], blocks[:-1, -1]])
    alive = (blocks == ends[:, None]).reshape(-1).astype(f32)
    tail = (blocks == blocks[:, -1:]).reshape(-1).astype(f32)
    joined = (segment == jnp.concatenate([before[None], segment[:-1]])).astype(f32)
    zero = jnp.zeros_like(alive)
    aux_t = jnp.stack([alive, tail, segment.astype(f32), joined, zero, zero, zero, zero])
    last = (blocks[:, -1] == ends).astype(f32)[:, None]
    return aux_t.T, aux_t, last


def end_state(mixed, side):
    tokens, channels = mixed.shape[0], (mixed.shape[1] - HEAD) // 3
    tiles, mixed_s, rows, states, side_s, row, state = scan_specs(tokens, channels, False)
    return scan_call(
        end_state_kernel,
        "end_state",
        tiles,
        [mixed_s, *side_s],
        state,
        jax.ShapeDtypeStruct((STATE, channels), f32),
        scan_scratch(channels),
        10**7,
    )(mixed, *side)


def forward_scan(mixed, side, skip, start):
    tokens, channels = mixed.shape[0], (mixed.shape[1] - HEAD) // 3
    tiles, mixed_s, rows, states, side_s, row, state = scan_specs(tokens, channels, False)
    return scan_call(
        forward_kernel,
        "forward_scan",
        tiles,
        [mixed_s, *side_s, row, state],
        [rows, states, state],
        [
            jax.ShapeDtypeStruct((tokens, channels), bf16),
            jax.ShapeDtypeStruct((tokens // SUB * STATE, channels), bf16),
            jax.ShapeDtypeStruct((STATE, channels), f32),
        ],
        scan_scratch(channels),
        10**7,
    )(mixed, *side, skip, start)


def end_adjoint(gated_grad, mixed, side, source, height, count, collective):
    each = source.shape[1] // count
    tokens, channels = mixed.shape[0], (mixed.shape[1] - HEAD) // 3
    tiles, mixed_s, rows, states, side_s, row, state = scan_specs(tokens, channels, True)
    return scan_call(
        functools.partial(end_adjoint_kernel, count),
        "end_adjoint",
        tiles,
        [rows, mixed_s, *side_s, pl.BlockSpec(memory_space=pl.ANY)],
        [state, pl.BlockSpec((height, each), lambda i: (0, 0))],
        [
            jax.ShapeDtypeStruct((STATE, channels), f32),
            jax.ShapeDtypeStruct((height, each), f32),
        ],
        scan_scratch(channels) + line_sum_scratch(count, height, each),
        10**10,
        collective,
        24,
    )(gated_grad, mixed, *side, source)


def backward_scan(gated_grad, mixed, states, side, skip, start, final, source, height, count, collective):
    each = source.shape[1] // count
    tokens, channels = mixed.shape[0], (mixed.shape[1] - HEAD) // 3
    tiles, mixed_s, rows, states_s, side_s, row, state = scan_specs(tokens, channels, True)
    return scan_call(
        functools.partial(backward_kernel, count),
        "backward_scan",
        tiles,
        [
            rows,
            mixed_s,
            states_s,
            *side_s,
            row,
            state,
            state,
            pl.BlockSpec(memory_space=pl.ANY),
        ],
        [
            mixed_s,
            pl.BlockSpec((8, channels), lambda i: (0, 0)),
            pl.BlockSpec((height, each), lambda i: (0, 0)),
        ],
        [
            jax.ShapeDtypeStruct(mixed.shape, bf16),
            jax.ShapeDtypeStruct((8, channels), f32),
            jax.ShapeDtypeStruct((height, each), f32),
        ],
        scan_scratch(channels)
        + [
            pltpu.VMEM((TILE // SUB * STATE, channels), bf16),
            pltpu.VMEM((TILE // SUB, channels), f32),
            pltpu.VMEM((1, channels), f32),
        ]
        + line_sum_scratch(count, height, each),
        36 * 10**9,
        collective,
        48,
    )(gated_grad, mixed, states, *side, skip, start, final, source)


MESH = pl.DeviceIdType.MESH
COMM = {"has_side_effects": True}


def neighbour_barrier(count):
    place = lax.axis_index("tp")
    ready = pltpu.get_barrier_semaphore()
    sides = ((place < count - 1, place + 1), (place > 0, place - 1))
    for there, other in sides:

        @pl.when(there)
        def _():
            pl.semaphore_signal(ready, inc=1, device_id={"tp": other}, device_id_type=MESH)

    peers = jnp.where(place < count - 1, 1, 0) + jnp.where(place > 0, 1, 0)
    pl.semaphore_wait(ready, peers)


def line_steps(count, source, target, copies, send_sems, recv_sems):
    place = lax.axis_index("tp")
    width = source.shape[1]

    def at(owner):
        return target.at[:, pl.ds(pl.multiple_of(owner * width, width), width)]

    def local():
        return pltpu.make_async_copy(source, at(place), copies)

    def remote(side, step):
        owner = place - step if side == 0 else place + step
        return pltpu.make_async_remote_copy(
            src_ref=source if step == 0 else at(owner),
            dst_ref=at(owner),
            send_sem=send_sems.at[side, step],
            recv_sem=recv_sems.at[side, step],
            device_id={"tp": place + 1 if side == 0 else place - 1},
            device_id_type=MESH,
        )

    def has(side, step):
        return place - step >= 0 if side == 0 else place + step < count

    def neighbour(side):
        return place < count - 1 if side == 0 else place > 0

    def send(side, step):
        @pl.when(neighbour(side) & has(side, step))
        def _():
            remote(side, step).start()

    def receive(side, step):
        @pl.when(has(side, step + 1))
        def _():
            remote(side, step).wait_recv()

    def start():
        neighbour_barrier(count)
        local().start()
        for side in (0, 1):
            send(side, 0)

    def step(k):
        for side in (0, 1):
            receive(side, k - 1)
        for side in (0, 1):
            if k < count - 1:
                send(side, k)

    step.send, step.receive = send, receive

    def finish():
        for k in range(count - 1):
            for side in (0, 1):

                @pl.when(neighbour(side) & has(side, k))
                def _():
                    remote(side, k).wait_send()

        local().wait()

    return start, step, finish


def line_scratch(count):
    return [
        pltpu.SemaphoreType.DMA,
        pltpu.SemaphoreType.DMA((2, count - 1)),
        pltpu.SemaphoreType.DMA((2, count - 1)),
    ]


def line_gather_kernel(count, source, target, copies, send_sems, recv_sems):
    start, step, finish = line_steps(count, source, target, copies, send_sems, recv_sems)
    start()
    for k in range(1, count):
        step(k)
    finish()


def line_gather(source, count, collective):
    return pl.pallas_call(
        functools.partial(line_gather_kernel, count),
        name="line_gather",
        in_specs=[pl.BlockSpec(memory_space=pl.ANY)],
        out_specs=pl.BlockSpec(memory_space=pl.ANY),
        out_shape=jax.ShapeDtypeStruct((source.shape[0], source.shape[1] * count), source.dtype),
        scratch_shapes=line_scratch(count),
        compiler_params=pltpu.CompilerParams(collective_id=collective, has_side_effects=True),
    )(source)


def line_sum_steps(count, source, own, sent, got, total, loads, send_sems, recv_sems):
    place = lax.axis_index("tp")
    width = total.shape[1]

    def whose(side, step):
        return place + (count - step) if side == 0 else place - (count - step)

    def sends(side, step):
        owner = whose(side, step)
        return owner < count if side == 0 else owner >= 0

    def receives(side, step):
        return (place >= 1) & (place <= step) if side == 0 else (place <= count - 2) & (place >= count - 1 - step)

    def load(side, step):
        owner = whose(side, step)
        return pltpu.make_async_copy(
            source.at[:, pl.ds(pl.multiple_of(owner * width, width), width)],
            sent.at[side, step - 1],
            loads.at[side, step - 1],
        )

    def mine():
        return pltpu.make_async_copy(
            source.at[:, pl.ds(pl.multiple_of(place * width, width), width)], own, loads.at[2, 0]
        )

    def remote(side, step):
        return pltpu.make_async_remote_copy(
            src_ref=sent.at[side, step - 1],
            dst_ref=got.at[side, step - 1],
            send_sem=send_sems.at[side, step - 1],
            recv_sem=recv_sems.at[side, step - 1],
            device_id={"tp": place + 1 if side == 0 else place - 1},
            device_id_type=MESH,
        )

    def start():
        neighbour_barrier(count)
        mine().start()
        for step in range(1, count):
            for side in (0, 1):

                @pl.when(sends(side, step))
                def _():
                    load(side, step).start()

        step_out(1)

    def step_out(step):
        for side in (0, 1):

            @pl.when(sends(side, step))
            def _():
                load(side, step).wait()

            if step > 1:

                @pl.when(sends(side, step) & receives(side, step - 1))
                def _():
                    sent[side, step - 1] = (
                        sent[side, step - 1].astype(f32) + got[side, step - 2].astype(f32)
                    ).astype(bf16)

            @pl.when(sends(side, step))
            def _():
                remote(side, step).start()

    def step(k):
        for side in (0, 1):

            @pl.when(receives(side, k))
            def _():
                remote(side, k).wait_recv()

        if k < count - 1:
            step_out(k + 1)

    def finish():
        mine().wait()
        total[...] = own[...].astype(f32)
        for side in (0, 1):

            @pl.when(receives(side, count - 1))
            def _():
                total[...] = total[...] + got[side, count - 2].astype(f32)

            for k in range(1, count):

                @pl.when(sends(side, k))
                def _():
                    remote(side, k).wait_send()

    return start, step, finish


def line_sum_scratch(count, height, width):
    return [
        pltpu.VMEM((height, width), bf16),
        pltpu.VMEM((2, count - 1, height, width), bf16),
        pltpu.VMEM((2, count - 1, height, width), bf16),
        pltpu.SemaphoreType.DMA((3, count - 1)),
        pltpu.SemaphoreType.DMA((2, count - 1)),
        pltpu.SemaphoreType.DMA((2, count - 1)),
    ]


def line_sum_kernel(count, source, total, own, sent, got, loads, send_sems, recv_sems):
    start, step, finish = line_sum_steps(
        count, source, own, sent, got, total, loads, send_sems, recv_sems
    )
    start()
    for k in range(1, count):
        step(k)
    finish()


def line_sum(source, count, collective):
    height, width = source.shape[0], source.shape[1] // count
    return pl.pallas_call(
        functools.partial(line_sum_kernel, count),
        name="line_sum",
        in_specs=[pl.BlockSpec(memory_space=pl.ANY)],
        out_specs=pl.BlockSpec(memory_space=pltpu.VMEM),
        out_shape=jax.ShapeDtypeStruct((height, width), f32),
        scratch_shapes=line_sum_scratch(count, height, width),
        compiler_params=pltpu.CompilerParams(
            vmem_limit_bytes=24 << 20, collective_id=collective, has_side_effects=True
        ),
        cost_estimate=pl.CostEstimate(flops=5 * 10**10, bytes_accessed=1 << 24, transcendentals=0),
    )(source)


def feed_kernel(
    count,
    blocks,
    source,
    other,
    weights,
    group,
    gate_up_grad,
    hidden,
    part_sum,
    maps,
    tokens,
    grads,
    grad_rows,
    hidden_rows,
    partial,
    copies,
    loads,
    stores,
    send_sems,
    recv_sems,
):
    place = lax.axis_index("tp")
    start, step, finish = line_steps(count, source, group, copies, send_sems, recv_sems)
    receive, send = step.receive, step.send
    ff = hidden.shape[1]
    width = source.shape[1]
    near = jnp.minimum(place, count - 1 - place)

    def owner_of(q):
        spread_out = jnp.where(q % 2 == 1, place - (q + 1) // 2, place + q // 2)
        rest = jnp.where(place < count - 1 - place, q, count - 1 - q)
        return jnp.where(q <= 2 * near, spread_out, rest)

    def reach(q):
        return jnp.where(q <= 2 * near, (q + 1) // 2, q - near)

    def load(what, where, k):
        return pltpu.make_async_copy(what, where, loads.at[k])

    def columns(array, owner):
        return array.at[:, pl.ds(pl.multiple_of(owner * width, width), width)]

    def store(q):
        owner, slot = owner_of(q), q % 2
        at = pl.ds(pl.multiple_of(owner * width, width), width)
        return [
            pltpu.make_async_copy(grad_rows.at[slot], gate_up_grad.at[at, :], stores.at[slot, 0]),
            pltpu.make_async_copy(hidden_rows.at[slot], hidden.at[at, :], stores.at[slot, 1]),
            pltpu.make_async_copy(partial.at[slot], columns(part_sum, owner), stores.at[slot, 2]),
        ]

    start()
    load(other, grads, 2).start()
    load(weights.at[:, : 3 * ff], maps, 0).start()

    def one(q, carry):
        owner, slot = owner_of(q), q % 2
        for far in range(1, count):

            @pl.when((reach(q) == far) & (reach(q - 1) < far))
            def _():
                for side in (0, 1):
                    receive(side, far - 1)
                for side in (0, 1):
                    if far < count - 1:
                        send(side, far)

        @pl.when(q == 0)
        def _():
            load(source, tokens, 1).start()
            load(source, tokens, 1).wait()

        @pl.when(q > 0)
        def _():
            load(columns(group, owner), tokens, 1).start()
            load(columns(group, owner), tokens, 1).wait()

        @pl.when(q == 0)
        def _():
            load(other, grads, 2).wait()
            load(weights.at[:, : 3 * ff], maps, 0).wait()

        @pl.when(q > 1)
        def _():
            for copy in store(q - 2):
                copy.wait()

        rows = tokens[...].T
        outs = columns(grads, owner)[...].T
        for begin, wide in blocks:
            gate = mm(rows, maps[:, begin : begin + wide])
            up = mm(rows, maps[:, ff + begin : ff + begin + wide])
            grad = mm(outs, maps[:, 2 * ff + begin : 2 * ff + begin + wide])
            sigma = lax.logistic(gate)
            active = gate * sigma
            hidden_rows[slot, :, begin : begin + wide] = (active * up).astype(bf16)
            grad_rows[slot, :, begin : begin + wide] = (
                grad * up * (sigma * (1.0 + gate * (1.0 - sigma)))
            ).astype(bf16)
            grad_rows[slot, :, ff + begin : ff + begin + wide] = (grad * active).astype(bf16)
        partial[slot] = mm_nt(maps[:, : 2 * ff], grad_rows[slot]).astype(bf16)
        for copy in store(q):
            copy.start()
        return carry

    lax.fori_loop(0, count, one, 0)
    for q in (count - 2, count - 1):
        for copy in store(q):
            copy.wait()
    finish()


def feed_forward(source, other, weights, ff, count, collective):
    depth, width = source.shape
    blocks = []
    begin = 0
    while begin < ff:
        blocks.append((begin, min(256, ff - begin)))
        begin = begin + 256
    anywhere = pl.BlockSpec(memory_space=pl.ANY)
    return pl.pallas_call(
        functools.partial(feed_kernel, count, tuple(blocks)),
        name="feed_forward",
        in_specs=[anywhere] * 3,
        out_specs=[anywhere] * 4,
        out_shape=[
            jax.ShapeDtypeStruct((depth, width * count), bf16),
            jax.ShapeDtypeStruct((width * count, 2 * ff), bf16),
            jax.ShapeDtypeStruct((width * count, ff), bf16),
            jax.ShapeDtypeStruct((depth, width * count), bf16),
        ],
        scratch_shapes=[
            pltpu.VMEM((depth, 3 * ff), bf16),
            pltpu.VMEM((depth, width), bf16),
            pltpu.VMEM((depth, width * count), bf16),
            pltpu.VMEM((2, width, 2 * ff), bf16),
            pltpu.VMEM((2, width, ff), bf16),
            pltpu.VMEM((2, depth, width), bf16),
            pltpu.SemaphoreType.DMA,
            pltpu.SemaphoreType.DMA((3,)),
            pltpu.SemaphoreType.DMA((2, 3)),
            pltpu.SemaphoreType.DMA((2, count - 1)),
            pltpu.SemaphoreType.DMA((2, count - 1)),
        ],
        compiler_params=pltpu.CompilerParams(
            vmem_limit_bytes=56 << 20, collective_id=collective, has_side_effects=True
        ),
    )(source, other, weights)


def wide_sum_kernel(
    count,
    ups,
    downs,
    tokens,
    others,
    gate_up_grad,
    hidden,
    hidden_rows,
    maps,
    source,
    wide,
    out_part,
    total,
    own,
    sent,
    got,
    loads,
    send_sems,
    recv_sems,
):
    step, steps = pl.program_id(0), pl.num_programs(0)
    start, advance, finish = line_sum_steps(
        count, source, own, sent, got, total, loads, send_sems, recv_sems
    )

    @pl.when(step == 0)
    def _():
        start()

    for k in range(1, count - 1):

        @pl.when(step == steps * k // (count - 1))
        def _():
            advance(k)

    @pl.when(step < ups)
    def _():
        wide[...] = mm(tokens[...], gate_up_grad[...]).astype(bf16)

    @pl.when((step >= ups) & (step < ups + downs))
    def _():
        wide[...] = mm(others[...], hidden[...]).astype(bf16)

    @pl.when(step >= ups + downs)
    def _():
        out_part[...] = mm_nt(maps[...], hidden_rows[...]).astype(bf16)

    @pl.when(step == steps - 1)
    def _():
        advance(count - 1)
        finish()


def wide_sum(tokens, others, gate_up_grad, hidden, maps, source, count, collective):
    depth, span = tokens.shape
    ff = hidden.shape[1]
    ups, downs, strip = 2 * ff // 128, ff // 128, 320
    strips = depth // strip
    each = source.shape[1] // count

    def strip_of(j):
        return jnp.clip(j - ups - downs, 0, strips - 1)

    def whole(*shape):
        return pl.BlockSpec(shape, lambda j: (0, 0), pipeline_mode=pl.Buffered(1))

    return pl.pallas_call(
        functools.partial(wide_sum_kernel, count, ups, downs),
        name="wide_sum",
        grid=(ups + downs + strips,),
        in_specs=[
            whole(depth, span),
            whole(depth, span),
            pl.BlockSpec((span, 128), lambda j: (0, jnp.minimum(j, ups - 1))),
            pl.BlockSpec((span, 128), lambda j: (0, jnp.clip(j - ups, 0, downs - 1))),
            whole(span, ff),
            pl.BlockSpec((strip, ff), lambda j: (strip_of(j), 2)),
            pl.BlockSpec(memory_space=pl.ANY),
        ],
        out_specs=[
            pl.BlockSpec((depth, 128), lambda j: (0, jnp.minimum(j, ups + downs - 1))),
            pl.BlockSpec((strip, span), lambda j: (strip_of(j), 0)),
            pl.BlockSpec((depth, each), lambda j: (0, 0)),
        ],
        out_shape=[
            jax.ShapeDtypeStruct((depth, 3 * ff), bf16),
            jax.ShapeDtypeStruct((depth, span), bf16),
            jax.ShapeDtypeStruct((depth, each), f32),
        ],
        scratch_shapes=line_sum_scratch(count, depth, each),
        compiler_params=pltpu.CompilerParams(
            vmem_limit_bytes=48 << 20,
            dimension_semantics=("arbitrary",),
            collective_id=collective,
            has_side_effects=True,
        ),
    )(tokens, others, gate_up_grad, hidden, hidden, maps, source)


def attend_kernel(
    group,
    count,
    query_t,
    key_t,
    value_t,
    bias,
    source,
    out_t,
    log_total,
    total_out,
    own,
    sent,
    got,
    loads,
    send_sems,
    recv_sems,
):
    head, heads = pl.program_id(0), pl.num_programs(0)
    start, step, finish = line_sum_steps(
        count, source, own, sent, got, total_out, loads, send_sems, recv_sems
    )

    @pl.when(head == 0)
    def _():
        start()

    @pl.when(head == heads - 2)
    def _():
        step(1)

    keys = key_t[...].T
    values_t = value_t[...]
    for g in range(group):
        at = slice(g * HEAD_SIZE, (g + 1) * HEAD_SIZE)
        scores = mm(keys, query_t[at, :] * 0.125) + bias[...]
        top = jnp.max(scores, axis=0, keepdims=True)
        probs = jnp.exp(scores - top)
        total = jnp.sum(probs, axis=0, keepdims=True)
        out_t[at, :] = (mm(values_t, probs.astype(bf16)) / total).astype(bf16)
        log_total[g : g + 1, :] = top + jnp.log(total)

    @pl.when(head == heads - 1)
    def _():
        for k in range(2, count):
            step(k)
        finish()


def attend_back_kernel(
    group,
    count,
    query_t,
    key_t,
    value_t,
    bias,
    out_t,
    log_total,
    grad_t,
    source,
    query_grad_t,
    keyval_grad_t,
    target,
    copies,
    send_sems,
    recv_sems,
):
    head, heads = pl.program_id(0), pl.num_programs(0)
    start, step, finish = line_steps(count, source, target, copies, send_sems, recv_sems)

    @pl.when(head == 0)
    def _():
        start()

    @pl.when(head == heads - 2)
    def _():
        step(1)

    keys_t = key_t[...]
    keys = keys_t.T
    values = value_t[...].T
    key_sum = jnp.zeros(keys_t.shape, f32)
    value_sum = jnp.zeros(keys_t.shape, f32)
    for g in range(group):
        at = slice(g * HEAD_SIZE, (g + 1) * HEAD_SIZE)
        query = query_t[at, :] * 0.125
        grad = grad_t[at, :]
        probs = jnp.exp(mm(keys, query) + bias[...] - log_total[g : g + 1, :])
        centre = jnp.sum(grad.astype(f32) * out_t[at, :].astype(f32), axis=0, keepdims=True)
        score_grad = (probs * (mm(values, grad) - centre)).astype(bf16)
        query_grad_t[at, :] = (mm(keys_t, score_grad) * 0.125).astype(bf16)
        key_sum = key_sum + mm_nt(query, score_grad)
        value_sum = value_sum + mm_nt(grad, probs.astype(bf16))
    keyval_grad_t[0] = key_sum.astype(bf16)
    keyval_grad_t[1] = value_sum.astype(bf16)

    @pl.when(head == heads - 1)
    def _():
        for k in range(2, count):
            step(k)
        finish()


def attend(query_t, keyval_t, bias, source, key_value_heads, count, collective):
    width, rows = query_t.shape
    keys = keyval_t.shape[1]
    group = width // HEAD_SIZE // key_value_heads
    kv = key_value_heads
    height, each = source.shape[0], source.shape[1] // count
    return pl.pallas_call(
        functools.partial(attend_kernel, group, count),
        name="attend",
        grid=(kv,),
        in_specs=[
            pl.BlockSpec((group * HEAD_SIZE, rows), lambda h: (h, 0)),
            pl.BlockSpec((HEAD_SIZE, keys), lambda h: (h, 0)),
            pl.BlockSpec((HEAD_SIZE, keys), lambda h: (h + kv, 0)),
            pl.BlockSpec((keys, rows), lambda h: (0, 0)),
            pl.BlockSpec(memory_space=pl.ANY),
        ],
        out_specs=[
            pl.BlockSpec((group * HEAD_SIZE, rows), lambda h: (h, 0)),
            pl.BlockSpec((None, 8, rows), lambda h: (h, 0, 0)),
            pl.BlockSpec((height, each), lambda h: (0, 0)),
        ],
        out_shape=[
            jax.ShapeDtypeStruct((width, rows), bf16),
            jax.ShapeDtypeStruct((kv, 8, rows), f32),
            jax.ShapeDtypeStruct((height, each), f32),
        ],
        scratch_shapes=line_sum_scratch(count, height, each),
        compiler_params=pltpu.CompilerParams(
            vmem_limit_bytes=56 << 20,
            dimension_semantics=("arbitrary",),
            collective_id=collective,
            has_side_effects=True,
        ),
    )(query_t, keyval_t, keyval_t, bias, source)


def attend_back(query_t, keyval_t, bias, out_t, log_total, grad_t, source, key_value_heads, count, collective):
    width, rows = query_t.shape
    keys = keyval_t.shape[1]
    group = width // HEAD_SIZE // key_value_heads
    kv = key_value_heads
    wide = pl.BlockSpec((group * HEAD_SIZE, rows), lambda h: (h, 0))
    head = pl.BlockSpec((HEAD_SIZE, keys), lambda h: (h, 0))
    anywhere = pl.BlockSpec(memory_space=pl.ANY)
    return pl.pallas_call(
        functools.partial(attend_back_kernel, group, count),
        name="attend_back",
        grid=(kv,),
        in_specs=[
            wide,
            head,
            pl.BlockSpec((HEAD_SIZE, keys), lambda h: (h + kv, 0)),
            pl.BlockSpec((keys, rows), lambda h: (0, 0)),
            wide,
            pl.BlockSpec((None, 8, rows), lambda h: (h, 0, 0)),
            wide,
            anywhere,
        ],
        out_specs=[wide, pl.BlockSpec((2, HEAD_SIZE, keys), lambda h: (0, h, 0)), anywhere],
        out_shape=[
            jax.ShapeDtypeStruct((width, rows), bf16),
            jax.ShapeDtypeStruct((2, kv * HEAD_SIZE, keys), bf16),
            jax.ShapeDtypeStruct((source.shape[0], source.shape[1] * count), source.dtype),
        ],
        scratch_shapes=line_scratch(count),
        compiler_params=pltpu.CompilerParams(
            vmem_limit_bytes=56 << 20,
            dimension_semantics=("arbitrary",),
            collective_id=collective,
            has_side_effects=True,
        ),
    )(query_t, keyval_t, keyval_t, bias, out_t, log_total, grad_t, source)


def rms_norm(values, gain):
    return values * lax.rsqrt(jnp.mean(values * values, axis=0, keepdims=True) + epsilon) * gain


def rms_back(values, gain, grad):
    scale = lax.rsqrt(jnp.mean(values * values, axis=0, keepdims=True) + epsilon)
    normal = values * scale
    weighted = grad * gain
    back = scale * (weighted - normal * jnp.mean(weighted * normal, axis=0, keepdims=True))
    return back, grad * normal


def dot(left, right, left_dim, right_dim):
    return lax.dot_general(
        left, right, (((left_dim,), (right_dim,)), ((), ())), preferred_element_type=f32
    )


def gather_rows(whole):
    return lax.all_gather(whole, ("fsdp", "ctx"), axis=0, tiled=True)


def by_rows(values):
    return with_layout_constraint(values, Layout((0, 1)))


def scatter_rows(whole):
    return by_rows(
        lax.psum_scatter(by_rows(whole), ("fsdp", "ctx"), scatter_dimension=0, tiled=True)
    )


def send(values, by):
    count = lax.axis_size("tp")
    return lax.ppermute(values, "tp", [(i, (i + by) % count) for i in range(count)])


def permute_gather(own):
    count = lax.axis_size("tp")
    return [own] + [send(own, k) for k in range(1, count)]


def in_order(pieces):
    count, place = lax.axis_size("tp"), lax.axis_index("tp")
    return jnp.concatenate(
        [lax.select_n(lax.rem(place - p + count, count), *pieces) for p in range(count)], axis=1
    )


def permute_sums(values, axis):
    count, place = lax.axis_size("tp"), lax.axis_index("tp")
    each = values.shape[axis] // count
    shares = [
        lax.dynamic_slice_in_dim(values, lax.rem(place + k, count) * each, each, axis)
        for k in range(count)
    ]
    total = shares[0].astype(f32)
    for k in (2, 1, 3):
        total = total + send(shares[k], k).astype(f32)
    return total


def permute_exchange(values):
    count, place = lax.axis_size("tp"), lax.axis_index("tp")
    shares = values.reshape(count, values.shape[0] // count, values.shape[1])
    pieces = [
        lax.dynamic_index_in_dim(shares, lax.rem(place + k, count), 0, False) for k in range(count)
    ]
    return [pieces[0]] + [send(pieces[k], k) for k in range(1, count)]


def cut(values, widths):
    pieces = []
    offset = 0
    for count in widths:
        pieces.append(values[:, offset : offset + count])
        offset = offset + count
    return pieces


def per_device(
    tokens,
    segments,
    cotangent,
    meta_tokens,
    gain_mix,
    query_weight,
    key_value_weight,
    attn_output,
    gain_attn,
    mamba_input,
    mamba_select,
    step_bias,
    decay_log,
    state_skip,
    mamba_output,
    gain_mamba,
    gain_ffn,
    ffn_input,
    ffn_output,
):
    tokens_t, segments, cotangent_t = tokens[0].T, segments[0], cotangent[0].T
    width, rows = tokens_t.shape
    shard = meta_tokens.shape[0]
    tp = lax.axis_size("tp")
    tp_index = lax.axis_index("tp")
    ctx_index = lax.axis_index("ctx")
    span = rows * tp
    query_width = query_weight.shape[1]
    keyval_width = key_value_weight.shape[1]
    heads = keyval_width // (2 * HEAD_SIZE)
    channels = mamba_input.shape[2]
    ff = ffn_input.shape[2] // tp
    ff_wide = -(-ff // 128) * 128
    meta_count = meta_tokens.shape[1]
    window = WIN + rows

    place_of = jnp.arange(HEAD, dtype=jnp.int32)[None]
    head = jnp.pad(mamba_select, ((0, 0), (0, HEAD - 2 * STATE)))
    for k, gain in enumerate((gain_mix, gain_attn, gain_mamba, gain_ffn)):
        head = jnp.where(place_of == 2 * STATE + k, gain[:, None], head)
    first = jnp.concatenate([head] + [mamba_input[:, k] for k in range(3)], axis=1)
    first, second_parts = lax.optimization_barrier(
        (first, (key_value_weight, meta_tokens, query_weight, mamba_output))
    )
    second = jnp.concatenate(second_parts, axis=1)
    first, second, tokens_t = lax.optimization_barrier((first, second, tokens_t))
    first = gather_rows(first)
    second = gather_rows(second)
    tokens_group_t = line_gather(tokens_t, tp, 0)
    late_cotangent_t, tokens_group_t = lax.optimization_barrier((cotangent_t, tokens_group_t))
    cotangent_pieces = permute_gather(late_cotangent_t)

    gain_columns = first[:, 2 * STATE : 2 * STATE + 4]
    keyval_map, meta_full, query_map, state_out_map = cut(
        second, [keyval_width, meta_count, query_width, channels]
    )
    attn_map = gather_rows(attn_output)
    gain_columns = gain_columns.astype(f32)
    mix_gain, attn_gain, mamba_gain, ffn_gain = [gain_columns[:, k : k + 1] for k in range(4)]

    residual = tokens_t.astype(f32)
    residual_group = tokens_group_t.astype(f32)
    normed_t = rms_norm(residual, mix_gain).astype(bf16)
    normed_group_t = rms_norm(residual_group, mix_gain).astype(bf16)
    meta_rows = meta_full.astype(f32)
    meta_normed_t = rms_norm(meta_rows, mix_gain).astype(bf16)

    mixed = dot(normed_group_t, first, 0, 0)
    seg_current = lax.dynamic_slice_in_dim(segments, ctx_index * span, span, 0)
    seg_earlier = lax.dynamic_slice_in_dim(segments, jnp.maximum(ctx_index - 1, 0) * span, span, 0)
    seg_before = jnp.where(
        ctx_index > 0,
        lax.dynamic_index_in_dim(segments, jnp.maximum(ctx_index * span - 1, 0), 0, False),
        -1,
    )
    side = (
        *scan_aux(seg_current, seg_before),
        step_bias[None],
        jnp.exp(decay_log)[None],
        *scan_tables(),
    )
    skip_row = state_skip[None]
    state_end = end_state(mixed, side)
    state_end, late_up, late_down = lax.optimization_barrier((state_end, ffn_input, ffn_output))
    ffn_shards = [
        lax.dynamic_slice_in_dim(whole, tp_index * ff, ff, 1)
        for whole in (late_up[:, 0], late_up[:, 1], late_down)
    ]
    state_start = lax.ppermute(state_end, "ctx", [(0, 1)])

    query_t = dot(query_map, normed_t, 0, 0).astype(bf16)
    keyval_group_t = dot(keyval_map, normed_group_t, 0, 0).astype(bf16)
    meta_keyval_t = dot(keyval_map, meta_normed_t, 0, 0).astype(bf16)
    earlier_t = lax.ppermute(keyval_group_t, "ctx", [(0, 1)])

    gated, states, state_final = forward_scan(mixed, side, skip_row, state_start)
    third = jnp.concatenate(
        [jnp.pad(piece, ((0, 0), (0, ff_wide - ff))) for piece in ffn_shards] + [attn_output],
        axis=1,
    )
    third, gated, *cotangent_pieces = lax.optimization_barrier((third, gated, *cotangent_pieces))
    third = gather_rows(third)
    mamba_part_t = dot(state_out_map, gated, 1, 1).astype(bf16)
    up_map, down_map, attn_map = cut(third, [2 * ff_wide, ff_wide, query_width])

    key_start = span + tp_index * rows - WIN
    keyval_t = jnp.concatenate(
        [
            meta_keyval_t,
            lax.dynamic_slice_in_dim(
                jnp.concatenate([earlier_t, keyval_group_t], axis=1), key_start, window, 1
            ),
        ],
        axis=1,
    )
    query_pos = ctx_index * span + tp_index * rows + jnp.arange(rows, dtype=jnp.int32)
    key_pos = (ctx_index - 1) * span + key_start + jnp.arange(window, dtype=jnp.int32)
    seg_query = lax.dynamic_slice_in_dim(seg_current, tp_index * rows, rows, 0)
    seg_keys = lax.dynamic_slice_in_dim(
        jnp.concatenate([seg_earlier, seg_current]), key_start, window, 0
    )
    keep = (
        (key_pos[:, None] <= query_pos[None, :])
        & (query_pos[None, :] - key_pos[:, None] < WIN)
        & (key_pos[:, None] >= 0)
        & (seg_keys[:, None] == seg_query[None, :])
    )
    bias = jnp.concatenate(
        [jnp.zeros((meta_count, rows), f32), jnp.where(keep, 0.0, masked_score)], axis=0
    )
    cotangent_group_t = in_order(cotangent_pieces)
    attended_t, log_total, mamba_out = attend(
        query_t, keyval_t, bias, mamba_part_t, heads, tp, 3
    )
    attn_out = dot(attn_map, attended_t, 1, 0)

    mid = residual + 0.5 * (rms_norm(attn_out, attn_gain) + rms_norm(mamba_out, mamba_gain))
    ffn_normed_t = rms_norm(mid, ffn_gain).astype(bf16)
    ffn_normed_group_t, gate_up_grad, hidden, ffn_grad_part_t = feed_forward(
        ffn_normed_t, cotangent_group_t, third, ff_wide, tp, 1
    )
    fourth = width // 6 // 16 * 16
    ffn_wide, out_part_t, ffn_normed_grad_t = wide_sum(
        ffn_normed_group_t, cotangent_group_t, gate_up_grad, hidden, third, ffn_grad_part_t, tp, 7
    )
    ffn_columns = scatter_rows(ffn_wide)

    ffn_normed_grad = ffn_normed_grad_t.astype(f32)
    mid_extra, ffn_gain_terms = rms_back(mid, ffn_gain, ffn_normed_grad)
    mid_grad = cotangent_t.astype(f32) + mid_extra
    attn_grad, attn_gain_terms = rms_back(attn_out, attn_gain, 0.5 * mid_grad)
    mamba_grad, mamba_gain_terms = rms_back(mamba_out, mamba_gain, 0.5 * mid_grad)
    attn_grad_t = attn_grad.astype(bf16)
    mamba_grad_t = mamba_grad.astype(bf16)
    attended_grad_t = dot(attn_map, attn_grad_t, 0, 0).astype(bf16)
    query_grad_t, keyval_grad_t, mamba_grad_group_t = attend_back(
        query_t,
        keyval_t,
        bias,
        attended_t,
        log_total,
        attended_grad_t,
        mamba_grad_t,
        heads,
        tp,
        2,
    )
    query_pieces = permute_exchange(query_grad_t)
    keyval_grad_t = keyval_grad_t.reshape(keyval_width, meta_count + window)
    placed = lax.dynamic_update_slice_in_dim(
        jnp.zeros((keyval_width, 2 * span), bf16), keyval_grad_t[:, meta_count:], key_start, 1
    )
    earlier_back = lax.ppermute(placed[:, :span], "ctx", [(1, 0)])
    current = placed[:, span:].astype(f32) + earlier_back.astype(f32)
    keyval_part_t = current.astype(bf16)
    keyval_meta_t = keyval_grad_t[:, :meta_count]
    gated_grad = dot(mamba_grad_group_t, state_out_map, 0, 0)
    adjoint_end, out_head = end_adjoint(
        gated_grad, mixed, side, out_part_t, fourth, tp, 6
    )
    adjoint_end, late_attended_t, late_gated, query_pieces = lax.optimization_barrier(
        (adjoint_end, attended_t, gated, query_pieces)
    )
    adjoint_start = lax.ppermute(adjoint_end, "ctx", [(1, 0)])
    meta_back, meta_terms = rms_back(meta_rows, mix_gain, dot(keyval_map, keyval_meta_t, 1, 0))
    query_columns_t = in_order(query_pieces)
    each = query_width // tp

    def room(count):
        return ((0, -count % 128), (0, 0))

    query_wide = dot(normed_group_t, jnp.pad(query_columns_t, room(each)), 1, 1)
    keyval_wide = dot(normed_group_t, keyval_part_t, 1, 1) + dot(
        meta_normed_t, keyval_meta_t, 1, 1
    )
    early_pieces = [
        dot(attn_grad_t, jnp.pad(late_attended_t, room(query_width)), 1, 1),
        query_wide,
        meta_back,
        keyval_wide,
        dot(mamba_grad_group_t, late_gated, 1, 0),
    ]
    early_wide = by_rows(
        jnp.concatenate([by_rows(piece.astype(bf16)) for piece in early_pieces], axis=1)
    )
    early_columns = scatter_rows(early_wide)
    adjoint_start, early_wide, ffn_columns = lax.optimization_barrier(
        (adjoint_start, early_wide, ffn_columns)
    )
    mix_grad, scan_sums, out_rest = backward_scan(
        gated_grad,
        mixed,
        states,
        side,
        skip_row,
        adjoint_start,
        state_final,
        out_part_t,
        width - fourth,
        tp,
        5,
    )
    layer_out_t = (mid + jnp.concatenate([out_head, out_rest], axis=0)).astype(bf16)
    query_term = dot(query_map, query_grad_t, 1, 0)
    normed_grad_part = dot(first, mix_grad, 1, 1) + dot(keyval_map, keyval_part_t, 1, 0)
    _, group_terms = rms_back(residual_group, mix_gain, normed_grad_part)
    _, query_terms = rms_back(residual, mix_gain, query_term)
    normed_grad_low, mix_grad = lax.optimization_barrier(
        (normed_grad_part.astype(bf16), mix_grad)
    )
    vector_columns = -(-3 * channels // shard)
    vectors = jnp.pad(scan_sums[:3].reshape(-1), (0, vector_columns * shard - 3 * channels))
    vectors = jnp.tile(vectors.reshape(shard, vector_columns), (width // shard, 1))
    tail = [
        (jnp.sum(group_terms, 1) + jnp.sum(meta_terms, 1) + jnp.sum(query_terms, 1))[:, None],
        jnp.sum(attn_gain_terms, 1, keepdims=True),
        jnp.sum(mamba_gain_terms, 1, keepdims=True),
        jnp.sum(ffn_gain_terms, 1, keepdims=True),
        vectors,
    ]
    tail = jnp.concatenate(tail, axis=1)
    tail = jnp.pad(tail, ((0, 0), (2 * STATE, first.shape[1] - 2 * STATE - tail.shape[1])))
    last_wide = by_rows((dot(normed_group_t, mix_grad, 1, 0) + tail).astype(bf16))
    last_wide, early_columns = lax.optimization_barrier((last_wide, early_columns))
    last_columns = scatter_rows(last_wide)
    attn_shares, _, grad_query, _, meta_shares, keyval_shares, grad_mamba_output = cut(
        early_columns,
        [
            query_width,
            -query_width % 128,
            each,
            -each % 128,
            meta_count,
            keyval_width,
            channels,
        ],
    )

    def to_device(values):
        return jnp.swapaxes(values.reshape(shard, tp, values.shape[1] // tp), 0, 1)

    shares = jnp.concatenate(
        [to_device(attn_shares), to_device(keyval_shares), to_device(meta_shares)], axis=2
    )
    normed_grad_low, last_wide, shares = lax.optimization_barrier(
        (normed_grad_low, last_wide, shares)
    )
    grad_attn_output, grad_keyval, grad_meta = cut(
        permute_sums(shares, 0)[0], [each, keyval_width // tp, meta_count // tp]
    )
    normed_grad = line_sum(normed_grad_low, tp, 4) + query_term
    ffn_columns, normed_grad = lax.optimization_barrier((ffn_columns, normed_grad))
    residual_extra, _ = rms_back(residual, mix_gain, normed_grad)
    grad_tokens_t = (mid_grad + residual_extra).astype(bf16)
    grad_gate, grad_up, grad_ffn_output = [
        piece[:, :ff].astype(f32) for piece in cut(ffn_columns, [ff_wide] * 3)
    ]
    grad_ffn_input = jnp.stack([grad_gate, grad_up], axis=1)
    select_shares, gain_shares, grad_vectors = cut(last_columns, [2 * STATE, 4, vector_columns])
    shares = jnp.concatenate(
        [to_device(select_shares), jnp.broadcast_to(gain_shares[None], (tp, shard, 4))], axis=2
    )
    grad_select, grad_gains = cut(permute_sums(shares, 0)[0], [2 * STATE // tp, 4])
    grad_mamba_input = jnp.stack(
        [
            last_columns[:, HEAD + k * channels : HEAD + (k + 1) * channels].astype(f32)
            for k in range(3)
        ],
        axis=1,
    )
    grad_mamba_output, grad_query, grad_vectors = [
        v.astype(f32) for v in (grad_mamba_output, grad_query, grad_vectors)
    ]
    grad_vectors = grad_vectors.reshape(-1)[: 3 * channels].reshape(3, channels)
    return (
        layer_out_t.T[None],
        grad_tokens_t.T[None],
        grad_meta,
        grad_gains[:, 0],
        grad_query,
        grad_keyval,
        grad_attn_output,
        grad_gains[:, 1],
        grad_mamba_input,
        grad_select,
        grad_vectors[0],
        grad_vectors[1],
        grad_vectors[2],
        grad_mamba_output,
        grad_gains[:, 2],
        grad_gains[:, 3],
        grad_ffn_input,
        grad_ffn_output,
    )


def solution(mesh):
    rows = ("fsdp", "ctx")
    in_specs = (
        P("fsdp", ("ctx", "tp"), None),
        P("fsdp", None),
        P("fsdp", ("ctx", "tp"), None),
        P(rows, None),
        P(rows),
        P(rows, None),
        P(rows, None),
        P(rows, None),
        P(rows),
        P(rows, None, "tp"),
        P(rows, None),
        P("tp"),
        P("tp"),
        P("tp"),
        P(rows, "tp"),
        P(rows),
        P(rows),
        P(rows, None, None),
        P(rows, None),
    )
    out_specs = (
        P("fsdp", ("ctx", "tp"), None),
        P("fsdp", ("ctx", "tp"), None),
        P(rows, "tp"),
        P(rows),
        P(rows, "tp"),
        P(rows, "tp"),
        P(rows, "tp"),
        P(rows),
        P(rows, None, "tp"),
        P(rows, "tp"),
        P("tp"),
        P("tp"),
        P("tp"),
        P(rows, "tp"),
        P(rows),
        P(rows),
        P(rows, None, "tp"),
        P(rows, "tp"),
    )
    return jax.shard_map(
        per_device, mesh=mesh, in_specs=in_specs, out_specs=out_specs, check_vma=False
    )
```

```python
import functools

import jax
import jax.numpy as jnp
from jax import lax
from jax.experimental import pallas as pl
from jax.experimental.layout import Layout, with_layout_constraint
from jax.experimental.pallas import tpu as pltpu
from jax.sharding import PartitionSpec as P

HEAD_SIZE = 64
STATE = 16
WIN = 1024
SUB = 4
TILE = 128
HEAD = 128

bf16 = jnp.bfloat16
f32 = jnp.float32
epsilon = 1e-05
masked_score = -1e30


def mm(a, b):
    return lax.dot_general(a, b, (((1,), (0,)), ((), ())), preferred_element_type=f32)


def mm_nt(a, b):
    return lax.dot_general(a, b, (((1,), (1,)), ((), ())), preferred_element_type=f32)


def iota(shape, dim):
    return lax.broadcasted_iota(jnp.int32, shape, dim)


def split_mm(a, b):
    high = b.astype(bf16)
    return mm(a, high) + mm(a, (b - high.astype(f32)).astype(bf16))


def ones_where(cond):
    return jnp.where(cond, 1.0, 0.0)


def softplus(v):
    return jnp.maximum(v, 0.0) + jnp.log1p(jnp.exp(-jnp.abs(v)))


def group_mask(rows, columns, row_unit, column_unit):
    return iota((rows, columns), 0) // row_unit == iota((rows, columns), 1) // column_unit


def scan_tables():
    rows = 2 * TILE + TILE // SUB
    width = TILE // SUB * STATE
    row = iota((rows, TILE), 0)
    column = iota((rows, TILE), 1)
    token = row % TILE
    same = token // SUB == column // SUB
    upto = (row < TILE) & same & (column <= token)
    after = (row >= TILE) & (row < 2 * TILE) & same & (column > token)
    whole = (row >= 2 * TILE) & (row - 2 * TILE == column // SUB)
    places = iota((STATE, width), 0) == iota((STATE, width), 1) % STATE
    tables = (upto | after | whole, group_mask(width, TILE, STATE, SUB), places)
    sums, mask, places = [ones_where(table).astype(bf16) for table in tables]
    return sums, mask, mask.T, places, places.T


def part(mixed, k):
    channels = (mixed.shape[1] - HEAD) // 3
    return mixed[:, HEAD + k * channels : HEAD + (k + 1) * channels].astype(f32)


def both_ways(mixed):
    head = mixed[:, :HEAD]
    return head, head.astype(f32).T.astype(bf16)


def decays(step_raw, bias_ref, rate_ref, alive_last_ref, sums_ref):
    raw = step_raw + bias_ref[...]
    step = softplus(raw)
    log_decay = -step * rate_ref[...]
    sums = split_mm(sums_ref[...], log_decay)
    upto = jnp.exp(sums[:TILE])
    after = sums[TILE : 2 * TILE]
    block = jnp.exp(sums[2 * TILE :]) * alive_last_ref[...]
    return raw, step, log_decay, upto, after, block


def in_blocks(values_t, factor_t, mask):
    kept = values_t * factor_t.astype(bf16)
    return jnp.concatenate([kept] * (TILE // SUB), axis=0) * mask[...]


def spread(values, factor, mask_t, places):
    return mm(values * factor.astype(bf16), places[...]).astype(bf16) * mask_t[...]


def fold(wide, factor, mask_t, places_t):
    return mm(wide.astype(bf16) * mask_t[...], places_t[...]) * factor


def pairs(aux_ref, aux_t_ref, lower):
    row, column = iota((TILE, TILE), 0), iota((TILE, TILE), 1)
    order = column <= row if lower else column >= row
    return (row // SUB == column // SUB) & order & (aux_ref[:, 2:3] == aux_t_ref[2:3, :])


def run_states(state, local_ref, block_ref, keep=None):
    def one(k, state):
        if keep is not None:
            keep[pl.ds(pl.multiple_of(k * STATE, STATE), STATE), :] = state.astype(bf16)
        return block_ref[pl.ds(k, 1), :] * state + local_ref[pl.ds(pl.multiple_of(k * STATE, STATE), STATE), :]

    return lax.fori_loop(0, TILE // SUB, one, state, unroll=True)


def end_state_kernel(
    mixed, aux, aux_t, alive_last, bias, rate, sums_table, mask, mask_t, places, places_t, end, state, local, block
):
    @pl.when(pl.program_id(0) == 0)
    def _():
        state[...] = jnp.zeros_like(state)

    _, maps_t = both_ways(mixed)
    raw, step, log_decay, upto, after, total = decays(
        part(mixed, 2), bias, rate, alive_last, sums_table
    )
    driven = (jnp.exp(after) * step * part(mixed, 0)).astype(bf16)
    local[...] = mm(in_blocks(maps_t[:STATE], aux_t[1:2, :], mask), driven)
    block[...] = total
    state[...] = run_states(state[...], local, block)
    end[...] = state[...]


def forward_kernel(
    mixed,
    aux,
    aux_t,
    alive_last,
    bias,
    rate,
    sums_table,
    mask,
    mask_t,
    places,
    places_t,
    skip,
    start,
    gated,
    states,
    end,
    state,
    local,
    block,
):
    @pl.when(pl.program_id(0) == 0)
    def _():
        state[...] = start[...]

    maps, maps_t = both_ways(mixed)
    raw, step, log_decay, upto, after, total = decays(
        part(mixed, 2), bias, rate, alive_last, sums_table
    )
    x = part(mixed, 0)
    driven = (jnp.exp(after) * step * x).astype(bf16)
    local[...] = mm(in_blocks(maps_t[:STATE], aux_t[1:2, :], mask), driven)
    block[...] = total
    state[...] = run_states(state[...], local, block, states)
    end[...] = state[...]
    out_part = maps[:, STATE : 2 * STATE]
    cross = jnp.where(pairs(aux, aux_t, True), mm(out_part, maps_t[:STATE]), 0.0).astype(bf16)
    y = (
        upto * mm(spread(out_part, aux[:, 0:1], mask_t, places), states[...])
        + jnp.exp(-after) * mm(cross, driven)
        + skip[...] * x
    )
    gates = part(mixed, 1)
    gated[...] = (y * gates * lax.logistic(gates)).astype(bf16)


def back_run(carry, local_ref, block_ref, keep, states=None, bound=None):
    count = TILE // SUB

    def one(i, carry):
        k = count - 1 - i
        rows = pl.ds(pl.multiple_of(k * STATE, STATE), STATE)
        if keep is not None:
            keep[rows, :] = carry[0].astype(bf16)
            bound[pl.ds(k, 1), :] = carry[1]
        new = block_ref[pl.ds(k, 1), :] * carry[0] + local_ref[rows, :]
        if keep is None:
            return (new, carry[1])
        return (new, jnp.sum(new * states[rows, :].astype(f32), axis=0, keepdims=True))

    return lax.fori_loop(0, count, one, carry, unroll=True)


def end_adjoint_kernel(
    count,
    gated_grad,
    mixed,
    aux,
    aux_t,
    alive_last,
    bias,
    rate,
    sums_table,
    mask,
    mask_t,
    places,
    places_t,
    source,
    end,
    total_out,
    state,
    local,
    block,
    own,
    sent,
    got,
    loads,
    send_sems,
    recv_sems,
):
    tile, tiles = pl.program_id(0), pl.num_programs(0)
    begin, step_line, finish = line_sum_steps(
        count, source.at[: total_out.shape[0]], own, sent, got, total_out, loads, send_sems, recv_sems
    )

    @pl.when(tile == 0)
    def _():
        begin()
        state[...] = jnp.zeros_like(state)

    for k in range(1, count - 1):

        @pl.when(tile == tiles * k // (count - 1))
        def _():
            step_line(k)

    _, maps_t = both_ways(mixed)
    raw, step, log_decay, upto, after, total = decays(
        part(mixed, 2), bias, rate, alive_last, sums_table
    )
    gates = part(mixed, 1)
    dy = gated_grad[...] * gates * lax.logistic(gates)
    local[...] = mm(in_blocks(maps_t[STATE : 2 * STATE], aux_t[0:1, :], mask), (upto * dy).astype(bf16))
    block[...] = total
    state[...] = back_run((state[...], jnp.zeros((1, state.shape[1]), f32)), local, block, None)[0]
    end[...] = state[...]

    @pl.when(tile == tiles - 1)
    def _():
        step_line(count - 1)
        finish()


def backward_kernel(
    count,
    gated_grad,
    mixed,
    states,
    aux,
    aux_t,
    alive_last,
    bias,
    rate,
    sums_table,
    mask,
    mask_t,
    places,
    places_t,
    skip,
    start,
    final,
    source,
    mix_grad,
    sums,
    total_out,
    state,
    local,
    block,
    adjoint,
    bound,
    edge,
    own,
    sent,
    got,
    loads,
    send_sems,
    recv_sems,
):
    tile, tiles = pl.program_id(0), pl.num_programs(0)
    begin, step_line, finish = line_sum_steps(
        count, source.at[source.shape[0] - total_out.shape[0] :], own, sent, got, total_out, loads, send_sems, recv_sems
    )

    @pl.when(tile == 0)
    def _():
        begin()
        state[...] = start[...]
        edge[...] = jnp.sum(start[...] * final[...], axis=0, keepdims=True)
        sums[...] = jnp.zeros_like(sums)

    for k in range(1, count - 1):

        @pl.when(tile == tiles * k // (count - 1))
        def _():
            step_line(k)

    maps, maps_t = both_ways(mixed)
    raw, step, log_decay, upto, after, total = decays(
        part(mixed, 2), bias, rate, alive_last, sums_table
    )
    channels = state.shape[1]
    x = part(mixed, 0)
    decay_after = jnp.exp(after)
    grow = jnp.exp(-after)
    driven = (decay_after * step * x).astype(bf16)
    in_part, out_part = maps[:, :STATE], maps[:, STATE : 2 * STATE]
    in_part_t, out_part_t = maps_t[:STATE], maps_t[STATE : 2 * STATE]
    lower, upper = pairs(aux, aux_t, True), pairs(aux, aux_t, False)
    cross = jnp.where(lower, mm(out_part, in_part_t), 0.0).astype(bf16)
    cross_t = jnp.where(upper, mm(in_part, out_part_t), 0.0).astype(bf16)
    y = upto * mm(spread(out_part, aux[:, 0:1], mask_t, places), states[...]) + grow * mm(cross, driven)
    gates = part(mixed, 1)
    sigma = lax.logistic(gates)
    grad = gated_grad[...]
    dy = grad * gates * sigma
    mix_grad[:, HEAD + channels : HEAD + 2 * channels] = (
        grad * (y + skip[...] * x) * (sigma * (1.0 + gates * (1.0 - sigma)))
    ).astype(bf16)
    dy_low = (upto * dy).astype(bf16)
    dy_grown = (grow * dy).astype(bf16)
    local[...] = mm(in_blocks(out_part_t, aux_t[0:1, :], mask), dy_low)
    block[...] = total
    new_state, new_edge = back_run((state[...], edge[...]), local, block, adjoint, states, bound)
    state[...] = new_state
    edge[...] = new_edge
    du = decay_after * (
        mm(spread(in_part, aux[:, 1:2], mask_t, places), adjoint[...]) + mm(cross_t, dy_grown)
    )
    out_grad = fold(mm_nt(dy_low, states[...]), aux[:, 0:1], mask_t, places_t)
    in_grad = fold(mm_nt(driven, adjoint[...]), aux[:, 1:2], mask_t, places_t)
    cross_grad = jnp.where(lower, mm_nt(dy_grown, driven), 0.0).astype(bf16)
    cross_grad_t = jnp.where(upper, mm_nt(driven, dy_grown), 0.0).astype(bf16)
    out_grad = out_grad + mm(cross_grad, in_part)
    in_grad = in_grad + mm(cross_grad_t, out_part)
    mix_grad[:, :HEAD] = jnp.concatenate(
        [in_grad, out_grad, jnp.zeros((TILE, HEAD - 2 * STATE), f32)], axis=1
    ).astype(bf16)
    flow = dy * y - step * x * du
    to_tokens = ones_where(group_mask(TILE, TILE // SUB, SUB, 1)) * aux[:, 1:2]
    decay_grad = aux[:, 3:4] * (
        mm(ones_where(upper).astype(bf16), flow.astype(bf16))
        + split_mm(to_tokens.astype(bf16), bound[...])
    )
    step_grad = (x * du - rate[...] * decay_grad) * lax.logistic(raw)
    mix_grad[:, HEAD : HEAD + channels] = (skip[...] * dy + step * du).astype(bf16)
    mix_grad[:, HEAD + 2 * channels :] = step_grad.astype(bf16)
    sums[0:1, :] += jnp.sum(step_grad, axis=0, keepdims=True)
    sums[1:2, :] += jnp.sum(decay_grad * log_decay, axis=0, keepdims=True)
    sums[2:3, :] += jnp.sum(dy * x, axis=0, keepdims=True)

    @pl.when(tile == tiles - 1)
    def _():
        step_line(count - 1)
        finish()


def scan_specs(tokens, channels, back):
    tiles = tokens // TILE
    at = (lambda i: tiles - 1 - i) if back else (lambda i: i)

    def fixed(*shape):
        return pl.BlockSpec(shape, lambda i: (0,) * len(shape))

    width = TILE // SUB * STATE
    mixed = pl.BlockSpec((TILE, HEAD + 3 * channels), lambda i: (at(i), 0))
    rows = pl.BlockSpec((TILE, channels), lambda i: (at(i), 0))
    states = pl.BlockSpec((width, channels), lambda i: (at(i), 0))
    side = [
        pl.BlockSpec((TILE, 8), lambda i: (at(i), 0)),
        pl.BlockSpec((8, TILE), lambda i: (0, at(i))),
        pl.BlockSpec((TILE // SUB, 1), lambda i: (at(i), 0)),
        fixed(1, channels),
        fixed(1, channels),
        fixed(2 * TILE + TILE // SUB, TILE),
        fixed(width, TILE),
        fixed(TILE, width),
        fixed(STATE, width),
        fixed(width, STATE),
    ]
    return tiles, mixed, rows, states, side, fixed(1, channels), fixed(STATE, channels)


def scan_scratch(channels):
    return [
        pltpu.VMEM((STATE, channels), f32),
        pltpu.VMEM((TILE // SUB * STATE, channels), f32),
        pltpu.VMEM((TILE // SUB, channels), f32),
    ]


def scan_call(kernel, name, tiles, in_specs, out_specs, out_shape, scratch, flops, collective=None, room=16):
    return pl.pallas_call(
        kernel,
        name=name,
        grid=(tiles,),
        in_specs=in_specs,
        out_specs=out_specs,
        scratch_shapes=scratch,
        out_shape=out_shape,
        compiler_params=pltpu.CompilerParams(
            vmem_limit_bytes=room << 20,
            dimension_semantics=("arbitrary",),
            collective_id=collective,
            has_side_effects=collective is not None,
        ),
        cost_estimate=pl.CostEstimate(flops=flops, bytes_accessed=flops // 100, transcendentals=0),
    )


def scan_aux(segment, before):
    count = segment.shape[0]
    blocks = segment.reshape(count // SUB, SUB)
    ends = jnp.concatenate([before[None], blocks[:-1, -1]])
    alive = (blocks == ends[:, None]).reshape(-1).astype(f32)
    tail = (blocks == blocks[:, -1:]).reshape(-1).astype(f32)
    joined = (segment == jnp.concatenate([before[None], segment[:-1]])).astype(f32)
    zero = jnp.zeros_like(alive)
    aux_t = jnp.stack([alive, tail, segment.astype(f32), joined, zero, zero, zero, zero])
    last = (blocks[:, -1] == ends).astype(f32)[:, None]
    return aux_t.T, aux_t, last


def end_state(mixed, side):
    tokens, channels = mixed.shape[0], (mixed.shape[1] - HEAD) // 3
    tiles, mixed_s, rows, states, side_s, row, state = scan_specs(tokens, channels, False)
    return scan_call(
        end_state_kernel,
        "end_state",
        tiles,
        [mixed_s, *side_s],
        state,
        jax.ShapeDtypeStruct((STATE, channels), f32),
        scan_scratch(channels),
        10**7,
    )(mixed, *side)


def forward_scan(mixed, side, skip, start):
    tokens, channels = mixed.shape[0], (mixed.shape[1] - HEAD) // 3
    tiles, mixed_s, rows, states, side_s, row, state = scan_specs(tokens, channels, False)
    return scan_call(
        forward_kernel,
        "forward_scan",
        tiles,
        [mixed_s, *side_s, row, state],
        [rows, states, state],
        [
            jax.ShapeDtypeStruct((tokens, channels), bf16),
            jax.ShapeDtypeStruct((tokens // SUB * STATE, channels), bf16),
            jax.ShapeDtypeStruct((STATE, channels), f32),
        ],
        scan_scratch(channels),
        10**7,
    )(mixed, *side, skip, start)


def end_adjoint(gated_grad, mixed, side, source, height, count, collective):
    each = source.shape[1] // count
    tokens, channels = mixed.shape[0], (mixed.shape[1] - HEAD) // 3
    tiles, mixed_s, rows, states, side_s, row, state = scan_specs(tokens, channels, True)
    return scan_call(
        functools.partial(end_adjoint_kernel, count),
        "end_adjoint",
        tiles,
        [rows, mixed_s, *side_s, pl.BlockSpec(memory_space=pl.ANY)],
        [state, pl.BlockSpec((height, each), lambda i: (0, 0))],
        [
            jax.ShapeDtypeStruct((STATE, channels), f32),
            jax.ShapeDtypeStruct((height, each), f32),
        ],
        scan_scratch(channels) + line_sum_scratch(count, height, each),
        10**10,
        collective,
        24,
    )(gated_grad, mixed, *side, source)


def backward_scan(gated_grad, mixed, states, side, skip, start, final, source, height, count, collective):
    each = source.shape[1] // count
    tokens, channels = mixed.shape[0], (mixed.shape[1] - HEAD) // 3
    tiles, mixed_s, rows, states_s, side_s, row, state = scan_specs(tokens, channels, True)
    return scan_call(
        functools.partial(backward_kernel, count),
        "backward_scan",
        tiles,
        [
            rows,
            mixed_s,
            states_s,
            *side_s,
            row,
            state,
            state,
            pl.BlockSpec(memory_space=pl.ANY),
        ],
        [
            mixed_s,
            pl.BlockSpec((8, channels), lambda i: (0, 0)),
            pl.BlockSpec((height, each), lambda i: (0, 0)),
        ],
        [
            jax.ShapeDtypeStruct(mixed.shape, bf16),
            jax.ShapeDtypeStruct((8, channels), f32),
            jax.ShapeDtypeStruct((height, each), f32),
        ],
        scan_scratch(channels)
        + [
            pltpu.VMEM((TILE // SUB * STATE, channels), bf16),
            pltpu.VMEM((TILE // SUB, channels), f32),
            pltpu.VMEM((1, channels), f32),
        ]
        + line_sum_scratch(count, height, each),
        36 * 10**9,
        collective,
        48,
    )(gated_grad, mixed, states, *side, skip, start, final, source)


MESH = pl.DeviceIdType.MESH
COMM = {"has_side_effects": True}


def neighbour_barrier(count):
    place = lax.axis_index("tp")
    ready = pltpu.get_barrier_semaphore()
    sides = ((place < count - 1, place + 1), (place > 0, place - 1))
    for there, other in sides:

        @pl.when(there)
        def _():
            pl.semaphore_signal(ready, inc=1, device_id={"tp": other}, device_id_type=MESH)

    peers = jnp.where(place < count - 1, 1, 0) + jnp.where(place > 0, 1, 0)
    pl.semaphore_wait(ready, peers)


def line_steps(count, source, target, copies, send_sems, recv_sems):
    place = lax.axis_index("tp")
    width = source.shape[1]

    def at(owner):
        return target.at[:, pl.ds(pl.multiple_of(owner * width, width), width)]

    def local():
        return pltpu.make_async_copy(source, at(place), copies)

    def remote(side, step):
        owner = place - step if side == 0 else place + step
        return pltpu.make_async_remote_copy(
            src_ref=source if step == 0 else at(owner),
            dst_ref=at(owner),
            send_sem=send_sems.at[side, step],
            recv_sem=recv_sems.at[side, step],
            device_id={"tp": place + 1 if side == 0 else place - 1},
            device_id_type=MESH,
        )

    def has(side, step):
        return place - step >= 0 if side == 0 else place + step < count

    def neighbour(side):
        return place < count - 1 if side == 0 else place > 0

    def send(side, step):
        @pl.when(neighbour(side) & has(side, step))
        def _():
            remote(side, step).start()

    def receive(side, step):
        @pl.when(has(side, step + 1))
        def _():
            remote(side, step).wait_recv()

    def start():
        neighbour_barrier(count)
        local().start()
        for side in (0, 1):
            send(side, 0)

    def step(k):
        for side in (0, 1):
            receive(side, k - 1)
        for side in (0, 1):
            if k < count - 1:
                send(side, k)

    step.send, step.receive = send, receive

    def finish():
        for k in range(count - 1):
            for side in (0, 1):

                @pl.when(neighbour(side) & has(side, k))
                def _():
                    remote(side, k).wait_send()

        local().wait()

    return start, step, finish


def line_scratch(count):
    return [
        pltpu.SemaphoreType.DMA,
        pltpu.SemaphoreType.DMA((2, count - 1)),
        pltpu.SemaphoreType.DMA((2, count - 1)),
    ]


def line_gather_kernel(count, source, target, copies, send_sems, recv_sems):
    start, step, finish = line_steps(count, source, target, copies, send_sems, recv_sems)
    start()
    for k in range(1, count):
        step(k)
    finish()


def line_gather(source, count, collective):
    return pl.pallas_call(
        functools.partial(line_gather_kernel, count),
        name="line_gather",
        in_specs=[pl.BlockSpec(memory_space=pl.ANY)],
        out_specs=pl.BlockSpec(memory_space=pl.ANY),
        out_shape=jax.ShapeDtypeStruct((source.shape[0], source.shape[1] * count), source.dtype),
        scratch_shapes=line_scratch(count),
        compiler_params=pltpu.CompilerParams(collective_id=collective, has_side_effects=True),
    )(source)


def line_sum_steps(count, source, own, sent, got, total, loads, send_sems, recv_sems):
    place = lax.axis_index("tp")
    width = total.shape[1]

    def whose(side, step):
        return place + (count - step) if side == 0 else place - (count - step)

    def sends(side, step):
        owner = whose(side, step)
        return owner < count if side == 0 else owner >= 0

    def receives(side, step):
        return (place >= 1) & (place <= step) if side == 0 else (place <= count - 2) & (place >= count - 1 - step)

    def load(side, step):
        owner = whose(side, step)
        return pltpu.make_async_copy(
            source.at[:, pl.ds(pl.multiple_of(owner * width, width), width)],
            sent.at[side, step - 1],
            loads.at[side, step - 1],
        )

    def mine():
        return pltpu.make_async_copy(
            source.at[:, pl.ds(pl.multiple_of(place * width, width), width)], own, loads.at[2, 0]
        )

    def remote(side, step):
        return pltpu.make_async_remote_copy(
            src_ref=sent.at[side, step - 1],
            dst_ref=got.at[side, step - 1],
            send_sem=send_sems.at[side, step - 1],
            recv_sem=recv_sems.at[side, step - 1],
            device_id={"tp": place + 1 if side == 0 else place - 1},
            device_id_type=MESH,
        )

    def start():
        neighbour_barrier(count)
        mine().start()
        for step in range(1, count):
            for side in (0, 1):

                @pl.when(sends(side, step))
                def _():
                    load(side, step).start()

        step_out(1)

    def step_out(step):
        for side in (0, 1):

            @pl.when(sends(side, step))
            def _():
                load(side, step).wait()

            if step > 1:

                @pl.when(sends(side, step) & receives(side, step - 1))
                def _():
                    sent[side, step - 1] = (
                        sent[side, step - 1].astype(f32) + got[side, step - 2].astype(f32)
                    ).astype(bf16)

            @pl.when(sends(side, step))
            def _():
                remote(side, step).start()

    def step(k):
        for side in (0, 1):

            @pl.when(receives(side, k))
            def _():
                remote(side, k).wait_recv()

        if k < count - 1:
            step_out(k + 1)

    def finish():
        mine().wait()
        total[...] = own[...].astype(f32)
        for side in (0, 1):

            @pl.when(receives(side, count - 1))
            def _():
                total[...] = total[...] + got[side, count - 2].astype(f32)

            for k in range(1, count):

                @pl.when(sends(side, k))
                def _():
                    remote(side, k).wait_send()

    return start, step, finish


def line_sum_scratch(count, height, width):
    return [
        pltpu.VMEM((height, width), bf16),
        pltpu.VMEM((2, count - 1, height, width), bf16),
        pltpu.VMEM((2, count - 1, height, width), bf16),
        pltpu.SemaphoreType.DMA((3, count - 1)),
        pltpu.SemaphoreType.DMA((2, count - 1)),
        pltpu.SemaphoreType.DMA((2, count - 1)),
    ]


def line_sum_kernel(count, source, total, own, sent, got, loads, send_sems, recv_sems):
    start, step, finish = line_sum_steps(
        count, source, own, sent, got, total, loads, send_sems, recv_sems
    )
    start()
    for k in range(1, count):
        step(k)
    finish()


def line_sum(source, count, collective):
    height, width = source.shape[0], source.shape[1] // count
    return pl.pallas_call(
        functools.partial(line_sum_kernel, count),
        name="line_sum",
        in_specs=[pl.BlockSpec(memory_space=pl.ANY)],
        out_specs=pl.BlockSpec(memory_space=pltpu.VMEM),
        out_shape=jax.ShapeDtypeStruct((height, width), f32),
        scratch_shapes=line_sum_scratch(count, height, width),
        compiler_params=pltpu.CompilerParams(
            vmem_limit_bytes=24 << 20, collective_id=collective, has_side_effects=True
        ),
        cost_estimate=pl.CostEstimate(flops=5 * 10**10, bytes_accessed=1 << 24, transcendentals=0),
    )(source)


def feed_kernel(
    count,
    blocks,
    source,
    other,
    weights,
    group,
    gate_up_grad,
    hidden,
    part_sum,
    maps,
    tokens,
    grads,
    grad_rows,
    hidden_rows,
    partial,
    copies,
    loads,
    stores,
    send_sems,
    recv_sems,
):
    place = lax.axis_index("tp")
    start, step, finish = line_steps(count, source, group, copies, send_sems, recv_sems)
    receive, send = step.receive, step.send
    ff = hidden.shape[1]
    width = source.shape[1]
    near = jnp.minimum(place, count - 1 - place)

    def owner_of(q):
        spread_out = jnp.where(q % 2 == 1, place - (q + 1) // 2, place + q // 2)
        rest = jnp.where(place < count - 1 - place, q, count - 1 - q)
        return jnp.where(q <= 2 * near, spread_out, rest)

    def reach(q):
        return jnp.where(q <= 2 * near, (q + 1) // 2, q - near)

    def load(what, where, k):
        return pltpu.make_async_copy(what, where, loads.at[k])

    def columns(array, owner):
        return array.at[:, pl.ds(pl.multiple_of(owner * width, width), width)]

    def store(q):
        owner, slot = owner_of(q), q % 2
        at = pl.ds(pl.multiple_of(owner * width, width), width)
        return [
            pltpu.make_async_copy(grad_rows.at[slot], gate_up_grad.at[at, :], stores.at[slot, 0]),
            pltpu.make_async_copy(hidden_rows.at[slot], hidden.at[at, :], stores.at[slot, 1]),
            pltpu.make_async_copy(partial.at[slot], columns(part_sum, owner), stores.at[slot, 2]),
        ]

    start()
    load(other, grads, 2).start()
    load(weights.at[:, : 3 * ff], maps, 0).start()

    def one(q, carry):
        owner, slot = owner_of(q), q % 2
        for far in range(1, count):

            @pl.when((reach(q) == far) & (reach(q - 1) < far))
            def _():
                for side in (0, 1):
                    receive(side, far - 1)
                for side in (0, 1):
                    if far < count - 1:
                        send(side, far)

        @pl.when(q == 0)
        def _():
            load(source, tokens, 1).start()
            load(source, tokens, 1).wait()

        @pl.when(q > 0)
        def _():
            load(columns(group, owner), tokens, 1).start()
            load(columns(group, owner), tokens, 1).wait()

        @pl.when(q == 0)
        def _():
            load(other, grads, 2).wait()
            load(weights.at[:, : 3 * ff], maps, 0).wait()

        @pl.when(q > 1)
        def _():
            for copy in store(q - 2):
                copy.wait()

        rows = tokens[...].T
        outs = columns(grads, owner)[...].T
        for begin, wide in blocks:
            gate = mm(rows, maps[:, begin : begin + wide])
            up = mm(rows, maps[:, ff + begin : ff + begin + wide])
            grad = mm(outs, maps[:, 2 * ff + begin : 2 * ff + begin + wide])
            sigma = lax.logistic(gate)
            active = gate * sigma
            hidden_rows[slot, :, begin : begin + wide] = (active * up).astype(bf16)
            grad_rows[slot, :, begin : begin + wide] = (
                grad * up * (sigma * (1.0 + gate * (1.0 - sigma)))
            ).astype(bf16)
            grad_rows[slot, :, ff + begin : ff + begin + wide] = (grad * active).astype(bf16)
        partial[slot] = mm_nt(maps[:, : 2 * ff], grad_rows[slot]).astype(bf16)
        for copy in store(q):
            copy.start()
        return carry

    lax.fori_loop(0, count, one, 0)
    for q in (count - 2, count - 1):
        for copy in store(q):
            copy.wait()
    finish()


def feed_forward(source, other, weights, ff, count, collective):
    depth, width = source.shape
    blocks = []
    begin = 0
    while begin < ff:
        blocks.append((begin, min(256, ff - begin)))
        begin = begin + 256
    anywhere = pl.BlockSpec(memory_space=pl.ANY)
    return pl.pallas_call(
        functools.partial(feed_kernel, count, tuple(blocks)),
        name="feed_forward",
        in_specs=[anywhere] * 3,
        out_specs=[anywhere] * 4,
        out_shape=[
            jax.ShapeDtypeStruct((depth, width * count), bf16),
            jax.ShapeDtypeStruct((width * count, 2 * ff), bf16),
            jax.ShapeDtypeStruct((width * count, ff), bf16),
            jax.ShapeDtypeStruct((depth, width * count), bf16),
        ],
        scratch_shapes=[
            pltpu.VMEM((depth, 3 * ff), bf16),
            pltpu.VMEM((depth, width), bf16),
            pltpu.VMEM((depth, width * count), bf16),
            pltpu.VMEM((2, width, 2 * ff), bf16),
            pltpu.VMEM((2, width, ff), bf16),
            pltpu.VMEM((2, depth, width), bf16),
            pltpu.SemaphoreType.DMA,
            pltpu.SemaphoreType.DMA((3,)),
            pltpu.SemaphoreType.DMA((2, 3)),
            pltpu.SemaphoreType.DMA((2, count - 1)),
            pltpu.SemaphoreType.DMA((2, count - 1)),
        ],
        compiler_params=pltpu.CompilerParams(
            vmem_limit_bytes=56 << 20, collective_id=collective, has_side_effects=True
        ),
    )(source, other, weights)


def wide_sum_kernel(
    count,
    ups,
    downs,
    tokens,
    others,
    gate_up_grad,
    hidden,
    hidden_rows,
    maps,
    source,
    wide,
    out_part,
    total,
    own,
    sent,
    got,
    loads,
    send_sems,
    recv_sems,
):
    step, steps = pl.program_id(0), pl.num_programs(0)
    start, advance, finish = line_sum_steps(
        count, source, own, sent, got, total, loads, send_sems, recv_sems
    )

    @pl.when(step == 0)
    def _():
        start()

    for k in range(1, count - 1):

        @pl.when(step == steps * k // (count - 1))
        def _():
            advance(k)

    @pl.when(step < ups)
    def _():
        wide[...] = mm(tokens[...], gate_up_grad[...]).astype(bf16)

    @pl.when((step >= ups) & (step < ups + downs))
    def _():
        wide[...] = mm(others[...], hidden[...]).astype(bf16)

    @pl.when(step >= ups + downs)
    def _():
        out_part[...] = mm_nt(maps[...], hidden_rows[...]).astype(bf16)

    @pl.when(step == steps - 1)
    def _():
        advance(count - 1)
        finish()


def wide_sum(tokens, others, gate_up_grad, hidden, maps, source, count, collective):
    depth, span = tokens.shape
    ff = hidden.shape[1]
    ups, downs, strip = 2 * ff // 128, ff // 128, 320
    strips = depth // strip
    each = source.shape[1] // count

    def strip_of(j):
        return jnp.clip(j - ups - downs, 0, strips - 1)

    def whole(*shape):
        return pl.BlockSpec(shape, lambda j: (0, 0), pipeline_mode=pl.Buffered(1))

    return pl.pallas_call(
        functools.partial(wide_sum_kernel, count, ups, downs),
        name="wide_sum",
        grid=(ups + downs + strips,),
        in_specs=[
            whole(depth, span),
            whole(depth, span),
            pl.BlockSpec((span, 128), lambda j: (0, jnp.minimum(j, ups - 1))),
            pl.BlockSpec((span, 128), lambda j: (0, jnp.clip(j - ups, 0, downs - 1))),
            whole(span, ff),
            pl.BlockSpec((strip, ff), lambda j: (strip_of(j), 2)),
            pl.BlockSpec(memory_space=pl.ANY),
        ],
        out_specs=[
            pl.BlockSpec((depth, 128), lambda j: (0, jnp.minimum(j, ups + downs - 1))),
            pl.BlockSpec((strip, span), lambda j: (strip_of(j), 0)),
            pl.BlockSpec((depth, each), lambda j: (0, 0)),
        ],
        out_shape=[
            jax.ShapeDtypeStruct((depth, 3 * ff), bf16),
            jax.ShapeDtypeStruct((depth, span), bf16),
            jax.ShapeDtypeStruct((depth, each), f32),
        ],
        scratch_shapes=line_sum_scratch(count, depth, each),
        compiler_params=pltpu.CompilerParams(
            vmem_limit_bytes=48 << 20,
            dimension_semantics=("arbitrary",),
            collective_id=collective,
            has_side_effects=True,
        ),
    )(tokens, others, gate_up_grad, hidden, hidden, maps, source)


def attend_kernel(
    group,
    count,
    query_t,
    key_t,
    value_t,
    bias,
    source,
    out_t,
    log_total,
    total_out,
    own,
    sent,
    got,
    loads,
    send_sems,
    recv_sems,
):
    head, heads = pl.program_id(0), pl.num_programs(0)
    start, step, finish = line_sum_steps(
        count, source, own, sent, got, total_out, loads, send_sems, recv_sems
    )

    @pl.when(head == 0)
    def _():
        start()

    @pl.when(head == heads - 2)
    def _():
        step(1)

    keys = key_t[...].T
    values_t = value_t[...]
    for g in range(group):
        at = slice(g * HEAD_SIZE, (g + 1) * HEAD_SIZE)
        scores = mm(keys, query_t[at, :] * 0.125) + bias[...]
        top = jnp.max(scores, axis=0, keepdims=True)
        probs = jnp.exp(scores - top)
        total = jnp.sum(probs, axis=0, keepdims=True)
        out_t[at, :] = (mm(values_t, probs.astype(bf16)) / total).astype(bf16)
        log_total[g : g + 1, :] = top + jnp.log(total)

    @pl.when(head == heads - 1)
    def _():
        for k in range(2, count):
            step(k)
        finish()


def attend_back_kernel(
    group,
    count,
    query_t,
    key_t,
    value_t,
    bias,
    out_t,
    log_total,
    grad_t,
    source,
    query_grad_t,
    keyval_grad_t,
    target,
    copies,
    send_sems,
    recv_sems,
):
    head, heads = pl.program_id(0), pl.num_programs(0)
    start, step, finish = line_steps(count, source, target, copies, send_sems, recv_sems)

    @pl.when(head == 0)
    def _():
        start()

    @pl.when(head == heads - 2)
    def _():
        step(1)

    keys_t = key_t[...]
    keys = keys_t.T
    values = value_t[...].T
    key_sum = jnp.zeros(keys_t.shape, f32)
    value_sum = jnp.zeros(keys_t.shape, f32)
    for g in range(group):
        at = slice(g * HEAD_SIZE, (g + 1) * HEAD_SIZE)
        query = query_t[at, :] * 0.125
        grad = grad_t[at, :]
        probs = jnp.exp(mm(keys, query) + bias[...] - log_total[g : g + 1, :])
        centre = jnp.sum(grad.astype(f32) * out_t[at, :].astype(f32), axis=0, keepdims=True)
        score_grad = (probs * (mm(values, grad) - centre)).astype(bf16)
        query_grad_t[at, :] = (mm(keys_t, score_grad) * 0.125).astype(bf16)
        key_sum = key_sum + mm_nt(query, score_grad)
        value_sum = value_sum + mm_nt(grad, probs.astype(bf16))
    keyval_grad_t[0] = key_sum.astype(bf16)
    keyval_grad_t[1] = value_sum.astype(bf16)

    @pl.when(head == heads - 1)
    def _():
        for k in range(2, count):
            step(k)
        finish()


def attend(query_t, keyval_t, bias, source, key_value_heads, count, collective):
    width, rows = query_t.shape
    keys = keyval_t.shape[1]
    group = width // HEAD_SIZE // key_value_heads
    kv = key_value_heads
    height, each = source.shape[0], source.shape[1] // count
    return pl.pallas_call(
        functools.partial(attend_kernel, group, count),
        name="attend",
        grid=(kv,),
        in_specs=[
            pl.BlockSpec((group * HEAD_SIZE, rows), lambda h: (h, 0)),
            pl.BlockSpec((HEAD_SIZE, keys), lambda h: (h, 0)),
            pl.BlockSpec((HEAD_SIZE, keys), lambda h: (h + kv, 0)),
            pl.BlockSpec((keys, rows), lambda h: (0, 0)),
            pl.BlockSpec(memory_space=pl.ANY),
        ],
        out_specs=[
            pl.BlockSpec((group * HEAD_SIZE, rows), lambda h: (h, 0)),
            pl.BlockSpec((None, 8, rows), lambda h: (h, 0, 0)),
            pl.BlockSpec((height, each), lambda h: (0, 0)),
        ],
        out_shape=[
            jax.ShapeDtypeStruct((width, rows), bf16),
            jax.ShapeDtypeStruct((kv, 8, rows), f32),
            jax.ShapeDtypeStruct((height, each), f32),
        ],
        scratch_shapes=line_sum_scratch(count, height, each),
        compiler_params=pltpu.CompilerParams(
            vmem_limit_bytes=56 << 20,
            dimension_semantics=("arbitrary",),
            collective_id=collective,
            has_side_effects=True,
        ),
    )(query_t, keyval_t, keyval_t, bias, source)


def attend_back(query_t, keyval_t, bias, out_t, log_total, grad_t, source, key_value_heads, count, collective):
    width, rows = query_t.shape
    keys = keyval_t.shape[1]
    group = width // HEAD_SIZE // key_value_heads
    kv = key_value_heads
    wide = pl.BlockSpec((group * HEAD_SIZE, rows), lambda h: (h, 0))
    head = pl.BlockSpec((HEAD_SIZE, keys), lambda h: (h, 0))
    anywhere = pl.BlockSpec(memory_space=pl.ANY)
    return pl.pallas_call(
        functools.partial(attend_back_kernel, group, count),
        name="attend_back",
        grid=(kv,),
        in_specs=[
            wide,
            head,
            pl.BlockSpec((HEAD_SIZE, keys), lambda h: (h + kv, 0)),
            pl.BlockSpec((keys, rows), lambda h: (0, 0)),
            wide,
            pl.BlockSpec((None, 8, rows), lambda h: (h, 0, 0)),
            wide,
            anywhere,
        ],
        out_specs=[wide, pl.BlockSpec((2, HEAD_SIZE, keys), lambda h: (0, h, 0)), anywhere],
        out_shape=[
            jax.ShapeDtypeStruct((width, rows), bf16),
            jax.ShapeDtypeStruct((2, kv * HEAD_SIZE, keys), bf16),
            jax.ShapeDtypeStruct((source.shape[0], source.shape[1] * count), source.dtype),
        ],
        scratch_shapes=line_scratch(count),
        compiler_params=pltpu.CompilerParams(
            vmem_limit_bytes=56 << 20,
            dimension_semantics=("arbitrary",),
            collective_id=collective,
            has_side_effects=True,
        ),
    )(query_t, keyval_t, keyval_t, bias, out_t, log_total, grad_t, source)


def rms_norm(values, gain):
    return values * lax.rsqrt(jnp.mean(values * values, axis=0, keepdims=True) + epsilon) * gain


def rms_back(values, gain, grad):
    scale = lax.rsqrt(jnp.mean(values * values, axis=0, keepdims=True) + epsilon)
    normal = values * scale
    weighted = grad * gain
    back = scale * (weighted - normal * jnp.mean(weighted * normal, axis=0, keepdims=True))
    return back, grad * normal


def dot(left, right, left_dim, right_dim):
    return lax.dot_general(
        left, right, (((left_dim,), (right_dim,)), ((), ())), preferred_element_type=f32
    )


def gather_rows(whole):
    return lax.all_gather(whole, ("fsdp", "ctx"), axis=0, tiled=True)


def by_rows(values):
    return with_layout_constraint(values, Layout((0, 1)))


def scatter_rows(whole):
    return by_rows(
        lax.psum_scatter(by_rows(whole), ("fsdp", "ctx"), scatter_dimension=0, tiled=True)
    )


def send(values, by):
    count = lax.axis_size("tp")
    return lax.ppermute(values, "tp", [(i, (i + by) % count) for i in range(count)])


def permute_gather(own):
    count = lax.axis_size("tp")
    return [own] + [send(own, k) for k in range(1, count)]


def in_order(pieces):
    count, place = lax.axis_size("tp"), lax.axis_index("tp")
    return jnp.concatenate(
        [lax.select_n(lax.rem(place - p + count, count), *pieces) for p in range(count)], axis=1
    )


def permute_sums(values, axis):
    count, place = lax.axis_size("tp"), lax.axis_index("tp")
    each = values.shape[axis] // count
    shares = [
        lax.dynamic_slice_in_dim(values, lax.rem(place + k, count) * each, each, axis)
        for k in range(count)
    ]
    total = shares[0].astype(f32)
    for k in (2, 1, 3):
        total = total + send(shares[k], k).astype(f32)
    return total


def permute_exchange(values):
    count, place = lax.axis_size("tp"), lax.axis_index("tp")
    shares = values.reshape(count, values.shape[0] // count, values.shape[1])
    pieces = [
        lax.dynamic_index_in_dim(shares, lax.rem(place + k, count), 0, False) for k in range(count)
    ]
    return [pieces[0]] + [send(pieces[k], k) for k in range(1, count)]


def cut(values, widths):
    pieces = []
    offset = 0
    for count in widths:
        pieces.append(values[:, offset : offset + count])
        offset = offset + count
    return pieces


def per_device(
    tokens,
    segments,
    cotangent,
    meta_tokens,
    gain_mix,
    query_weight,
    key_value_weight,
    attn_output,
    gain_attn,
    mamba_input,
    mamba_select,
    step_bias,
    decay_log,
    state_skip,
    mamba_output,
    gain_mamba,
    gain_ffn,
    ffn_input,
    ffn_output,
):
    tokens_t, segments, cotangent_t = tokens[0].T, segments[0], cotangent[0].T
    width, rows = tokens_t.shape
    shard = meta_tokens.shape[0]
    tp = lax.axis_size("tp")
    tp_index = lax.axis_index("tp")
    ctx_index = lax.axis_index("ctx")
    span = rows * tp
    query_width = query_weight.shape[1]
    keyval_width = key_value_weight.shape[1]
    heads = keyval_width // (2 * HEAD_SIZE)
    channels = mamba_input.shape[2]
    ff = ffn_input.shape[2] // tp
    ff_wide = -(-ff // 128) * 128
    meta_count = meta_tokens.shape[1]
    window = WIN + rows

    place_of = jnp.arange(HEAD, dtype=jnp.int32)[None]
    head = jnp.pad(mamba_select, ((0, 0), (0, HEAD - 2 * STATE)))
    for k, gain in enumerate((gain_mix, gain_attn, gain_mamba, gain_ffn)):
        head = jnp.where(place_of == 2 * STATE + k, gain[:, None], head)
    first = jnp.concatenate([head] + [mamba_input[:, k] for k in range(3)], axis=1)
    first, second_parts = lax.optimization_barrier(
        (first, (key_value_weight, meta_tokens, query_weight, mamba_output))
    )
    second = jnp.concatenate(second_parts, axis=1)
    first, second, tokens_t = lax.optimization_barrier((first, second, tokens_t))
    first = gather_rows(first)
    second = gather_rows(second)
    tokens_group_t = line_gather(tokens_t, tp, 0)
    late_cotangent_t, tokens_group_t = lax.optimization_barrier((cotangent_t, tokens_group_t))
    cotangent_pieces = permute_gather(late_cotangent_t)

    gain_columns = first[:, 2 * STATE : 2 * STATE + 4]
    keyval_map, meta_full, query_map, state_out_map = cut(
        second, [keyval_width, meta_count, query_width, channels]
    )
    attn_map = gather_rows(attn_output)
    gain_columns = gain_columns.astype(f32)
    mix_gain, attn_gain, mamba_gain, ffn_gain = [gain_columns[:, k : k + 1] for k in range(4)]

    residual = tokens_t.astype(f32)
    residual_group = tokens_group_t.astype(f32)
    normed_t = rms_norm(residual, mix_gain).astype(bf16)
    normed_group_t = rms_norm(residual_group, mix_gain).astype(bf16)
    meta_rows = meta_full.astype(f32)
    meta_normed_t = rms_norm(meta_rows, mix_gain).astype(bf16)

    mixed = dot(normed_group_t, first, 0, 0).astype(bf16)
    seg_current = lax.dynamic_slice_in_dim(segments, ctx_index * span, span, 0)
    seg_earlier = lax.dynamic_slice_in_dim(segments, jnp.maximum(ctx_index - 1, 0) * span, span, 0)
    seg_before = jnp.where(
        ctx_index > 0,
        lax.dynamic_index_in_dim(segments, jnp.maximum(ctx_index * span - 1, 0), 0, False),
        -1,
    )
    side = (
        *scan_aux(seg_current, seg_before),
        step_bias[None],
        jnp.exp(decay_log)[None],
        *scan_tables(),
    )
    skip_row = state_skip[None]
    state_end = end_state(mixed, side)
    state_end, late_up, late_down = lax.optimization_barrier((state_end, ffn_input, ffn_output))
    ffn_shards = [
        lax.dynamic_slice_in_dim(whole, tp_index * ff, ff, 1)
        for whole in (late_up[:, 0], late_up[:, 1], late_down)
    ]
    state_start = lax.ppermute(state_end, "ctx", [(0, 1)])

    query_t = dot(query_map, normed_t, 0, 0).astype(bf16)
    keyval_group_t = dot(keyval_map, normed_group_t, 0, 0).astype(bf16)
    meta_keyval_t = dot(keyval_map, meta_normed_t, 0, 0).astype(bf16)
    earlier_t = lax.ppermute(keyval_group_t, "ctx", [(0, 1)])

    gated, states, state_final = forward_scan(mixed, side, skip_row, state_start)
    third = jnp.concatenate(
        [jnp.pad(piece, ((0, 0), (0, ff_wide - ff))) for piece in ffn_shards] + [attn_output],
        axis=1,
    )
    third, gated, *cotangent_pieces = lax.optimization_barrier((third, gated, *cotangent_pieces))
    third = gather_rows(third)
    mamba_part_t = dot(state_out_map, gated, 1, 1).astype(bf16)
    up_map, down_map, attn_map = cut(third, [2 * ff_wide, ff_wide, query_width])

    key_start = span + tp_index * rows - WIN
    keyval_t = jnp.concatenate(
        [
            meta_keyval_t,
            lax.dynamic_slice_in_dim(
                jnp.concatenate([earlier_t, keyval_group_t], axis=1), key_start, window, 1
            ),
        ],
        axis=1,
    )
    query_pos = ctx_index * span + tp_index * rows + jnp.arange(rows, dtype=jnp.int32)
    key_pos = (ctx_index - 1) * span + key_start + jnp.arange(window, dtype=jnp.int32)
    seg_query = lax.dynamic_slice_in_dim(seg_current, tp_index * rows, rows, 0)
    seg_keys = lax.dynamic_slice_in_dim(
        jnp.concatenate([seg_earlier, seg_current]), key_start, window, 0
    )
    keep = (
        (key_pos[:, None] <= query_pos[None, :])
        & (query_pos[None, :] - key_pos[:, None] < WIN)
        & (key_pos[:, None] >= 0)
        & (seg_keys[:, None] == seg_query[None, :])
    )
    bias = jnp.concatenate(
        [jnp.zeros((meta_count, rows), f32), jnp.where(keep, 0.0, masked_score)], axis=0
    )
    cotangent_group_t = in_order(cotangent_pieces)
    attended_t, log_total, mamba_out = attend(
        query_t, keyval_t, bias, mamba_part_t, heads, tp, 3
    )
    attn_out = dot(attn_map, attended_t, 1, 0)

    mid = residual + 0.5 * (rms_norm(attn_out, attn_gain) + rms_norm(mamba_out, mamba_gain))
    ffn_normed_t = rms_norm(mid, ffn_gain).astype(bf16)
    ffn_normed_group_t, gate_up_grad, hidden, ffn_grad_part_t = feed_forward(
        ffn_normed_t, cotangent_group_t, third, ff_wide, tp, 1
    )
    fourth = width // 6 // 16 * 16
    ffn_wide, out_part_t, ffn_normed_grad_t = wide_sum(
        ffn_normed_group_t, cotangent_group_t, gate_up_grad, hidden, third, ffn_grad_part_t, tp, 7
    )
    ffn_columns = scatter_rows(ffn_wide)

    ffn_normed_grad = ffn_normed_grad_t.astype(f32)
    mid_extra, ffn_gain_terms = rms_back(mid, ffn_gain, ffn_normed_grad)
    mid_grad = cotangent_t.astype(f32) + mid_extra
    attn_grad, attn_gain_terms = rms_back(attn_out, attn_gain, 0.5 * mid_grad)
    mamba_grad, mamba_gain_terms = rms_back(mamba_out, mamba_gain, 0.5 * mid_grad)
    attn_grad_t = attn_grad.astype(bf16)
    mamba_grad_t = mamba_grad.astype(bf16)
    attended_grad_t = dot(attn_map, attn_grad_t, 0, 0).astype(bf16)
    query_grad_t, keyval_grad_t, mamba_grad_group_t = attend_back(
        query_t,
        keyval_t,
        bias,
        attended_t,
        log_total,
        attended_grad_t,
        mamba_grad_t,
        heads,
        tp,
        2,
    )
    query_pieces = permute_exchange(query_grad_t)
    keyval_grad_t = keyval_grad_t.reshape(keyval_width, meta_count + window)
    placed = lax.dynamic_update_slice_in_dim(
        jnp.zeros((keyval_width, 2 * span), bf16), keyval_grad_t[:, meta_count:], key_start, 1
    )
    earlier_back = lax.ppermute(placed[:, :span], "ctx", [(1, 0)])
    current = placed[:, span:].astype(f32) + earlier_back.astype(f32)
    keyval_part_t = current.astype(bf16)
    keyval_meta_t = keyval_grad_t[:, :meta_count]
    gated_grad = dot(mamba_grad_group_t, state_out_map, 0, 0)
    adjoint_end, out_head = end_adjoint(
        gated_grad, mixed, side, out_part_t, fourth, tp, 6
    )
    adjoint_end, late_attended_t, late_gated, query_pieces = lax.optimization_barrier(
        (adjoint_end, attended_t, gated, query_pieces)
    )
    adjoint_start = lax.ppermute(adjoint_end, "ctx", [(1, 0)])
    meta_back, meta_terms = rms_back(meta_rows, mix_gain, dot(keyval_map, keyval_meta_t, 1, 0))
    query_columns_t = in_order(query_pieces)
    each = query_width // tp

    def room(count):
        return ((0, -count % 128), (0, 0))

    query_wide = dot(normed_group_t, jnp.pad(query_columns_t, room(each)), 1, 1)
    keyval_wide = dot(normed_group_t, keyval_part_t, 1, 1) + dot(
        meta_normed_t, keyval_meta_t, 1, 1
    )
    early_pieces = [
        dot(attn_grad_t, jnp.pad(late_attended_t, room(query_width)), 1, 1),
        query_wide,
        meta_back,
        keyval_wide,
        dot(mamba_grad_group_t, late_gated, 1, 0),
    ]
    early_wide = by_rows(
        jnp.concatenate([by_rows(piece.astype(bf16)) for piece in early_pieces], axis=1)
    )
    early_columns = scatter_rows(early_wide)
    adjoint_start, early_wide, ffn_columns = lax.optimization_barrier(
        (adjoint_start, early_wide, ffn_columns)
    )
    mix_grad, scan_sums, out_rest = backward_scan(
        gated_grad,
        mixed,
        states,
        side,
        skip_row,
        adjoint_start,
        state_final,
        out_part_t,
        width - fourth,
        tp,
        5,
    )
    layer_out_t = (mid + jnp.concatenate([out_head, out_rest], axis=0)).astype(bf16)
    query_term = dot(query_map, query_grad_t, 1, 0)
    keyval_term = dot(keyval_map, keyval_part_t, 1, 0).astype(bf16)
    normed_grad_part = dot(first, mix_grad, 1, 1) + keyval_term.astype(f32)
    _, group_terms = rms_back(residual_group, mix_gain, normed_grad_part)
    _, query_terms = rms_back(residual, mix_gain, query_term)
    normed_grad_low, mix_grad = lax.optimization_barrier(
        (normed_grad_part.astype(bf16), mix_grad)
    )
    vector_columns = -(-3 * channels // shard)
    vectors = jnp.pad(scan_sums[:3].reshape(-1), (0, vector_columns * shard - 3 * channels))
    vectors = jnp.tile(vectors.reshape(shard, vector_columns), (width // shard, 1))
    tail = [
        (jnp.sum(group_terms, 1) + jnp.sum(meta_terms, 1) + jnp.sum(query_terms, 1))[:, None],
        jnp.sum(attn_gain_terms, 1, keepdims=True),
        jnp.sum(mamba_gain_terms, 1, keepdims=True),
        jnp.sum(ffn_gain_terms, 1, keepdims=True),
        vectors,
    ]
    tail = jnp.concatenate(tail, axis=1)
    tail = jnp.pad(tail, ((0, 0), (2 * STATE, first.shape[1] - 2 * STATE - tail.shape[1])))
    last_wide = by_rows((dot(normed_group_t, mix_grad, 1, 0) + tail).astype(bf16))
    last_wide, early_columns = lax.optimization_barrier((last_wide, early_columns))
    last_columns = scatter_rows(last_wide)
    attn_shares, _, grad_query, _, meta_shares, keyval_shares, grad_mamba_output = cut(
        early_columns,
        [
            query_width,
            -query_width % 128,
            each,
            -each % 128,
            meta_count,
            keyval_width,
            channels,
        ],
    )

    def to_device(values):
        return jnp.swapaxes(values.reshape(shard, tp, values.shape[1] // tp), 0, 1)

    shares = jnp.concatenate(
        [to_device(attn_shares), to_device(keyval_shares), to_device(meta_shares)], axis=2
    )
    normed_grad_low, last_wide, shares = lax.optimization_barrier(
        (normed_grad_low, last_wide, shares)
    )
    grad_attn_output, grad_keyval, grad_meta = cut(
        permute_sums(shares, 0)[0], [each, keyval_width // tp, meta_count // tp]
    )
    normed_grad = line_sum(normed_grad_low, tp, 4) + query_term
    ffn_columns, normed_grad = lax.optimization_barrier((ffn_columns, normed_grad))
    residual_extra, _ = rms_back(residual, mix_gain, normed_grad)
    grad_tokens_t = (mid_grad + residual_extra).astype(bf16)
    grad_gate, grad_up, grad_ffn_output = [
        piece[:, :ff].astype(f32) for piece in cut(ffn_columns, [ff_wide] * 3)
    ]
    grad_ffn_input = jnp.stack([grad_gate, grad_up], axis=1)
    select_shares, gain_shares, grad_vectors = cut(last_columns, [2 * STATE, 4, vector_columns])
    shares = jnp.concatenate(
        [to_device(select_shares), jnp.broadcast_to(gain_shares[None], (tp, shard, 4))], axis=2
    )
    grad_select, grad_gains = cut(permute_sums(shares, 0)[0], [2 * STATE // tp, 4])
    grad_mamba_input = jnp.stack(
        [
            last_columns[:, HEAD + k * channels : HEAD + (k + 1) * channels].astype(f32)
            for k in range(3)
        ],
        axis=1,
    )
    grad_mamba_output, grad_query, grad_vectors = [
        v.astype(f32) for v in (grad_mamba_output, grad_query, grad_vectors)
    ]
    grad_vectors = grad_vectors.reshape(-1)[: 3 * channels].reshape(3, channels)
    return (
        layer_out_t.T[None],
        grad_tokens_t.T[None],
        grad_meta,
        grad_gains[:, 0],
        grad_query,
        grad_keyval,
        grad_attn_output,
        grad_gains[:, 1],
        grad_mamba_input,
        grad_select,
        grad_vectors[0],
        grad_vectors[1],
        grad_vectors[2],
        grad_mamba_output,
        grad_gains[:, 2],
        grad_gains[:, 3],
        grad_ffn_input,
        grad_ffn_output,
    )


def solution(mesh):
    rows = ("fsdp", "ctx")
    in_specs = (
        P("fsdp", ("ctx", "tp"), None),
        P("fsdp", None),
        P("fsdp", ("ctx", "tp"), None),
        P(rows, None),
        P(rows),
        P(rows, None),
        P(rows, None),
        P(rows, None),
        P(rows),
        P(rows, None, "tp"),
        P(rows, None),
        P("tp"),
        P("tp"),
        P("tp"),
        P(rows, "tp"),
        P(rows),
        P(rows),
        P(rows, None, None),
        P(rows, None),
    )
    out_specs = (
        P("fsdp", ("ctx", "tp"), None),
        P("fsdp", ("ctx", "tp"), None),
        P(rows, "tp"),
        P(rows),
        P(rows, "tp"),
        P(rows, "tp"),
        P(rows, "tp"),
        P(rows),
        P(rows, None, "tp"),
        P(rows, "tp"),
        P("tp"),
        P("tp"),
        P("tp"),
        P(rows, "tp"),
        P(rows),
        P(rows),
        P(rows, None, "tp"),
        P(rows, "tp"),
    )
    return jax.shard_map(
        per_device, mesh=mesh, in_specs=in_specs, out_specs=out_specs, check_vma=False
    )
```

```python
import functools

import jax
import jax.numpy as jnp
from jax import lax
from jax.experimental import pallas as pl
from jax.experimental.layout import Layout, with_layout_constraint
from jax.experimental.pallas import tpu as pltpu
from jax.sharding import PartitionSpec as P

HEAD_SIZE = 64
STATE = 16
WIN = 1024
SUB = 4
TILE = 128
HEAD = 128

bf16 = jnp.bfloat16
f32 = jnp.float32
epsilon = 1e-05
masked_score = -1e30


def mm(a, b):
    return lax.dot_general(a, b, (((1,), (0,)), ((), ())), preferred_element_type=f32)


def mm_nt(a, b):
    return lax.dot_general(a, b, (((1,), (1,)), ((), ())), preferred_element_type=f32)


def iota(shape, dim):
    return lax.broadcasted_iota(jnp.int32, shape, dim)


def split_mm(a, b):
    high = b.astype(bf16)
    return mm(a, high) + mm(a, (b - high.astype(f32)).astype(bf16))


def ones_where(cond):
    return jnp.where(cond, 1.0, 0.0)


def softplus(v):
    return jnp.maximum(v, 0.0) + jnp.log1p(jnp.exp(-jnp.abs(v)))


def group_mask(rows, columns, row_unit, column_unit):
    return iota((rows, columns), 0) // row_unit == iota((rows, columns), 1) // column_unit


def scan_tables():
    rows = 2 * TILE + TILE // SUB
    width = TILE // SUB * STATE
    row = iota((rows, TILE), 0)
    column = iota((rows, TILE), 1)
    token = row % TILE
    same = token // SUB == column // SUB
    upto = (row < TILE) & same & (column <= token)
    after = (row >= TILE) & (row < 2 * TILE) & same & (column > token)
    whole = (row >= 2 * TILE) & (row - 2 * TILE == column // SUB)
    places = iota((STATE, width), 0) == iota((STATE, width), 1) % STATE
    tables = (upto | after | whole, group_mask(width, TILE, STATE, SUB), places)
    sums, mask, places = [ones_where(table).astype(bf16) for table in tables]
    return sums, mask, mask.T, places, places.T


def part(mixed, k):
    channels = (mixed.shape[1] - HEAD) // 3
    return mixed[:, HEAD + k * channels : HEAD + (k + 1) * channels].astype(f32)


def both_ways(mixed):
    head = mixed[:, :HEAD]
    return head, head.astype(f32).T.astype(bf16)


def decays(step_raw, bias_ref, rate_ref, alive_last_ref, sums_ref):
    raw = step_raw + bias_ref[...]
    step = softplus(raw)
    log_decay = -step * rate_ref[...]
    sums = split_mm(sums_ref[...], log_decay)
    upto = jnp.exp(sums[:TILE])
    after = sums[TILE : 2 * TILE]
    block = jnp.exp(sums[2 * TILE :]) * alive_last_ref[...]
    return raw, step, log_decay, upto, after, block


def in_blocks(values_t, factor_t, mask):
    kept = values_t * factor_t.astype(bf16)
    return jnp.concatenate([kept] * (TILE // SUB), axis=0) * mask[...]


def spread(values, factor, mask_t, places):
    return mm(values * factor.astype(bf16), places[...]).astype(bf16) * mask_t[...]


def fold(wide, factor, mask_t, places_t):
    return mm(wide.astype(bf16) * mask_t[...], places_t[...]) * factor


def pairs(aux_ref, aux_t_ref, lower):
    row, column = iota((TILE, TILE), 0), iota((TILE, TILE), 1)
    order = column <= row if lower else column >= row
    return (row // SUB == column // SUB) & order & (aux_ref[:, 2:3] == aux_t_ref[2:3, :])


def run_states(state, local_ref, block_ref, keep=None):
    def one(k, state):
        if keep is not None:
            keep[pl.ds(pl.multiple_of(k * STATE, STATE), STATE), :] = state.astype(bf16)
        return block_ref[pl.ds(k, 1), :] * state + local_ref[pl.ds(pl.multiple_of(k * STATE, STATE), STATE), :]

    return lax.fori_loop(0, TILE // SUB, one, state, unroll=True)


def end_state_kernel(
    mixed, aux, aux_t, alive_last, bias, rate, sums_table, mask, mask_t, places, places_t, end, state, local, block
):
    @pl.when(pl.program_id(0) == 0)
    def _():
        state[...] = jnp.zeros_like(state)

    _, maps_t = both_ways(mixed)
    raw, step, log_decay, upto, after, total = decays(
        part(mixed, 2), bias, rate, alive_last, sums_table
    )
    driven = (jnp.exp(after) * step * part(mixed, 0)).astype(bf16)
    local[...] = mm(in_blocks(maps_t[:STATE], aux_t[1:2, :], mask), driven)
    block[...] = total
    state[...] = run_states(state[...], local, block)
    end[...] = state[...]


def forward_kernel(
    mixed,
    aux,
    aux_t,
    alive_last,
    bias,
    rate,
    sums_table,
    mask,
    mask_t,
    places,
    places_t,
    skip,
    start,
    gated,
    states,
    end,
    state,
    local,
    block,
):
    @pl.when(pl.program_id(0) == 0)
    def _():
        state[...] = start[...]

    maps, maps_t = both_ways(mixed)
    raw, step, log_decay, upto, after, total = decays(
        part(mixed, 2), bias, rate, alive_last, sums_table
    )
    x = part(mixed, 0)
    driven = (jnp.exp(after) * step * x).astype(bf16)
    local[...] = mm(in_blocks(maps_t[:STATE], aux_t[1:2, :], mask), driven)
    block[...] = total
    state[...] = run_states(state[...], local, block, states)
    end[...] = state[...]
    out_part = maps[:, STATE : 2 * STATE]
    cross = jnp.where(pairs(aux, aux_t, True), mm(out_part, maps_t[:STATE]), 0.0).astype(bf16)
    y = (
        upto * mm(spread(out_part, aux[:, 0:1], mask_t, places), states[...])
        + jnp.exp(-after) * mm(cross, driven)
        + skip[...] * x
    )
    gates = part(mixed, 1)
    gated[...] = (y * gates * lax.logistic(gates)).astype(bf16)


def back_run(carry, local_ref, block_ref, keep, states=None, bound=None):
    count = TILE // SUB

    def one(i, carry):
        k = count - 1 - i
        rows = pl.ds(pl.multiple_of(k * STATE, STATE), STATE)
        if keep is not None:
            keep[rows, :] = carry[0].astype(bf16)
            bound[pl.ds(k, 1), :] = carry[1]
        new = block_ref[pl.ds(k, 1), :] * carry[0] + local_ref[rows, :]
        if keep is None:
            return (new, carry[1])
        return (new, jnp.sum(new * states[rows, :].astype(f32), axis=0, keepdims=True))

    return lax.fori_loop(0, count, one, carry, unroll=True)


def end_adjoint_kernel(
    count,
    gated_grad,
    mixed,
    aux,
    aux_t,
    alive_last,
    bias,
    rate,
    sums_table,
    mask,
    mask_t,
    places,
    places_t,
    source,
    end,
    total_out,
    state,
    local,
    block,
    own,
    sent,
    got,
    loads,
    send_sems,
    recv_sems,
):
    tile, tiles = pl.program_id(0), pl.num_programs(0)
    begin, step_line, finish = line_sum_steps(
        count, source.at[: total_out.shape[0]], own, sent, got, total_out, loads, send_sems, recv_sems
    )

    @pl.when(tile == 0)
    def _():
        begin()
        state[...] = jnp.zeros_like(state)

    for k in range(1, count - 1):

        @pl.when(tile == tiles * k // (count - 1))
        def _():
            step_line(k)

    _, maps_t = both_ways(mixed)
    raw, step, log_decay, upto, after, total = decays(
        part(mixed, 2), bias, rate, alive_last, sums_table
    )
    gates = part(mixed, 1)
    dy = gated_grad[...] * gates * lax.logistic(gates)
    local[...] = mm(in_blocks(maps_t[STATE : 2 * STATE], aux_t[0:1, :], mask), (upto * dy).astype(bf16))
    block[...] = total
    state[...] = back_run((state[...], jnp.zeros((1, state.shape[1]), f32)), local, block, None)[0]
    end[...] = state[...]

    @pl.when(tile == tiles - 1)
    def _():
        step_line(count - 1)
        finish()


def backward_kernel(
    count,
    gated_grad,
    mixed,
    states,
    aux,
    aux_t,
    alive_last,
    bias,
    rate,
    sums_table,
    mask,
    mask_t,
    places,
    places_t,
    skip,
    start,
    final,
    source,
    mix_grad,
    sums,
    total_out,
    state,
    local,
    block,
    adjoint,
    bound,
    edge,
    own,
    sent,
    got,
    loads,
    send_sems,
    recv_sems,
):
    tile, tiles = pl.program_id(0), pl.num_programs(0)
    begin, step_line, finish = line_sum_steps(
        count, source.at[source.shape[0] - total_out.shape[0] :], own, sent, got, total_out, loads, send_sems, recv_sems
    )

    @pl.when(tile == 0)
    def _():
        begin()
        state[...] = start[...]
        edge[...] = jnp.sum(start[...] * final[...], axis=0, keepdims=True)
        sums[...] = jnp.zeros_like(sums)

    for k in range(1, count - 1):

        @pl.when(tile == tiles * k // (count - 1))
        def _():
            step_line(k)

    maps, maps_t = both_ways(mixed)
    raw, step, log_decay, upto, after, total = decays(
        part(mixed, 2), bias, rate, alive_last, sums_table
    )
    channels = state.shape[1]
    x = part(mixed, 0)
    decay_after = jnp.exp(after)
    grow = jnp.exp(-after)
    driven = (decay_after * step * x).astype(bf16)
    in_part, out_part = maps[:, :STATE], maps[:, STATE : 2 * STATE]
    in_part_t, out_part_t = maps_t[:STATE], maps_t[STATE : 2 * STATE]
    lower, upper = pairs(aux, aux_t, True), pairs(aux, aux_t, False)
    cross = jnp.where(lower, mm(out_part, in_part_t), 0.0).astype(bf16)
    cross_t = jnp.where(upper, mm(in_part, out_part_t), 0.0).astype(bf16)
    y = upto * mm(spread(out_part, aux[:, 0:1], mask_t, places), states[...]) + grow * mm(cross, driven)
    gates = part(mixed, 1)
    sigma = lax.logistic(gates)
    grad = gated_grad[...]
    dy = grad * gates * sigma
    mix_grad[:, HEAD + channels : HEAD + 2 * channels] = (
        grad * (y + skip[...] * x) * (sigma * (1.0 + gates * (1.0 - sigma)))
    ).astype(bf16)
    dy_low = (upto * dy).astype(bf16)
    dy_grown = (grow * dy).astype(bf16)
    local[...] = mm(in_blocks(out_part_t, aux_t[0:1, :], mask), dy_low)
    block[...] = total
    new_state, new_edge = back_run((state[...], edge[...]), local, block, adjoint, states, bound)
    state[...] = new_state
    edge[...] = new_edge
    du = decay_after * (
        mm(spread(in_part, aux[:, 1:2], mask_t, places), adjoint[...]) + mm(cross_t, dy_grown)
    )
    out_grad = fold(mm_nt(dy_low, states[...]), aux[:, 0:1], mask_t, places_t)
    in_grad = fold(mm_nt(driven, adjoint[...]), aux[:, 1:2], mask_t, places_t)
    cross_grad = jnp.where(lower, mm_nt(dy_grown, driven), 0.0).astype(bf16)
    cross_grad_t = jnp.where(upper, mm_nt(driven, dy_grown), 0.0).astype(bf16)
    out_grad = out_grad + mm(cross_grad, in_part)
    in_grad = in_grad + mm(cross_grad_t, out_part)
    mix_grad[:, :HEAD] = jnp.concatenate(
        [in_grad, out_grad, jnp.zeros((TILE, HEAD - 2 * STATE), f32)], axis=1
    ).astype(bf16)
    flow = dy * y - step * x * du
    to_tokens = ones_where(group_mask(TILE, TILE // SUB, SUB, 1)) * aux[:, 1:2]
    decay_grad = aux[:, 3:4] * (
        mm(ones_where(upper).astype(bf16), flow.astype(bf16))
        + split_mm(to_tokens.astype(bf16), bound[...])
    )
    step_grad = (x * du - rate[...] * decay_grad) * lax.logistic(raw)
    mix_grad[:, HEAD : HEAD + channels] = (skip[...] * dy + step * du).astype(bf16)
    mix_grad[:, HEAD + 2 * channels :] = step_grad.astype(bf16)
    sums[0:1, :] += jnp.sum(step_grad, axis=0, keepdims=True)
    sums[1:2, :] += jnp.sum(decay_grad * log_decay, axis=0, keepdims=True)
    sums[2:3, :] += jnp.sum(dy * x, axis=0, keepdims=True)

    @pl.when(tile == tiles - 1)
    def _():
        step_line(count - 1)
        finish()


def scan_specs(tokens, channels, back):
    tiles = tokens // TILE
    at = (lambda i: tiles - 1 - i) if back else (lambda i: i)

    def fixed(*shape):
        return pl.BlockSpec(shape, lambda i: (0,) * len(shape))

    width = TILE // SUB * STATE
    mixed = pl.BlockSpec((TILE, HEAD + 3 * channels), lambda i: (at(i), 0))
    rows = pl.BlockSpec((TILE, channels), lambda i: (at(i), 0))
    states = pl.BlockSpec((width, channels), lambda i: (at(i), 0))
    side = [
        pl.BlockSpec((TILE, 8), lambda i: (at(i), 0)),
        pl.BlockSpec((8, TILE), lambda i: (0, at(i))),
        pl.BlockSpec((TILE // SUB, 1), lambda i: (at(i), 0)),
        fixed(1, channels),
        fixed(1, channels),
        fixed(2 * TILE + TILE // SUB, TILE),
        fixed(width, TILE),
        fixed(TILE, width),
        fixed(STATE, width),
        fixed(width, STATE),
    ]
    return tiles, mixed, rows, states, side, fixed(1, channels), fixed(STATE, channels)


def scan_scratch(channels):
    return [
        pltpu.VMEM((STATE, channels), f32),
        pltpu.VMEM((TILE // SUB * STATE, channels), f32),
        pltpu.VMEM((TILE // SUB, channels), f32),
    ]


def scan_call(kernel, name, tiles, in_specs, out_specs, out_shape, scratch, flops, collective=None, room=16):
    return pl.pallas_call(
        kernel,
        name=name,
        grid=(tiles,),
        in_specs=in_specs,
        out_specs=out_specs,
        scratch_shapes=scratch,
        out_shape=out_shape,
        compiler_params=pltpu.CompilerParams(
            vmem_limit_bytes=room << 20,
            dimension_semantics=("arbitrary",),
            collective_id=collective,
            has_side_effects=collective is not None,
        ),
        cost_estimate=pl.CostEstimate(flops=flops, bytes_accessed=flops // 100, transcendentals=0),
    )


def scan_aux(segment, before):
    count = segment.shape[0]
    blocks = segment.reshape(count // SUB, SUB)
    ends = jnp.concatenate([before[None], blocks[:-1, -1]])
    alive = (blocks == ends[:, None]).reshape(-1).astype(f32)
    tail = (blocks == blocks[:, -1:]).reshape(-1).astype(f32)
    joined = (segment == jnp.concatenate([before[None], segment[:-1]])).astype(f32)
    zero = jnp.zeros_like(alive)
    aux_t = jnp.stack([alive, tail, segment.astype(f32), joined, zero, zero, zero, zero])
    last = (blocks[:, -1] == ends).astype(f32)[:, None]
    return aux_t.T, aux_t, last


def end_state(mixed, side):
    tokens, channels = mixed.shape[0], (mixed.shape[1] - HEAD) // 3
    tiles, mixed_s, rows, states, side_s, row, state = scan_specs(tokens, channels, False)
    return scan_call(
        end_state_kernel,
        "end_state",
        tiles,
        [mixed_s, *side_s],
        state,
        jax.ShapeDtypeStruct((STATE, channels), f32),
        scan_scratch(channels),
        10**7,
    )(mixed, *side)


def forward_scan(mixed, side, skip, start):
    tokens, channels = mixed.shape[0], (mixed.shape[1] - HEAD) // 3
    tiles, mixed_s, rows, states, side_s, row, state = scan_specs(tokens, channels, False)
    return scan_call(
        forward_kernel,
        "forward_scan",
        tiles,
        [mixed_s, *side_s, row, state],
        [rows, states, state],
        [
            jax.ShapeDtypeStruct((tokens, channels), bf16),
            jax.ShapeDtypeStruct((tokens // SUB * STATE, channels), bf16),
            jax.ShapeDtypeStruct((STATE, channels), f32),
        ],
        scan_scratch(channels),
        10**7,
    )(mixed, *side, skip, start)


def end_adjoint(gated_grad, mixed, side, source, height, count, collective):
    each = source.shape[1] // count
    tokens, channels = mixed.shape[0], (mixed.shape[1] - HEAD) // 3
    tiles, mixed_s, rows, states, side_s, row, state = scan_specs(tokens, channels, True)
    return scan_call(
        functools.partial(end_adjoint_kernel, count),
        "end_adjoint",
        tiles,
        [rows, mixed_s, *side_s, pl.BlockSpec(memory_space=pl.ANY)],
        [state, pl.BlockSpec((height, each), lambda i: (0, 0))],
        [
            jax.ShapeDtypeStruct((STATE, channels), f32),
            jax.ShapeDtypeStruct((height, each), f32),
        ],
        scan_scratch(channels) + line_sum_scratch(count, height, each),
        10**10,
        collective,
        24,
    )(gated_grad, mixed, *side, source)


def backward_scan(gated_grad, mixed, states, side, skip, start, final, source, height, count, collective):
    each = source.shape[1] // count
    tokens, channels = mixed.shape[0], (mixed.shape[1] - HEAD) // 3
    tiles, mixed_s, rows, states_s, side_s, row, state = scan_specs(tokens, channels, True)
    return scan_call(
        functools.partial(backward_kernel, count),
        "backward_scan",
        tiles,
        [
            rows,
            mixed_s,
            states_s,
            *side_s,
            row,
            state,
            state,
            pl.BlockSpec(memory_space=pl.ANY),
        ],
        [
            mixed_s,
            pl.BlockSpec((8, channels), lambda i: (0, 0)),
            pl.BlockSpec((height, each), lambda i: (0, 0)),
        ],
        [
            jax.ShapeDtypeStruct(mixed.shape, bf16),
            jax.ShapeDtypeStruct((8, channels), f32),
            jax.ShapeDtypeStruct((height, each), f32),
        ],
        scan_scratch(channels)
        + [
            pltpu.VMEM((TILE // SUB * STATE, channels), bf16),
            pltpu.VMEM((TILE // SUB, channels), f32),
            pltpu.VMEM((1, channels), f32),
        ]
        + line_sum_scratch(count, height, each),
        36 * 10**9,
        collective,
        48,
    )(gated_grad, mixed, states, *side, skip, start, final, source)


MESH = pl.DeviceIdType.MESH
COMM = {"has_side_effects": True}


def neighbour_barrier(count):
    place = lax.axis_index("tp")
    ready = pltpu.get_barrier_semaphore()
    sides = ((place < count - 1, place + 1), (place > 0, place - 1))
    for there, other in sides:

        @pl.when(there)
        def _():
            pl.semaphore_signal(ready, inc=1, device_id={"tp": other}, device_id_type=MESH)

    peers = jnp.where(place < count - 1, 1, 0) + jnp.where(place > 0, 1, 0)
    pl.semaphore_wait(ready, peers)


def line_steps(count, source, target, copies, send_sems, recv_sems):
    place = lax.axis_index("tp")
    width = source.shape[1]

    def at(owner):
        return target.at[:, pl.ds(pl.multiple_of(owner * width, width), width)]

    def local():
        return pltpu.make_async_copy(source, at(place), copies)

    def remote(side, step):
        owner = place - step if side == 0 else place + step
        return pltpu.make_async_remote_copy(
            src_ref=source if step == 0 else at(owner),
            dst_ref=at(owner),
            send_sem=send_sems.at[side, step],
            recv_sem=recv_sems.at[side, step],
            device_id={"tp": place + 1 if side == 0 else place - 1},
            device_id_type=MESH,
        )

    def has(side, step):
        return place - step >= 0 if side == 0 else place + step < count

    def neighbour(side):
        return place < count - 1 if side == 0 else place > 0

    def send(side, step):
        @pl.when(neighbour(side) & has(side, step))
        def _():
            remote(side, step).start()

    def receive(side, step):
        @pl.when(has(side, step + 1))
        def _():
            remote(side, step).wait_recv()

    def start():
        neighbour_barrier(count)
        local().start()
        for side in (0, 1):
            send(side, 0)

    def step(k):
        for side in (0, 1):
            receive(side, k - 1)
        for side in (0, 1):
            if k < count - 1:
                send(side, k)

    step.send, step.receive = send, receive

    def finish():
        for k in range(count - 1):
            for side in (0, 1):

                @pl.when(neighbour(side) & has(side, k))
                def _():
                    remote(side, k).wait_send()

        local().wait()

    return start, step, finish


def line_scratch(count):
    return [
        pltpu.SemaphoreType.DMA,
        pltpu.SemaphoreType.DMA((2, count - 1)),
        pltpu.SemaphoreType.DMA((2, count - 1)),
    ]


def line_gather_kernel(count, source, target, copies, send_sems, recv_sems):
    start, step, finish = line_steps(count, source, target, copies, send_sems, recv_sems)
    start()
    for k in range(1, count):
        step(k)
    finish()


def line_gather(source, count, collective):
    return pl.pallas_call(
        functools.partial(line_gather_kernel, count),
        name="line_gather",
        in_specs=[pl.BlockSpec(memory_space=pl.ANY)],
        out_specs=pl.BlockSpec(memory_space=pl.ANY),
        out_shape=jax.ShapeDtypeStruct((source.shape[0], source.shape[1] * count), source.dtype),
        scratch_shapes=line_scratch(count),
        compiler_params=pltpu.CompilerParams(collective_id=collective, has_side_effects=True),
    )(source)


def line_sum_steps(count, source, own, sent, got, total, loads, send_sems, recv_sems):
    place = lax.axis_index("tp")
    width = total.shape[1]

    def whose(side, step):
        return place + (count - step) if side == 0 else place - (count - step)

    def sends(side, step):
        owner = whose(side, step)
        return owner < count if side == 0 else owner >= 0

    def receives(side, step):
        return (place >= 1) & (place <= step) if side == 0 else (place <= count - 2) & (place >= count - 1 - step)

    def load(side, step):
        owner = whose(side, step)
        return pltpu.make_async_copy(
            source.at[:, pl.ds(pl.multiple_of(owner * width, width), width)],
            sent.at[side, step - 1],
            loads.at[side, step - 1],
        )

    def mine():
        return pltpu.make_async_copy(
            source.at[:, pl.ds(pl.multiple_of(place * width, width), width)], own, loads.at[2, 0]
        )

    def remote(side, step):
        return pltpu.make_async_remote_copy(
            src_ref=sent.at[side, step - 1],
            dst_ref=got.at[side, step - 1],
            send_sem=send_sems.at[side, step - 1],
            recv_sem=recv_sems.at[side, step - 1],
            device_id={"tp": place + 1 if side == 0 else place - 1},
            device_id_type=MESH,
        )

    def start():
        neighbour_barrier(count)
        mine().start()
        for step in range(1, count):
            for side in (0, 1):

                @pl.when(sends(side, step))
                def _():
                    load(side, step).start()

        step_out(1)

    def step_out(step):
        for side in (0, 1):

            @pl.when(sends(side, step))
            def _():
                load(side, step).wait()

            if step > 1:

                @pl.when(sends(side, step) & receives(side, step - 1))
                def _():
                    sent[side, step - 1] = (
                        sent[side, step - 1].astype(f32) + got[side, step - 2].astype(f32)
                    ).astype(bf16)

            @pl.when(sends(side, step))
            def _():
                remote(side, step).start()

    def step(k):
        for side in (0, 1):

            @pl.when(receives(side, k))
            def _():
                remote(side, k).wait_recv()

        if k < count - 1:
            step_out(k + 1)

    def finish():
        mine().wait()
        total[...] = own[...].astype(f32)
        for side in (0, 1):

            @pl.when(receives(side, count - 1))
            def _():
                total[...] = total[...] + got[side, count - 2].astype(f32)

            for k in range(1, count):

                @pl.when(sends(side, k))
                def _():
                    remote(side, k).wait_send()

    return start, step, finish


def line_sum_scratch(count, height, width):
    return [
        pltpu.VMEM((height, width), bf16),
        pltpu.VMEM((2, count - 1, height, width), bf16),
        pltpu.VMEM((2, count - 1, height, width), bf16),
        pltpu.SemaphoreType.DMA((3, count - 1)),
        pltpu.SemaphoreType.DMA((2, count - 1)),
        pltpu.SemaphoreType.DMA((2, count - 1)),
    ]


def line_sum_kernel(count, source, total, own, sent, got, loads, send_sems, recv_sems):
    start, step, finish = line_sum_steps(
        count, source, own, sent, got, total, loads, send_sems, recv_sems
    )
    start()
    for k in range(1, count):
        step(k)
    finish()


def line_sum(source, count, collective):
    height, width = source.shape[0], source.shape[1] // count
    return pl.pallas_call(
        functools.partial(line_sum_kernel, count),
        name="line_sum",
        in_specs=[pl.BlockSpec(memory_space=pl.ANY)],
        out_specs=pl.BlockSpec(memory_space=pltpu.VMEM),
        out_shape=jax.ShapeDtypeStruct((height, width), f32),
        scratch_shapes=line_sum_scratch(count, height, width),
        compiler_params=pltpu.CompilerParams(
            vmem_limit_bytes=24 << 20, collective_id=collective, has_side_effects=True
        ),
        cost_estimate=pl.CostEstimate(flops=5 * 10**10, bytes_accessed=1 << 24, transcendentals=0),
    )(source)


def feed_kernel(
    count,
    blocks,
    source,
    other,
    weights,
    group,
    gate_up_grad,
    hidden,
    part_sum,
    maps,
    tokens,
    grads,
    grad_rows,
    hidden_rows,
    partial,
    copies,
    loads,
    stores,
    send_sems,
    recv_sems,
):
    place = lax.axis_index("tp")
    start, step, finish = line_steps(count, source, group, copies, send_sems, recv_sems)
    receive, send = step.receive, step.send
    ff = hidden.shape[1]
    width = source.shape[1]
    near = jnp.minimum(place, count - 1 - place)

    def owner_of(q):
        spread_out = jnp.where(q % 2 == 1, place - (q + 1) // 2, place + q // 2)
        rest = jnp.where(place < count - 1 - place, q, count - 1 - q)
        return jnp.where(q <= 2 * near, spread_out, rest)

    def reach(q):
        return jnp.where(q <= 2 * near, (q + 1) // 2, q - near)

    def load(what, where, k):
        return pltpu.make_async_copy(what, where, loads.at[k])

    def columns(array, owner):
        return array.at[:, pl.ds(pl.multiple_of(owner * width, width), width)]

    def store(q):
        owner, slot = owner_of(q), q % 2
        at = pl.ds(pl.multiple_of(owner * width, width), width)
        return [
            pltpu.make_async_copy(grad_rows.at[slot], gate_up_grad.at[at, :], stores.at[slot, 0]),
            pltpu.make_async_copy(hidden_rows.at[slot], hidden.at[at, :], stores.at[slot, 1]),
            pltpu.make_async_copy(partial.at[slot], columns(part_sum, owner), stores.at[slot, 2]),
        ]

    start()
    load(other, grads, 2).start()
    load(weights.at[:, : 3 * ff], maps, 0).start()

    def one(q, carry):
        owner, slot = owner_of(q), q % 2
        for far in range(1, count):

            @pl.when((reach(q) == far) & (reach(q - 1) < far))
            def _():
                for side in (0, 1):
                    receive(side, far - 1)
                for side in (0, 1):
                    if far < count - 1:
                        send(side, far)

        @pl.when(q == 0)
        def _():
            load(source, tokens, 1).start()
            load(source, tokens, 1).wait()

        @pl.when(q > 0)
        def _():
            load(columns(group, owner), tokens, 1).start()
            load(columns(group, owner), tokens, 1).wait()

        @pl.when(q == 0)
        def _():
            load(other, grads, 2).wait()
            load(weights.at[:, : 3 * ff], maps, 0).wait()

        @pl.when(q > 1)
        def _():
            for copy in store(q - 2):
                copy.wait()

        rows = tokens[...].T
        outs = columns(grads, owner)[...].T
        for begin, wide in blocks:
            gate = mm(rows, maps[:, begin : begin + wide])
            up = mm(rows, maps[:, ff + begin : ff + begin + wide])
            grad = mm(outs, maps[:, 2 * ff + begin : 2 * ff + begin + wide])
            sigma = lax.logistic(gate)
            active = gate * sigma
            hidden_rows[slot, :, begin : begin + wide] = (active * up).astype(bf16)
            grad_rows[slot, :, begin : begin + wide] = (
                grad * up * (sigma * (1.0 + gate * (1.0 - sigma)))
            ).astype(bf16)
            grad_rows[slot, :, ff + begin : ff + begin + wide] = (grad * active).astype(bf16)
        partial[slot] = mm_nt(maps[:, : 2 * ff], grad_rows[slot]).astype(bf16)
        for copy in store(q):
            copy.start()
        return carry

    lax.fori_loop(0, count, one, 0)
    for q in (count - 2, count - 1):
        for copy in store(q):
            copy.wait()
    finish()


def feed_forward(source, other, weights, ff, count, collective):
    depth, width = source.shape
    blocks = []
    begin = 0
    while begin < ff:
        blocks.append((begin, min(256, ff - begin)))
        begin = begin + 256
    anywhere = pl.BlockSpec(memory_space=pl.ANY)
    return pl.pallas_call(
        functools.partial(feed_kernel, count, tuple(blocks)),
        name="feed_forward",
        in_specs=[anywhere] * 3,
        out_specs=[anywhere] * 4,
        out_shape=[
            jax.ShapeDtypeStruct((depth, width * count), bf16),
            jax.ShapeDtypeStruct((width * count, 2 * ff), bf16),
            jax.ShapeDtypeStruct((width * count, ff), bf16),
            jax.ShapeDtypeStruct((depth, width * count), bf16),
        ],
        scratch_shapes=[
            pltpu.VMEM((depth, 3 * ff), bf16),
            pltpu.VMEM((depth, width), bf16),
            pltpu.VMEM((depth, width * count), bf16),
            pltpu.VMEM((2, width, 2 * ff), bf16),
            pltpu.VMEM((2, width, ff), bf16),
            pltpu.VMEM((2, depth, width), bf16),
            pltpu.SemaphoreType.DMA,
            pltpu.SemaphoreType.DMA((3,)),
            pltpu.SemaphoreType.DMA((2, 3)),
            pltpu.SemaphoreType.DMA((2, count - 1)),
            pltpu.SemaphoreType.DMA((2, count - 1)),
        ],
        compiler_params=pltpu.CompilerParams(
            vmem_limit_bytes=56 << 20, collective_id=collective, has_side_effects=True
        ),
    )(source, other, weights)


def wide_sum_kernel(
    count,
    ups,
    downs,
    tokens,
    others,
    gate_up_grad,
    hidden,
    hidden_rows,
    maps,
    source,
    wide,
    out_part,
    total,
    own,
    sent,
    got,
    loads,
    send_sems,
    recv_sems,
):
    step, steps = pl.program_id(0), pl.num_programs(0)
    start, advance, finish = line_sum_steps(
        count, source, own, sent, got, total, loads, send_sems, recv_sems
    )

    @pl.when(step == 0)
    def _():
        start()

    for k in range(1, count - 1):

        @pl.when(step == steps * k // (count - 1))
        def _():
            advance(k)

    @pl.when(step < ups)
    def _():
        wide[...] = mm(tokens[...], gate_up_grad[...]).astype(bf16)

    @pl.when((step >= ups) & (step < ups + downs))
    def _():
        wide[...] = mm(others[...], hidden[...]).astype(bf16)

    @pl.when(step >= ups + downs)
    def _():
        out_part[...] = mm_nt(maps[...], hidden_rows[...]).astype(bf16)

    @pl.when(step == steps - 1)
    def _():
        advance(count - 1)
        finish()


def wide_sum(tokens, others, gate_up_grad, hidden, maps, source, count, collective):
    depth, span = tokens.shape
    ff = hidden.shape[1]
    ups, downs, strip = 2 * ff // 128, ff // 128, 320
    strips = depth // strip
    each = source.shape[1] // count

    def strip_of(j):
        return jnp.clip(j - ups - downs, 0, strips - 1)

    def whole(*shape):
        return pl.BlockSpec(shape, lambda j: (0, 0), pipeline_mode=pl.Buffered(1))

    return pl.pallas_call(
        functools.partial(wide_sum_kernel, count, ups, downs),
        name="wide_sum",
        grid=(ups + downs + strips,),
        in_specs=[
            whole(depth, span),
            whole(depth, span),
            pl.BlockSpec((span, 128), lambda j: (0, jnp.minimum(j, ups - 1))),
            pl.BlockSpec((span, 128), lambda j: (0, jnp.clip(j - ups, 0, downs - 1))),
            whole(span, ff),
            pl.BlockSpec((strip, ff), lambda j: (strip_of(j), 2)),
            pl.BlockSpec(memory_space=pl.ANY),
        ],
        out_specs=[
            pl.BlockSpec((depth, 128), lambda j: (0, jnp.minimum(j, ups + downs - 1))),
            pl.BlockSpec((strip, span), lambda j: (strip_of(j), 0)),
            pl.BlockSpec((depth, each), lambda j: (0, 0)),
        ],
        out_shape=[
            jax.ShapeDtypeStruct((depth, 3 * ff), bf16),
            jax.ShapeDtypeStruct((depth, span), bf16),
            jax.ShapeDtypeStruct((depth, each), f32),
        ],
        scratch_shapes=line_sum_scratch(count, depth, each),
        compiler_params=pltpu.CompilerParams(
            vmem_limit_bytes=48 << 20,
            dimension_semantics=("arbitrary",),
            collective_id=collective,
            has_side_effects=True,
        ),
    )(tokens, others, gate_up_grad, hidden, hidden, maps, source)


def attend_kernel(
    group,
    count,
    query_t,
    key_t,
    value_t,
    bias,
    source,
    out_t,
    log_total,
    total_out,
    own,
    sent,
    got,
    loads,
    send_sems,
    recv_sems,
):
    head, heads = pl.program_id(0), pl.num_programs(0)
    start, step, finish = line_sum_steps(
        count, source, own, sent, got, total_out, loads, send_sems, recv_sems
    )

    @pl.when(head == 0)
    def _():
        start()

    @pl.when(head == heads - 2)
    def _():
        step(1)

    keys = key_t[...].T
    values_t = value_t[...]
    for g in range(group):
        at = slice(g * HEAD_SIZE, (g + 1) * HEAD_SIZE)
        scores = mm(keys, query_t[at, :] * 0.125) + bias[...]
        top = jnp.max(scores, axis=0, keepdims=True)
        probs = jnp.exp(scores - top)
        total = jnp.sum(probs, axis=0, keepdims=True)
        out_t[at, :] = (mm(values_t, probs.astype(bf16)) / total).astype(bf16)
        log_total[g : g + 1, :] = top + jnp.log(total)

    @pl.when(head == heads - 1)
    def _():
        for k in range(2, count):
            step(k)
        finish()


def attend_back_kernel(
    group,
    count,
    query_t,
    key_t,
    value_t,
    bias,
    out_t,
    log_total,
    grad_t,
    source,
    query_grad_t,
    keyval_grad_t,
    target,
    copies,
    send_sems,
    recv_sems,
):
    head, heads = pl.program_id(0), pl.num_programs(0)
    start, step, finish = line_steps(count, source, target, copies, send_sems, recv_sems)

    @pl.when(head == 0)
    def _():
        start()

    @pl.when(head == heads - 2)
    def _():
        step(1)

    keys_t = key_t[...]
    keys = keys_t.T
    values = value_t[...].T
    key_sum = jnp.zeros(keys_t.shape, f32)
    value_sum = jnp.zeros(keys_t.shape, f32)
    for g in range(group):
        at = slice(g * HEAD_SIZE, (g + 1) * HEAD_SIZE)
        query = query_t[at, :] * 0.125
        grad = grad_t[at, :]
        probs = jnp.exp(mm(keys, query) + bias[...] - log_total[g : g + 1, :])
        centre = jnp.sum(grad.astype(f32) * out_t[at, :].astype(f32), axis=0, keepdims=True)
        score_grad = (probs * (mm(values, grad) - centre)).astype(bf16)
        query_grad_t[at, :] = (mm(keys_t, score_grad) * 0.125).astype(bf16)
        key_sum = key_sum + mm_nt(query, score_grad)
        value_sum = value_sum + mm_nt(grad, probs.astype(bf16))
    keyval_grad_t[0] = key_sum.astype(bf16)
    keyval_grad_t[1] = value_sum.astype(bf16)

    @pl.when(head == heads - 1)
    def _():
        for k in range(2, count):
            step(k)
        finish()


def attend(query_t, keyval_t, bias, source, key_value_heads, count, collective):
    width, rows = query_t.shape
    keys = keyval_t.shape[1]
    group = width // HEAD_SIZE // key_value_heads
    kv = key_value_heads
    height, each = source.shape[0], source.shape[1] // count
    return pl.pallas_call(
        functools.partial(attend_kernel, group, count),
        name="attend",
        grid=(kv,),
        in_specs=[
            pl.BlockSpec((group * HEAD_SIZE, rows), lambda h: (h, 0)),
            pl.BlockSpec((HEAD_SIZE, keys), lambda h: (h, 0)),
            pl.BlockSpec((HEAD_SIZE, keys), lambda h: (h + kv, 0)),
            pl.BlockSpec((keys, rows), lambda h: (0, 0)),
            pl.BlockSpec(memory_space=pl.ANY),
        ],
        out_specs=[
            pl.BlockSpec((group * HEAD_SIZE, rows), lambda h: (h, 0)),
            pl.BlockSpec((None, 8, rows), lambda h: (h, 0, 0)),
            pl.BlockSpec((height, each), lambda h: (0, 0)),
        ],
        out_shape=[
            jax.ShapeDtypeStruct((width, rows), bf16),
            jax.ShapeDtypeStruct((kv, 8, rows), f32),
            jax.ShapeDtypeStruct((height, each), f32),
        ],
        scratch_shapes=line_sum_scratch(count, height, each),
        compiler_params=pltpu.CompilerParams(
            vmem_limit_bytes=56 << 20,
            dimension_semantics=("arbitrary",),
            collective_id=collective,
            has_side_effects=True,
        ),
    )(query_t, keyval_t, keyval_t, bias, source)


def attend_back(query_t, keyval_t, bias, out_t, log_total, grad_t, source, key_value_heads, count, collective):
    width, rows = query_t.shape
    keys = keyval_t.shape[1]
    group = width // HEAD_SIZE // key_value_heads
    kv = key_value_heads
    wide = pl.BlockSpec((group * HEAD_SIZE, rows), lambda h: (h, 0))
    head = pl.BlockSpec((HEAD_SIZE, keys), lambda h: (h, 0))
    anywhere = pl.BlockSpec(memory_space=pl.ANY)
    return pl.pallas_call(
        functools.partial(attend_back_kernel, group, count),
        name="attend_back",
        grid=(kv,),
        in_specs=[
            wide,
            head,
            pl.BlockSpec((HEAD_SIZE, keys), lambda h: (h + kv, 0)),
            pl.BlockSpec((keys, rows), lambda h: (0, 0)),
            wide,
            pl.BlockSpec((None, 8, rows), lambda h: (h, 0, 0)),
            wide,
            anywhere,
        ],
        out_specs=[wide, pl.BlockSpec((2, HEAD_SIZE, keys), lambda h: (0, h, 0)), anywhere],
        out_shape=[
            jax.ShapeDtypeStruct((width, rows), bf16),
            jax.ShapeDtypeStruct((2, kv * HEAD_SIZE, keys), bf16),
            jax.ShapeDtypeStruct((source.shape[0], source.shape[1] * count), source.dtype),
        ],
        scratch_shapes=line_scratch(count),
        compiler_params=pltpu.CompilerParams(
            vmem_limit_bytes=56 << 20,
            dimension_semantics=("arbitrary",),
            collective_id=collective,
            has_side_effects=True,
        ),
    )(query_t, keyval_t, keyval_t, bias, out_t, log_total, grad_t, source)


def rms_norm(values, gain):
    return values * lax.rsqrt(jnp.mean(values * values, axis=0, keepdims=True) + epsilon) * gain


def rms_back(values, gain, grad):
    scale = lax.rsqrt(jnp.mean(values * values, axis=0, keepdims=True) + epsilon)
    normal = values * scale
    weighted = grad * gain
    back = scale * (weighted - normal * jnp.mean(weighted * normal, axis=0, keepdims=True))
    return back, grad * normal


def dot(left, right, left_dim, right_dim):
    return lax.dot_general(
        left, right, (((left_dim,), (right_dim,)), ((), ())), preferred_element_type=f32
    )


def gather_rows(whole):
    return lax.all_gather(whole, ("fsdp", "ctx"), axis=0, tiled=True)


def by_rows(values):
    return with_layout_constraint(values, Layout((0, 1)))


def scatter_rows(whole):
    return by_rows(
        lax.psum_scatter(by_rows(whole), ("fsdp", "ctx"), scatter_dimension=0, tiled=True)
    )


def send(values, by):
    count = lax.axis_size("tp")
    return lax.ppermute(values, "tp", [(i, (i + by) % count) for i in range(count)])


def permute_gather(own):
    count = lax.axis_size("tp")
    return [own] + [send(own, k) for k in range(1, count)]


def in_order(pieces):
    count, place = lax.axis_size("tp"), lax.axis_index("tp")
    return jnp.concatenate(
        [lax.select_n(lax.rem(place - p + count, count), *pieces) for p in range(count)], axis=1
    )


def permute_sums(values, axis):
    count, place = lax.axis_size("tp"), lax.axis_index("tp")
    each = values.shape[axis] // count
    shares = [
        lax.dynamic_slice_in_dim(values, lax.rem(place + k, count) * each, each, axis)
        for k in range(count)
    ]
    total = shares[0].astype(f32)
    for k in (2, 1, 3):
        total = total + send(shares[k], k).astype(f32)
    return total


def permute_exchange(values):
    count, place = lax.axis_size("tp"), lax.axis_index("tp")
    shares = values.reshape(count, values.shape[0] // count, values.shape[1])
    pieces = [
        lax.dynamic_index_in_dim(shares, lax.rem(place + k, count), 0, False) for k in range(count)
    ]
    return [pieces[0]] + [send(pieces[k], k) for k in range(1, count)]


def cut(values, widths):
    pieces = []
    offset = 0
    for count in widths:
        pieces.append(values[:, offset : offset + count])
        offset = offset + count
    return pieces


def per_device(
    tokens,
    segments,
    cotangent,
    meta_tokens,
    gain_mix,
    query_weight,
    key_value_weight,
    attn_output,
    gain_attn,
    mamba_input,
    mamba_select,
    step_bias,
    decay_log,
    state_skip,
    mamba_output,
    gain_mamba,
    gain_ffn,
    ffn_input,
    ffn_output,
):
    tokens_t, segments, cotangent_t = tokens[0].T, segments[0], cotangent[0].T
    width, rows = tokens_t.shape
    shard = meta_tokens.shape[0]
    tp = lax.axis_size("tp")
    tp_index = lax.axis_index("tp")
    ctx_index = lax.axis_index("ctx")
    span = rows * tp
    query_width = query_weight.shape[1]
    keyval_width = key_value_weight.shape[1]
    heads = keyval_width // (2 * HEAD_SIZE)
    channels = mamba_input.shape[2]
    ff = ffn_input.shape[2] // tp
    ff_wide = -(-ff // 128) * 128
    meta_count = meta_tokens.shape[1]
    window = WIN + rows

    place_of = jnp.arange(HEAD, dtype=jnp.int32)[None]
    head = jnp.pad(mamba_select, ((0, 0), (0, HEAD - 2 * STATE)))
    for k, gain in enumerate((gain_mix, gain_attn, gain_mamba, gain_ffn)):
        head = jnp.where(place_of == 2 * STATE + k, gain[:, None], head)
    first = jnp.concatenate([head] + [mamba_input[:, k] for k in range(3)], axis=1)
    first, second_parts = lax.optimization_barrier(
        (first, (key_value_weight, meta_tokens, query_weight, mamba_output))
    )
    second = jnp.concatenate(second_parts, axis=1)
    first, second, tokens_t = lax.optimization_barrier((first, second, tokens_t))
    first = gather_rows(first)
    second = gather_rows(second)
    tokens_group_t = line_gather(tokens_t, tp, 0)
    late_cotangent_t, tokens_group_t = lax.optimization_barrier((cotangent_t, tokens_group_t))
    cotangent_pieces = permute_gather(late_cotangent_t)

    gain_columns = first[:, 2 * STATE : 2 * STATE + 4]
    keyval_map, meta_full, query_map, state_out_map = cut(
        second, [keyval_width, meta_count, query_width, channels]
    )
    attn_map = gather_rows(attn_output)
    gain_columns = gain_columns.astype(f32)
    mix_gain, attn_gain, mamba_gain, ffn_gain = [gain_columns[:, k : k + 1] for k in range(4)]

    residual = tokens_t.astype(f32)
    residual_group = tokens_group_t.astype(f32)
    normed_t = rms_norm(residual, mix_gain).astype(bf16)
    normed_group_t = rms_norm(residual_group, mix_gain).astype(bf16)
    meta_rows = meta_full.astype(f32)
    meta_normed_t = rms_norm(meta_rows, mix_gain).astype(bf16)

    mixed = dot(normed_group_t, first, 0, 0).astype(bf16)
    seg_current = lax.dynamic_slice_in_dim(segments, ctx_index * span, span, 0)
    seg_earlier = lax.dynamic_slice_in_dim(segments, jnp.maximum(ctx_index - 1, 0) * span, span, 0)
    seg_before = jnp.where(
        ctx_index > 0,
        lax.dynamic_index_in_dim(segments, jnp.maximum(ctx_index * span - 1, 0), 0, False),
        -1,
    )
    side = (
        *scan_aux(seg_current, seg_before),
        step_bias[None],
        jnp.exp(decay_log)[None],
        *scan_tables(),
    )
    skip_row = state_skip[None]
    state_end = end_state(mixed, side)
    state_end, late_up, late_down = lax.optimization_barrier((state_end, ffn_input, ffn_output))
    ffn_shards = [
        lax.dynamic_slice_in_dim(whole, tp_index * ff, ff, 1)
        for whole in (late_up[:, 0], late_up[:, 1], late_down)
    ]
    state_start = lax.ppermute(state_end, "ctx", [(0, 1)])

    query_t = dot(query_map, normed_t, 0, 0).astype(bf16)
    keyval_group_t = dot(keyval_map, normed_group_t, 0, 0).astype(bf16)
    meta_keyval_t = dot(keyval_map, meta_normed_t, 0, 0).astype(bf16)
    earlier_t = lax.ppermute(keyval_group_t, "ctx", [(0, 1)])

    gated, states, state_final = forward_scan(mixed, side, skip_row, state_start)
    third = jnp.concatenate(
        [jnp.pad(piece, ((0, 0), (0, ff_wide - ff))) for piece in ffn_shards] + [attn_output],
        axis=1,
    )
    third, gated, cotangent_pieces[2] = lax.optimization_barrier(
        (third, gated, cotangent_pieces[2])
    )
    third = gather_rows(third)
    mamba_part_t = dot(state_out_map, gated, 1, 1).astype(bf16)
    mamba_part_t, cotangent_pieces[1], cotangent_pieces[3] = lax.optimization_barrier(
        (mamba_part_t, cotangent_pieces[1], cotangent_pieces[3])
    )
    up_map, down_map, attn_map = cut(third, [2 * ff_wide, ff_wide, query_width])

    key_start = span + tp_index * rows - WIN
    keyval_t = jnp.concatenate(
        [
            meta_keyval_t,
            lax.dynamic_slice_in_dim(
                jnp.concatenate([earlier_t, keyval_group_t], axis=1), key_start, window, 1
            ),
        ],
        axis=1,
    )
    query_pos = ctx_index * span + tp_index * rows + jnp.arange(rows, dtype=jnp.int32)
    key_pos = (ctx_index - 1) * span + key_start + jnp.arange(window, dtype=jnp.int32)
    seg_query = lax.dynamic_slice_in_dim(seg_current, tp_index * rows, rows, 0)
    seg_keys = lax.dynamic_slice_in_dim(
        jnp.concatenate([seg_earlier, seg_current]), key_start, window, 0
    )
    keep = (
        (key_pos[:, None] <= query_pos[None, :])
        & (query_pos[None, :] - key_pos[:, None] < WIN)
        & (key_pos[:, None] >= 0)
        & (seg_keys[:, None] == seg_query[None, :])
    )
    bias = jnp.concatenate(
        [jnp.zeros((meta_count, rows), f32), jnp.where(keep, 0.0, masked_score)], axis=0
    )
    cotangent_group_t = in_order(cotangent_pieces)
    attended_t, log_total, mamba_out = attend(
        query_t, keyval_t, bias, mamba_part_t, heads, tp, 3
    )
    attn_out = dot(attn_map, attended_t, 1, 0)

    mid = residual + 0.5 * (rms_norm(attn_out, attn_gain) + rms_norm(mamba_out, mamba_gain))
    ffn_normed_t = rms_norm(mid, ffn_gain).astype(bf16)
    ffn_normed_group_t, gate_up_grad, hidden, ffn_grad_part_t = feed_forward(
        ffn_normed_t, cotangent_group_t, third, ff_wide, tp, 1
    )
    fourth = width // 6 // 16 * 16
    ffn_wide, out_part_t, ffn_normed_grad_t = wide_sum(
        ffn_normed_group_t, cotangent_group_t, gate_up_grad, hidden, third, ffn_grad_part_t, tp, 7
    )
    ffn_columns = scatter_rows(ffn_wide)

    ffn_normed_grad = ffn_normed_grad_t.astype(f32)
    mid_extra, ffn_gain_terms = rms_back(mid, ffn_gain, ffn_normed_grad)
    mid_grad = cotangent_t.astype(f32) + mid_extra
    attn_grad, attn_gain_terms = rms_back(attn_out, attn_gain, 0.5 * mid_grad)
    mamba_grad, mamba_gain_terms = rms_back(mamba_out, mamba_gain, 0.5 * mid_grad)
    attn_grad_t = attn_grad.astype(bf16)
    mamba_grad_t = mamba_grad.astype(bf16)
    attended_grad_t = dot(attn_map, attn_grad_t, 0, 0).astype(bf16)
    query_grad_t, keyval_grad_t, mamba_grad_group_t = attend_back(
        query_t,
        keyval_t,
        bias,
        attended_t,
        log_total,
        attended_grad_t,
        mamba_grad_t,
        heads,
        tp,
        2,
    )
    query_pieces = permute_exchange(query_grad_t)
    keyval_grad_t = keyval_grad_t.reshape(keyval_width, meta_count + window)
    placed = lax.dynamic_update_slice_in_dim(
        jnp.zeros((keyval_width, 2 * span), bf16), keyval_grad_t[:, meta_count:], key_start, 1
    )
    earlier_back = lax.ppermute(placed[:, :span], "ctx", [(1, 0)])
    current = placed[:, span:].astype(f32) + earlier_back.astype(f32)
    keyval_part_t = current.astype(bf16)
    keyval_meta_t = keyval_grad_t[:, :meta_count]
    gated_grad = dot(mamba_grad_group_t, state_out_map, 0, 0)
    adjoint_end, out_head = end_adjoint(
        gated_grad, mixed, side, out_part_t, fourth, tp, 6
    )
    adjoint_end, late_attended_t, late_gated, query_pieces = lax.optimization_barrier(
        (adjoint_end, attended_t, gated, query_pieces)
    )
    adjoint_start = lax.ppermute(adjoint_end, "ctx", [(1, 0)])
    meta_back, meta_terms = rms_back(meta_rows, mix_gain, dot(keyval_map, keyval_meta_t, 1, 0))
    query_columns_t = in_order(query_pieces)
    each = query_width // tp

    def room(count):
        return ((0, -count % 128), (0, 0))

    query_wide = dot(normed_group_t, jnp.pad(query_columns_t, room(each)), 1, 1)
    keyval_wide = dot(normed_group_t, keyval_part_t, 1, 1) + dot(
        meta_normed_t, keyval_meta_t, 1, 1
    )
    early_pieces = [
        dot(attn_grad_t, jnp.pad(late_attended_t, room(query_width)), 1, 1),
        query_wide,
        meta_back,
        keyval_wide,
        dot(mamba_grad_group_t, late_gated, 1, 0),
    ]
    early_wide = by_rows(
        jnp.concatenate([by_rows(piece.astype(bf16)) for piece in early_pieces], axis=1)
    )
    early_columns = scatter_rows(early_wide)
    adjoint_start, early_wide, ffn_columns = lax.optimization_barrier(
        (adjoint_start, early_wide, ffn_columns)
    )
    mix_grad, scan_sums, out_rest = backward_scan(
        gated_grad,
        mixed,
        states,
        side,
        skip_row,
        adjoint_start,
        state_final,
        out_part_t,
        width - fourth,
        tp,
        5,
    )
    layer_out_t = (mid + jnp.concatenate([out_head, out_rest], axis=0)).astype(bf16)
    query_term = dot(query_map, query_grad_t, 1, 0)
    keyval_term = dot(keyval_map, keyval_part_t, 1, 0).astype(bf16)
    normed_grad_part = dot(first, mix_grad, 1, 1) + keyval_term.astype(f32)
    _, group_terms = rms_back(residual_group, mix_gain, normed_grad_part)
    _, query_terms = rms_back(residual, mix_gain, query_term)
    normed_grad_low, mix_grad = lax.optimization_barrier(
        (normed_grad_part.astype(bf16), mix_grad)
    )
    vector_columns = -(-3 * channels // shard)
    vectors = jnp.pad(scan_sums[:3].reshape(-1), (0, vector_columns * shard - 3 * channels))
    vectors = jnp.tile(vectors.reshape(shard, vector_columns), (width // shard, 1))
    tail = [
        (jnp.sum(group_terms, 1) + jnp.sum(meta_terms, 1) + jnp.sum(query_terms, 1))[:, None],
        jnp.sum(attn_gain_terms, 1, keepdims=True),
        jnp.sum(mamba_gain_terms, 1, keepdims=True),
        jnp.sum(ffn_gain_terms, 1, keepdims=True),
        vectors,
    ]
    tail = jnp.concatenate(tail, axis=1)
    tail = jnp.pad(tail, ((0, 0), (2 * STATE, first.shape[1] - 2 * STATE - tail.shape[1])))
    last_wide = by_rows((dot(normed_group_t, mix_grad, 1, 0) + tail).astype(bf16))
    last_wide, early_columns = lax.optimization_barrier((last_wide, early_columns))
    last_columns = scatter_rows(last_wide)
    attn_shares, _, grad_query, _, meta_shares, keyval_shares, grad_mamba_output = cut(
        early_columns,
        [
            query_width,
            -query_width % 128,
            each,
            -each % 128,
            meta_count,
            keyval_width,
            channels,
        ],
    )

    def to_device(values):
        return jnp.swapaxes(values.reshape(shard, tp, values.shape[1] // tp), 0, 1)

    shares = jnp.concatenate(
        [to_device(attn_shares), to_device(keyval_shares), to_device(meta_shares)], axis=2
    )
    normed_grad_low, last_wide, shares = lax.optimization_barrier(
        (normed_grad_low, last_wide, shares)
    )
    grad_attn_output, grad_keyval, grad_meta = cut(
        permute_sums(shares, 0)[0], [each, keyval_width // tp, meta_count // tp]
    )
    normed_grad = line_sum(normed_grad_low, tp, 4) + query_term
    ffn_columns, normed_grad = lax.optimization_barrier((ffn_columns, normed_grad))
    residual_extra, _ = rms_back(residual, mix_gain, normed_grad)
    grad_tokens_t = (mid_grad + residual_extra).astype(bf16)
    grad_gate, grad_up, grad_ffn_output = [
        piece[:, :ff].astype(f32) for piece in cut(ffn_columns, [ff_wide] * 3)
    ]
    grad_ffn_input = jnp.stack([grad_gate, grad_up], axis=1)
    select_shares, gain_shares, grad_vectors = cut(last_columns, [2 * STATE, 4, vector_columns])
    shares = jnp.concatenate(
        [to_device(select_shares), jnp.broadcast_to(gain_shares[None], (tp, shard, 4))], axis=2
    )
    grad_select, grad_gains = cut(permute_sums(shares, 0)[0], [2 * STATE // tp, 4])
    grad_mamba_input = jnp.stack(
        [
            last_columns[:, HEAD + k * channels : HEAD + (k + 1) * channels].astype(f32)
            for k in range(3)
        ],
        axis=1,
    )
    grad_mamba_output, grad_query, grad_vectors = [
        v.astype(f32) for v in (grad_mamba_output, grad_query, grad_vectors)
    ]
    grad_vectors = grad_vectors.reshape(-1)[: 3 * channels].reshape(3, channels)
    return (
        layer_out_t.T[None],
        grad_tokens_t.T[None],
        grad_meta,
        grad_gains[:, 0],
        grad_query,
        grad_keyval,
        grad_attn_output,
        grad_gains[:, 1],
        grad_mamba_input,
        grad_select,
        grad_vectors[0],
        grad_vectors[1],
        grad_vectors[2],
        grad_mamba_output,
        grad_gains[:, 2],
        grad_gains[:, 3],
        grad_ffn_input,
        grad_ffn_output,
    )


def solution(mesh):
    rows = ("fsdp", "ctx")
    in_specs = (
        P("fsdp", ("ctx", "tp"), None),
        P("fsdp", None),
        P("fsdp", ("ctx", "tp"), None),
        P(rows, None),
        P(rows),
        P(rows, None),
        P(rows, None),
        P(rows, None),
        P(rows),
        P(rows, None, "tp"),
        P(rows, None),
        P("tp"),
        P("tp"),
        P("tp"),
        P(rows, "tp"),
        P(rows),
        P(rows),
        P(rows, None, None),
        P(rows, None),
    )
    out_specs = (
        P("fsdp", ("ctx", "tp"), None),
        P("fsdp", ("ctx", "tp"), None),
        P(rows, "tp"),
        P(rows),
        P(rows, "tp"),
        P(rows, "tp"),
        P(rows, "tp"),
        P(rows),
        P(rows, None, "tp"),
        P(rows, "tp"),
        P("tp"),
        P("tp"),
        P("tp"),
        P(rows, "tp"),
        P(rows),
        P(rows),
        P(rows, None, "tp"),
        P(rows, "tp"),
    )
    return jax.shard_map(
        per_device, mesh=mesh, in_specs=in_specs, out_specs=out_specs, check_vma=False
    )
```
